32 devices in a mesh: dp: 4 (over x, core), expert: 8 (over z, y).
Axes of the slice: x: 2, y: 2, z: 4, core: 2. Of those that a mesh axis runs over, the one named last changes fastest.
Arguments:
- hidden_in: bfloat16 [8192, 1024], P(('dp', 'expert')), may hold values from -6 to 6
- d_out: bfloat16 [8192, 1024], P(('dp', 'expert')), may hold values from -6 to 6
- gain_attn: bfloat16 [1024], P('dp'), may hold values from 0.25 to 1.75
- w_qkv: bfloat16 [1024, 2048], P('dp'), may hold values from -0.1875 to 0.1875
- w_o: bfloat16 [1024, 1024], P('dp'), may hold values from -1.5 to 1.5
- gain_moe: bfloat16 [1024], P('dp'), may hold values from 0.25 to 1.75
- w_router: bfloat16 [1024, 16], P('dp'), may hold values from -0.375 to 0.375
- w_in: bfloat16 [16, 1024, 1024], P('expert', 'dp'), may hold values from -0.1875 to 0.1875
- w_out: bfloat16 [16, 512, 1024], P('expert', None, 'dp'), may hold values from -0.75 to 0.75
- seq_lengths: int32 [4, 4], P('dp'), may hold values from 1 to 1024, 2048 in all within a row
- assign: int32 [4, 2048], P('dp', 'expert'), may hold values from 0 to 2047, each once within a row
- routes: int32 [8192, 8], P(('dp', 'expert')), may hold values from 0 to 15, all different within a row; in each aligned block of 256 rows (0 to 255, 256 to 511, ...) at most 192 rows name the same one
Outputs:
- layer_out: bfloat16 [8192, 1024], P(('dp', 'expert'))
- grad_in: float32 [8192, 1024], P(('dp', 'expert'))
- grad_gain_attn: float32 [1024], P('dp')
- grad_w_qkv: float32 [1024, 2048], P('dp')
- grad_w_o: float32 [1024, 1024], P('dp')
- grad_gain_moe: float32 [1024], P('dp')
- grad_w_router: float32 [1024, 16], P('dp')
- grad_w_in: float32 [16, 1024, 1024], P('expert', 'dp')
- grad_w_out: float32 [16, 512, 1024], P('expert', None, 'dp')
The draws below stay inside these ranges and needn't reach their ends.
Inputs may be any that keep to these rules, and one draw needn't show every extreme that they name: `assign`: each row of a batch group's stream positions names every position of the group once. `seq_lengths`: each row holds 4 lengths that sum to 2048; the longest is 1024. `routes`: A token names 8 different experts. Within the rows of one device no expert is named by more than 192 rows, and in every draw some device has an expert named by exactly 192 of its rows.
All inputs are finite; a program needn't handle non-finite values.
Results may differ from the reference program's by a relative error of at most 0.015.
Values may be sent and summed in bfloat16 or wider, within the bound.
A program may use at most 192 MiB of HBM per device.

```python
import math
import jax
import jax.numpy as jnp
import numpy as np
from jax import lax

D = 1024
HEADS = 16
KV_HEADS = 8
HEAD_DIM = 64
FF = 512
TOP = 8
NSEQ = 4
SEQ_MAX = 1024
EXPERTS = 16
GROUP_TOK = 2048
TOK_DEV = 256
TOKENS = 8192
CAP = 192
N_DP = 4
DEVICES = 32


def block_scale(key, extent, cuts, low, top_value):
    level = 1.0
    for position, shards_of in cuts:
        steps = jax.random.uniform(jax.random.fold_in(jax.random.fold_in(key, 6), position), (shards_of,), jnp.float32, low / len(cuts), top_value / len(cuts))
        level = level * jnp.repeat(jnp.exp(steps), extent[position] // shards_of).reshape((-1,) + (1,) * (len(extent) - 1 - position))
    return level


def length_profile(number_of, total, limit, lean):
    loads = [(1 << 20) // math.isqrt(standing ** lean) + 1 for standing in range(2, number_of + 1)]
    surplus, given = total - limit - (number_of - 1), [1] * (number_of - 1)
    while surplus > 0:
        candidates = [i for i in range(number_of - 1) if given[i] < limit]
        pool, budget = sum([loads[i] for i in candidates]), surplus
        for i in candidates:
            more = min(limit - given[i], max(1, budget * loads[i] // pool), surplus)
            given[i] = given[i] + more
            surplus = surplus - more
    return np.array([limit] + given)


def ragged(stream_key, count, total, most, slope):
    if count == 2:
        one = jax.random.randint(stream_key, (), max(1, total - most), min(most, total - 1) + 1)
        return jnp.stack([one, total - one])
    lengths = jnp.asarray(length_profile(count, total, most, slope), jnp.int32)
    pairs = (count - 1) // 2
    donor, taker = lengths[1:1 + 2 * pairs:2], lengths[2:2 + 2 * pairs:2]
    slack = jnp.minimum(donor - 1, most - taker)
    shifted = jax.random.randint(jax.random.fold_in(stream_key, 1), (pairs,), 0, 1 << 20) % (slack + 1)
    lengths = lengths.at[1:1 + 2 * pairs:2].set(donor - shifted).at[2:2 + 2 * pairs:2].set(taker + shifted)
    return lengths[jax.random.permutation(jax.random.fold_in(stream_key, 2), count)]


def deal_out(rng, own, number, rows, count, top, most, lean):
    order = jax.random.permutation(rng, count)
    packed, common = load_shares(count, rows * top, most, lean, True), load_shares(count, rows * top, most, lean, False)
    places = jnp.arange(count)

    def named(sizes, offset_by):
        used = int((sizes > 0).sum())
        fixed = max(1, used // 4)
        shifted = fixed + (places - fixed + offset_by * (used - fixed)) % max(1, count - fixed)
        return jnp.zeros((count,), jnp.int32).at[order[jnp.where(places < fixed, places, shifted)]].set(jnp.asarray(sizes, jnp.int32))

    sizes = jnp.where(number % 4 == 0, named(packed, number // 4), named(common, number - number // 4 - 1))
    mixed = jax.random.permutation(jax.random.fold_in(own, 3), count)
    donor, receiver = mixed[0:count // 2 * 2:2], mixed[1:count // 2 * 2:2]
    slack = jnp.minimum(sizes[donor] - 1, most - sizes[receiver]) // 2
    slack = jnp.where((donor == order[0]) | (receiver == order[0]) | (sizes[receiver] == 0), 0, jnp.maximum(slack, 0))
    shifted = jax.random.randint(jax.random.fold_in(own, 4), (count // 2,), 0, 1 << 20) % (slack + 1)
    sizes = sizes.at[donor].add(-shifted).at[receiver].add(shifted)
    items = jnp.searchsorted(jnp.cumsum(sizes), jnp.arange(rows * top), side="right").astype(jnp.int32)
    grid = items.reshape(top, rows).T
    grid = grid[jax.random.permutation(jax.random.fold_in(own, 1), rows)]
    offset_by = jax.random.randint(jax.random.fold_in(own, 2), (rows, 1), 0, top)
    return jnp.take_along_axis(grid, (jnp.arange(top)[None, :] + offset_by) % top, axis=1)


def load_shares(number_of, total, reach, lean, full):
    portions = [(1 << 20) // math.isqrt(rank ** lean) + 1 for rank in range(1, number_of + 1)]
    largest = reach if full else min(reach, max(-(-total // number_of), total * portions[0] // sum(portions)))
    least = 1 if total - largest >= number_of - 1 else 0
    holding, surplus = [largest] + [least] * (number_of - 1), total - largest - least * (number_of - 1)
    while surplus > 0:
        candidates = [i for i in range(1, number_of) if holding[i] < largest] or [i for i in range(1, number_of) if holding[i] < reach]
        mass, left = sum([portions[i] for i in candidates]), surplus
        for i in candidates:
            addition = min(reach - holding[i], max(1, left * portions[i] // mass), surplus)
            holding[i] = holding[i] + addition
            surplus = surplus - addition
    return np.array(holding)


def scatter_about(rng, dims, deviation, reach, cuts=(), kind=jnp.bfloat16):
    drawn = deviation * jax.random.normal(rng, dims, jnp.float32)
    if cuts:
        drawn = drawn * block_scale(rng, dims, cuts, -0.22, 0.18)
    return jnp.clip(drawn, -reach, reach).astype(kind)


def setup_inputs(seed: int = 0) -> dict:
    key_of = jax.random.split(jax.random.key(seed), 13)
    hidden_in = scatter_about(key_of[0], (TOKENS, D), 1.0, 6.0, ((0, 32),))
    d_out = scatter_about(key_of[1], (TOKENS, D), 1.0, 6.0, ((0, 32),))
    gain_attn = jnp.clip(1.0 + 0.15 * jax.random.normal(key_of[2], (D,), jnp.float32), 0.25, 1.75).astype(jnp.bfloat16)
    w_qkv = scatter_about(key_of[3], (D, (HEADS + 2 * KV_HEADS) * HEAD_DIM), D ** -0.5, 0.1875, ((0, 4),))
    w_o = scatter_about(key_of[4], (HEADS * HEAD_DIM, D), 16 ** -0.5, 1.5, ((0, 4),))
    gain_moe = jnp.clip(1.0 + 0.15 * jax.random.normal(key_of[5], (D,), jnp.float32), 0.25, 1.75).astype(jnp.bfloat16)
    w_router = scatter_about(key_of[6], (D, EXPERTS), (D // 4) ** -0.5, 0.375, ((0, 4),))
    w_in = scatter_about(key_of[7], (EXPERTS, D, 2 * FF), D ** -0.5, 0.1875, ((0, 8), (1, 4)))
    w_out = scatter_about(key_of[8], (EXPERTS, FF, D), (FF // 8) ** -0.5, 0.75, ((0, 8), (2, 4)))
    seq_lengths = jax.vmap(lambda own: ragged(own, NSEQ, GROUP_TOK, SEQ_MAX, 2))(jax.random.split(key_of[9], N_DP)).reshape((N_DP, NSEQ)).astype(jnp.int32)
    assign = jax.vmap(lambda own: jax.random.permutation(own, GROUP_TOK))(jax.random.split(key_of[10], N_DP)).reshape((N_DP, GROUP_TOK)).astype(jnp.int32)
    routes_keys = jax.random.split(jax.random.fold_in(key_of[11], 1), TOKENS // TOK_DEV)
    routes_turns = jax.random.permutation(jax.random.fold_in(key_of[11], 3), TOKENS // TOK_DEV)
    routes = jax.vmap(lambda own, number: deal_out(jax.random.fold_in(key_of[11], 2), own, number, TOK_DEV, EXPERTS, TOP, CAP, 1))(routes_keys, routes_turns).reshape((TOKENS, TOP))
    return {"hidden_in": hidden_in, "d_out": d_out, "gain_attn": gain_attn, "w_qkv": w_qkv, "w_o": w_o, "gain_moe": gain_moe, "w_router": w_router, "w_in": w_in, "w_out": w_out, "seq_lengths": seq_lengths, "assign": assign, "routes": routes}


EPSILON = 1e-06
ROPE_BASE = 10000.0
SCORE_SCALE = 0.015625
MASKED = -1e+30

def rms_norm(values, gain_vec):
    factor = lax.rsqrt(lax.optimization_barrier(jnp.mean(values * values, axis=-1, keepdims=True)) + EPSILON)
    return values * factor * gain_vec

def rounded(values):
    return lax.optimization_barrier(values.astype(jnp.bfloat16))

def rotary_tables(positions):
    half_dim = HEAD_DIM // 2
    exponent = jnp.arange(half_dim).astype(jnp.float32) * (2.0 / HEAD_DIM)
    frequency = ROPE_BASE ** (-exponent)
    angles = positions.astype(jnp.float32)[:, None] * frequency[None, :]
    angles = jnp.concatenate([angles, angles], axis=1)
    return (jnp.cos(angles), jnp.sin(angles))

def rotate(values, cosine_tab, sine_tab):
    half_dim = HEAD_DIM // 2
    turned = jnp.concatenate([-values[..., half_dim:], values[..., :half_dim]], axis=-1)
    return values * cosine_tab[:, None, :] + turned * sine_tab[:, None, :]

def rotate_back(grads, cosine_tab, sine_tab):
    half_dim = HEAD_DIM // 2
    scaled = grads * sine_tab[:, None, :]
    turned = jnp.concatenate([scaled[..., half_dim:], -scaled[..., :half_dim]], axis=-1)
    return grads * cosine_tab[:, None, :] + turned

def stream_info(assigned, seq_lengths):
    seq_ends = jnp.cumsum(seq_lengths).astype(jnp.int32)
    seq_starts = seq_ends - seq_lengths
    seq_id = lax.optimization_barrier(jnp.sum((assigned[:, None] >= seq_ends[None, :]).astype(jnp.int32), axis=1))
    matches = seq_id[:, None] == jnp.arange(seq_lengths.shape[0], dtype=jnp.int32)[None, :]
    start_of = lax.optimization_barrier(jnp.sum(jnp.where(matches, seq_starts[None, :], 0), axis=1))
    return (seq_id, assigned - start_of)

def gate_up_grad(gate_pre, up_pre, d_hidden):
    sigmoid = jax.nn.sigmoid(gate_pre)
    activated = gate_pre * sigmoid
    d_gate = d_hidden * up_pre * sigmoid * (1.0 + gate_pre * (1.0 - sigmoid))
    return jnp.concatenate([d_gate, d_hidden * activated], axis=-1)

def masked_scores(query_blk, key_grp, query_pos, query_seg, key_pos, key_seg):
    scores = jnp.einsum('tgrd,kgd->tgrk', query_blk.astype(jnp.float32), key_grp.astype(jnp.float32)) * SCORE_SCALE
    allowed = (query_seg[:, None] == key_seg[None, :]) & (key_pos[None, :] <= query_pos[:, None])
    return jnp.where(allowed[:, None, None, :], scores, MASKED)

def group_forward(query_grp, key_grp, value_grp, positions, segments):
    query_block = min(512, GROUP_TOK)
    block_count = GROUP_TOK // query_block
    groups = HEADS // KV_HEADS
    value_wide = value_grp.astype(jnp.float32)

    def one_block(inputs):
        query_blk, block_pos, block_seg = inputs
        scores = masked_scores(query_blk, key_grp, block_pos, block_seg, positions, segments)
        row_max = lax.optimization_barrier(jnp.max(scores, axis=-1))
        log_total = row_max + jnp.log(lax.optimization_barrier(jnp.sum(jnp.exp(scores - row_max[..., None]), axis=-1)))
        soft_weights = rounded(jnp.exp(scores - log_total[..., None])).astype(jnp.float32)
        attended = jnp.einsum('tgrk,kgd->tgrd', soft_weights, value_wide).astype(jnp.bfloat16)
        return (attended, log_total)
    attended, log_total = lax.map(one_block, (query_grp.reshape(block_count, query_block, KV_HEADS, groups, HEAD_DIM), positions.reshape(block_count, query_block), segments.reshape(block_count, query_block)))
    return (attended.reshape(GROUP_TOK, KV_HEADS, groups, HEAD_DIM), log_total.reshape(GROUP_TOK, KV_HEADS, groups))

def group_backward(query_grp, key_grp, value_grp, positions, segments, attended, log_total, d_attended):
    query_block = min(512, GROUP_TOK)
    block_count = GROUP_TOK // query_block
    groups = HEADS // KV_HEADS
    key_wide = key_grp.astype(jnp.float32)
    value_wide = value_grp.astype(jnp.float32)

    def one_block(running, inputs):
        key_acc, value_acc = running
        query_blk, block_pos, block_seg, attended_blk, total_blk, grad_blk = inputs
        scores = masked_scores(query_blk, key_grp, block_pos, block_seg, positions, segments)
        soft_exact = jnp.exp(scores - total_blk[..., None])
        soft_round = rounded(soft_exact).astype(jnp.float32)
        grad_wide = grad_blk.astype(jnp.float32)
        row_delta = lax.optimization_barrier(jnp.sum(grad_wide * attended_blk.astype(jnp.float32), axis=-1))
        d_soft = jnp.einsum('tgrd,kgd->tgrk', grad_wide, value_wide)
        d_scores = rounded(soft_exact * (d_soft - row_delta[..., None])).astype(jnp.float32)
        d_query = jnp.einsum('tgrk,kgd->tgrd', d_scores, key_wide) * SCORE_SCALE
        key_acc = key_acc + jnp.einsum('tgrk,tgrd->kgd', d_scores, query_blk.astype(jnp.float32)) * SCORE_SCALE
        value_acc = value_acc + jnp.einsum('tgrk,tgrd->kgd', soft_round, grad_wide)
        return ((key_acc, value_acc), d_query)
    start_acc = jnp.zeros((GROUP_TOK, KV_HEADS, HEAD_DIM), jnp.float32)
    shape_q = (block_count, query_block, KV_HEADS, groups, HEAD_DIM)
    (key_acc, value_acc), d_query = lax.scan(one_block, (start_acc, start_acc), (query_grp.reshape(shape_q), positions.reshape(block_count, query_block), segments.reshape(block_count, query_block), attended.reshape(shape_q), log_total.reshape(block_count, query_block, KV_HEADS, groups), d_attended.reshape(shape_q)))
    return (d_query.reshape(GROUP_TOK, HEADS, HEAD_DIM), key_acc, value_acc)

def reference(hidden_in, d_out, gain_attn, w_qkv, w_o, gain_moe, w_router, w_in, w_out, seq_lengths, assign, routes):
    groups = HEADS // KV_HEADS
    q_cols = HEADS * HEAD_DIM
    k_cols = KV_HEADS * HEAD_DIM
    stream_in = hidden_in.astype(jnp.float32)
    gain_one = gain_attn.astype(jnp.float32)
    gain_two = gain_moe.astype(jnp.float32)
    normed_one = rms_norm(stream_in, gain_one).astype(jnp.bfloat16)
    projected = jnp.dot(normed_one, w_qkv, preferred_element_type=jnp.float32)
    segments, rot_pos = jax.vmap(stream_info)(assign, seq_lengths)
    cosine_tab, sine_tab = rotary_tables(rot_pos.reshape(TOKENS))
    query_rot = rotate(projected[:, :q_cols].reshape(TOKENS, HEADS, HEAD_DIM), cosine_tab, sine_tab).astype(jnp.bfloat16)
    key_rot = rotate(projected[:, q_cols:q_cols + k_cols].reshape(TOKENS, KV_HEADS, HEAD_DIM), cosine_tab, sine_tab).astype(jnp.bfloat16)
    value_all = projected[:, q_cols + k_cols:].astype(jnp.bfloat16).reshape(TOKENS, KV_HEADS, HEAD_DIM)
    shape_q = (N_DP, GROUP_TOK, KV_HEADS, groups, HEAD_DIM)
    shape_k = (N_DP, GROUP_TOK, KV_HEADS, HEAD_DIM)
    query_groups = query_rot.reshape(shape_q)
    key_groups = key_rot.reshape(shape_k)
    value_groups = value_all.reshape(shape_k)

    def forward_group(inputs):
        return group_forward(*inputs)
    attended, log_total = lax.map(forward_group, (query_groups, key_groups, value_groups, assign, segments))
    attended_flat = attended.reshape(TOKENS, q_cols)
    mid_stream = stream_in + jnp.dot(attended_flat, w_o, preferred_element_type=jnp.float32)
    normed_two = rms_norm(mid_stream, gain_two).astype(jnp.bfloat16)
    logits = jnp.dot(normed_two, w_router, preferred_element_type=jnp.float32)
    gate_probs = jax.nn.softmax(jnp.take_along_axis(logits, routes, axis=1), axis=1)
    route_hits = (routes[:, :, None] == jnp.arange(EXPERTS, dtype=jnp.int32)[None, None, :]).astype(jnp.int32)
    per_row = lax.optimization_barrier(jnp.sum(route_hits, axis=1)).reshape(DEVICES, TOK_DEV, EXPERTS)
    before = (jnp.cumsum(per_row, axis=1) - per_row).reshape(TOKENS, EXPERTS)
    slot_of = lax.optimization_barrier(jnp.sum(route_hits * before[:, None, :], axis=2))
    rows_per = DEVICES * CAP
    device_of = (jnp.arange(TOKENS, dtype=jnp.int32) // TOK_DEV)[:, None]
    target = (routes * rows_per + device_of * CAP + slot_of).reshape(-1)
    token_of = jnp.broadcast_to(jnp.arange(TOKENS, dtype=jnp.int32)[:, None], (TOKENS, TOP)).reshape(-1)
    row_table = jnp.full((EXPERTS * rows_per,), TOKENS, jnp.int32).at[target].set(token_of).reshape(EXPERTS, rows_per)
    gate_table = jnp.zeros((EXPERTS * rows_per,), jnp.float32).at[target].set(gate_probs.reshape(-1)).reshape(EXPERTS, rows_per)
    normed_pad = jnp.concatenate([normed_two, jnp.zeros((1, D), jnp.bfloat16)], axis=0)
    cotangent = d_out.astype(jnp.float32)
    cotangent_pad = jnp.concatenate([cotangent, jnp.zeros((1, D), jnp.float32)], axis=0)

    def expert_step(running, inputs):
        moe_acc, back_acc = running
        row_ids, gate_rows, weight_in, weight_out = inputs
        rows_in = normed_pad[row_ids]
        gate_up = jnp.dot(rows_in, weight_in, preferred_element_type=jnp.float32)
        gate_pre = gate_up[:, :FF]
        up_pre = gate_up[:, FF:]
        hidden = (jax.nn.silu(gate_pre) * up_pre).astype(jnp.bfloat16)
        expert_y = rounded(jnp.dot(hidden, weight_out, preferred_element_type=jnp.float32)).astype(jnp.float32)
        moe_acc = moe_acc.at[row_ids].add(gate_rows[:, None] * expert_y)
        cot_rows = cotangent_pad[row_ids]
        d_gate_rows = lax.optimization_barrier(jnp.sum(cot_rows * expert_y, axis=1))
        d_y = (gate_rows[:, None] * cot_rows).astype(jnp.bfloat16)
        d_hidden = jnp.dot(d_y, weight_out.T, preferred_element_type=jnp.float32)
        grad_out_e = jnp.dot(hidden.T, d_y, preferred_element_type=jnp.float32)
        d_gate_up = gate_up_grad(gate_pre, up_pre, d_hidden).astype(jnp.bfloat16)
        grad_in_e = jnp.dot(rows_in.T, d_gate_up, preferred_element_type=jnp.float32)
        d_slot = rounded(jnp.dot(d_gate_up, weight_in.T, preferred_element_type=jnp.float32)).astype(jnp.float32)
        back_acc = back_acc.at[row_ids].add(d_slot)
        return ((moe_acc, back_acc), (d_gate_rows, grad_in_e, grad_out_e))
    zeros_pad = jnp.zeros((TOKENS + 1, D), jnp.float32)
    (moe_acc, back_acc), (d_gate_tab, grad_w_in, grad_w_out) = lax.scan(expert_step, (zeros_pad, zeros_pad), (row_table, gate_table, w_in, w_out))
    layer_out = (mid_stream + moe_acc[:TOKENS]).astype(jnp.bfloat16)
    d_gate = d_gate_tab.reshape(-1)[target].reshape(TOKENS, TOP)
    d_chosen = gate_probs * (d_gate - lax.optimization_barrier(jnp.sum(gate_probs * d_gate, axis=1, keepdims=True)))
    d_logits = rounded(jnp.einsum('tj,tje->te', d_chosen, route_hits.astype(jnp.float32)))
    grad_w_router = jnp.dot(normed_two.T, d_logits, preferred_element_type=jnp.float32)
    d_normed_two = back_acc[:TOKENS] + jnp.dot(d_logits, w_router.T, preferred_element_type=jnp.float32)
    norm_two_out, norm_two_back = jax.vjp(rms_norm, mid_stream, gain_two)
    d_mid_norm, grad_gain_moe = norm_two_back(d_normed_two)
    d_mid = cotangent + d_mid_norm
    d_attn = d_mid.astype(jnp.bfloat16)
    grad_w_o = jnp.dot(attended_flat.T, d_attn, preferred_element_type=jnp.float32)
    d_attended = jnp.dot(d_attn, w_o.T, preferred_element_type=jnp.float32).astype(jnp.bfloat16)

    def backward_group(inputs):
        return group_backward(*inputs)
    d_query, d_key, d_value = lax.map(backward_group, (query_groups, key_groups, value_groups, assign, segments, attended, log_total, d_attended.reshape(shape_q)))
    dq_pre = rotate_back(d_query.reshape(TOKENS, HEADS, HEAD_DIM), cosine_tab, sine_tab)
    dk_pre = rotate_back(d_key.reshape(TOKENS, KV_HEADS, HEAD_DIM), cosine_tab, sine_tab)
    d_projected = jnp.concatenate([dq_pre.reshape(TOKENS, q_cols), dk_pre.reshape(TOKENS, k_cols), d_value.reshape(TOKENS, k_cols)], axis=1).astype(jnp.bfloat16)
    grad_w_qkv = jnp.dot(normed_one.T, d_projected, preferred_element_type=jnp.float32)
    d_normed_one = jnp.dot(d_projected, w_qkv.T, preferred_element_type=jnp.float32)
    norm_one_out, norm_one_back = jax.vjp(rms_norm, stream_in, gain_one)
    d_in_norm, grad_gain_attn = norm_one_back(d_normed_one)
    grad_in = d_mid + d_in_norm
    return (layer_out, grad_in, grad_gain_attn, grad_w_qkv, grad_w_o, grad_gain_moe, grad_w_router, grad_w_in, grad_w_out)
```

```python
import jax
import jax.numpy as jnp
from jax import lax
from jax.experimental import pallas as pl
from jax.experimental.pallas import tpu as pltpu
from jax.sharding import PartitionSpec as P

HEADS = 16
KV_HEADS = 8
HEAD_DIM = 64
GROUPS = HEADS // KV_HEADS
EPSILON = 1e-06
ROPE_BASE = 10000.0
SCORE_SCALE = 0.015625
MASKED = -1e30
F32 = jnp.float32
BF16 = jnp.bfloat16
Q_TILE = 256
K_TILE = 256


def rms_norm(values, gain_vec):
    factor = lax.rsqrt(jnp.mean(values * values, axis=-1, keepdims=True) + EPSILON)
    return values * factor * gain_vec


def dot(left, right, left_dim=1, right_dim=0):
    return lax.dot_general(
        left, right, (((left_dim,), (right_dim,)), ((), ())), preferred_element_type=F32
    )


def rotate(values, cosine, sine):
    half = HEAD_DIM // 2
    one, two = values[:half], values[half:]
    return jnp.concatenate([one * cosine - two * sine, two * cosine + one * sine], axis=0)


def rotate_back(grads, cosine, sine):
    half = HEAD_DIM // 2
    one, two = grads[:half], grads[half:]
    return jnp.concatenate([one * cosine + two * sine, two * cosine - one * sine], axis=0)


def attend_kernel(low, high, key_pos, query, key, value_t, out, lse, score_buf, weight_buf):
    heads = query.shape[0]
    low_row, high_row = low[...], high[...]
    steps = key.shape[0] // K_TILE

    def score_step(step, maxima):
        rows = pl.ds(pl.multiple_of(step * K_TILE, K_TILE), K_TILE)
        at = key_pos[rows, :]
        allowed = (at >= low_row) & (at <= high_row)
        found = []
        for head in range(heads):
            scores = jnp.dot(key[rows, :], query[head], preferred_element_type=F32)
            scores = jnp.where(allowed, scores, MASKED)
            score_buf[head, rows, :] = scores
            found.append(jnp.maximum(maxima[head], jnp.max(scores, axis=0, keepdims=True)))
        return tuple(found)

    start = tuple(jnp.full(low_row.shape, MASKED, F32) for _ in range(heads))
    maxima = lax.fori_loop(0, steps, score_step, start)

    def weight_step(step, totals):
        rows = pl.ds(pl.multiple_of(step * K_TILE, K_TILE), K_TILE)
        found = []
        for head in range(heads):
            weights = jnp.exp(score_buf[head, rows, :] - maxima[head])
            weight_buf[head, rows, :] = weights.astype(BF16)
            found.append(totals[head] + jnp.sum(weights, axis=0, keepdims=True))
        return tuple(found)

    start = tuple(jnp.zeros(low_row.shape, F32) for _ in range(heads))
    totals = lax.fori_loop(0, steps, weight_step, start)
    for head in range(heads):
        summed = jnp.dot(value_t[...], weight_buf[head], preferred_element_type=F32)
        out[head] = (summed / totals[head]).astype(BF16)
        lse[head] = maxima[head] + jnp.log(totals[head])


def attend(low, high, key_pos, query, key, value_t):
    heads, width, rows = query.shape
    tile = low_tile(rows)
    whole = lambda i: (0, 0)
    lane = lambda i: (0, i)
    return pl.pallas_call(
        attend_kernel,
        grid=(rows // tile,),
        in_specs=[
            pl.BlockSpec((1, tile), lane),
            pl.BlockSpec((1, tile), lane),
            pl.BlockSpec((rows, tile), whole),
            pl.BlockSpec((heads, width, tile), lambda i: (0, 0, i)),
            pl.BlockSpec((rows, width), whole),
            pl.BlockSpec((width, rows), whole),
        ],
        out_specs=[
            pl.BlockSpec((heads, width, tile), lambda i: (0, 0, i)),
            pl.BlockSpec((heads, 1, tile), lambda i: (0, 0, i)),
        ],
        out_shape=[
            jax.ShapeDtypeStruct((heads, width, rows), BF16),
            jax.ShapeDtypeStruct((heads, 1, rows), F32),
        ],
        scratch_shapes=[
            pltpu.VMEM((heads, rows, tile), F32),
            pltpu.VMEM((heads, rows, tile), BF16),
        ],
        cost_estimate=pl.CostEstimate(
            flops=4 * heads * rows * rows * 256,
            bytes_accessed=8 * rows * 256,
            transcendentals=heads * rows * rows,
        ),
        name="attend",
    )(low, high, key_pos, query, key, value_t)


def low_tile(rows):
    return min(Q_TILE, rows)


def attend_back_kernel(
    low, high, key_pos, query, query_n, key, key_t, value, grad, grad_n, lse, delta,
    d_query, d_key, d_value, score_buf,
):
    heads = query.shape[0]
    low_row, high_row = low[...], high[...]
    steps = key.shape[0] // K_TILE

    @pl.when(pl.program_id(0) == 0)
    def _():
        d_key[...] = jnp.zeros_like(d_key)
        d_value[...] = jnp.zeros_like(d_value)

    @pl.loop(0, steps)
    def _(step):
        rows = pl.ds(pl.multiple_of(step * K_TILE, K_TILE), K_TILE)
        at = key_pos[rows, :]
        allowed = (at >= low_row) & (at <= high_row)
        key_sum, value_sum = d_key[rows, :], d_value[rows, :]
        for head in range(heads):
            scores = jnp.dot(key[rows, :], query[head], preferred_element_type=F32)
            weights = jnp.exp(jnp.where(allowed, scores - lse[head], MASKED))
            d_soft = jnp.dot(value[rows, :], grad[head], preferred_element_type=F32)
            d_scores = (weights * (d_soft - delta[head])).astype(BF16)
            score_buf[head, rows, :] = d_scores
            key_sum += jnp.dot(d_scores, query_n[head], preferred_element_type=F32)
            value_sum += jnp.dot(weights.astype(BF16), grad_n[head], preferred_element_type=F32)
        d_key[rows, :] = key_sum
        d_value[rows, :] = value_sum

    for head in range(heads):
        d_query[head] = jnp.dot(key_t[...], score_buf[head], preferred_element_type=F32)


def attend_back(
    low, high, key_pos, query, query_n, key, key_t, value, grad, grad_n, lse, delta
):
    heads, width, rows = query.shape
    tile = low_tile(rows)
    whole = lambda i: (0, 0)
    lane = lambda i: (0, i)
    wide = pl.BlockSpec((heads, width, tile), lambda i: (0, 0, i))
    tall = pl.BlockSpec((heads, tile, width), lambda i: (0, i, 0))
    row = pl.BlockSpec((heads, 1, tile), lambda i: (0, 0, i))
    keys = pl.BlockSpec((rows, width), whole)
    return pl.pallas_call(
        attend_back_kernel,
        grid=(rows // tile,),
        in_specs=[
            pl.BlockSpec((1, tile), lane),
            pl.BlockSpec((1, tile), lane),
            pl.BlockSpec((rows, tile), whole),
            wide, tall, keys, pl.BlockSpec((width, rows), whole), keys, wide, tall, row, row,
        ],
        out_specs=[wide, keys, keys],
        out_shape=[
            jax.ShapeDtypeStruct((heads, width, rows), F32),
            jax.ShapeDtypeStruct((rows, width), F32),
            jax.ShapeDtypeStruct((rows, width), F32),
        ],
        scratch_shapes=[pltpu.VMEM((heads, rows, tile), BF16)],
        cost_estimate=pl.CostEstimate(
            flops=10 * heads * rows * rows * 256,
            bytes_accessed=8 * rows * 256,
            transcendentals=heads * rows * rows,
        ),
        name="attend_back",
    )(low, high, key_pos, query, query_n, key, key_t, value, grad, grad_n, lse, delta)


def gather(values, name, axis=0):
    return lax.all_gather(values, name, axis=axis, tiled=True)


def exchange(values, name="expert"):
    return lax.all_to_all(values, name, split_axis=0, concat_axis=0, tiled=True)


def give_back(partial):
    return lax.psum_scatter(
        partial.astype(BF16), "expert", scatter_dimension=0, tiled=True
    ).astype(F32)


def local(
    hidden_in, d_out, gain_attn, w_qkv, w_o, gain_moe, w_router, w_in, w_out,
    seq_lengths, assign, routes,
):
    tok_rows, width = hidden_in.shape
    exp_dev, _, ff_two = w_in.shape
    ff = ff_two // 2
    n_expert = lax.axis_size("expert")
    me = lax.axis_index("expert")
    experts = exp_dev * n_expert
    group_rows = tok_rows * n_expert
    q_per = HEADS // n_expert
    share = GROUPS // q_per
    q_cols = q_per * HEAD_DIM
    k_base = HEADS * HEAD_DIM
    v_base = k_base + KV_HEADS * HEAD_DIM
    cols = q_cols + 2 * HEAD_DIM

    pack = gather(
        jnp.concatenate([gain_attn[None], gain_moe[None], w_router.T], axis=0), "dp", axis=1
    )
    gain_one, gain_two = pack[0].astype(F32), pack[1].astype(F32)
    router_t = pack[2:]
    kv_head = (me * q_per) // GROUPS
    w_heads = gather(
        jnp.concatenate(
            [
                lax.dynamic_slice_in_dim(w_qkv, me * q_cols, q_cols, 1),
                lax.dynamic_slice_in_dim(w_qkv, k_base + kv_head * HEAD_DIM, HEAD_DIM, 1),
                lax.dynamic_slice_in_dim(w_qkv, v_base + kv_head * HEAD_DIM, HEAD_DIM, 1),
            ],
            axis=1,
        ),
        "dp",
    )
    stream_in = hidden_in.astype(F32)
    normed_one = rms_norm(stream_in, gain_one).astype(BF16)
    normed_all = gather(normed_one, "expert")
    position = gather(assign[0], "expert")
    proj_full = gather(w_o, "dp")
    weight_in = gather(w_in, "dp", axis=1)
    d_out_all = gather(d_out, "expert")
    routes_all = gather(routes, "expert")
    weight_out = gather(w_out, "dp", axis=2)
    pieces = []
    for dev in range(n_expert):
        head = (dev * q_per) // GROUPS * HEAD_DIM
        pieces += [
            w_qkv[:, dev * q_cols : (dev + 1) * q_cols],
            w_qkv[:, k_base + head : k_base + head + HEAD_DIM],
            w_qkv[:, v_base + head : v_base + head + HEAD_DIM],
        ]
    qkv_full = gather(jnp.concatenate(pieces, axis=1), "dp")

    lengths = seq_lengths[0]
    order = jnp.arange(lengths.shape[0], dtype=jnp.int32)
    ends = jnp.sum(jnp.where(order[None, :] <= order[:, None], lengths[None, :], 0), axis=1)
    starts = ends - lengths
    seq_id = jnp.sum((position[None, :] >= ends[:, None]).astype(jnp.int32), axis=0)
    picks = seq_id[None, :] == jnp.arange(lengths.shape[0], dtype=jnp.int32)[:, None]
    start_of = jnp.sum(jnp.where(picks, starts[:, None], 0), axis=0)
    rot_pos = position - start_of
    half = HEAD_DIM // 2
    frequency = ROPE_BASE ** (-(jnp.arange(half).astype(F32) * (2.0 / HEAD_DIM)))
    angles = frequency[:, None] * rot_pos.astype(F32)[None, :]
    cosine, sine = jnp.cos(angles), jnp.sin(angles)
    low, high = start_of[None, :], position[None, :]
    key_pos = jnp.broadcast_to(position[:, None], (group_rows, low_tile(group_rows)))

    projected = dot(w_heads, normed_all, 0, 1)
    query = jnp.stack(
        [
            rotate(projected[h * HEAD_DIM : (h + 1) * HEAD_DIM], cosine, sine).astype(BF16)
            for h in range(q_per)
        ]
    ) * jnp.asarray(SCORE_SCALE, BF16)
    key_t = rotate(projected[q_cols : q_cols + HEAD_DIM], cosine, sine).astype(BF16)
    value_t = projected[q_cols + HEAD_DIM :].astype(BF16)
    key, value = key_t.T, value_t.T
    heads_out, lse = attend(low, high, key_pos, query, key, value_t)
    heads_out, weight_in, weight_out = lax.optimization_barrier(
        (heads_out, weight_in, weight_out)
    )
    attended_t = heads_out.reshape(q_cols, group_rows)
    attended = exchange(attended_t.T.reshape(n_expert, tok_rows, q_cols))
    attended = attended.transpose(1, 0, 2).reshape(tok_rows, HEADS * HEAD_DIM)
    mid_stream = stream_in + dot(attended, proj_full)
    normed_two = rms_norm(mid_stream, gain_two).astype(BF16)

    normed_two, d_out_all = lax.optimization_barrier((normed_two, d_out_all))
    rows_all = gather(normed_two, "expert")
    named = jnp.any(
        routes_all[:, :, None] == jnp.arange(experts, dtype=jnp.int32)[None, None, :], axis=1
    )
    gates = jax.nn.softmax(jnp.where(named, dot(rows_all, router_t, 1, 1), -jnp.inf), axis=1)
    mine = lax.dynamic_slice_in_dim(gates, me * exp_dev, exp_dev, 1)
    made, d_rows, gate_cols, grads_in, grads_out = 0.0, 0.0, [], [], []
    for one in range(exp_dev):
        weight = mine[:, one : one + 1]
        d_plain = dot(d_out_all, weight_out[one], 1, 1)
        gate_up = dot(rows_all, weight_in[one])
        gate_pre, up_pre = gate_up[:, :ff], gate_up[:, ff:]
        sigmoid = jax.nn.sigmoid(gate_pre)
        active = gate_pre * sigmoid
        hidden = active * up_pre
        gate_cols.append(jnp.sum(hidden * d_plain, axis=1))
        scaled = (weight * hidden).astype(BF16)
        d_hidden = weight * d_plain
        d_gate_up = jnp.concatenate(
            [
                d_hidden * up_pre * sigmoid * (1.0 + gate_pre * (1.0 - sigmoid)),
                d_hidden * active,
            ],
            axis=1,
        ).astype(BF16)
        d_rows = d_rows + dot(d_gate_up, weight_in[one], 1, 1)
        made = made + dot(scaled, weight_out[one])
        grads_out.append(dot(scaled, d_out_all, 0, 0))
        grads_in.append(dot(rows_all, d_gate_up, 0, 0))
    d_gate = exchange(
        jnp.stack(gate_cols).reshape(exp_dev, n_expert, tok_rows).transpose(1, 0, 2)
    )
    d_gate = d_gate.reshape(experts, tok_rows).T
    d_back = give_back(d_rows)
    grads_in = jnp.stack(grads_in).astype(BF16)
    grads_out = jnp.stack(grads_out).astype(BF16)
    made = made.astype(BF16)
    d_back, grads_in, grads_out, made = lax.optimization_barrier(
        (d_back, grads_in, grads_out, made)
    )

    own_gates = lax.dynamic_slice_in_dim(gates, me * tok_rows, tok_rows, 0)
    d_logits = (
        own_gates * (d_gate - jnp.sum(own_gates * d_gate, axis=1, keepdims=True))
    ).astype(BF16)
    grad_router = dot(d_logits, normed_two, 0, 0)
    d_normed_two = d_back + dot(d_logits, router_t)
    _, norm_two_back = jax.vjp(rms_norm, mid_stream, gain_two)
    d_mid_norm, grad_gain_two = norm_two_back(d_normed_two)
    d_mid = d_out.astype(F32) + d_mid_norm

    d_attn_all = gather(d_mid.astype(BF16), "expert")
    d_attn_all, grads_in, grads_out, made = lax.optimization_barrier(
        (d_attn_all, grads_in, grads_out, made)
    )
    grad_w_in = lax.psum_scatter(grads_in, "dp", scatter_dimension=1, tiled=True).astype(F32)
    grad_w_out = lax.psum_scatter(grads_out, "dp", scatter_dimension=2, tiled=True).astype(F32)
    returned = exchange(made.reshape(n_expert, tok_rows, width))
    layer_out = (mid_stream + jnp.sum(returned.astype(F32), axis=0)).astype(BF16)
    w_o_mine = lax.dynamic_slice_in_dim(proj_full, me * q_cols, q_cols, 0)
    d_heads = dot(w_o_mine, d_attn_all, 1, 1).astype(BF16).reshape(q_per, HEAD_DIM, group_rows)
    delta = jnp.sum(d_heads.astype(F32) * heads_out.astype(F32), axis=1, keepdims=True)
    d_query, d_key, d_value = attend_back(
        low, high, key_pos, query, jnp.swapaxes(query, 1, 2), key, key_t, value,
        d_heads, jnp.swapaxes(d_heads, 1, 2), lse, delta,
    )
    d_projected = jnp.concatenate(
        [rotate_back(d_query[h] * SCORE_SCALE, cosine, sine) for h in range(q_per)]
        + [rotate_back(d_key.T, cosine, sine), d_value.T],
        axis=0,
    ).astype(BF16)
    d_projected = d_projected.T
    d_own = exchange(d_projected.reshape(n_expert, tok_rows, cols))
    d_own = d_own.transpose(1, 0, 2).reshape(tok_rows, n_expert * cols)
    d_normed_one = dot(d_own, qkv_full, 1, 1)
    _, norm_one_back = jax.vjp(rms_norm, stream_in, gain_one)
    d_in_norm, grad_gain_one = norm_one_back(d_normed_one)
    grad_in = d_mid + d_in_norm

    part_o = lax.psum_scatter(
        dot(attended_t, d_attn_all), "dp", scatter_dimension=1, tiled=True
    )
    grad_w_o = lax.all_to_all(
        gather(part_o, "expert"), "dp", split_axis=0, concat_axis=1, tiled=True
    )
    part_qkv = lax.psum_scatter(
        dot(normed_all, d_projected, 0, 0), "dp", scatter_dimension=0, tiled=True
    )
    joined = lax.all_gather(part_qkv, "expert", axis=0)

    def columns(stack):
        return stack.transpose(1, 0, 2).reshape(stack.shape[1], -1)

    def shared(stack):
        return columns(stack.reshape((KV_HEADS, share) + stack.shape[1:]).sum(axis=1))

    grad_w_qkv = jnp.concatenate(
        [
            columns(joined[:, :, :q_cols]),
            shared(joined[:, :, q_cols : q_cols + HEAD_DIM]),
            shared(joined[:, :, q_cols + HEAD_DIM :]),
        ],
        axis=1,
    )
    small = jnp.concatenate([grad_gain_one[None], grad_gain_two[None], grad_router], axis=0)
    small = lax.psum(
        lax.psum_scatter(small, "dp", scatter_dimension=1, tiled=True), "expert"
    )
    return (
        layer_out, grad_in, small[0], grad_w_qkv, grad_w_o, small[1], small[2:].T,
        grad_w_in, grad_w_out,
    )


def solution(mesh):
    rows = P(("dp", "expert"), None)
    in_specs = (
        rows, rows, P("dp"), P("dp", None), P("dp", None), P("dp"), P("dp", None),
        P("expert", "dp", None), P("expert", None, "dp"), P("dp", None), P("dp", "expert"), rows,
    )
    out_specs = (
        rows, rows, P("dp"), P("dp", None), P("dp", None), P("dp"), P("dp", None),
        P("expert", "dp", None), P("expert", None, "dp"),
    )
    return jax.shard_map(local, mesh=mesh, in_specs=in_specs, out_specs=out_specs, check_vma=False)
```

```python
import functools

import jax
import jax.numpy as jnp
from jax import lax
from jax.experimental import pallas as pl
from jax.experimental.pallas import tpu as pltpu
from jax.sharding import PartitionSpec as P

HEADS = 16
KV_HEADS = 8
HEAD_DIM = 64
GROUPS = HEADS // KV_HEADS
EPSILON = 1e-06
ROPE_BASE = 10000.0
SCORE_SCALE = 0.015625
MASKED = -1e30
F32 = jnp.float32
BF16 = jnp.bfloat16
Q_TILE = 256
K_TILE = 256


MESH = pl.DeviceIdType.MESH
Z_SIZE = 4

def grid_of(n_expert):
    nz = Z_SIZE if n_expert % Z_SIZE == 0 else 1
    return nz, n_expert // nz

def places(nz, ny):
    me = lax.axis_index("expert")
    return me // ny, lax.rem(me, ny)

def device(z, y, nz, ny):
    return lax.rem(z + 2 * nz, nz) * ny + lax.rem(y + 2 * ny, ny)

def greet(nz, ny, z, y):
    barrier = pltpu.get_barrier_semaphore()
    near = []
    for step in sorted({1, nz - 1} - {0}):
        near.append(device(z + step, y, nz, ny))
    for step in sorted({1, ny - 1} - {0}):
        near.append(device(z, y + step, nz, ny))
    for other in near:
        pl.semaphore_signal(barrier, inc=1, device_id={"expert": other}, device_id_type=MESH)
    pl.semaphore_wait(barrier, len(near))

def gather_kernel(nz, ny, own, out, local_sem, send_sem, recv_sem):
    z, y = places(nz, ny)
    rows = own.shape[0]
    half = rows // 2
    greet(nz, ny, z, y)

    def piece(s, t, h):
        sign = -1 if h == 0 else 1
        start = device(z + sign * s, y + sign * t, nz, ny) * rows + h * half
        return pl.ds(pl.multiple_of(start, half), half)

    def copy(s, t, h, s2, t2):
        step = 1 if h == 0 else -1
        source = own.at[pl.ds(h * half, half)] if s == 0 and t == 0 else out.at[piece(s, t, h)]
        to = device(z + step, y, nz, ny) if t2 == 0 else device(z, y + step, nz, ny)
        return pltpu.make_async_remote_copy(
            src_ref=source, dst_ref=out.at[piece(s, t, h)],
            send_sem=send_sem.at[s2, t2, h], recv_sem=recv_sem.at[s2, t2, h],
            device_id={"expert": to}, device_id_type=MESH)

    def arrival(s, t, h):
        return pltpu.make_async_remote_copy(
            src_ref=out.at[piece(s, t, h)], dst_ref=out.at[piece(s, t, h)],
            send_sem=send_sem.at[s, t, h], recv_sem=recv_sem.at[s, t, h],
            device_id={"expert": device(z, y, nz, ny)}, device_id_type=MESH)

    mine = pltpu.make_async_copy(own, out.at[pl.ds(pl.multiple_of(device(z, y, nz, ny) * rows, rows), rows)], local_sem)
    started = []
    def start(*key):
        c = copy(*key); c.start(); started.append(c)
    for h in range(2):
        start(0, 0, h, 1, 0)
    if ny > 1:
        for h in range(2):
            start(0, 0, h, 0, 1)
    mine.start()
    for s in range(1, nz):
        for h in range(2):
            arrival(s, 0, h).wait_recv()
            if s + 1 < nz:
                start(s, 0, h, s + 1, 0)
            if ny > 1:
                start(s, 0, h, s, 1)
    for t in range(1, ny):
        for s in range(nz):
            for h in range(2):
                arrival(s, t, h).wait_recv()
                if t + 1 < ny:
                    start(s, t, h, s, t + 1)
    mine.wait()
    for c in started:
        c.wait_send()

def all_rows(own, n_expert, cid, name):
    nz, ny = grid_of(n_expert)
    rows, width = own.shape
    return pl.pallas_call(
        functools.partial(gather_kernel, nz, ny),
        out_shape=jax.ShapeDtypeStruct((rows * n_expert, width), own.dtype),
        in_specs=[pl.BlockSpec(memory_space=pl.ANY)],
        out_specs=pl.BlockSpec(memory_space=pl.ANY),
        scratch_shapes=[pltpu.SemaphoreType.DMA, pltpu.SemaphoreType.DMA((nz, ny, 2)), pltpu.SemaphoreType.DMA((nz, ny, 2))],
        compiler_params=pltpu.CompilerParams(collective_id=cid, has_side_effects=True),
        name=name,
    )(own)

def scatter_kernel(nz, ny, whole, out, from_y, from_z, to_y, to_z, send_y, recv_y, send_z, recv_z):
    z, y = places(nz, ny)
    rows = out.shape[0]
    half = rows // 2
    greet(nz, ny, z, y)

    def piece(s, t, h):
        sign = -1 if h == 0 else 1
        start = device(z + sign * (s + 1), y + sign * (t + 1), nz, ny) * rows + h * half
        return pl.ds(pl.multiple_of(start, half), half)

    def y_copy(s, t, h):
        step = 1 if h == 0 else -1
        source = whole.at[piece(s, 0, h)] if t == 0 else to_y.at[s, t - 1, h]
        return pltpu.make_async_remote_copy(
            src_ref=source, dst_ref=from_y.at[s, t, h], send_sem=send_y.at[s, t, h], recv_sem=recv_y.at[s, t, h],
            device_id={"expert": device(z, y + step, nz, ny)}, device_id_type=MESH)

    def z_copy(s, h):
        step = 1 if h == 0 else -1
        return pltpu.make_async_remote_copy(
            src_ref=to_z.at[s, h], dst_ref=from_z.at[s, h], send_sem=send_z.at[s, h], recv_sem=recv_z.at[s, h],
            device_id={"expert": device(z + step, y, nz, ny)}, device_id_type=MESH)

    if ny > 1:
        for s in range(nz):
            for h in range(2):
                y_copy(s, 0, h).start()
    for s in range(nz):
        for t in range(1, ny - 1):
            for h in range(2):
                y_copy(s, t - 1, h).wait_recv()
                to_y[s, t - 1, h] = (whole[piece(s, t, h), :].astype(F32) + from_y[s, t - 1, h].astype(F32)).astype(BF16)
                y_copy(s, t, h).start()
        for h in range(2):
            total = whole[piece(s, ny - 1, h), :].astype(F32)
            if ny > 1:
                y_copy(s, ny - 2, h).wait_recv()
                total += from_y[s, ny - 2, h].astype(F32)
            if s > 0:
                z_copy(s - 1, h).wait_recv()
                total += from_z[s - 1, h].astype(F32)
            if s < nz - 1:
                to_z[s, h] = total.astype(BF16)
                z_copy(s, h).start()
            else:
                out[h * half : (h + 1) * half, :] = total
    for s in range(nz):
        for h in range(2):
            for t in range(ny - 1):
                y_copy(s, t, h).wait_send()
            if s < nz - 1:
                z_copy(s, h).wait_send()

def own_sum(whole, n_expert, cid, name):
    nz, ny = grid_of(n_expert)
    all_, width = whole.shape
    rows = all_ // n_expert
    half = rows // 2
    D = pltpu.SemaphoreType.DMA
    return pl.pallas_call(
        functools.partial(scatter_kernel, nz, ny),
        out_shape=jax.ShapeDtypeStruct((rows, width), F32),
        in_specs=[pl.BlockSpec(memory_space=pltpu.VMEM)],
        out_specs=pl.BlockSpec(memory_space=pltpu.VMEM),
        scratch_shapes=[
            pltpu.VMEM((nz, max(ny - 1, 1), 2, half, width), BF16),
            pltpu.VMEM((max(nz - 1, 1), 2, half, width), BF16),
            pltpu.VMEM((nz, max(ny - 2, 1), 2, half, width), BF16),
            pltpu.VMEM((max(nz - 1, 1), 2, half, width), BF16),
            D((nz, max(ny - 1, 1), 2)), D((nz, max(ny - 1, 1), 2)), D((max(nz - 1, 1), 2)), D((max(nz - 1, 1), 2))],
        compiler_params=pltpu.CompilerParams(collective_id=cid, has_side_effects=True, vmem_limit_bytes=48 << 20),
        name=name,
    )(whole)


def rms_norm(values, gain_vec):
    factor = lax.rsqrt(jnp.mean(values * values, axis=-1, keepdims=True) + EPSILON)
    return values * factor * gain_vec


def dot(left, right, left_dim=1, right_dim=0):
    return lax.dot_general(
        left, right, (((left_dim,), (right_dim,)), ((), ())), preferred_element_type=F32
    )


def rotate(values, cosine, sine):
    half = HEAD_DIM // 2
    one, two = values[:half], values[half:]
    return jnp.concatenate([one * cosine - two * sine, two * cosine + one * sine], axis=0)


def rotate_back(grads, cosine, sine):
    half = HEAD_DIM // 2
    one, two = grads[:half], grads[half:]
    return jnp.concatenate([one * cosine + two * sine, two * cosine - one * sine], axis=0)


def attend_kernel(low, high, key_pos, query, key, value_t, out, lse, score_buf, weight_buf):
    heads = query.shape[0]
    low_row, high_row = low[...], high[...]
    steps = key.shape[0] // K_TILE

    def score_step(step, maxima):
        rows = pl.ds(pl.multiple_of(step * K_TILE, K_TILE), K_TILE)
        at = key_pos[rows, :]
        allowed = (at >= low_row) & (at <= high_row)
        found = []
        for head in range(heads):
            scores = jnp.dot(key[rows, :], query[head], preferred_element_type=F32)
            scores = jnp.where(allowed, scores, MASKED)
            score_buf[head, rows, :] = scores
            found.append(jnp.maximum(maxima[head], jnp.max(scores, axis=0, keepdims=True)))
        return tuple(found)

    start = tuple(jnp.full(low_row.shape, MASKED, F32) for _ in range(heads))
    maxima = lax.fori_loop(0, steps, score_step, start)

    def weight_step(step, totals):
        rows = pl.ds(pl.multiple_of(step * K_TILE, K_TILE), K_TILE)
        found = []
        for head in range(heads):
            weights = jnp.exp(score_buf[head, rows, :] - maxima[head])
            weight_buf[head, rows, :] = weights.astype(BF16)
            found.append(totals[head] + jnp.sum(weights, axis=0, keepdims=True))
        return tuple(found)

    start = tuple(jnp.zeros(low_row.shape, F32) for _ in range(heads))
    totals = lax.fori_loop(0, steps, weight_step, start)
    for head in range(heads):
        summed = jnp.dot(value_t[...], weight_buf[head], preferred_element_type=F32)
        out[head] = (summed / totals[head]).astype(BF16)
        lse[head] = maxima[head] + jnp.log(totals[head])


def attend(low, high, key_pos, query, key, value_t):
    heads, width, rows = query.shape
    tile = low_tile(rows)
    whole = lambda i: (0, 0)
    lane = lambda i: (0, i)
    return pl.pallas_call(
        attend_kernel,
        grid=(rows // tile,),
        in_specs=[
            pl.BlockSpec((1, tile), lane),
            pl.BlockSpec((1, tile), lane),
            pl.BlockSpec((rows, tile), whole),
            pl.BlockSpec((heads, width, tile), lambda i: (0, 0, i)),
            pl.BlockSpec((rows, width), whole),
            pl.BlockSpec((width, rows), whole),
        ],
        out_specs=[
            pl.BlockSpec((heads, width, tile), lambda i: (0, 0, i)),
            pl.BlockSpec((heads, 1, tile), lambda i: (0, 0, i)),
        ],
        out_shape=[
            jax.ShapeDtypeStruct((heads, width, rows), BF16),
            jax.ShapeDtypeStruct((heads, 1, rows), F32),
        ],
        scratch_shapes=[
            pltpu.VMEM((heads, rows, tile), F32),
            pltpu.VMEM((heads, rows, tile), BF16),
        ],
        cost_estimate=pl.CostEstimate(
            flops=4 * heads * rows * rows * 256,
            bytes_accessed=8 * rows * 256,
            transcendentals=heads * rows * rows,
        ),
        name="attend",
    )(low, high, key_pos, query, key, value_t)


def low_tile(rows):
    return min(Q_TILE, rows)


def attend_back_kernel(
    low, high, key_pos, query, query_n, key, key_t, value, grad, grad_n, lse, delta,
    d_query, d_key, d_value, score_buf,
):
    heads = query.shape[0]
    low_row, high_row = low[...], high[...]
    steps = key.shape[0] // K_TILE

    @pl.when(pl.program_id(0) == 0)
    def _():
        d_key[...] = jnp.zeros_like(d_key)
        d_value[...] = jnp.zeros_like(d_value)

    @pl.loop(0, steps)
    def _(step):
        rows = pl.ds(pl.multiple_of(step * K_TILE, K_TILE), K_TILE)
        at = key_pos[rows, :]
        allowed = (at >= low_row) & (at <= high_row)
        key_sum, value_sum = d_key[rows, :], d_value[rows, :]
        for head in range(heads):
            scores = jnp.dot(key[rows, :], query[head], preferred_element_type=F32)
            weights = jnp.exp(jnp.where(allowed, scores - lse[head], MASKED))
            d_soft = jnp.dot(value[rows, :], grad[head], preferred_element_type=F32)
            d_scores = (weights * (d_soft - delta[head])).astype(BF16)
            score_buf[head, rows, :] = d_scores
            key_sum += jnp.dot(d_scores, query_n[head], preferred_element_type=F32)
            value_sum += jnp.dot(weights.astype(BF16), grad_n[head], preferred_element_type=F32)
        d_key[rows, :] = key_sum
        d_value[rows, :] = value_sum

    for head in range(heads):
        d_query[head] = jnp.dot(key_t[...], score_buf[head], preferred_element_type=F32)


def attend_back(
    low, high, key_pos, query, query_n, key, key_t, value, grad, grad_n, lse, delta
):
    heads, width, rows = query.shape
    tile = low_tile(rows)
    whole = lambda i: (0, 0)
    lane = lambda i: (0, i)
    wide = pl.BlockSpec((heads, width, tile), lambda i: (0, 0, i))
    tall = pl.BlockSpec((heads, tile, width), lambda i: (0, i, 0))
    row = pl.BlockSpec((heads, 1, tile), lambda i: (0, 0, i))
    keys = pl.BlockSpec((rows, width), whole)
    return pl.pallas_call(
        attend_back_kernel,
        grid=(rows // tile,),
        in_specs=[
            pl.BlockSpec((1, tile), lane),
            pl.BlockSpec((1, tile), lane),
            pl.BlockSpec((rows, tile), whole),
            wide, tall, keys, pl.BlockSpec((width, rows), whole), keys, wide, tall, row, row,
        ],
        out_specs=[wide, keys, keys],
        out_shape=[
            jax.ShapeDtypeStruct((heads, width, rows), F32),
            jax.ShapeDtypeStruct((rows, width), F32),
            jax.ShapeDtypeStruct((rows, width), F32),
        ],
        scratch_shapes=[pltpu.VMEM((heads, rows, tile), BF16)],
        cost_estimate=pl.CostEstimate(
            flops=10 * heads * rows * rows * 256,
            bytes_accessed=8 * rows * 256,
            transcendentals=heads * rows * rows,
        ),
        name="attend_back",
    )(low, high, key_pos, query, query_n, key, key_t, value, grad, grad_n, lse, delta)


def gather(values, name, axis=0):
    return lax.all_gather(values, name, axis=axis, tiled=True)


def exchange(values, name="expert"):
    return lax.all_to_all(values, name, split_axis=0, concat_axis=0, tiled=True)


def give_back(partial):
    return lax.psum_scatter(
        partial.astype(BF16), "expert", scatter_dimension=0, tiled=True
    ).astype(F32)


def local(
    hidden_in, d_out, gain_attn, w_qkv, w_o, gain_moe, w_router, w_in, w_out,
    seq_lengths, assign, routes,
):
    tok_rows, width = hidden_in.shape
    exp_dev, _, ff_two = w_in.shape
    ff = ff_two // 2
    n_expert = lax.axis_size("expert")
    me = lax.axis_index("expert")
    experts = exp_dev * n_expert
    group_rows = tok_rows * n_expert
    q_per = HEADS // n_expert
    share = GROUPS // q_per
    q_cols = q_per * HEAD_DIM
    k_base = HEADS * HEAD_DIM
    v_base = k_base + KV_HEADS * HEAD_DIM
    cols = q_cols + 2 * HEAD_DIM

    pack = gather(
        jnp.concatenate([gain_attn[None], gain_moe[None], w_router.T], axis=0), "dp", axis=1
    )
    gain_one, gain_two = pack[0].astype(F32), pack[1].astype(F32)
    router_t = pack[2:]
    kv_head = (me * q_per) // GROUPS
    w_heads = gather(
        jnp.concatenate(
            [
                lax.dynamic_slice_in_dim(w_qkv, me * q_cols, q_cols, 1),
                lax.dynamic_slice_in_dim(w_qkv, k_base + kv_head * HEAD_DIM, HEAD_DIM, 1),
                lax.dynamic_slice_in_dim(w_qkv, v_base + kv_head * HEAD_DIM, HEAD_DIM, 1),
            ],
            axis=1,
        ),
        "dp",
    )
    stream_in = hidden_in.astype(F32)
    normed_one = rms_norm(stream_in, gain_one).astype(BF16)
    normed_all = all_rows(normed_one, n_expert, 0, "gather_one")
    position = gather(assign[0], "expert")
    proj_full = gather(w_o, "dp")
    weight_in = gather(w_in, "dp", axis=1)
    d_out_all = gather(d_out, "expert")
    routes_all = gather(routes, "expert")
    weight_out = gather(w_out, "dp", axis=2)
    pieces = []
    for dev in range(n_expert):
        head = (dev * q_per) // GROUPS * HEAD_DIM
        pieces += [
            w_qkv[:, dev * q_cols : (dev + 1) * q_cols],
            w_qkv[:, k_base + head : k_base + head + HEAD_DIM],
            w_qkv[:, v_base + head : v_base + head + HEAD_DIM],
        ]
    qkv_full = gather(jnp.concatenate(pieces, axis=1), "dp")

    lengths = seq_lengths[0]
    order = jnp.arange(lengths.shape[0], dtype=jnp.int32)
    ends = jnp.sum(jnp.where(order[None, :] <= order[:, None], lengths[None, :], 0), axis=1)
    starts = ends - lengths
    seq_id = jnp.sum((position[None, :] >= ends[:, None]).astype(jnp.int32), axis=0)
    picks = seq_id[None, :] == jnp.arange(lengths.shape[0], dtype=jnp.int32)[:, None]
    start_of = jnp.sum(jnp.where(picks, starts[:, None], 0), axis=0)
    rot_pos = position - start_of
    half = HEAD_DIM // 2
    frequency = ROPE_BASE ** (-(jnp.arange(half).astype(F32) * (2.0 / HEAD_DIM)))
    angles = frequency[:, None] * rot_pos.astype(F32)[None, :]
    cosine, sine = jnp.cos(angles), jnp.sin(angles)
    low, high = start_of[None, :], position[None, :]
    key_pos = jnp.broadcast_to(position[:, None], (group_rows, low_tile(group_rows)))

    projected = dot(w_heads, normed_all, 0, 1)
    query = jnp.stack(
        [
            rotate(projected[h * HEAD_DIM : (h + 1) * HEAD_DIM], cosine, sine).astype(BF16)
            for h in range(q_per)
        ]
    ) * jnp.asarray(SCORE_SCALE, BF16)
    key_t = rotate(projected[q_cols : q_cols + HEAD_DIM], cosine, sine).astype(BF16)
    value_t = projected[q_cols + HEAD_DIM :].astype(BF16)
    key, value = key_t.T, value_t.T
    heads_out, lse = attend(low, high, key_pos, query, key, value_t)
    heads_out, weight_in, weight_out = lax.optimization_barrier(
        (heads_out, weight_in, weight_out)
    )
    attended_t = heads_out.reshape(q_cols, group_rows)
    attended = exchange(attended_t.T.reshape(n_expert, tok_rows, q_cols))
    attended = attended.transpose(1, 0, 2).reshape(tok_rows, HEADS * HEAD_DIM)
    mid_stream = stream_in + dot(attended, proj_full)
    normed_two = rms_norm(mid_stream, gain_two).astype(BF16)

    normed_two, d_out_all = lax.optimization_barrier((normed_two, d_out_all))
    rows_all = all_rows(normed_two, n_expert, 1, "gather_two")
    named = jnp.any(
        routes_all[:, :, None] == jnp.arange(experts, dtype=jnp.int32)[None, None, :], axis=1
    )
    gates = jax.nn.softmax(jnp.where(named, dot(rows_all, router_t, 1, 1), -jnp.inf), axis=1)
    mine = lax.dynamic_slice_in_dim(gates, me * exp_dev, exp_dev, 1)
    made, d_rows, gate_cols, grads_in, grads_out = 0.0, 0.0, [], [], []
    for one in range(exp_dev):
        weight = mine[:, one : one + 1]
        d_plain = dot(d_out_all, weight_out[one], 1, 1)
        gate_up = dot(rows_all, weight_in[one])
        gate_pre, up_pre = gate_up[:, :ff], gate_up[:, ff:]
        sigmoid = jax.nn.sigmoid(gate_pre)
        active = gate_pre * sigmoid
        hidden = active * up_pre
        gate_cols.append(jnp.sum(hidden * d_plain, axis=1))
        scaled = (weight * hidden).astype(BF16)
        d_hidden = weight * d_plain
        d_gate_up = jnp.concatenate(
            [
                d_hidden * up_pre * sigmoid * (1.0 + gate_pre * (1.0 - sigmoid)),
                d_hidden * active,
            ],
            axis=1,
        ).astype(BF16)
        d_rows = d_rows + dot(d_gate_up, weight_in[one], 1, 1)
        made = made + dot(scaled, weight_out[one])
        grads_out.append(dot(scaled, d_out_all, 0, 0))
        grads_in.append(dot(rows_all, d_gate_up, 0, 0))
    d_gate = exchange(
        jnp.stack(gate_cols).reshape(exp_dev, n_expert, tok_rows).transpose(1, 0, 2)
    )
    d_gate = d_gate.reshape(experts, tok_rows).T
    d_back = own_sum(d_rows.astype(BF16), n_expert, 3, "scatter_rows")
    grads_in = jnp.stack(grads_in).astype(BF16)
    grads_out = jnp.stack(grads_out).astype(BF16)
    made = made.astype(BF16)
    d_back, grads_in, grads_out, made = lax.optimization_barrier(
        (d_back, grads_in, grads_out, made)
    )

    own_gates = lax.dynamic_slice_in_dim(gates, me * tok_rows, tok_rows, 0)
    d_logits = (
        own_gates * (d_gate - jnp.sum(own_gates * d_gate, axis=1, keepdims=True))
    ).astype(BF16)
    grad_router = dot(d_logits, normed_two, 0, 0)
    d_normed_two = d_back + dot(d_logits, router_t)
    _, norm_two_back = jax.vjp(rms_norm, mid_stream, gain_two)
    d_mid_norm, grad_gain_two = norm_two_back(d_normed_two)
    d_mid = d_out.astype(F32) + d_mid_norm

    d_attn_all = all_rows(d_mid.astype(BF16), n_expert, 2, "gather_attn")
    d_attn_all, grads_in, grads_out, made = lax.optimization_barrier(
        (d_attn_all, grads_in, grads_out, made)
    )
    grad_w_in = lax.psum_scatter(grads_in, "dp", scatter_dimension=1, tiled=True).astype(F32)
    grad_w_out = lax.psum_scatter(grads_out, "dp", scatter_dimension=2, tiled=True).astype(F32)
    returned = lax.psum_scatter(made, "expert", scatter_dimension=0, tiled=True)
    layer_out = (mid_stream + returned.astype(F32)).astype(BF16)
    w_o_mine = lax.dynamic_slice_in_dim(proj_full, me * q_cols, q_cols, 0)
    d_heads = dot(w_o_mine, d_attn_all, 1, 1).astype(BF16).reshape(q_per, HEAD_DIM, group_rows)
    delta = jnp.sum(d_heads.astype(F32) * heads_out.astype(F32), axis=1, keepdims=True)
    d_query, d_key, d_value = attend_back(
        low, high, key_pos, query, jnp.swapaxes(query, 1, 2), key, key_t, value,
        d_heads, jnp.swapaxes(d_heads, 1, 2), lse, delta,
    )
    d_projected = jnp.concatenate(
        [rotate_back(d_query[h] * SCORE_SCALE, cosine, sine) for h in range(q_per)]
        + [rotate_back(d_key.T, cosine, sine), d_value.T],
        axis=0,
    ).astype(BF16)
    d_projected = d_projected.T
    d_own = exchange(d_projected.reshape(n_expert, tok_rows, cols))
    d_own = d_own.transpose(1, 0, 2).reshape(tok_rows, n_expert * cols)
    d_normed_one = dot(d_own, qkv_full, 1, 1)
    _, norm_one_back = jax.vjp(rms_norm, stream_in, gain_one)
    d_in_norm, grad_gain_one = norm_one_back(d_normed_one)
    grad_in = d_mid + d_in_norm

    part_o = lax.psum_scatter(
        dot(attended_t, d_attn_all), "dp", scatter_dimension=1, tiled=True
    )
    grad_w_o = lax.all_to_all(
        gather(part_o, "expert"), "dp", split_axis=0, concat_axis=1, tiled=True
    )
    part_qkv = lax.psum_scatter(
        dot(normed_all, d_projected, 0, 0), "dp", scatter_dimension=0, tiled=True
    )
    joined = lax.all_gather(part_qkv, "expert", axis=0)

    def columns(stack):
        return stack.transpose(1, 0, 2).reshape(stack.shape[1], -1)

    def shared(stack):
        return columns(stack.reshape((KV_HEADS, share) + stack.shape[1:]).sum(axis=1))

    grad_w_qkv = jnp.concatenate(
        [
            columns(joined[:, :, :q_cols]),
            shared(joined[:, :, q_cols : q_cols + HEAD_DIM]),
            shared(joined[:, :, q_cols + HEAD_DIM :]),
        ],
        axis=1,
    )
    small = jnp.concatenate([grad_gain_one[None], grad_gain_two[None], grad_router], axis=0)
    small = lax.psum(
        lax.psum_scatter(small, "dp", scatter_dimension=1, tiled=True), "expert"
    )
    return (
        layer_out, grad_in, small[0], grad_w_qkv, grad_w_o, small[1], small[2:].T,
        grad_w_in, grad_w_out,
    )


def solution(mesh):
    rows = P(("dp", "expert"), None)
    in_specs = (
        rows, rows, P("dp"), P("dp", None), P("dp", None), P("dp"), P("dp", None),
        P("expert", "dp", None), P("expert", None, "dp"), P("dp", None), P("dp", "expert"), rows,
    )
    out_specs = (
        rows, rows, P("dp"), P("dp", None), P("dp", None), P("dp"), P("dp", None),
        P("expert", "dp", None), P("expert", None, "dp"),
    )
    return jax.shard_map(local, mesh=mesh, in_specs=in_specs, out_specs=out_specs, check_vma=False)
```

```python
import functools

import jax
import jax.numpy as jnp
from jax import lax
from jax.experimental import pallas as pl
from jax.experimental.pallas import tpu as pltpu
from jax.sharding import PartitionSpec as P

HEADS = 16
KV_HEADS = 8
HEAD_DIM = 64
GROUPS = HEADS // KV_HEADS
EPSILON = 1e-06
ROPE_BASE = 10000.0
SCORE_SCALE = 0.015625
MASKED = -1e30
F32 = jnp.float32
BF16 = jnp.bfloat16
Q_TILE = 256
K_TILE = 256


MESH = pl.DeviceIdType.MESH
Z_SIZE = 4

def grid_of(n_expert):
    nz = Z_SIZE if n_expert % Z_SIZE == 0 else 1
    return nz, n_expert // nz

def places(nz, ny):
    me = lax.axis_index("expert")
    return me // ny, lax.rem(me, ny)

def device(z, y, nz, ny):
    return lax.rem(z + 2 * nz, nz) * ny + lax.rem(y + 2 * ny, ny)

def greet(nz, ny, z, y):
    barrier = pltpu.get_barrier_semaphore()
    near = []
    for step in sorted({1, nz - 1} - {0}):
        near.append(device(z + step, y, nz, ny))
    for step in sorted({1, ny - 1} - {0}):
        near.append(device(z, y + step, nz, ny))
    for other in near:
        pl.semaphore_signal(barrier, inc=1, device_id={"expert": other}, device_id_type=MESH)
    pl.semaphore_wait(barrier, len(near))

def gather_kernel(nz, ny, own, out, local_sem, send_sem, recv_sem):
    z, y = places(nz, ny)
    rows = own.shape[0]
    half = rows // 2
    greet(nz, ny, z, y)

    def piece(s, t, h):
        sign = -1 if h == 0 else 1
        start = device(z + sign * s, y + sign * t, nz, ny) * rows + h * half
        return pl.ds(pl.multiple_of(start, half), half)

    def copy(s, t, h, s2, t2):
        step = 1 if h == 0 else -1
        source = own.at[pl.ds(h * half, half)] if s == 0 and t == 0 else out.at[piece(s, t, h)]
        to = device(z + step, y, nz, ny) if t2 == 0 else device(z, y + step, nz, ny)
        return pltpu.make_async_remote_copy(
            src_ref=source, dst_ref=out.at[piece(s, t, h)],
            send_sem=send_sem.at[s2, t2, h], recv_sem=recv_sem.at[s2, t2, h],
            device_id={"expert": to}, device_id_type=MESH)

    def arrival(s, t, h):
        return pltpu.make_async_remote_copy(
            src_ref=out.at[piece(s, t, h)], dst_ref=out.at[piece(s, t, h)],
            send_sem=send_sem.at[s, t, h], recv_sem=recv_sem.at[s, t, h],
            device_id={"expert": device(z, y, nz, ny)}, device_id_type=MESH)

    mine = pltpu.make_async_copy(own, out.at[pl.ds(pl.multiple_of(device(z, y, nz, ny) * rows, rows), rows)], local_sem)
    started = []
    def start(*key):
        c = copy(*key); c.start(); started.append(c)
    for h in range(2):
        start(0, 0, h, 1, 0)
    if ny > 1:
        for h in range(2):
            start(0, 0, h, 0, 1)
    mine.start()
    for s in range(1, nz):
        for h in range(2):
            arrival(s, 0, h).wait_recv()
            if s + 1 < nz:
                start(s, 0, h, s + 1, 0)
            if ny > 1:
                start(s, 0, h, s, 1)
    for t in range(1, ny):
        for s in range(nz):
            for h in range(2):
                arrival(s, t, h).wait_recv()
                if t + 1 < ny:
                    start(s, t, h, s, t + 1)
    mine.wait()
    for c in started:
        c.wait_send()

def all_rows(own, n_expert, cid, name):
    nz, ny = grid_of(n_expert)
    rows, width = own.shape
    return pl.pallas_call(
        functools.partial(gather_kernel, nz, ny),
        out_shape=jax.ShapeDtypeStruct((rows * n_expert, width), own.dtype),
        in_specs=[pl.BlockSpec(memory_space=pl.ANY)],
        out_specs=pl.BlockSpec(memory_space=pl.ANY),
        scratch_shapes=[pltpu.SemaphoreType.DMA, pltpu.SemaphoreType.DMA((nz, ny, 2)), pltpu.SemaphoreType.DMA((nz, ny, 2))],
        compiler_params=pltpu.CompilerParams(collective_id=cid, has_side_effects=True),
        name=name,
    )(own)

def scatter_kernel(nz, ny, whole, out, from_y, from_z, to_y, to_z, send_y, recv_y, send_z, recv_z):
    z, y = places(nz, ny)
    rows = out.shape[0]
    half = rows // 2
    greet(nz, ny, z, y)

    def piece(s, t, h):
        sign = -1 if h == 0 else 1
        start = device(z + sign * (s + 1), y + sign * (t + 1), nz, ny) * rows + h * half
        return pl.ds(pl.multiple_of(start, half), half)

    def y_copy(s, t, h):
        step = 1 if h == 0 else -1
        source = whole.at[piece(s, 0, h)] if t == 0 else to_y.at[s, t - 1, h]
        return pltpu.make_async_remote_copy(
            src_ref=source, dst_ref=from_y.at[s, t, h], send_sem=send_y.at[s, t, h], recv_sem=recv_y.at[s, t, h],
            device_id={"expert": device(z, y + step, nz, ny)}, device_id_type=MESH)

    def z_copy(s, h):
        step = 1 if h == 0 else -1
        return pltpu.make_async_remote_copy(
            src_ref=to_z.at[s, h], dst_ref=from_z.at[s, h], send_sem=send_z.at[s, h], recv_sem=recv_z.at[s, h],
            device_id={"expert": device(z + step, y, nz, ny)}, device_id_type=MESH)

    if ny > 1:
        for s in range(nz):
            for h in range(2):
                y_copy(s, 0, h).start()
    for s in range(nz):
        for t in range(1, ny - 1):
            for h in range(2):
                y_copy(s, t - 1, h).wait_recv()
                to_y[s, t - 1, h] = (whole[piece(s, t, h), :].astype(F32) + from_y[s, t - 1, h].astype(F32)).astype(BF16)
                y_copy(s, t, h).start()
        for h in range(2):
            total = whole[piece(s, ny - 1, h), :].astype(F32)
            if ny > 1:
                y_copy(s, ny - 2, h).wait_recv()
                total += from_y[s, ny - 2, h].astype(F32)
            if s > 0:
                z_copy(s - 1, h).wait_recv()
                total += from_z[s - 1, h].astype(F32)
            if s < nz - 1:
                to_z[s, h] = total.astype(BF16)
                z_copy(s, h).start()
            else:
                out[h * half : (h + 1) * half, :] = total
    for s in range(nz):
        for h in range(2):
            for t in range(ny - 1):
                y_copy(s, t, h).wait_send()
            if s < nz - 1:
                z_copy(s, h).wait_send()

def own_sum(whole, n_expert, cid, name):
    nz, ny = grid_of(n_expert)
    all_, width = whole.shape
    rows = all_ // n_expert
    half = rows // 2
    D = pltpu.SemaphoreType.DMA
    return pl.pallas_call(
        functools.partial(scatter_kernel, nz, ny),
        out_shape=jax.ShapeDtypeStruct((rows, width), F32),
        in_specs=[pl.BlockSpec(memory_space=pltpu.VMEM)],
        out_specs=pl.BlockSpec(memory_space=pltpu.VMEM),
        scratch_shapes=[
            pltpu.VMEM((nz, max(ny - 1, 1), 2, half, width), BF16),
            pltpu.VMEM((max(nz - 1, 1), 2, half, width), BF16),
            pltpu.VMEM((nz, max(ny - 2, 1), 2, half, width), BF16),
            pltpu.VMEM((max(nz - 1, 1), 2, half, width), BF16),
            D((nz, max(ny - 1, 1), 2)), D((nz, max(ny - 1, 1), 2)), D((max(nz - 1, 1), 2)), D((max(nz - 1, 1), 2))],
        compiler_params=pltpu.CompilerParams(collective_id=cid, has_side_effects=True, vmem_limit_bytes=48 << 20),
        name=name,
    )(whole)


def rms_norm(values, gain_vec):
    factor = lax.rsqrt(jnp.mean(values * values, axis=-1, keepdims=True) + EPSILON)
    return values * factor * gain_vec


def dot(left, right, left_dim=1, right_dim=0):
    return lax.dot_general(
        left, right, (((left_dim,), (right_dim,)), ((), ())), preferred_element_type=F32
    )


def rotate(values, cosine, sine):
    half = HEAD_DIM // 2
    one, two = values[:half], values[half:]
    return jnp.concatenate([one * cosine - two * sine, two * cosine + one * sine], axis=0)


def rotate_back(grads, cosine, sine):
    half = HEAD_DIM // 2
    one, two = grads[:half], grads[half:]
    return jnp.concatenate([one * cosine + two * sine, two * cosine - one * sine], axis=0)


def attend_kernel(low, high, key_pos, query, key, value_t, out, lse, score_buf, weight_buf):
    heads = query.shape[0]
    low_row, high_row = low[...], high[...]
    steps = key.shape[0] // K_TILE

    def score_step(step, maxima):
        rows = pl.ds(pl.multiple_of(step * K_TILE, K_TILE), K_TILE)
        at = key_pos[rows, :]
        allowed = (at >= low_row) & (at <= high_row)
        found = []
        for head in range(heads):
            scores = jnp.dot(key[rows, :], query[head], preferred_element_type=F32)
            scores = jnp.where(allowed, scores, MASKED)
            score_buf[head, rows, :] = scores
            found.append(jnp.maximum(maxima[head], jnp.max(scores, axis=0, keepdims=True)))
        return tuple(found)

    start = tuple(jnp.full(low_row.shape, MASKED, F32) for _ in range(heads))
    maxima = lax.fori_loop(0, steps, score_step, start)

    def weight_step(step, totals):
        rows = pl.ds(pl.multiple_of(step * K_TILE, K_TILE), K_TILE)
        found = []
        for head in range(heads):
            weights = jnp.exp(score_buf[head, rows, :] - maxima[head])
            weight_buf[head, rows, :] = weights.astype(BF16)
            found.append(totals[head] + jnp.sum(weights, axis=0, keepdims=True))
        return tuple(found)

    start = tuple(jnp.zeros(low_row.shape, F32) for _ in range(heads))
    totals = lax.fori_loop(0, steps, weight_step, start)
    for head in range(heads):
        summed = jnp.dot(value_t[...], weight_buf[head], preferred_element_type=F32)
        out[head] = (summed / totals[head]).astype(BF16)
        lse[head] = maxima[head] + jnp.log(totals[head])


def attend(low, high, key_pos, query, key, value_t):
    heads, width, rows = query.shape
    tile = low_tile(rows)
    whole = lambda i: (0, 0)
    lane = lambda i: (0, i)
    return pl.pallas_call(
        attend_kernel,
        grid=(rows // tile,),
        in_specs=[
            pl.BlockSpec((1, tile), lane),
            pl.BlockSpec((1, tile), lane),
            pl.BlockSpec((rows, tile), whole),
            pl.BlockSpec((heads, width, tile), lambda i: (0, 0, i)),
            pl.BlockSpec((rows, width), whole),
            pl.BlockSpec((width, rows), whole),
        ],
        out_specs=[
            pl.BlockSpec((heads, width, tile), lambda i: (0, 0, i)),
            pl.BlockSpec((heads, 1, tile), lambda i: (0, 0, i)),
        ],
        out_shape=[
            jax.ShapeDtypeStruct((heads, width, rows), BF16),
            jax.ShapeDtypeStruct((heads, 1, rows), F32),
        ],
        scratch_shapes=[
            pltpu.VMEM((heads, rows, tile), F32),
            pltpu.VMEM((heads, rows, tile), BF16),
        ],
        cost_estimate=pl.CostEstimate(
            flops=4 * heads * rows * rows * 256,
            bytes_accessed=8 * rows * 256,
            transcendentals=heads * rows * rows,
        ),
        name="attend",
    )(low, high, key_pos, query, key, value_t)


def low_tile(rows):
    return min(Q_TILE, rows)


def attend_back_kernel(
    nz, ny,
    low, high, key_pos, query, query_n, key, key_t, value, grad, grad_n, lse, delta,
    cos_tab, sin_tab, made,
    own_in, proj, summed,
    d_key, d_value, score_buf, send_buf, part_buf, from_y, from_z, to_y, to_z,
    part_sem, own_send, own_recv, tail_send, tail_recv, keep_sem,
    send_y, recv_y, send_z, recv_z,
):
    z, y = places(nz, ny)
    me = lax.axis_index("expert")
    n_expert = nz * ny
    heads, width, tile = query.shape
    low_row, high_row = low[...], high[...]
    steps = key.shape[0] // K_TILE
    tok_rows = summed.shape[0]
    half_rows = tok_rows // 2
    per_tile = tile // tok_rows
    i = pl.program_id(0)
    count = key.shape[0] // tile
    q_cols = heads * width

    def piece(r, t, h):
        sign = -1 if h == 0 else 1
        start = device(z + sign * (r + 1), y + sign * (t + 1), nz, ny) * tok_rows + h * half_rows
        return pl.ds(pl.multiple_of(start, half_rows), half_rows)

    def near(along_z, h):
        step = 1 if h == 0 else -1
        to = device(z + step, y, nz, ny) if along_z else device(z, y + step, nz, ny)
        return {"expert": to}

    def part_copy(r, t, h):
        return pltpu.make_async_copy(
            made.at[piece(r, t, h)], part_buf.at[r, t, h], part_sem.at[r, t, h]
        )

    def y_copy(r, t, h):
        source = made.at[piece(r, 0, h)] if t == 0 else to_y.at[r, t - 1, h]
        return pltpu.make_async_remote_copy(
            src_ref=source, dst_ref=from_y.at[r, t, h],
            send_sem=send_y.at[r, t, h], recv_sem=recv_y.at[r, t, h],
            device_id=near(False, h), device_id_type=MESH,
        )

    def z_copy(r, h):
        return pltpu.make_async_remote_copy(
            src_ref=to_z.at[r, h], dst_ref=from_z.at[r, h],
            send_sem=send_z.at[r, h], recv_sem=recv_z.at[r, h],
            device_id=near(True, h), device_id_type=MESH,
        )

    def finish(r):
        for t in range(1, ny - 1):
            for h in range(2):
                y_copy(r, t - 1, h).wait_recv()
                part_copy(r, t, h).wait()
                to_y[r, t - 1, h] = (
                    part_buf[r, t, h].astype(F32) + from_y[r, t - 1, h].astype(F32)
                ).astype(BF16)
                y_copy(r, t, h).start()
        for h in range(2):
            part_copy(r, ny - 1, h).wait()
            total = part_buf[r, ny - 1, h].astype(F32)
            if ny > 1:
                y_copy(r, ny - 2, h).wait_recv()
                total += from_y[r, ny - 2, h].astype(F32)
            if r > 0:
                z_copy(r - 1, h).wait_recv()
                total += from_z[r - 1, h].astype(F32)
            if r < nz - 1:
                to_z[r, h] = total.astype(BF16)
                z_copy(r, h).start()
            else:
                summed[h * half_rows : (h + 1) * half_rows, :] = total

    head_rows, tail_rows = pl.ds(0, q_cols), pl.ds(q_cols, 2 * width)

    def own_copy(rows, other, source, sends, receives):
        return pltpu.make_async_remote_copy(
            src_ref=send_buf.at[other, rows], dst_ref=own_in.at[source, rows],
            send_sem=sends.at[other], recv_sem=receives.at[source],
            device_id={"expert": other}, device_id_type=MESH,
        )

    @pl.when(i == 0)
    def _():
        barrier = pltpu.get_barrier_semaphore()
        for k in range(1, n_expert):
            pl.semaphore_signal(
                barrier, inc=1, device_id={"expert": lax.rem(me + k, n_expert)}, device_id_type=MESH
            )
        pl.semaphore_wait(barrier, n_expert - 1)
        for r in range(nz):
            for h in range(2):
                if ny > 1:
                    y_copy(r, 0, h).start()
                for t in range(1, ny - 1):
                    part_copy(r, t, h).start()
                part_copy(r, ny - 1, h).start()
        d_key[...] = jnp.zeros_like(d_key)
        d_value[...] = jnp.zeros_like(d_value)

    for r in range(nz - 1):
        pl.when(i == (r + 1) * count // nz)(functools.partial(finish, r))

    @pl.loop(0, steps)
    def _(step):
        rows = pl.ds(pl.multiple_of(step * K_TILE, K_TILE), K_TILE)
        at = key_pos[rows, :]
        allowed = (at >= low_row) & (at <= high_row)
        key_sum, value_sum = d_key[rows, :], d_value[rows, :]
        for head in range(heads):
            scores = jnp.dot(key[rows, :], query[head], preferred_element_type=F32)
            weights = jnp.exp(jnp.where(allowed, scores - lse[head], MASKED))
            d_soft = jnp.dot(value[rows, :], grad[head], preferred_element_type=F32)
            d_scores = (weights * (d_soft - delta[head])).astype(BF16)
            score_buf[head, rows, :] = d_scores
            key_sum += jnp.dot(d_scores, query_n[head], preferred_element_type=F32)
            value_sum += jnp.dot(weights.astype(BF16), grad_n[head], preferred_element_type=F32)
        d_key[rows, :] = key_sum
        d_value[rows, :] = value_sum

    lanes = pl.ds(pl.multiple_of(i * tile, tile), tile)
    for head in range(heads):
        d_query = jnp.dot(key_t[...], score_buf[head], preferred_element_type=F32) * SCORE_SCALE
        turned = rotate_back(d_query, cos_tab[:, lanes], sin_tab[:, lanes]).astype(BF16)
        for j in range(per_tile):
            send_buf[i * per_tile + j, head * width : (head + 1) * width, :] = turned[
                :, j * tok_rows : (j + 1) * tok_rows
            ]
    for j in range(per_tile):
        other = i * per_tile + j

        @pl.when(other != me)
        def _():
            own_copy(head_rows, other, me, own_send, own_recv).start()

    @pl.when(i == count - 1)
    def _():
        for other in range(n_expert):
            rows = pl.ds(other * tok_rows, tok_rows)
            turned = rotate_back(d_key[rows, :].T, cos_tab[:, rows], sin_tab[:, rows])
            send_buf[other, q_cols : q_cols + width, :] = turned.astype(BF16)
            send_buf[other, q_cols + width :, :] = d_value[rows, :].T.astype(BF16)

            @pl.when(other != me)
            def _():
                own_copy(tail_rows, other, me, tail_send, tail_recv).start()

        keep = pltpu.make_async_copy(send_buf, proj, keep_sem.at[0])
        mine = pltpu.make_async_copy(send_buf.at[me], own_in.at[me], keep_sem.at[1])
        keep.start()
        mine.start()
        finish(nz - 1)
        for k in range(1, n_expert):
            other = lax.rem(me + k, n_expert)
            for rows, sends, receives in (
                (head_rows, own_send, own_recv), (tail_rows, tail_send, tail_recv)
            ):
                own_copy(rows, other, other, sends, receives).wait_recv()
                own_copy(rows, other, other, sends, receives).wait_send()
        for r in range(nz):
            for h in range(2):
                for t in range(ny - 1):
                    y_copy(r, t, h).wait_send()
                if r < nz - 1:
                    z_copy(r, h).wait_send()
        keep.wait()
        mine.wait()


def attend_back(
    low, high, key_pos, query, query_n, key, key_t, value, grad, grad_n, lse, delta,
    cosine, sine, made, tok_rows, cid,
):
    heads, width, rows = query.shape
    n_expert = rows // tok_rows
    nz, ny = grid_of(n_expert)
    cols = (heads + 2) * width
    half_rows, model = tok_rows // 2, made.shape[1]
    tile = low_tile(rows)
    whole = lambda i: (0, 0)
    lane = lambda i: (0, i)
    wide = pl.BlockSpec((heads, width, tile), lambda i: (0, 0, i))
    tall = pl.BlockSpec((heads, tile, width), lambda i: (0, i, 0))
    row = pl.BlockSpec((heads, 1, tile), lambda i: (0, 0, i))
    keys = pl.BlockSpec((rows, width), whole)
    anywhere = pl.BlockSpec(memory_space=pl.ANY)
    dma = pltpu.SemaphoreType.DMA
    y_steps, y_mid, z_steps = max(ny - 1, 1), max(ny - 2, 1), max(nz - 1, 1)
    return pl.pallas_call(
        functools.partial(attend_back_kernel, nz, ny),
        grid=(rows // tile,),
        in_specs=[
            pl.BlockSpec((1, tile), lane),
            pl.BlockSpec((1, tile), lane),
            pl.BlockSpec((rows, tile), whole),
            wide, tall, keys, pl.BlockSpec((width, rows), whole), keys, wide, tall, row, row,
            pl.BlockSpec((width // 2, rows), whole), pl.BlockSpec((width // 2, rows), whole),
            anywhere,
        ],
        out_specs=[anywhere, anywhere, pl.BlockSpec((tok_rows, model), whole)],
        out_shape=[
            jax.ShapeDtypeStruct((n_expert, cols, tok_rows), BF16),
            jax.ShapeDtypeStruct((n_expert, cols, tok_rows), BF16),
            jax.ShapeDtypeStruct((tok_rows, model), F32),
        ],
        scratch_shapes=[
            pltpu.VMEM((rows, width), F32),
            pltpu.VMEM((rows, width), F32),
            pltpu.VMEM((heads, rows, tile), BF16),
            pltpu.VMEM((n_expert, cols, tok_rows), BF16),
            pltpu.VMEM((nz, ny, 2, half_rows, model), BF16),
            pltpu.VMEM((nz, y_steps, 2, half_rows, model), BF16),
            pltpu.VMEM((z_steps, 2, half_rows, model), BF16),
            pltpu.VMEM((nz, y_mid, 2, half_rows if ny > 2 else 16, model), BF16),
            pltpu.VMEM((z_steps, 2, half_rows, model), BF16),
            dma((nz, ny, 2)), dma((n_expert,)), dma((n_expert,)), dma((n_expert,)), dma((n_expert,)), dma((2,)),
            dma((nz, y_steps, 2)), dma((nz, y_steps, 2)), dma((z_steps, 2)), dma((z_steps, 2)),
        ],
        compiler_params=pltpu.CompilerParams(
            collective_id=cid, has_side_effects=True, vmem_limit_bytes=56 << 20
        ),
        cost_estimate=pl.CostEstimate(
            flops=10 * heads * rows * rows * 256,
            bytes_accessed=8 * rows * 256,
            transcendentals=heads * rows * rows,
        ),
        name="attend_back",
    )(low, high, key_pos, query, query_n, key, key_t, value, grad, grad_n, lse, delta, cosine, sine, made)


def finish_kernel(
    n_dp, nz, ny, qkv, proj, small,
    qkv_all, proj_rows, small_sum,
    qkv_in, proj_in, small_in, own_qkv, own_proj, own_small, proj_all, small_all, proj_got,
    dp_send, dp_recv, ring_send, ring_recv, last_send, last_recv, keep_sem,
):
    z, y = places(nz, ny)
    me, group = lax.axis_index("expert"), lax.axis_index("dp")
    n_expert = nz * ny
    share = n_expert // n_dp
    barrier = pltpu.get_barrier_semaphore()
    near = [{"dp": lax.rem(group + k, n_dp)} for k in range(1, n_dp)]
    near += [{"expert": device(z + k, y, nz, ny)} for k in sorted({1, nz - 1} - {0})]
    near += [{"expert": device(z, y + k, nz, ny)} for k in sorted({1, ny - 1} - {0})]
    for other in near:
        pl.semaphore_signal(barrier, inc=1, device_id=other, device_id_type=MESH)
    pl.semaphore_wait(barrier, len(near))

    arrays = ((qkv, qkv_in, own_qkv), (proj, proj_in, own_proj), (small, small_in, own_small))

    def across(k, a):
        source, target, _ = arrays[a]
        other = lax.rem(group + k, n_dp)
        return pltpu.make_async_remote_copy(
            src_ref=source.at[other], dst_ref=target.at[k - 1],
            send_sem=dp_send.at[k - 1, a], recv_sem=dp_recv.at[k - 1, a],
            device_id={"dp": other}, device_id_type=MESH,
        )

    for k in range(1, n_dp):
        for a in range(3):
            across(k, a).start()
    for a, (source, target, own) in enumerate(arrays):
        total = source[group].astype(F32)
        for k in range(1, n_dp):
            across(k, a).wait_recv()
            total += target[k - 1].astype(F32)
        own[...] = total.astype(own.dtype)

    rings = ((own_qkv, qkv_all), (own_proj, proj_all), (own_small, small_all))

    def origin(s, t, h):
        sign = -1 if h == 0 else 1
        return device(z + sign * s, y + sign * t, nz, ny)

    def ring_copy(s, t, h, s2, t2, a):
        own, everyone = rings[a]
        of = origin(s, t, h)
        rows = own.shape[0] // 2 if a < 2 else own.shape[0]
        part = pl.ds(h * rows, rows)
        source = own.at[part] if s == 0 and t == 0 else everyone.at[of, part]
        step = 1 if h == 0 else -1
        to = device(z + step, y, nz, ny) if t2 == 0 else device(z, y + step, nz, ny)
        return pltpu.make_async_remote_copy(
            src_ref=source, dst_ref=everyone.at[of, part],
            send_sem=ring_send.at[s2, t2, h, a], recv_sem=ring_recv.at[s2, t2, h, a],
            device_id={"expert": to}, device_id_type=MESH,
        )

    def arrive(s, t, h, a):
        own, everyone = rings[a]
        rows = own.shape[0] // 2 if a < 2 else own.shape[0]
        place = everyone.at[origin(s, t, h), pl.ds(h * rows, rows)]
        pltpu.make_async_remote_copy(
            src_ref=place, dst_ref=place,
            send_sem=ring_send.at[s, t, h, a], recv_sem=ring_recv.at[s, t, h, a],
            device_id={"expert": device(z + 1, y, nz, ny)}, device_id_type=MESH,
        ).wait_recv()

    keeps = [
        pltpu.make_async_copy(own, everyone.at[me], keep_sem.at[a])
        for a, (own, everyone) in enumerate(rings)
    ]
    for copy in keeps:
        copy.start()
    moves = [(h, a) for h in range(2) for a in range(3) if a < 2 or h == 0]
    sent = []

    def start(*key):
        copy = ring_copy(*key)
        copy.start()
        sent.append(copy)

    for h, a in moves:
        if nz > 1:
            start(0, 0, h, 1, 0, a)
        if ny > 1:
            start(0, 0, h, 0, 1, a)
    for s in range(1, nz):
        for h, a in moves:
            arrive(s, 0, h, a)
            if s + 1 < nz:
                start(s, 0, h, s + 1, 0, a)
            if ny > 1:
                start(s, 0, h, s, 1, a)
    for t in range(1, ny):
        for s in range(nz):
            for h, a in moves:
                arrive(s, t, h, a)
                if t + 1 < ny:
                    start(s, t, h, s, t + 1, a)
    for copy in keeps:
        copy.wait()

    def last(k):
        other = lax.rem(group + k, n_dp)
        return pltpu.make_async_remote_copy(
            src_ref=proj_all.at[pl.ds(other * share, share)], dst_ref=proj_got.at[group],
            send_sem=last_send.at[k - 1], recv_sem=last_recv.at[k - 1],
            device_id={"dp": other}, device_id_type=MESH,
        )

    for k in range(1, n_dp):
        last(k).start()
    mine = pltpu.make_async_copy(
        proj_all.at[pl.ds(group * share, share)], proj_got.at[group], keep_sem.at[3]
    )
    mine.start()
    total = small_all[0]
    for other in range(1, n_expert):
        total += small_all[other]
    small_sum[...] = total
    for k in range(1, n_dp):
        last(k).wait_recv()
    mine.wait()
    high, wide = own_proj.shape
    for c in range(n_dp):
        for part in range(share):
            proj_rows[part * high : (part + 1) * high, c * wide : (c + 1) * wide] = proj_got[
                c, part
            ].astype(F32)
    for copy in sent:
        copy.wait_send()
    for k in range(1, n_dp):
        last(k).wait_send()
        for a in range(3):
            across(k, a).wait_send()


def finish_sums(qkv, proj, small, n_expert, cid):
    nz, ny = grid_of(n_expert)
    n_dp, high, wide = proj.shape
    share = n_expert // n_dp
    whole = pl.BlockSpec(memory_space=pltpu.VMEM)
    dma = pltpu.SemaphoreType.DMA
    peers = max(n_dp - 1, 1)
    return pl.pallas_call(
        functools.partial(finish_kernel, n_dp, nz, ny),
        out_shape=[
            jax.ShapeDtypeStruct((n_expert,) + qkv.shape[1:], BF16),
            jax.ShapeDtypeStruct((share * high, n_dp * wide), F32),
            jax.ShapeDtypeStruct(small.shape[1:], F32),
        ],
        in_specs=[whole] * 3,
        out_specs=[whole] * 3,
        scratch_shapes=[
            pltpu.VMEM((peers,) + qkv.shape[1:], BF16),
            pltpu.VMEM((peers,) + proj.shape[1:], BF16),
            pltpu.VMEM((peers,) + small.shape[1:], F32),
            pltpu.VMEM(qkv.shape[1:], BF16),
            pltpu.VMEM(proj.shape[1:], BF16),
            pltpu.VMEM(small.shape[1:], F32),
            pltpu.VMEM((n_expert,) + proj.shape[1:], BF16),
            pltpu.VMEM((n_expert,) + small.shape[1:], F32),
            pltpu.VMEM((n_dp, share, high, wide), BF16),
            dma((peers, 3)), dma((peers, 3)), dma((nz, ny, 2, 3)), dma((nz, ny, 2, 3)),
            dma((peers,)), dma((peers,)), dma((4,)),
        ],
        compiler_params=pltpu.CompilerParams(
            collective_id=cid, has_side_effects=True, vmem_limit_bytes=32 << 20
        ),
        name="finish_sums",
    )(qkv, proj, small)


def experts_kernel(
    nz, ny, own, named, router, cotangent, weight_in, weight_out,
    back, d_gate, made, grads_in, grads_out,
    rows_buf, cot_buf, in_buf, out_buf, hid_buf, gu_buf, part_buf, made_buf, gin_buf, gout_buf,
    gate_out, gate_in, from_y, from_z, to_y, to_z,
    load_sem, cot_sem, made_sem, grad_sem, send_sem, recv_sem, gate_send, gate_recv,
    send_y, recv_y, send_z, recv_z,
):
    z, y = places(nz, ny)
    me = lax.axis_index("expert")
    n_expert = nz * ny
    tok_rows, width = own.shape
    half = tok_rows // 2
    step_rows = ny * tok_rows
    exp_dev, ff, _ = out_buf.shape
    experts = named.shape[1]

    barrier = pltpu.get_barrier_semaphore()
    for k in range(1, n_expert):
        pl.semaphore_signal(
            barrier, inc=1, device_id={"expert": lax.rem(me + k, n_expert)}, device_id_type=MESH
        )
    pl.semaphore_wait(barrier, n_expert - 1)

    def owner(s, t, h):
        sign = -1 if h == 0 else 1
        return device(z + sign * s, y + sign * t, nz, ny)

    def piece(s, t, h):
        return pl.ds(pl.multiple_of(owner(s, t, h) * tok_rows + h * half, half), half)

    def slot(s, t, h):
        return pl.ds(((s * ny + t) * 2 + h) * half, half)

    def near(along_z, h):
        step = 1 if h == 0 else -1
        to = device(z + step, y, nz, ny) if along_z else device(z, y + step, nz, ny)
        return {"expert": to}

    def row_copy(s, t, h, s2, t2):
        source = own.at[pl.ds(h * half, half)] if s == 0 and t == 0 else rows_buf.at[slot(s, t, h)]
        return pltpu.make_async_remote_copy(
            src_ref=source, dst_ref=rows_buf.at[slot(s2, t2, h)],
            send_sem=send_sem.at[s2, t2, h], recv_sem=recv_sem.at[s2, t2, h],
            device_id=near(t2 == 0, h), device_id_type=MESH,
        )

    def arrive(s, t, h):
        if t == 0:
            row_copy(s - 1, 0, h, s, 0).wait_recv()
        else:
            row_copy(s, t - 1, h, s, t).wait_recv()

    sent = []

    def start(*key):
        copy = row_copy(*key)
        copy.start()
        sent.append(copy)

    for h in range(2):
        start(0, 0, h, 1, 0)
    if ny > 1:
        for h in range(2):
            start(0, 0, h, 0, 1)
    loads = [
        pltpu.make_async_copy(weight_in, in_buf, load_sem.at[0]),
        pltpu.make_async_copy(weight_out, out_buf, load_sem.at[1]),
    ]
    for copy in loads:
        copy.start()
    cots = {
        (s, t, h): pltpu.make_async_copy(
            cotangent.at[piece(s, t, h)], cot_buf.at[slot(s, t, h)], cot_sem.at[s, t, h]
        )
        for s in range(nz) for t in range(ny) for h in range(2)
    }
    for copy in cots.values():
        copy.start()
    rows_buf[0:tok_rows, :] = own[...]
    for copy in loads:
        copy.wait()

    lane = lax.broadcasted_iota(jnp.int32, (step_rows, experts), 1)
    wide_lane = lax.broadcasted_iota(jnp.int32, (step_rows, 128), 1)
    tile = 256

    def compute(s):
        rows = pl.ds(s * step_rows, step_rows)
        picked = jnp.concatenate(
            [named[piece(s, t, h), :] for t in range(ny) for h in range(2)], axis=0
        ) > 0.5
        logits = jnp.where(picked, dot(rows_buf[rows, :], router[...], 1, 1), MASKED)
        powers = jnp.exp(logits - jnp.max(logits, axis=1, keepdims=True))
        powers = jnp.where(picked, powers, 0.0)
        gates = powers / jnp.sum(powers, axis=1, keepdims=True)
        found = jnp.zeros((step_rows, 128), F32)
        for e in range(exp_dev):
            weight = jnp.sum(
                jnp.where(lane == me * exp_dev + e, gates, 0.0), axis=1, keepdims=True
            )

            def hidden_step(j, total):
                at = pl.multiple_of(j * tile, tile)
                cols, late = pl.ds(at, tile), pl.ds(pl.multiple_of(ff + at, tile), tile)
                gate_pre = dot(rows_buf[rows, :], in_buf[e, :, cols])
                up_pre = dot(rows_buf[rows, :], in_buf[e, :, late])
                d_plain = dot(cot_buf[rows, :], out_buf[e, cols, :], 1, 1)
                sigmoid = jax.nn.sigmoid(gate_pre)
                active = gate_pre * sigmoid
                hidden = active * up_pre
                hid_buf[e, rows, cols] = (weight * hidden).astype(BF16)
                d_hidden = weight * d_plain
                gu_buf[e, rows, cols] = (
                    d_hidden * up_pre * sigmoid * (1.0 + gate_pre * (1.0 - sigmoid))
                ).astype(BF16)
                gu_buf[e, rows, late] = (d_hidden * active).astype(BF16)
                return total + jnp.sum(hidden * d_plain, axis=1, keepdims=True)

            total = lax.fori_loop(0, ff // tile, hidden_step, jnp.zeros((step_rows, 1), F32))
            found += jnp.where(wide_lane == me * exp_dev + e, total, 0.0)

        @pl.loop(0, width // tile)
        def _(n):
            cols = pl.ds(pl.multiple_of(n * tile, tile), tile)
            d_rows = dot(gu_buf[0, rows, :], in_buf[0, cols, :], 1, 1)
            for e in range(1, exp_dev):
                d_rows += dot(gu_buf[e, rows, :], in_buf[e, cols, :], 1, 1)
            part_buf[rows, cols] = d_rows.astype(BF16)
            made_sum = dot(hid_buf[0, rows, :], out_buf[0, :, cols])
            for e in range(1, exp_dev):
                made_sum += dot(hid_buf[e, rows, :], out_buf[e, :, cols])
            made_buf[rows, cols] = made_sum.astype(BF16)

        for t in range(ny):
            for h in range(2):
                low = (t * 2 + h) * half
                gate_out[s, t, h] = found[low : low + half, :].T[:experts, :]
                if s or t:
                    gate_copy(s, t, h).start()
                made_copy(s, t, h).start()

    def gate_copy(s, t, h):
        return pltpu.make_async_remote_copy(
            src_ref=gate_out.at[s, t, h], dst_ref=gate_in.at[s, t, h],
            send_sem=gate_send.at[s, t, h], recv_sem=gate_recv.at[s, t, h],
            device_id={"expert": owner(s, t, h)}, device_id_type=MESH,
        )

    def made_copy(s, t, h):
        return pltpu.make_async_copy(
            made_buf.at[slot(s, t, h)], made.at[piece(s, t, h)], made_sem.at[s, t, h]
        )

    def part(r, t, h):
        return slot((r + 1) % nz, (t + 1) % ny, h)

    def y_copy(r, t, h):
        source = part_buf.at[part(r, 0, h)] if t == 0 else to_y.at[r, t - 1, h]
        return pltpu.make_async_remote_copy(
            src_ref=source, dst_ref=from_y.at[r, t, h],
            send_sem=send_y.at[r, t, h], recv_sem=recv_y.at[r, t, h],
            device_id=near(False, h), device_id_type=MESH,
        )

    def z_copy(r, h):
        return pltpu.make_async_remote_copy(
            src_ref=to_z.at[r, h], dst_ref=from_z.at[r, h],
            send_sem=send_z.at[r, h], recv_sem=recv_z.at[r, h],
            device_id=near(True, h), device_id_type=MESH,
        )

    def first_y(r):
        if ny > 1:
            for h in range(2):
                y_copy(r, 0, h).start()

    def finish(r):
        for t in range(1, ny - 1):
            for h in range(2):
                y_copy(r, t - 1, h).wait_recv()
                to_y[r, t - 1, h] = (
                    part_buf[part(r, t, h), :].astype(F32) + from_y[r, t - 1, h].astype(F32)
                ).astype(BF16)
                y_copy(r, t, h).start()
        for h in range(2):
            total = part_buf[part(r, ny - 1, h), :].astype(F32)
            if ny > 1:
                y_copy(r, ny - 2, h).wait_recv()
                total += from_y[r, ny - 2, h].astype(F32)
            if r > 0:
                z_copy(r - 1, h).wait_recv()
                total += from_z[r - 1, h].astype(F32)
            if r < nz - 1:
                to_z[r, h] = total.astype(BF16)
                z_copy(r, h).start()
            else:
                back[h * half : (h + 1) * half, :] = total

    def forward(s):
        for h in range(2):
            arrive(s, 0, h)
            if s + 1 < nz:
                start(s, 0, h, s + 1, 0)
            if ny > 1:
                start(s, 0, h, s, 1)

    def whole_step(s):
        for t in range(1, ny):
            for h in range(2):
                arrive(s, t, h)
                if t + 1 < ny:
                    start(s, t, h, s, t + 1)
        for t in range(ny):
            for h in range(2):
                cots[s, t, h].wait()
        compute(s)

    for s in range(nz):
        if s + 1 < nz:
            forward(s + 1)
        whole_step(s)
        if s > 0:
            first_y(s - 1)
        if s > 1:
            finish(s - 2)
    first_y(nz - 1)

    def grad_step(i):
        cols = pl.ds(pl.multiple_of(i * tile, tile), tile)
        for e in range(exp_dev):
            gin_buf[e, cols, :] = dot(rows_buf[:, cols], gu_buf[e], 0, 0).astype(BF16)

    def grad_out_step(i):
        cols = pl.ds(pl.multiple_of(i * tile, tile), tile)
        for e in range(exp_dev):
            gout_buf[e, cols, :] = dot(hid_buf[e, :, cols], cot_buf[...], 0, 0).astype(BF16)

    pl.loop(0, ff // tile)(grad_out_step)
    gout_copy = pltpu.make_async_copy(gout_buf, grads_out, grad_sem.at[0])
    gout_copy.start()
    if nz > 1:
        finish(nz - 2)
    pl.loop(0, width // tile)(grad_step)
    gin_copy = pltpu.make_async_copy(gin_buf, grads_in, grad_sem.at[1])
    gin_copy.start()
    finish(nz - 1)
    for h in range(2):
        gate_sum = gate_out[0, 0, h]
        for s in range(nz):
            for t in range(ny):
                if s or t:
                    gate_copy(s, t, h).wait_recv()
                    gate_sum += gate_in[s, t, h]
        d_gate[h] = gate_sum
    for copy in sent:
        copy.wait_send()
    for s in range(nz):
        for h in range(2):
            for t in range(ny):
                made_copy(s, t, h).wait()
                if s or t:
                    gate_copy(s, t, h).wait_send()
            for t in range(ny - 1):
                y_copy(s, t, h).wait_send()
            if s < nz - 1:
                z_copy(s, h).wait_send()
    gout_copy.wait()
    gin_copy.wait()


def experts_pass(own, named, router, cotangent, weight_in, weight_out, n_expert, cid):
    nz, ny = grid_of(n_expert)
    tok_rows, width = own.shape
    exp_dev, ff, _ = weight_out.shape
    half, group = tok_rows // 2, tok_rows * n_expert
    experts = named.shape[1]
    whole, anywhere = pl.BlockSpec(memory_space=pltpu.VMEM), pl.BlockSpec(memory_space=pl.ANY)
    dma = pltpu.SemaphoreType.DMA
    ring = dma((nz, ny, 2))
    y_steps, y_mid, z_steps = max(ny - 1, 1), max(ny - 2, 1), max(nz - 1, 1)
    return pl.pallas_call(
        functools.partial(experts_kernel, nz, ny),
        out_shape=[
            jax.ShapeDtypeStruct((tok_rows, width), F32),
            jax.ShapeDtypeStruct((2, experts, half), F32),
            jax.ShapeDtypeStruct((group, width), BF16),
            jax.ShapeDtypeStruct((exp_dev, width, 2 * ff), BF16),
            jax.ShapeDtypeStruct((exp_dev, ff, width), BF16),
        ],
        in_specs=[whole, whole, whole, anywhere, anywhere, anywhere],
        out_specs=[whole, whole, anywhere, anywhere, anywhere],
        scratch_shapes=[
            pltpu.VMEM((group, width), BF16),
            pltpu.VMEM((group, width), BF16),
            pltpu.VMEM((exp_dev, width, 2 * ff), BF16),
            pltpu.VMEM((exp_dev, ff, width), BF16),
            pltpu.VMEM((exp_dev, group, ff), BF16),
            pltpu.VMEM((exp_dev, group, 2 * ff), BF16),
            pltpu.VMEM((group, width), BF16),
            pltpu.VMEM((group, width), BF16),
            pltpu.VMEM((exp_dev, width, 2 * ff), BF16),
            pltpu.VMEM((exp_dev, ff, width), BF16),
            pltpu.VMEM((nz, ny, 2, experts, half), F32),
            pltpu.VMEM((nz, ny, 2, experts, half), F32),
            pltpu.VMEM((nz, y_steps, 2, half, width), BF16),
            pltpu.VMEM((z_steps, 2, half, width), BF16),
            pltpu.VMEM((nz, y_mid, 2, half if ny > 2 else 16, width), BF16),
            pltpu.VMEM((z_steps, 2, half, width), BF16),
            dma((2,)), ring, ring, dma((2,)), ring, ring, ring, ring,
            dma((nz, y_steps, 2)), dma((nz, y_steps, 2)), dma((z_steps, 2)), dma((z_steps, 2)),
        ],
        compiler_params=pltpu.CompilerParams(
            collective_id=cid, has_side_effects=True, vmem_limit_bytes=60 << 20
        ),
        cost_estimate=pl.CostEstimate(
            flops=18 * exp_dev * group * width * ff,
            bytes_accessed=16 * group * width,
            transcendentals=exp_dev * group * ff,
        ),
        name="experts_pass",
    )(own, named, router, cotangent, weight_in, weight_out)


def gather(values, name, axis=0):
    return lax.all_gather(values, name, axis=axis, tiled=True)


def exchange(values, name="expert"):
    return lax.all_to_all(values, name, split_axis=0, concat_axis=0, tiled=True)


def give_back(partial):
    return lax.psum_scatter(
        partial.astype(BF16), "expert", scatter_dimension=0, tiled=True
    ).astype(F32)


def local(
    hidden_in, d_out, gain_attn, w_qkv, w_o, gain_moe, w_router, w_in, w_out,
    seq_lengths, assign, routes,
):
    tok_rows, width = hidden_in.shape
    exp_dev, _, ff_two = w_in.shape
    ff = ff_two // 2
    n_expert = lax.axis_size("expert")
    me = lax.axis_index("expert")
    experts = exp_dev * n_expert
    group_rows = tok_rows * n_expert
    q_per = HEADS // n_expert
    share = GROUPS // q_per
    q_cols = q_per * HEAD_DIM
    k_base = HEADS * HEAD_DIM
    v_base = k_base + KV_HEADS * HEAD_DIM
    cols = q_cols + 2 * HEAD_DIM

    pack = gather(
        jnp.concatenate([gain_attn[None], gain_moe[None], w_router.T], axis=0), "dp", axis=1
    )
    gain_one, gain_two = pack[0].astype(F32), pack[1].astype(F32)
    router_t = pack[2:]
    kv_head = (me * q_per) // GROUPS
    w_heads = gather(
        jnp.concatenate(
            [
                lax.dynamic_slice_in_dim(w_qkv, me * q_cols, q_cols, 1),
                lax.dynamic_slice_in_dim(w_qkv, k_base + kv_head * HEAD_DIM, HEAD_DIM, 1),
                lax.dynamic_slice_in_dim(w_qkv, v_base + kv_head * HEAD_DIM, HEAD_DIM, 1),
            ],
            axis=1,
        ),
        "dp",
    )
    stream_in = hidden_in.astype(F32)
    normed_one = rms_norm(stream_in, gain_one).astype(BF16)
    normed_all = all_rows(normed_one, n_expert, 0, "gather_one")
    position = gather(assign[0], "expert")
    proj_full = gather(w_o, "dp")
    weight_in = gather(w_in, "dp", axis=1)
    d_out_all = gather(d_out, "expert")
    routes_all = gather(routes, "expert")
    weight_out = gather(w_out, "dp", axis=2)
    pieces = []
    for dev in range(n_expert):
        head = (dev * q_per) // GROUPS * HEAD_DIM
        pieces += [
            w_qkv[:, dev * q_cols : (dev + 1) * q_cols],
            w_qkv[:, k_base + head : k_base + head + HEAD_DIM],
            w_qkv[:, v_base + head : v_base + head + HEAD_DIM],
        ]
    qkv_full = gather(jnp.concatenate(pieces, axis=1), "dp")

    lengths = seq_lengths[0]
    order = jnp.arange(lengths.shape[0], dtype=jnp.int32)
    ends = jnp.sum(jnp.where(order[None, :] <= order[:, None], lengths[None, :], 0), axis=1)
    starts = ends - lengths
    seq_id = jnp.sum((position[None, :] >= ends[:, None]).astype(jnp.int32), axis=0)
    picks = seq_id[None, :] == jnp.arange(lengths.shape[0], dtype=jnp.int32)[:, None]
    start_of = jnp.sum(jnp.where(picks, starts[:, None], 0), axis=0)
    rot_pos = position - start_of
    half = HEAD_DIM // 2
    frequency = ROPE_BASE ** (-(jnp.arange(half).astype(F32) * (2.0 / HEAD_DIM)))
    angles = frequency[:, None] * rot_pos.astype(F32)[None, :]
    cosine, sine = jnp.cos(angles), jnp.sin(angles)
    low, high = start_of[None, :], position[None, :]
    key_pos = jnp.broadcast_to(position[:, None], (group_rows, low_tile(group_rows)))

    projected = dot(w_heads, normed_all, 0, 1)
    query = jnp.stack(
        [
            rotate(projected[h * HEAD_DIM : (h + 1) * HEAD_DIM], cosine, sine).astype(BF16)
            for h in range(q_per)
        ]
    ) * jnp.asarray(SCORE_SCALE, BF16)
    key_t = rotate(projected[q_cols : q_cols + HEAD_DIM], cosine, sine).astype(BF16)
    value_t = projected[q_cols + HEAD_DIM :].astype(BF16)
    key, value = key_t.T, value_t.T
    heads_out, lse = attend(low, high, key_pos, query, key, value_t)
    heads_out, weight_in, weight_out = lax.optimization_barrier(
        (heads_out, weight_in, weight_out)
    )
    attended_t = heads_out.reshape(q_cols, group_rows)
    attended = exchange(attended_t.T.reshape(n_expert, tok_rows, q_cols))
    attended = attended.transpose(1, 0, 2).reshape(tok_rows, HEADS * HEAD_DIM)
    mid_stream = stream_in + dot(attended, proj_full)
    normed_two = rms_norm(mid_stream, gain_two).astype(BF16)

    named = jnp.any(
        routes_all[:, :, None] == jnp.arange(experts, dtype=jnp.int32)[None, None, :], axis=1
    )
    d_back, d_gate, made, grads_in, grads_out = experts_pass(
        normed_two, named.astype(F32), router_t, d_out_all, weight_in, weight_out, n_expert, 1
    )
    d_gate = d_gate.transpose(0, 2, 1).reshape(tok_rows, experts)
    own_named = jnp.any(
        routes[:, :, None] == jnp.arange(experts, dtype=jnp.int32)[None, None, :], axis=1
    )
    own_gates = jax.nn.softmax(
        jnp.where(own_named, dot(normed_two, router_t, 1, 1), -jnp.inf), axis=1
    )
    d_logits = (
        own_gates * (d_gate - jnp.sum(own_gates * d_gate, axis=1, keepdims=True))
    ).astype(BF16)
    grad_router = dot(d_logits, normed_two, 0, 0)
    d_normed_two = d_back + dot(d_logits, router_t)
    _, norm_two_back = jax.vjp(rms_norm, mid_stream, gain_two)
    d_mid_norm, grad_gain_two = norm_two_back(d_normed_two)
    d_mid = d_out.astype(F32) + d_mid_norm

    d_attn_all = all_rows(d_mid.astype(BF16), n_expert, 2, "gather_attn")
    d_attn_all, grads_in, grads_out, made = lax.optimization_barrier(
        (d_attn_all, grads_in, grads_out, made)
    )
    grad_w_in = lax.psum_scatter(grads_in, "dp", scatter_dimension=1, tiled=True).astype(F32)
    grad_w_out = lax.psum_scatter(grads_out, "dp", scatter_dimension=2, tiled=True).astype(F32)
    w_o_mine = lax.dynamic_slice_in_dim(proj_full, me * q_cols, q_cols, 0)
    d_heads = dot(w_o_mine, d_attn_all, 1, 1).astype(BF16).reshape(q_per, HEAD_DIM, group_rows)
    delta = jnp.sum(d_heads.astype(F32) * heads_out.astype(F32), axis=1, keepdims=True)
    d_own, d_projected, returned = attend_back(
        low, high, key_pos, query, jnp.swapaxes(query, 1, 2), key, key_t, value,
        d_heads, jnp.swapaxes(d_heads, 1, 2), lse, delta, cosine, sine, made, tok_rows, 4,
    )
    layer_out = (mid_stream + returned).astype(BF16)
    d_normed_one = dot(d_own.reshape(n_expert * cols, tok_rows), qkv_full, 0, 1)
    _, norm_one_back = jax.vjp(rms_norm, stream_in, gain_one)
    d_in_norm, grad_gain_one = norm_one_back(d_normed_one)
    grad_in = d_mid + d_in_norm

    n_dp = lax.axis_size("dp")
    wide = width // n_dp
    part_o = dot(attended_t, d_attn_all).astype(BF16)
    part_o = part_o.reshape(q_cols, n_dp, wide).transpose(1, 0, 2)
    part_qkv = dot(
        normed_all, d_projected.transpose(1, 0, 2).reshape(cols, group_rows), 0, 1
    ).astype(BF16).reshape(n_dp, wide, cols)
    few = 2 + experts
    small = jnp.concatenate(
        [grad_gain_one[None], grad_gain_two[None], grad_router, jnp.zeros((-few % 8, width), F32)], axis=0
    )
    small = small.reshape(-1, n_dp, wide).transpose(1, 0, 2)
    joined, grad_w_o, small = finish_sums(part_qkv, part_o, small, n_expert, 5)
    joined = joined.astype(F32)

    def columns(stack):
        return stack.transpose(1, 0, 2).reshape(stack.shape[1], -1)

    def shared(stack):
        return columns(stack.reshape((KV_HEADS, share) + stack.shape[1:]).sum(axis=1))

    grad_w_qkv = jnp.concatenate(
        [
            columns(joined[:, :, :q_cols]),
            shared(joined[:, :, q_cols : q_cols + HEAD_DIM]),
            shared(joined[:, :, q_cols + HEAD_DIM :]),
        ],
        axis=1,
    )
    return (
        layer_out, grad_in, small[0], grad_w_qkv, grad_w_o, small[1], small[2:few].T,
        grad_w_in, grad_w_out,
    )


def solution(mesh):
    rows = P(("dp", "expert"), None)
    in_specs = (
        rows, rows, P("dp"), P("dp", None), P("dp", None), P("dp"), P("dp", None),
        P("expert", "dp", None), P("expert", None, "dp"), P("dp", None), P("dp", "expert"), rows,
    )
    out_specs = (
        rows, rows, P("dp"), P("dp", None), P("dp", None), P("dp"), P("dp", None),
        P("expert", "dp", None), P("expert", None, "dp"),
    )
    return jax.shard_map(local, mesh=mesh, in_specs=in_specs, out_specs=out_specs, check_vma=False)
```

```python
import functools

import jax
import jax.numpy as jnp
from jax import lax
from jax.experimental import pallas as pl
from jax.experimental.pallas import tpu as pltpu
from jax.sharding import PartitionSpec as P

HEADS = 16
KV_HEADS = 8
HEAD_DIM = 64
GROUPS = HEADS // KV_HEADS
EPSILON = 1e-06
ROPE_BASE = 10000.0
SCORE_SCALE = 0.015625
MASKED = -1e30
F32 = jnp.float32
BF16 = jnp.bfloat16
Q_TILE = 256
K_TILE = 256


MESH = pl.DeviceIdType.MESH
Z_SIZE = 4

def grid_of(n_expert):
    nz = Z_SIZE if n_expert % Z_SIZE == 0 else 1
    return nz, n_expert // nz

def places(nz, ny):
    me = lax.axis_index("expert")
    return me // ny, lax.rem(me, ny)

def device(z, y, nz, ny):
    return lax.rem(z + 2 * nz, nz) * ny + lax.rem(y + 2 * ny, ny)

def greet(nz, ny, z, y):
    barrier = pltpu.get_barrier_semaphore()
    near = []
    for step in sorted({1, nz - 1} - {0}):
        near.append(device(z + step, y, nz, ny))
    for step in sorted({1, ny - 1} - {0}):
        near.append(device(z, y + step, nz, ny))
    for other in near:
        pl.semaphore_signal(barrier, inc=1, device_id={"expert": other}, device_id_type=MESH)
    pl.semaphore_wait(barrier, len(near))

def gather_kernel(nz, ny, own, out, local_sem, send_sem, recv_sem):
    z, y = places(nz, ny)
    rows = own.shape[0]
    half = rows // 2
    greet(nz, ny, z, y)

    def piece(s, t, h):
        sign = -1 if h == 0 else 1
        start = device(z + sign * s, y + sign * t, nz, ny) * rows + h * half
        return pl.ds(pl.multiple_of(start, half), half)

    def copy(s, t, h, s2, t2):
        step = 1 if h == 0 else -1
        source = own.at[pl.ds(h * half, half)] if s == 0 and t == 0 else out.at[piece(s, t, h)]
        to = device(z + step, y, nz, ny) if t2 == 0 else device(z, y + step, nz, ny)
        return pltpu.make_async_remote_copy(
            src_ref=source, dst_ref=out.at[piece(s, t, h)],
            send_sem=send_sem.at[s2, t2, h], recv_sem=recv_sem.at[s2, t2, h],
            device_id={"expert": to}, device_id_type=MESH)

    def arrival(s, t, h):
        return pltpu.make_async_remote_copy(
            src_ref=out.at[piece(s, t, h)], dst_ref=out.at[piece(s, t, h)],
            send_sem=send_sem.at[s, t, h], recv_sem=recv_sem.at[s, t, h],
            device_id={"expert": device(z, y, nz, ny)}, device_id_type=MESH)

    mine = pltpu.make_async_copy(own, out.at[pl.ds(pl.multiple_of(device(z, y, nz, ny) * rows, rows), rows)], local_sem)
    started = []
    def start(*key):
        c = copy(*key); c.start(); started.append(c)
    for h in range(2):
        start(0, 0, h, 1, 0)
    if ny > 1:
        for h in range(2):
            start(0, 0, h, 0, 1)
    mine.start()
    for s in range(1, nz):
        for h in range(2):
            arrival(s, 0, h).wait_recv()
            if s + 1 < nz:
                start(s, 0, h, s + 1, 0)
            if ny > 1:
                start(s, 0, h, s, 1)
    for t in range(1, ny):
        for s in range(nz):
            for h in range(2):
                arrival(s, t, h).wait_recv()
                if t + 1 < ny:
                    start(s, t, h, s, t + 1)
    mine.wait()
    for c in started:
        c.wait_send()

def all_rows(own, n_expert, cid, name):
    nz, ny = grid_of(n_expert)
    rows, width = own.shape
    return pl.pallas_call(
        functools.partial(gather_kernel, nz, ny),
        out_shape=jax.ShapeDtypeStruct((rows * n_expert, width), own.dtype),
        in_specs=[pl.BlockSpec(memory_space=pl.ANY)],
        out_specs=pl.BlockSpec(memory_space=pl.ANY),
        scratch_shapes=[pltpu.SemaphoreType.DMA, pltpu.SemaphoreType.DMA((nz, ny, 2)), pltpu.SemaphoreType.DMA((nz, ny, 2))],
        compiler_params=pltpu.CompilerParams(collective_id=cid, has_side_effects=True),
        name=name,
    )(own)

def scatter_kernel(nz, ny, whole, out, from_y, from_z, to_y, to_z, send_y, recv_y, send_z, recv_z):
    z, y = places(nz, ny)
    rows = out.shape[0]
    half = rows // 2
    greet(nz, ny, z, y)

    def piece(s, t, h):
        sign = -1 if h == 0 else 1
        start = device(z + sign * (s + 1), y + sign * (t + 1), nz, ny) * rows + h * half
        return pl.ds(pl.multiple_of(start, half), half)

    def y_copy(s, t, h):
        step = 1 if h == 0 else -1
        source = whole.at[piece(s, 0, h)] if t == 0 else to_y.at[s, t - 1, h]
        return pltpu.make_async_remote_copy(
            src_ref=source, dst_ref=from_y.at[s, t, h], send_sem=send_y.at[s, t, h], recv_sem=recv_y.at[s, t, h],
            device_id={"expert": device(z, y + step, nz, ny)}, device_id_type=MESH)

    def z_copy(s, h):
        step = 1 if h == 0 else -1
        return pltpu.make_async_remote_copy(
            src_ref=to_z.at[s, h], dst_ref=from_z.at[s, h], send_sem=send_z.at[s, h], recv_sem=recv_z.at[s, h],
            device_id={"expert": device(z + step, y, nz, ny)}, device_id_type=MESH)

    if ny > 1:
        for s in range(nz):
            for h in range(2):
                y_copy(s, 0, h).start()
    for s in range(nz):
        for t in range(1, ny - 1):
            for h in range(2):
                y_copy(s, t - 1, h).wait_recv()
                to_y[s, t - 1, h] = (whole[piece(s, t, h), :].astype(F32) + from_y[s, t - 1, h].astype(F32)).astype(BF16)
                y_copy(s, t, h).start()
        for h in range(2):
            total = whole[piece(s, ny - 1, h), :].astype(F32)
            if ny > 1:
                y_copy(s, ny - 2, h).wait_recv()
                total += from_y[s, ny - 2, h].astype(F32)
            if s > 0:
                z_copy(s - 1, h).wait_recv()
                total += from_z[s - 1, h].astype(F32)
            if s < nz - 1:
                to_z[s, h] = total.astype(BF16)
                z_copy(s, h).start()
            else:
                out[h * half : (h + 1) * half, :] = total
    for s in range(nz):
        for h in range(2):
            for t in range(ny - 1):
                y_copy(s, t, h).wait_send()
            if s < nz - 1:
                z_copy(s, h).wait_send()

def own_sum(whole, n_expert, cid, name):
    nz, ny = grid_of(n_expert)
    all_, width = whole.shape
    rows = all_ // n_expert
    half = rows // 2
    D = pltpu.SemaphoreType.DMA
    return pl.pallas_call(
        functools.partial(scatter_kernel, nz, ny),
        out_shape=jax.ShapeDtypeStruct((rows, width), F32),
        in_specs=[pl.BlockSpec(memory_space=pltpu.VMEM)],
        out_specs=pl.BlockSpec(memory_space=pltpu.VMEM),
        scratch_shapes=[
            pltpu.VMEM((nz, max(ny - 1, 1), 2, half, width), BF16),
            pltpu.VMEM((max(nz - 1, 1), 2, half, width), BF16),
            pltpu.VMEM((nz, max(ny - 2, 1), 2, half, width), BF16),
            pltpu.VMEM((max(nz - 1, 1), 2, half, width), BF16),
            D((nz, max(ny - 1, 1), 2)), D((nz, max(ny - 1, 1), 2)), D((max(nz - 1, 1), 2)), D((max(nz - 1, 1), 2))],
        compiler_params=pltpu.CompilerParams(collective_id=cid, has_side_effects=True, vmem_limit_bytes=48 << 20),
        name=name,
    )(whole)


def rms_norm(values, gain_vec):
    factor = lax.rsqrt(jnp.mean(values * values, axis=-1, keepdims=True) + EPSILON)
    return values * factor * gain_vec


def dot(left, right, left_dim=1, right_dim=0):
    return lax.dot_general(
        left, right, (((left_dim,), (right_dim,)), ((), ())), preferred_element_type=F32
    )


def rotate(values, cosine, sine):
    half = HEAD_DIM // 2
    one, two = values[:half], values[half:]
    return jnp.concatenate([one * cosine - two * sine, two * cosine + one * sine], axis=0)


def rotate_back(grads, cosine, sine):
    half = HEAD_DIM // 2
    one, two = grads[:half], grads[half:]
    return jnp.concatenate([one * cosine + two * sine, two * cosine - one * sine], axis=0)


def first_kernel(
    n_dp, nz, ny, rows, meta, heads, pack,
    rows_all, meta_all, heads_all, pack_all,
    send_sem, recv_sem, meta_send, meta_recv, dp_send, dp_recv, keep_sem,
):
    z, y = places(nz, ny)
    me, group = lax.axis_index("expert"), lax.axis_index("dp")
    count = rows.shape[0]
    half = count // 2
    barrier = pltpu.get_barrier_semaphore()
    near = [{"dp": lax.rem(group + k, n_dp)} for k in range(1, n_dp)]
    near += [{"expert": device(z + k, y, nz, ny)} for k in sorted({1, nz - 1} - {0})]
    near += [{"expert": device(z, y + k, nz, ny)} for k in sorted({1, ny - 1} - {0})]
    for other in near:
        pl.semaphore_signal(barrier, inc=1, device_id=other, device_id_type=MESH)
    pl.semaphore_wait(barrier, len(near))

    def origin(s, t, h):
        sign = -1 if h == 0 else 1
        return device(z + sign * s, y + sign * t, nz, ny)

    def copies(s, t, h, s2, t2):
        of = origin(s, t, h)
        mine = s == 0 and t == 0
        part = pl.ds(pl.multiple_of(of * count + h * half, half), half)
        step = 1 if h == 0 else -1
        to = device(z + step, y, nz, ny) if t2 == 0 else device(z, y + step, nz, ny)
        big = pltpu.make_async_remote_copy(
            src_ref=rows.at[pl.ds(h * half, half)] if mine else rows_all.at[part],
            dst_ref=rows_all.at[part],
            send_sem=send_sem.at[s2, t2, h], recv_sem=recv_sem.at[s2, t2, h],
            device_id={"expert": to}, device_id_type=MESH,
        )
        little = pltpu.make_async_remote_copy(
            src_ref=meta.at[h] if mine else meta_all.at[of, h], dst_ref=meta_all.at[of, h],
            send_sem=meta_send.at[s2, t2, h], recv_sem=meta_recv.at[s2, t2, h],
            device_id={"expert": to}, device_id_type=MESH,
        )
        return little, big

    def arrive(s, t, h):
        of = origin(s, t, h)
        part = pl.ds(pl.multiple_of(of * count + h * half, half), half)
        for place, sends, receives in (
            (meta_all.at[of, h], meta_send, meta_recv), (rows_all.at[part], send_sem, recv_sem)
        ):
            pltpu.make_async_remote_copy(
                src_ref=place, dst_ref=place, send_sem=sends.at[s, t, h], recv_sem=receives.at[s, t, h],
                device_id={"expert": device(z + 1, y, nz, ny)}, device_id_type=MESH,
            ).wait_recv()

    sent = []

    def start(*key):
        for copy in copies(*key):
            copy.start()
            sent.append(copy)

    for h in range(2):
        start(0, 0, h, 1, 0)
    if ny > 1:
        for h in range(2):
            start(0, 0, h, 0, 1)

    def across(k, a):
        source, target = ((heads, heads_all), (pack, pack_all))[a]
        return pltpu.make_async_remote_copy(
            src_ref=source, dst_ref=target.at[group],
            send_sem=dp_send.at[k - 1, a], recv_sem=dp_recv.at[k - 1, a],
            device_id={"dp": lax.rem(group + k, n_dp)}, device_id_type=MESH,
        )

    for k in range(1, n_dp):
        for a in range(2):
            across(k, a).start()
    keeps = [
        pltpu.make_async_copy(
            rows, rows_all.at[pl.ds(pl.multiple_of(me * count, count), count)], keep_sem.at[0]
        ),
        pltpu.make_async_copy(meta, meta_all.at[me], keep_sem.at[1]),
        pltpu.make_async_copy(heads, heads_all.at[group], keep_sem.at[2]),
        pltpu.make_async_copy(pack, pack_all.at[group], keep_sem.at[3]),
    ]
    for copy in keeps:
        copy.start()
    for s in range(1, nz):
        for h in range(2):
            arrive(s, 0, h)
            if s + 1 < nz:
                start(s, 0, h, s + 1, 0)
            if ny > 1:
                start(s, 0, h, s, 1)
    for t in range(1, ny):
        for s in range(nz):
            for h in range(2):
                arrive(s, t, h)
                if t + 1 < ny:
                    start(s, t, h, s, t + 1)
    for k in range(1, n_dp):
        for a, target in enumerate((heads_all, pack_all)):
            place = target.at[lax.rem(group + n_dp - k, n_dp)]
            pltpu.make_async_remote_copy(
                src_ref=place, dst_ref=place, send_sem=dp_send.at[k - 1, a], recv_sem=dp_recv.at[k - 1, a],
                device_id={"dp": lax.rem(group + k, n_dp)}, device_id_type=MESH,
            ).wait_recv()
    for copy in keeps:
        copy.wait()
    for copy in sent:
        copy.wait_send()
    for k in range(1, n_dp):
        for a in range(2):
            across(k, a).wait_send()


def first_gather(rows, meta, heads, pack, n_dp, n_expert, cid):
    nz, ny = grid_of(n_expert)
    anywhere = pl.BlockSpec(memory_space=pl.ANY)
    dma = pltpu.SemaphoreType.DMA
    ring, peers = dma((nz, ny, 2)), dma((max(n_dp - 1, 1), 2))
    return pl.pallas_call(
        functools.partial(first_kernel, n_dp, nz, ny),
        out_shape=[
            jax.ShapeDtypeStruct((rows.shape[0] * n_expert, rows.shape[1]), rows.dtype),
            jax.ShapeDtypeStruct((n_expert,) + meta.shape, meta.dtype),
            jax.ShapeDtypeStruct((n_dp,) + heads.shape, heads.dtype),
            jax.ShapeDtypeStruct((n_dp,) + pack.shape, pack.dtype),
        ],
        in_specs=[anywhere] * 4,
        out_specs=[anywhere] * 4,
        scratch_shapes=[ring, ring, ring, ring, peers, peers, dma((4,))],
        compiler_params=pltpu.CompilerParams(collective_id=cid, has_side_effects=True),
        name="first_gather",
    )(rows, meta, heads, pack)


def attend_kernel(
    nz, ny, low, high, key_pos, query, key, value_t, cotangent,
    out, lse, own_in, everyone,
    score_buf, weight_buf, send_buf, own_send, own_recv, send_sem, recv_sem, keep_sem,
):
    z, y = places(nz, ny)
    me = lax.axis_index("expert")
    n_expert = nz * ny
    heads, width, tile = query.shape
    low_row, high_row = low[...], high[...]
    steps = key.shape[0] // K_TILE
    tok_rows = cotangent.shape[0]
    half_rows = tok_rows // 2
    per_tile = tile // tok_rows
    i = pl.program_id(0)
    count = key.shape[0] // tile

    def piece(s, t, h):
        sign = -1 if h == 0 else 1
        begin = device(z + sign * s, y + sign * t, nz, ny) * tok_rows + h * half_rows
        return pl.ds(pl.multiple_of(begin, half_rows), half_rows)

    def row_copy(s, t, h, s2, t2):
        mine = s == 0 and t == 0
        step = 1 if h == 0 else -1
        to = device(z + step, y, nz, ny) if t2 == 0 else device(z, y + step, nz, ny)
        return pltpu.make_async_remote_copy(
            src_ref=cotangent.at[pl.ds(h * half_rows, half_rows)] if mine else everyone.at[piece(s, t, h)],
            dst_ref=everyone.at[piece(s, t, h)],
            send_sem=send_sem.at[s2, t2, h], recv_sem=recv_sem.at[s2, t2, h],
            device_id={"expert": to}, device_id_type=MESH,
        )

    def arrive(s, t, h):
        place = everyone.at[piece(s, t, h)]
        pltpu.make_async_remote_copy(
            src_ref=place, dst_ref=place, send_sem=send_sem.at[s, t, h], recv_sem=recv_sem.at[s, t, h],
            device_id={"expert": device(z + 1, y, nz, ny)}, device_id_type=MESH,
        ).wait_recv()

    def forward(s):
        for h in range(2):
            arrive(s, 0, h)
            if s + 1 < nz:
                row_copy(s, 0, h, s + 1, 0).start()
            if ny > 1:
                row_copy(s, 0, h, s, 1).start()

    def own_copy(other, source):
        return pltpu.make_async_remote_copy(
            src_ref=send_buf.at[other], dst_ref=own_in.at[source],
            send_sem=own_send.at[other], recv_sem=own_recv.at[source],
            device_id={"expert": other}, device_id_type=MESH,
        )

    keep = pltpu.make_async_copy(
        cotangent, everyone.at[pl.ds(pl.multiple_of(me * tok_rows, tok_rows), tok_rows)], keep_sem.at[0]
    )

    @pl.when(i == 0)
    def _():
        barrier = pltpu.get_barrier_semaphore()
        for k in range(1, n_expert):
            pl.semaphore_signal(
                barrier, inc=1, device_id={"expert": lax.rem(me + k, n_expert)}, device_id_type=MESH
            )
        pl.semaphore_wait(barrier, n_expert - 1)
        for h in range(2):
            row_copy(0, 0, h, 1, 0).start()
        if ny > 1:
            for h in range(2):
                row_copy(0, 0, h, 0, 1).start()
        keep.start()

    early = [s for s in range(1, nz) if 3 * s < count]
    for s in early:
        pl.when(i == 3 * s)(functools.partial(forward, s))

    def score_step(step, maxima):
        rows = pl.ds(pl.multiple_of(step * K_TILE, K_TILE), K_TILE)
        at = key_pos[rows, :]
        allowed = (at >= low_row) & (at <= high_row)
        found = []
        for head in range(heads):
            scores = jnp.dot(key[rows, :], query[head], preferred_element_type=F32)
            scores = jnp.where(allowed, scores, MASKED)
            score_buf[head, rows, :] = scores
            found.append(jnp.maximum(maxima[head], jnp.max(scores, axis=0, keepdims=True)))
        return tuple(found)

    begin = tuple(jnp.full(low_row.shape, MASKED, F32) for _ in range(heads))
    maxima = lax.fori_loop(0, steps, score_step, begin)

    def weight_step(step, totals):
        rows = pl.ds(pl.multiple_of(step * K_TILE, K_TILE), K_TILE)
        found = []
        for head in range(heads):
            weights = jnp.exp(score_buf[head, rows, :] - maxima[head])
            weight_buf[head, rows, :] = weights.astype(BF16)
            found.append(totals[head] + jnp.sum(weights, axis=0, keepdims=True))
        return tuple(found)

    begin = tuple(jnp.zeros(low_row.shape, F32) for _ in range(heads))
    totals = lax.fori_loop(0, steps, weight_step, begin)
    for head in range(heads):
        summed = jnp.dot(value_t[...], weight_buf[head], preferred_element_type=F32)
        attended = (summed / totals[head]).astype(BF16)
        out[head] = attended
        lse[head] = maxima[head] + jnp.log(totals[head])
        for j in range(per_tile):
            send_buf[i * per_tile + j, head * width : (head + 1) * width, :] = attended[
                :, j * tok_rows : (j + 1) * tok_rows
            ]
    for j in range(per_tile):
        other = i * per_tile + j

        @pl.when(other != me)
        def _():
            own_copy(other, me).start()

    @pl.when(i == count - 1)
    def _():
        mine = pltpu.make_async_copy(send_buf.at[me], own_in.at[me], keep_sem.at[1])
        mine.start()
        for s in range(1, nz):
            if s not in early:
                forward(s)
        for t in range(1, ny):
            for s in range(nz):
                for h in range(2):
                    arrive(s, t, h)
                    if t + 1 < ny:
                        row_copy(s, t, h, s, t + 1).start()
        for k in range(1, n_expert):
            other = lax.rem(me + k, n_expert)
            own_copy(other, other).wait_recv()
            own_copy(other, other).wait_send()
        for s in range(nz):
            for t in range(ny):
                for h in range(2):
                    if t > 0:
                        row_copy(s, t - 1, h, s, t).wait_send()
                    elif s > 0:
                        row_copy(s - 1, 0, h, s, 0).wait_send()
        keep.wait()
        mine.wait()


def attend(low, high, key_pos, query, key, value_t, cotangent, cid):
    heads, width, rows = query.shape
    tok_rows, model = cotangent.shape
    n_expert = rows // tok_rows
    nz, ny = grid_of(n_expert)
    tile = low_tile(rows)
    whole = lambda i: (0, 0)
    lane = lambda i: (0, i)
    anywhere = pl.BlockSpec(memory_space=pl.ANY)
    dma = pltpu.SemaphoreType.DMA
    return pl.pallas_call(
        functools.partial(attend_kernel, nz, ny),
        grid=(rows // tile,),
        in_specs=[
            pl.BlockSpec((1, tile), lane),
            pl.BlockSpec((1, tile), lane),
            pl.BlockSpec((rows, tile), whole),
            pl.BlockSpec((heads, width, tile), lambda i: (0, 0, i)),
            pl.BlockSpec((rows, width), whole),
            pl.BlockSpec((width, rows), whole),
            anywhere,
        ],
        out_specs=[
            pl.BlockSpec((heads, width, tile), lambda i: (0, 0, i)),
            pl.BlockSpec((heads, 1, tile), lambda i: (0, 0, i)),
            anywhere, anywhere,
        ],
        out_shape=[
            jax.ShapeDtypeStruct((heads, width, rows), BF16),
            jax.ShapeDtypeStruct((heads, 1, rows), F32),
            jax.ShapeDtypeStruct((n_expert, heads * width, tok_rows), BF16),
            jax.ShapeDtypeStruct((rows, model), BF16),
        ],
        scratch_shapes=[
            pltpu.VMEM((heads, rows, tile), F32),
            pltpu.VMEM((heads, rows, tile), BF16),
            pltpu.VMEM((n_expert, heads * width, tok_rows), BF16),
            dma((n_expert,)), dma((n_expert,)), dma((nz, ny, 2)), dma((nz, ny, 2)), dma((2,)),
        ],
        compiler_params=pltpu.CompilerParams(
            collective_id=cid, has_side_effects=True, vmem_limit_bytes=40 << 20
        ),
        cost_estimate=pl.CostEstimate(
            flops=4 * heads * rows * rows * 256,
            bytes_accessed=8 * rows * 256,
            transcendentals=heads * rows * rows,
        ),
        name="attend",
    )(low, high, key_pos, query, key, value_t, cotangent)


def low_tile(rows):
    return min(Q_TILE, rows)


def attend_back_kernel(
    nz, ny,
    low, high, key_pos, query, key, key_t, value, grad, lse, delta,
    cos_tab, sin_tab, made, out_part,
    own_in, proj, summed, out_sum,
    d_key, d_value, query_n, grad_n, out_in, score_buf, send_buf, part_buf, from_y, from_z, to_y, to_z,
    part_sem, own_send, own_recv, tail_send, tail_recv, keep_sem,
    send_y, recv_y, send_z, recv_z, dp_send, dp_recv,
):
    z, y = places(nz, ny)
    me, group = lax.axis_index("expert"), lax.axis_index("dp")
    n_expert, n_dp = nz * ny, out_part.shape[0]
    heads, width, tile = query.shape
    low_row, high_row = low[...], high[...]
    steps = key.shape[0] // K_TILE
    tok_rows = summed.shape[0]
    half_rows = tok_rows // 2
    per_tile = tile // tok_rows
    i = pl.program_id(0)
    count = key.shape[0] // tile
    q_cols = heads * width

    def piece(r, t, h):
        sign = -1 if h == 0 else 1
        start = device(z + sign * (r + 1), y + sign * (t + 1), nz, ny) * tok_rows + h * half_rows
        return pl.ds(pl.multiple_of(start, half_rows), half_rows)

    def near(along_z, h):
        step = 1 if h == 0 else -1
        to = device(z + step, y, nz, ny) if along_z else device(z, y + step, nz, ny)
        return {"expert": to}

    def part_copy(r, t, h):
        return pltpu.make_async_copy(
            made.at[piece(r, t, h)], part_buf.at[r, t, h], part_sem.at[r, t, h]
        )

    def y_copy(r, t, h):
        source = made.at[piece(r, 0, h)] if t == 0 else to_y.at[r, t - 1, h]
        return pltpu.make_async_remote_copy(
            src_ref=source, dst_ref=from_y.at[r, t, h],
            send_sem=send_y.at[r, t, h], recv_sem=recv_y.at[r, t, h],
            device_id=near(False, h), device_id_type=MESH,
        )

    def z_copy(r, h):
        return pltpu.make_async_remote_copy(
            src_ref=to_z.at[r, h], dst_ref=from_z.at[r, h],
            send_sem=send_z.at[r, h], recv_sem=recv_z.at[r, h],
            device_id=near(True, h), device_id_type=MESH,
        )

    def finish(r):
        for t in range(1, ny - 1):
            for h in range(2):
                y_copy(r, t - 1, h).wait_recv()
                part_copy(r, t, h).wait()
                to_y[r, t - 1, h] = (
                    part_buf[r, t, h].astype(F32) + from_y[r, t - 1, h].astype(F32)
                ).astype(BF16)
                y_copy(r, t, h).start()
        for h in range(2):
            part_copy(r, ny - 1, h).wait()
            total = part_buf[r, ny - 1, h].astype(F32)
            if ny > 1:
                y_copy(r, ny - 2, h).wait_recv()
                total += from_y[r, ny - 2, h].astype(F32)
            if r > 0:
                z_copy(r - 1, h).wait_recv()
                total += from_z[r - 1, h].astype(F32)
            if r < nz - 1:
                to_z[r, h] = total.astype(BF16)
                z_copy(r, h).start()
            else:
                summed[h * half_rows : (h + 1) * half_rows, :] = total

    def across(k):
        other = lax.rem(group + k, n_dp)
        return pltpu.make_async_remote_copy(
            src_ref=out_part.at[other], dst_ref=out_in.at[k - 1],
            send_sem=dp_send.at[k - 1], recv_sem=dp_recv.at[k - 1],
            device_id={"dp": other}, device_id_type=MESH,
        )

    head_rows, tail_rows = pl.ds(0, q_cols), pl.ds(q_cols, 2 * width)

    def own_copy(rows, other, source, sends, receives):
        return pltpu.make_async_remote_copy(
            src_ref=send_buf.at[other, rows], dst_ref=own_in.at[source, rows],
            send_sem=sends.at[other], recv_sem=receives.at[source],
            device_id={"expert": other}, device_id_type=MESH,
        )

    @pl.when(i == 0)
    def _():
        barrier = pltpu.get_barrier_semaphore()
        for k in range(1, n_expert):
            pl.semaphore_signal(
                barrier, inc=1, device_id={"expert": lax.rem(me + k, n_expert)}, device_id_type=MESH
            )
        for k in range(1, n_dp):
            pl.semaphore_signal(
                barrier, inc=1, device_id={"dp": lax.rem(group + k, n_dp)}, device_id_type=MESH
            )
        pl.semaphore_wait(barrier, n_expert + n_dp - 2)
        for k in range(1, n_dp):
            across(k).start()
        for r in range(nz):
            for h in range(2):
                if ny > 1:
                    y_copy(r, 0, h).start()
                for t in range(1, ny - 1):
                    part_copy(r, t, h).start()
                part_copy(r, ny - 1, h).start()
        d_key[...] = jnp.zeros_like(d_key)
        d_value[...] = jnp.zeros_like(d_value)

    for r in range(nz - 1):
        pl.when(i == (r + 1) * count // nz)(functools.partial(finish, r))

    for head in range(heads):
        query_n[head] = query[head].T
        grad_n[head] = grad[head].T

    @pl.loop(0, steps)
    def _(step):
        rows = pl.ds(pl.multiple_of(step * K_TILE, K_TILE), K_TILE)
        at = key_pos[rows, :]
        allowed = (at >= low_row) & (at <= high_row)
        key_sum, value_sum = d_key[rows, :], d_value[rows, :]
        for head in range(heads):
            scores = jnp.dot(key[rows, :], query[head], preferred_element_type=F32)
            weights = jnp.exp(jnp.where(allowed, scores - lse[head], MASKED))
            d_soft = jnp.dot(value[rows, :], grad[head], preferred_element_type=F32)
            d_scores = (weights * (d_soft - delta[head])).astype(BF16)
            score_buf[head, rows, :] = d_scores
            key_sum += jnp.dot(d_scores, query_n[head], preferred_element_type=F32)
            value_sum += jnp.dot(weights.astype(BF16), grad_n[head], preferred_element_type=F32)
        d_key[rows, :] = key_sum
        d_value[rows, :] = value_sum

    lanes = pl.ds(pl.multiple_of(i * tile, tile), tile)
    for head in range(heads):
        d_query = jnp.dot(key_t[...], score_buf[head], preferred_element_type=F32) * SCORE_SCALE
        turned = rotate_back(d_query, cos_tab[:, lanes], sin_tab[:, lanes]).astype(BF16)
        for j in range(per_tile):
            send_buf[i * per_tile + j, head * width : (head + 1) * width, :] = turned[
                :, j * tok_rows : (j + 1) * tok_rows
            ]
    for j in range(per_tile):
        other = i * per_tile + j

        @pl.when(other != me)
        def _():
            own_copy(head_rows, other, me, own_send, own_recv).start()

    @pl.when(i == count - 1)
    def _():
        for other in range(n_expert):
            rows = pl.ds(other * tok_rows, tok_rows)
            turned = rotate_back(d_key[rows, :].T, cos_tab[:, rows], sin_tab[:, rows])
            send_buf[other, q_cols : q_cols + width, :] = turned.astype(BF16)
            send_buf[other, q_cols + width :, :] = d_value[rows, :].T.astype(BF16)

            @pl.when(other != me)
            def _():
                own_copy(tail_rows, other, me, tail_send, tail_recv).start()

        keep = pltpu.make_async_copy(send_buf, proj, keep_sem.at[0])
        mine = pltpu.make_async_copy(send_buf.at[me], own_in.at[me], keep_sem.at[1])
        keep.start()
        mine.start()
        out_total = out_part[group].astype(F32)
        for k in range(1, n_dp):
            across(k).wait_recv()
            out_total += out_in[k - 1].astype(F32)
        out_sum[...] = out_total.astype(BF16)
        finish(nz - 1)
        for k in range(1, n_dp):
            across(k).wait_send()
        for k in range(1, n_expert):
            other = lax.rem(me + k, n_expert)
            for rows, sends, receives in (
                (head_rows, own_send, own_recv), (tail_rows, tail_send, tail_recv)
            ):
                own_copy(rows, other, other, sends, receives).wait_recv()
                own_copy(rows, other, other, sends, receives).wait_send()
        for r in range(nz):
            for h in range(2):
                for t in range(ny - 1):
                    y_copy(r, t, h).wait_send()
                if r < nz - 1:
                    z_copy(r, h).wait_send()
        keep.wait()
        mine.wait()


def attend_back(
    low, high, key_pos, query, key, key_t, value, grad, lse, delta,
    cosine, sine, made, out_part, tok_rows, cid,
):
    heads, width, rows = query.shape
    n_expert = rows // tok_rows
    nz, ny = grid_of(n_expert)
    cols = (heads + 2) * width
    half_rows, model = tok_rows // 2, made.shape[1]
    tile = low_tile(rows)
    whole = lambda i: (0, 0)
    lane = lambda i: (0, i)
    wide = pl.BlockSpec((heads, width, tile), lambda i: (0, 0, i))
    row = pl.BlockSpec((heads, 1, tile), lambda i: (0, 0, i))
    keys = pl.BlockSpec((rows, width), whole)
    anywhere = pl.BlockSpec(memory_space=pl.ANY)
    dma = pltpu.SemaphoreType.DMA
    y_steps, y_mid, z_steps = max(ny - 1, 1), max(ny - 2, 1), max(nz - 1, 1)
    peers = max(out_part.shape[0] - 1, 1)
    return pl.pallas_call(
        functools.partial(attend_back_kernel, nz, ny),
        grid=(rows // tile,),
        in_specs=[
            pl.BlockSpec((1, tile), lane),
            pl.BlockSpec((1, tile), lane),
            pl.BlockSpec((rows, tile), whole),
            wide, keys, pl.BlockSpec((width, rows), whole), keys, wide, row, row,
            pl.BlockSpec((width // 2, rows), whole), pl.BlockSpec((width // 2, rows), whole),
            anywhere, pl.BlockSpec(out_part.shape, lambda i: (0, 0, 0)),
        ],
        out_specs=[
            anywhere, anywhere, pl.BlockSpec((tok_rows, model), whole),
            pl.BlockSpec(out_part.shape[1:], whole),
        ],
        out_shape=[
            jax.ShapeDtypeStruct((n_expert, cols, tok_rows), BF16),
            jax.ShapeDtypeStruct((n_expert, cols, tok_rows), BF16),
            jax.ShapeDtypeStruct((tok_rows, model), F32),
            jax.ShapeDtypeStruct(out_part.shape[1:], BF16),
        ],
        scratch_shapes=[
            pltpu.VMEM((rows, width), F32),
            pltpu.VMEM((rows, width), F32),
            pltpu.VMEM((heads, tile, width), BF16),
            pltpu.VMEM((heads, tile, width), BF16),
            pltpu.VMEM((peers,) + out_part.shape[1:], BF16),
            pltpu.VMEM((heads, rows, tile), BF16),
            pltpu.VMEM((n_expert, cols, tok_rows), BF16),
            pltpu.VMEM((nz, ny, 2, half_rows, model), BF16),
            pltpu.VMEM((nz, y_steps, 2, half_rows, model), BF16),
            pltpu.VMEM((z_steps, 2, half_rows, model), BF16),
            pltpu.VMEM((nz, y_mid, 2, half_rows if ny > 2 else 16, model), BF16),
            pltpu.VMEM((z_steps, 2, half_rows, model), BF16),
            dma((nz, ny, 2)), dma((n_expert,)), dma((n_expert,)), dma((n_expert,)), dma((n_expert,)), dma((2,)),
            dma((nz, y_steps, 2)), dma((nz, y_steps, 2)), dma((z_steps, 2)), dma((z_steps, 2)),
            dma((peers,)), dma((peers,)),
        ],
        compiler_params=pltpu.CompilerParams(
            collective_id=cid, has_side_effects=True, vmem_limit_bytes=56 << 20
        ),
        cost_estimate=pl.CostEstimate(
            flops=10 * heads * rows * rows * 256,
            bytes_accessed=8 * rows * 256,
            transcendentals=heads * rows * rows,
        ),
        name="attend_back",
    )(low, high, key_pos, query, key, key_t, value, grad, lse, delta, cosine, sine, made, out_part)


def finish_kernel(
    n_dp, nz, ny, q_cols, qkv, own_proj, small,
    qkv_rows, proj_rows, small_sum,
    qkv_in, small_in, own_qkv, own_small, qkv_all, proj_all, small_all, proj_got,
    dp_send, dp_recv, ring_send, ring_recv, last_send, last_recv, keep_sem,
):
    z, y = places(nz, ny)
    me, group = lax.axis_index("expert"), lax.axis_index("dp")
    n_expert = nz * ny
    share = n_expert // n_dp
    barrier = pltpu.get_barrier_semaphore()
    near = [{"dp": lax.rem(group + k, n_dp)} for k in range(1, n_dp)]
    near += [{"expert": device(z + k, y, nz, ny)} for k in sorted({1, nz - 1} - {0})]
    near += [{"expert": device(z, y + k, nz, ny)} for k in sorted({1, ny - 1} - {0})]
    for other in near:
        pl.semaphore_signal(barrier, inc=1, device_id=other, device_id_type=MESH)
    pl.semaphore_wait(barrier, len(near))

    arrays = {0: (qkv, qkv_in, own_qkv), 2: (small, small_in, own_small)}

    def across(k, a):
        source, target, _ = arrays[a]
        other = lax.rem(group + k, n_dp)
        return pltpu.make_async_remote_copy(
            src_ref=source.at[other], dst_ref=target.at[k - 1],
            send_sem=dp_send.at[k - 1, a], recv_sem=dp_recv.at[k - 1, a],
            device_id={"dp": other}, device_id_type=MESH,
        )

    rings = ((own_qkv, qkv_all), (own_proj, proj_all), (own_small, small_all))

    def origin(s, t, h):
        sign = -1 if h == 0 else 1
        return device(z + sign * s, y + sign * t, nz, ny)

    def ring_copy(s, t, h, s2, t2, a):
        own, everyone = rings[a]
        of = origin(s, t, h)
        rows = own.shape[0] // 2 if a < 2 else own.shape[0]
        part = pl.ds(h * rows, rows)
        source = own.at[part] if s == 0 and t == 0 else everyone.at[of, part]
        step = 1 if h == 0 else -1
        to = device(z + step, y, nz, ny) if t2 == 0 else device(z, y + step, nz, ny)
        return pltpu.make_async_remote_copy(
            src_ref=source, dst_ref=everyone.at[of, part],
            send_sem=ring_send.at[s2, t2, h, a], recv_sem=ring_recv.at[s2, t2, h, a],
            device_id={"expert": to}, device_id_type=MESH,
        )

    def arrive(s, t, h, a):
        own, everyone = rings[a]
        rows = own.shape[0] // 2 if a < 2 else own.shape[0]
        place = everyone.at[origin(s, t, h), pl.ds(h * rows, rows)]
        pltpu.make_async_remote_copy(
            src_ref=place, dst_ref=place,
            send_sem=ring_send.at[s, t, h, a], recv_sem=ring_recv.at[s, t, h, a],
            device_id={"expert": device(z + 1, y, nz, ny)}, device_id_type=MESH,
        ).wait_recv()

    sent, keeps = [], []

    def start(*key):
        copy = ring_copy(*key)
        copy.start()
        sent.append(copy)

    def begin(moves):
        for a in sorted({a for _, a in moves}):
            own, everyone = rings[a]
            keeps.append(pltpu.make_async_copy(own, everyone.at[me], keep_sem.at[a]))
            keeps[-1].start()
        for h, a in moves:
            if nz > 1:
                start(0, 0, h, 1, 0, a)
            if ny > 1:
                start(0, 0, h, 0, 1, a)

    def along_z(moves):
        for s in range(1, nz):
            for h, a in moves:
                arrive(s, 0, h, a)
                if s + 1 < nz:
                    start(s, 0, h, s + 1, 0, a)
                if ny > 1:
                    start(s, 0, h, s, 1, a)

    def along_y(moves):
        for t in range(1, ny):
            for s in range(nz):
                for h, a in moves:
                    arrive(s, t, h, a)
                    if t + 1 < ny:
                        start(s, t, h, s, t + 1, a)

    early, late = [(0, 1), (1, 1)], [(0, 0), (1, 0), (0, 2)]
    for k in range(1, n_dp):
        for a in arrays:
            across(k, a).start()
    begin(early)
    for a, (source, target, own) in arrays.items():
        total = source[group].astype(F32)
        for k in range(1, n_dp):
            across(k, a).wait_recv()
            total += target[k - 1].astype(F32)
        own[...] = total.astype(own.dtype)
    begin(late)
    along_z(early)
    along_y(early)
    keeps[0].wait()

    def last(k):
        other = lax.rem(group + k, n_dp)
        return pltpu.make_async_remote_copy(
            src_ref=proj_all.at[pl.ds(other * share, share)], dst_ref=proj_got.at[group],
            send_sem=last_send.at[k - 1], recv_sem=last_recv.at[k - 1],
            device_id={"dp": other}, device_id_type=MESH,
        )

    for k in range(1, n_dp):
        last(k).start()
    mine = pltpu.make_async_copy(
        proj_all.at[pl.ds(group * share, share)], proj_got.at[group], keep_sem.at[3]
    )
    mine.start()
    along_z(late)
    along_y(late)
    for copy in keeps[1:]:
        copy.wait()
    total = small_all[0]
    for other in range(1, n_expert):
        total += small_all[other]
    small_sum[...] = total
    for k in range(1, n_dp):
        last(k).wait_recv()
    mine.wait()
    high, wide = own_proj.shape
    for c in range(n_dp):
        for part in range(share):
            proj_rows[part * high : (part + 1) * high, c * wide : (c + 1) * wide] = proj_got[
                c, part
            ].astype(F32)
    alike = max(n_expert // KV_HEADS, 1)
    pieces = [qkv_all[m, :, :q_cols].astype(F32) for m in range(n_expert)]
    for first in (q_cols, q_cols + HEAD_DIM):
        for head in range(KV_HEADS):
            total = qkv_all[head * alike, :, first : first + HEAD_DIM].astype(F32)
            for more in range(1, alike):
                total += qkv_all[head * alike + more, :, first : first + HEAD_DIM].astype(F32)
            pieces.append(total)
    at = 0
    while pieces:
        block = [pieces.pop(0)]
        if block[0].shape[1] % 128:
            block.append(pieces.pop(0))
        joined = jnp.concatenate(block, axis=1) if len(block) > 1 else block[0]
        qkv_rows[:, at : at + joined.shape[1]] = joined
        at += joined.shape[1]
    for copy in sent:
        copy.wait_send()
    for k in range(1, n_dp):
        last(k).wait_send()
        for a in arrays:
            across(k, a).wait_send()


def finish_sums(qkv, own_proj, small, q_cols, n_expert, cid):
    nz, ny = grid_of(n_expert)
    n_dp = qkv.shape[0]
    high, wide = own_proj.shape
    share = n_expert // n_dp
    whole = pl.BlockSpec(memory_space=pltpu.VMEM)
    dma = pltpu.SemaphoreType.DMA
    peers = max(n_dp - 1, 1)
    return pl.pallas_call(
        functools.partial(finish_kernel, n_dp, nz, ny, q_cols),
        out_shape=[
            jax.ShapeDtypeStruct((qkv.shape[1], (HEADS + 2 * KV_HEADS) * HEAD_DIM), F32),
            jax.ShapeDtypeStruct((share * high, n_dp * wide), F32),
            jax.ShapeDtypeStruct(small.shape[1:], F32),
        ],
        in_specs=[whole] * 3,
        out_specs=[whole] * 3,
        scratch_shapes=[
            pltpu.VMEM((peers,) + qkv.shape[1:], BF16),
            pltpu.VMEM((peers,) + small.shape[1:], F32),
            pltpu.VMEM(qkv.shape[1:], BF16),
            pltpu.VMEM(small.shape[1:], F32),
            pltpu.VMEM((n_expert,) + qkv.shape[1:], BF16),
            pltpu.VMEM((n_expert,) + own_proj.shape, BF16),
            pltpu.VMEM((n_expert,) + small.shape[1:], F32),
            pltpu.VMEM((n_dp, share, high, wide), BF16),
            dma((peers, 3)), dma((peers, 3)), dma((nz, ny, 2, 3)), dma((nz, ny, 2, 3)),
            dma((peers,)), dma((peers,)), dma((4,)),
        ],
        compiler_params=pltpu.CompilerParams(
            collective_id=cid, has_side_effects=True, vmem_limit_bytes=32 << 20
        ),
        name="finish_sums",
    )(qkv, own_proj, small)


def experts_kernel(
    nz, ny, own, named, router, cotangent, weight_in, weight_out,
    back, d_gate, made, grads_in, grads_out,
    rows_buf, cot_buf, in_buf, out_buf, hid_buf, gu_buf, part_buf, made_buf, gin_buf, gout_buf,
    gate_out, gate_in, from_y, from_z, to_y, to_z,
    load_sem, cot_sem, made_sem, grad_sem, send_sem, recv_sem, gate_send, gate_recv,
    send_y, recv_y, send_z, recv_z,
):
    z, y = places(nz, ny)
    me = lax.axis_index("expert")
    n_expert = nz * ny
    tok_rows, width = own.shape
    half = tok_rows // 2
    step_rows = ny * tok_rows
    exp_dev, ff, _ = out_buf.shape
    experts = named.shape[1]

    barrier = pltpu.get_barrier_semaphore()
    for k in range(1, n_expert):
        pl.semaphore_signal(
            barrier, inc=1, device_id={"expert": lax.rem(me + k, n_expert)}, device_id_type=MESH
        )
    pl.semaphore_wait(barrier, n_expert - 1)

    def owner(s, t, h):
        sign = -1 if h == 0 else 1
        return device(z + sign * s, y + sign * t, nz, ny)

    def piece(s, t, h):
        return pl.ds(pl.multiple_of(owner(s, t, h) * tok_rows + h * half, half), half)

    def slot(s, t, h):
        return pl.ds(((s * ny + t) * 2 + h) * half, half)

    def near(along_z, h):
        step = 1 if h == 0 else -1
        to = device(z + step, y, nz, ny) if along_z else device(z, y + step, nz, ny)
        return {"expert": to}

    def row_copy(s, t, h, s2, t2):
        source = own.at[pl.ds(h * half, half)] if s == 0 and t == 0 else rows_buf.at[slot(s, t, h)]
        return pltpu.make_async_remote_copy(
            src_ref=source, dst_ref=rows_buf.at[slot(s2, t2, h)],
            send_sem=send_sem.at[s2, t2, h], recv_sem=recv_sem.at[s2, t2, h],
            device_id=near(t2 == 0, h), device_id_type=MESH,
        )

    def arrive(s, t, h):
        if t == 0:
            row_copy(s - 1, 0, h, s, 0).wait_recv()
        else:
            row_copy(s, t - 1, h, s, t).wait_recv()

    sent = []

    def start(*key):
        copy = row_copy(*key)
        copy.start()
        sent.append(copy)

    for h in range(2):
        start(0, 0, h, 1, 0)
    if ny > 1:
        for h in range(2):
            start(0, 0, h, 0, 1)
    loads = [
        pltpu.make_async_copy(weight_in, in_buf, load_sem.at[0]),
        pltpu.make_async_copy(weight_out, out_buf, load_sem.at[1]),
    ]
    for copy in loads:
        copy.start()
    cots = {
        (s, t, h): pltpu.make_async_copy(
            cotangent.at[piece(s, t, h)], cot_buf.at[slot(s, t, h)], cot_sem.at[s, t, h]
        )
        for s in range(nz) for t in range(ny) for h in range(2)
    }
    for copy in cots.values():
        copy.start()
    rows_buf[0:tok_rows, :] = own[...]
    for copy in loads:
        copy.wait()

    lane = lax.broadcasted_iota(jnp.int32, (step_rows, experts), 1)
    wide_lane = lax.broadcasted_iota(jnp.int32, (step_rows, 128), 1)
    tile = 256

    def compute(s):
        rows = pl.ds(s * step_rows, step_rows)
        picked = jnp.concatenate(
            [named[piece(s, t, h), :] for t in range(ny) for h in range(2)], axis=0
        ) > 0.5
        logits = jnp.where(picked, dot(rows_buf[rows, :], router[...], 1, 1), MASKED)
        powers = jnp.exp(logits - jnp.max(logits, axis=1, keepdims=True))
        powers = jnp.where(picked, powers, 0.0)
        gates = powers / jnp.sum(powers, axis=1, keepdims=True)
        found = jnp.zeros((step_rows, 128), F32)
        for e in range(exp_dev):
            weight = jnp.sum(
                jnp.where(lane == me * exp_dev + e, gates, 0.0), axis=1, keepdims=True
            )

            def hidden_step(j, total):
                at = pl.multiple_of(j * tile, tile)
                cols, late = pl.ds(at, tile), pl.ds(pl.multiple_of(ff + at, tile), tile)
                gate_pre = dot(rows_buf[rows, :], in_buf[e, :, cols])
                up_pre = dot(rows_buf[rows, :], in_buf[e, :, late])
                d_plain = dot(cot_buf[rows, :], out_buf[e, cols, :], 1, 1)
                sigmoid = jax.nn.sigmoid(gate_pre)
                active = gate_pre * sigmoid
                hidden = active * up_pre
                hid_buf[e, rows, cols] = (weight * hidden).astype(BF16)
                d_hidden = weight * d_plain
                gu_buf[e, rows, cols] = (
                    d_hidden * up_pre * sigmoid * (1.0 + gate_pre * (1.0 - sigmoid))
                ).astype(BF16)
                gu_buf[e, rows, late] = (d_hidden * active).astype(BF16)
                return total + jnp.sum(hidden * d_plain, axis=1, keepdims=True)

            total = lax.fori_loop(0, ff // tile, hidden_step, jnp.zeros((step_rows, 1), F32))
            found += jnp.where(wide_lane == me * exp_dev + e, total, 0.0)

        @pl.loop(0, width // tile)
        def _(n):
            cols = pl.ds(pl.multiple_of(n * tile, tile), tile)
            d_rows = dot(gu_buf[0, rows, :], in_buf[0, cols, :], 1, 1)
            for e in range(1, exp_dev):
                d_rows += dot(gu_buf[e, rows, :], in_buf[e, cols, :], 1, 1)
            part_buf[rows, cols] = d_rows.astype(BF16)
            made_sum = dot(hid_buf[0, rows, :], out_buf[0, :, cols])
            for e in range(1, exp_dev):
                made_sum += dot(hid_buf[e, rows, :], out_buf[e, :, cols])
            made_buf[rows, cols] = made_sum.astype(BF16)

        for t in range(ny):
            for h in range(2):
                low = (t * 2 + h) * half
                gate_out[s, t, h] = found[low : low + half, :].T[:experts, :]
                if s or t:
                    gate_copy(s, t, h).start()
                made_copy(s, t, h).start()

    def gate_copy(s, t, h):
        return pltpu.make_async_remote_copy(
            src_ref=gate_out.at[s, t, h], dst_ref=gate_in.at[s, t, h],
            send_sem=gate_send.at[s, t, h], recv_sem=gate_recv.at[s, t, h],
            device_id={"expert": owner(s, t, h)}, device_id_type=MESH,
        )

    def made_copy(s, t, h):
        return pltpu.make_async_copy(
            made_buf.at[slot(s, t, h)], made.at[piece(s, t, h)], made_sem.at[s, t, h]
        )

    def part(r, t, h):
        return slot((r + 1) % nz, (t + 1) % ny, h)

    def y_copy(r, t, h):
        source = part_buf.at[part(r, 0, h)] if t == 0 else to_y.at[r, t - 1, h]
        return pltpu.make_async_remote_copy(
            src_ref=source, dst_ref=from_y.at[r, t, h],
            send_sem=send_y.at[r, t, h], recv_sem=recv_y.at[r, t, h],
            device_id=near(False, h), device_id_type=MESH,
        )

    def z_copy(r, h):
        return pltpu.make_async_remote_copy(
            src_ref=to_z.at[r, h], dst_ref=from_z.at[r, h],
            send_sem=send_z.at[r, h], recv_sem=recv_z.at[r, h],
            device_id=near(True, h), device_id_type=MESH,
        )

    def first_y(r):
        if ny > 1:
            for h in range(2):
                y_copy(r, 0, h).start()

    def finish(r):
        for t in range(1, ny - 1):
            for h in range(2):
                y_copy(r, t - 1, h).wait_recv()
                to_y[r, t - 1, h] = (
                    part_buf[part(r, t, h), :].astype(F32) + from_y[r, t - 1, h].astype(F32)
                ).astype(BF16)
                y_copy(r, t, h).start()
        for h in range(2):
            total = part_buf[part(r, ny - 1, h), :].astype(F32)
            if ny > 1:
                y_copy(r, ny - 2, h).wait_recv()
                total += from_y[r, ny - 2, h].astype(F32)
            if r > 0:
                z_copy(r - 1, h).wait_recv()
                total += from_z[r - 1, h].astype(F32)
            if r < nz - 1:
                to_z[r, h] = total.astype(BF16)
                z_copy(r, h).start()
            else:
                back[h * half : (h + 1) * half, :] = total

    def forward(s):
        for h in range(2):
            arrive(s, 0, h)
            if s + 1 < nz:
                start(s, 0, h, s + 1, 0)
            if ny > 1:
                start(s, 0, h, s, 1)

    def whole_step(s):
        for t in range(1, ny):
            for h in range(2):
                arrive(s, t, h)
                if t + 1 < ny:
                    start(s, t, h, s, t + 1)
        for t in range(ny):
            for h in range(2):
                cots[s, t, h].wait()
        compute(s)

    for s in range(nz):
        if s + 1 < nz:
            forward(s + 1)
        whole_step(s)
        if s > 0:
            first_y(s - 1)
        if s > 1:
            finish(s - 2)
    first_y(nz - 1)

    def grad_step(i):
        cols = pl.ds(pl.multiple_of(i * tile, tile), tile)
        for e in range(exp_dev):
            gin_buf[e, cols, :] = dot(rows_buf[:, cols], gu_buf[e], 0, 0).astype(BF16)

    def grad_out_step(i):
        cols = pl.ds(pl.multiple_of(i * tile, tile), tile)
        for e in range(exp_dev):
            gout_buf[e, cols, :] = dot(hid_buf[e, :, cols], cot_buf[...], 0, 0).astype(BF16)

    pl.loop(0, ff // tile)(grad_out_step)
    gout_copy = pltpu.make_async_copy(gout_buf, grads_out, grad_sem.at[0])
    gout_copy.start()
    if nz > 1:
        finish(nz - 2)
    pl.loop(0, width // tile)(grad_step)
    gin_copy = pltpu.make_async_copy(gin_buf, grads_in, grad_sem.at[1])
    gin_copy.start()
    finish(nz - 1)
    for h in range(2):
        gate_sum = gate_out[0, 0, h]
        for s in range(nz):
            for t in range(ny):
                if s or t:
                    gate_copy(s, t, h).wait_recv()
                    gate_sum += gate_in[s, t, h]
        d_gate[h] = gate_sum
    for copy in sent:
        copy.wait_send()
    for s in range(nz):
        for h in range(2):
            for t in range(ny):
                made_copy(s, t, h).wait()
                if s or t:
                    gate_copy(s, t, h).wait_send()
            for t in range(ny - 1):
                y_copy(s, t, h).wait_send()
            if s < nz - 1:
                z_copy(s, h).wait_send()
    gout_copy.wait()
    gin_copy.wait()


def experts_pass(own, named, router, cotangent, weight_in, weight_out, n_expert, cid):
    nz, ny = grid_of(n_expert)
    tok_rows, width = own.shape
    exp_dev, ff, _ = weight_out.shape
    half, group = tok_rows // 2, tok_rows * n_expert
    experts = named.shape[1]
    whole, anywhere = pl.BlockSpec(memory_space=pltpu.VMEM), pl.BlockSpec(memory_space=pl.ANY)
    dma = pltpu.SemaphoreType.DMA
    ring = dma((nz, ny, 2))
    y_steps, y_mid, z_steps = max(ny - 1, 1), max(ny - 2, 1), max(nz - 1, 1)
    return pl.pallas_call(
        functools.partial(experts_kernel, nz, ny),
        out_shape=[
            jax.ShapeDtypeStruct((tok_rows, width), F32),
            jax.ShapeDtypeStruct((2, experts, half), F32),
            jax.ShapeDtypeStruct((group, width), BF16),
            jax.ShapeDtypeStruct((exp_dev, width, 2 * ff), BF16),
            jax.ShapeDtypeStruct((exp_dev, ff, width), BF16),
        ],
        in_specs=[whole, whole, whole, anywhere, anywhere, anywhere],
        out_specs=[whole, whole, anywhere, anywhere, anywhere],
        scratch_shapes=[
            pltpu.VMEM((group, width), BF16),
            pltpu.VMEM((group, width), BF16),
            pltpu.VMEM((exp_dev, width, 2 * ff), BF16),
            pltpu.VMEM((exp_dev, ff, width), BF16),
            pltpu.VMEM((exp_dev, group, ff), BF16),
            pltpu.VMEM((exp_dev, group, 2 * ff), BF16),
            pltpu.VMEM((group, width), BF16),
            pltpu.VMEM((group, width), BF16),
            pltpu.VMEM((exp_dev, width, 2 * ff), BF16),
            pltpu.VMEM((exp_dev, ff, width), BF16),
            pltpu.VMEM((nz, ny, 2, experts, half), F32),
            pltpu.VMEM((nz, ny, 2, experts, half), F32),
            pltpu.VMEM((nz, y_steps, 2, half, width), BF16),
            pltpu.VMEM((z_steps, 2, half, width), BF16),
            pltpu.VMEM((nz, y_mid, 2, half if ny > 2 else 16, width), BF16),
            pltpu.VMEM((z_steps, 2, half, width), BF16),
            dma((2,)), ring, ring, dma((2,)), ring, ring, ring, ring,
            dma((nz, y_steps, 2)), dma((nz, y_steps, 2)), dma((z_steps, 2)), dma((z_steps, 2)),
        ],
        compiler_params=pltpu.CompilerParams(
            collective_id=cid, has_side_effects=True, vmem_limit_bytes=60 << 20
        ),
        cost_estimate=pl.CostEstimate(
            flops=18 * exp_dev * group * width * ff,
            bytes_accessed=16 * group * width,
            transcendentals=exp_dev * group * ff,
        ),
        name="experts_pass",
    )(own, named, router, cotangent, weight_in, weight_out)


def gather(values, name, axis=0):
    return lax.all_gather(values, name, axis=axis, tiled=True)


def exchange(values, name="expert"):
    return lax.all_to_all(values, name, split_axis=0, concat_axis=0, tiled=True)


def give_back(partial):
    return lax.psum_scatter(
        partial.astype(BF16), "expert", scatter_dimension=0, tiled=True
    ).astype(F32)


def local(
    hidden_in, d_out, gain_attn, w_qkv, w_o, gain_moe, w_router, w_in, w_out,
    seq_lengths, assign, routes,
):
    tok_rows, width = hidden_in.shape
    exp_dev, _, ff_two = w_in.shape
    ff = ff_two // 2
    n_expert = lax.axis_size("expert")
    me = lax.axis_index("expert")
    experts = exp_dev * n_expert
    group_rows = tok_rows * n_expert
    q_per = HEADS // n_expert
    share = GROUPS // q_per
    q_cols = q_per * HEAD_DIM
    k_base = HEADS * HEAD_DIM
    v_base = k_base + KV_HEADS * HEAD_DIM
    cols = q_cols + 2 * HEAD_DIM

    n_dp = lax.axis_size("dp")
    wide = width // n_dp
    kv_head = (me * q_per) // GROUPS
    heads_part = jnp.concatenate(
        [
            lax.dynamic_slice_in_dim(w_qkv, me * q_cols, q_cols, 1),
            lax.dynamic_slice_in_dim(w_qkv, k_base + kv_head * HEAD_DIM, HEAD_DIM, 1),
            lax.dynamic_slice_in_dim(w_qkv, v_base + kv_head * HEAD_DIM, HEAD_DIM, 1),
        ],
        axis=1,
    )
    few = 2 + experts
    pack = jnp.concatenate(
        [gain_attn[None], gain_moe[None], w_router.T, jnp.zeros((-few % 16, wide), BF16)], axis=0
    )
    top = routes.shape[1]
    meta = jnp.concatenate(
        [assign, routes.T, jnp.zeros((-(1 + top) % 8, tok_rows), jnp.int32)], axis=0
    )
    meta = meta.reshape(meta.shape[0], 2, tok_rows // 2).transpose(1, 0, 2)
    hidden_all, meta, w_heads, pack = first_gather(
        hidden_in, meta, heads_part, pack, n_dp, n_expert, 0
    )
    w_heads = w_heads.reshape(width, cols)
    pack = pack.transpose(1, 0, 2).reshape(-1, width)
    gain_one, gain_two = pack[0].astype(F32), pack[1].astype(F32)
    router_t = pack[2:few]
    position = meta[:, :, 0].reshape(group_rows)
    routes_all = meta[:, :, 1 : 1 + top]
    named = jnp.any(
        routes_all[:, :, :, None, :] == jnp.arange(experts, dtype=jnp.int32)[:, None], axis=2
    ).transpose(0, 1, 3, 2).reshape(group_rows, experts)
    stream_in = hidden_in.astype(F32)
    normed_all = rms_norm(hidden_all.astype(F32), gain_one).astype(BF16)
    proj_full = gather(w_o, "dp")
    weight_in = gather(w_in, "dp", axis=1)
    weight_out = gather(w_out, "dp", axis=2)
    pieces = []
    for dev in range(n_expert):
        head = (dev * q_per) // GROUPS * HEAD_DIM
        pieces += [
            w_qkv[:, dev * q_cols : (dev + 1) * q_cols],
            w_qkv[:, k_base + head : k_base + head + HEAD_DIM],
            w_qkv[:, v_base + head : v_base + head + HEAD_DIM],
        ]
    qkv_full = gather(jnp.concatenate(pieces, axis=1), "dp")

    lengths = seq_lengths[0]
    order = jnp.arange(lengths.shape[0], dtype=jnp.int32)
    ends = jnp.sum(jnp.where(order[None, :] <= order[:, None], lengths[None, :], 0), axis=1)
    starts = ends - lengths
    seq_id = jnp.sum((position[None, :] >= ends[:, None]).astype(jnp.int32), axis=0)
    picks = seq_id[None, :] == jnp.arange(lengths.shape[0], dtype=jnp.int32)[:, None]
    start_of = jnp.sum(jnp.where(picks, starts[:, None], 0), axis=0)
    rot_pos = position - start_of
    half = HEAD_DIM // 2
    frequency = ROPE_BASE ** (-(jnp.arange(half).astype(F32) * (2.0 / HEAD_DIM)))
    angles = frequency[:, None] * rot_pos.astype(F32)[None, :]
    cosine, sine = jnp.cos(angles), jnp.sin(angles)
    low, high = start_of[None, :], position[None, :]
    key_pos = jnp.broadcast_to(position[:, None], (group_rows, low_tile(group_rows)))

    projected = dot(w_heads, normed_all, 0, 1)
    query = jnp.stack(
        [
            rotate(projected[h * HEAD_DIM : (h + 1) * HEAD_DIM], cosine, sine).astype(BF16)
            for h in range(q_per)
        ]
    ) * jnp.asarray(SCORE_SCALE, BF16)
    key_t = rotate(projected[q_cols : q_cols + HEAD_DIM], cosine, sine).astype(BF16)
    value_t = projected[q_cols + HEAD_DIM :].astype(BF16)
    key, value = key_t.T, value_t.T
    heads_out, lse, attended, d_out_all = attend(low, high, key_pos, query, key, value_t, d_out, 6)
    attended_t = heads_out.reshape(q_cols, group_rows)
    mid_stream = stream_in + dot(attended.reshape(n_expert * q_cols, tok_rows), proj_full, 0, 0)
    normed_two = rms_norm(mid_stream, gain_two).astype(BF16)

    d_back, d_gate, made, grads_in, grads_out = experts_pass(
        normed_two, named.astype(F32), router_t, d_out_all, weight_in, weight_out, n_expert, 1
    )
    d_gate = d_gate.transpose(0, 2, 1).reshape(tok_rows, experts)
    own_named = jnp.any(
        routes[:, :, None] == jnp.arange(experts, dtype=jnp.int32)[None, None, :], axis=1
    )
    own_gates = jax.nn.softmax(
        jnp.where(own_named, dot(normed_two, router_t, 1, 1), -jnp.inf), axis=1
    )
    d_logits = (
        own_gates * (d_gate - jnp.sum(own_gates * d_gate, axis=1, keepdims=True))
    ).astype(BF16)
    grad_router = dot(d_logits, normed_two, 0, 0)
    d_normed_two = d_back + dot(d_logits, router_t)
    _, norm_two_back = jax.vjp(rms_norm, mid_stream, gain_two)
    d_mid_norm, grad_gain_two = norm_two_back(d_normed_two)
    d_mid = d_out.astype(F32) + d_mid_norm

    d_attn_all = all_rows(d_mid.astype(BF16), n_expert, 2, "gather_attn")
    d_attn_all, grads_in, grads_out, made = lax.optimization_barrier(
        (d_attn_all, grads_in, grads_out, made)
    )
    grad_w_in = lax.psum_scatter(grads_in, "dp", scatter_dimension=1, tiled=True).astype(F32)
    grad_w_out = lax.psum_scatter(grads_out, "dp", scatter_dimension=2, tiled=True).astype(F32)
    w_o_mine = lax.dynamic_slice_in_dim(proj_full, me * q_cols, q_cols, 0)
    d_heads = dot(w_o_mine, d_attn_all, 1, 1).astype(BF16).reshape(q_per, HEAD_DIM, group_rows)
    delta = jnp.sum(d_heads.astype(F32) * heads_out.astype(F32), axis=1, keepdims=True)
    part_o = dot(attended_t, d_attn_all).astype(BF16)
    part_o = part_o.reshape(q_cols, n_dp, wide).transpose(1, 0, 2)
    d_own, d_projected, returned, sum_o = attend_back(
        low, high, key_pos, query, key, key_t, value,
        d_heads, lse, delta, cosine, sine, made, part_o, tok_rows, 4,
    )
    layer_out = (mid_stream + returned).astype(BF16)
    d_normed_one = dot(d_own.reshape(n_expert * cols, tok_rows), qkv_full, 0, 1)
    _, norm_one_back = jax.vjp(rms_norm, stream_in, gain_one)
    d_in_norm, grad_gain_one = norm_one_back(d_normed_one)
    grad_in = d_mid + d_in_norm

    part_qkv = dot(
        normed_all, d_projected.transpose(1, 0, 2).reshape(cols, group_rows), 0, 1
    ).astype(BF16).reshape(n_dp, wide, cols)
    small = jnp.concatenate(
        [grad_gain_one[None], grad_gain_two[None], grad_router, jnp.zeros((-few % 8, width), F32)], axis=0
    )
    small = small.reshape(-1, n_dp, wide).transpose(1, 0, 2)
    grad_w_qkv, grad_w_o, small = finish_sums(part_qkv, sum_o, small, q_cols, n_expert, 5)
    return (
        layer_out, grad_in, small[0], grad_w_qkv, grad_w_o, small[1], small[2:few].T,
        grad_w_in, grad_w_out,
    )


def solution(mesh):
    rows = P(("dp", "expert"), None)
    in_specs = (
        rows, rows, P("dp"), P("dp", None), P("dp", None), P("dp"), P("dp", None),
        P("expert", "dp", None), P("expert", None, "dp"), P("dp", None), P("dp", "expert"), rows,
    )
    out_specs = (
        rows, rows, P("dp"), P("dp", None), P("dp", None), P("dp"), P("dp", None),
        P("expert", "dp", None), P("expert", None, "dp"),
    )
    return jax.shard_map(local, mesh=mesh, in_specs=in_specs, out_specs=out_specs, check_vma=False)
```

```python
import functools

import jax
import jax.numpy as jnp
from jax import lax
from jax.experimental import pallas as pl
from jax.experimental.pallas import tpu as pltpu
from jax.sharding import PartitionSpec as P

HEADS = 16
KV_HEADS = 8
HEAD_DIM = 64
GROUPS = HEADS // KV_HEADS
EPSILON = 1e-06
ROPE_BASE = 10000.0
SCORE_SCALE = 0.015625
MASKED = -1e30
F32 = jnp.float32
BF16 = jnp.bfloat16
Q_TILE = 256
K_TILE = 256


MESH = pl.DeviceIdType.MESH
Z_SIZE = 4

def grid_of(n_expert):
    nz = Z_SIZE if n_expert % Z_SIZE == 0 else 1
    return nz, n_expert // nz

def places(nz, ny):
    me = lax.axis_index("expert")
    return me // ny, lax.rem(me, ny)

def device(z, y, nz, ny):
    return lax.rem(z + 2 * nz, nz) * ny + lax.rem(y + 2 * ny, ny)

def rms_norm(values, gain_vec):
    factor = lax.rsqrt(jnp.mean(values * values, axis=-1, keepdims=True) + EPSILON)
    return values * factor * gain_vec


def dot(left, right, left_dim=1, right_dim=0):
    return lax.dot_general(
        left, right, (((left_dim,), (right_dim,)), ((), ())), preferred_element_type=F32
    )


def rotate(values, cosine, sine):
    half = HEAD_DIM // 2
    one, two = values[:half], values[half:]
    return jnp.concatenate([one * cosine - two * sine, two * cosine + one * sine], axis=0)


def rotate_back(grads, cosine, sine):
    half = HEAD_DIM // 2
    one, two = grads[:half], grads[half:]
    return jnp.concatenate([one * cosine + two * sine, two * cosine - one * sine], axis=0)


def first_kernel(
    n_dp, nz, ny, rows, meta, heads, pack,
    rows_all, meta_all, heads_all, pack_all,
    send_sem, recv_sem, meta_send, meta_recv, dp_send, dp_recv, keep_sem,
):
    z, y = places(nz, ny)
    me, group = lax.axis_index("expert"), lax.axis_index("dp")
    count = rows.shape[0]
    half = count // 2
    barrier = pltpu.get_barrier_semaphore()
    near = [{"dp": lax.rem(group + k, n_dp)} for k in range(1, n_dp)]
    near += [{"expert": device(z + k, y, nz, ny)} for k in sorted({1, nz - 1} - {0})]
    near += [{"expert": device(z, y + k, nz, ny)} for k in sorted({1, ny - 1} - {0})]
    for other in near:
        pl.semaphore_signal(barrier, inc=1, device_id=other, device_id_type=MESH)
    pl.semaphore_wait(barrier, len(near))

    def origin(s, t, h):
        sign = -1 if h == 0 else 1
        return device(z + sign * s, y + sign * t, nz, ny)

    def copies(s, t, h, s2, t2):
        of = origin(s, t, h)
        mine = s == 0 and t == 0
        part = pl.ds(pl.multiple_of(of * count + h * half, half), half)
        step = 1 if h == 0 else -1
        to = device(z + step, y, nz, ny) if t2 == 0 else device(z, y + step, nz, ny)
        big = pltpu.make_async_remote_copy(
            src_ref=rows.at[pl.ds(h * half, half)] if mine else rows_all.at[part],
            dst_ref=rows_all.at[part],
            send_sem=send_sem.at[s2, t2, h], recv_sem=recv_sem.at[s2, t2, h],
            device_id={"expert": to}, device_id_type=MESH,
        )
        little = pltpu.make_async_remote_copy(
            src_ref=meta.at[h] if mine else meta_all.at[of, h], dst_ref=meta_all.at[of, h],
            send_sem=meta_send.at[s2, t2, h], recv_sem=meta_recv.at[s2, t2, h],
            device_id={"expert": to}, device_id_type=MESH,
        )
        return little, big

    def arrive(s, t, h):
        of = origin(s, t, h)
        part = pl.ds(pl.multiple_of(of * count + h * half, half), half)
        for place, sends, receives in (
            (meta_all.at[of, h], meta_send, meta_recv), (rows_all.at[part], send_sem, recv_sem)
        ):
            pltpu.make_async_remote_copy(
                src_ref=place, dst_ref=place, send_sem=sends.at[s, t, h], recv_sem=receives.at[s, t, h],
                device_id={"expert": device(z + 1, y, nz, ny)}, device_id_type=MESH,
            ).wait_recv()

    sent = []

    def start(*key):
        for copy in copies(*key):
            copy.start()
            sent.append(copy)

    for h in range(2):
        start(0, 0, h, 1, 0)
    if ny > 1:
        for h in range(2):
            start(0, 0, h, 0, 1)

    def across(k, a):
        source, target = ((heads, heads_all), (pack, pack_all))[a]
        return pltpu.make_async_remote_copy(
            src_ref=source, dst_ref=target.at[group],
            send_sem=dp_send.at[k - 1, a], recv_sem=dp_recv.at[k - 1, a],
            device_id={"dp": lax.rem(group + k, n_dp)}, device_id_type=MESH,
        )

    for k in range(1, n_dp):
        for a in range(2):
            across(k, a).start()
    keeps = [
        pltpu.make_async_copy(
            rows, rows_all.at[pl.ds(pl.multiple_of(me * count, count), count)], keep_sem.at[0]
        ),
        pltpu.make_async_copy(meta, meta_all.at[me], keep_sem.at[1]),
        pltpu.make_async_copy(heads, heads_all.at[group], keep_sem.at[2]),
        pltpu.make_async_copy(pack, pack_all.at[group], keep_sem.at[3]),
    ]
    for copy in keeps:
        copy.start()
    for s in range(1, nz):
        for h in range(2):
            arrive(s, 0, h)
            if s + 1 < nz:
                start(s, 0, h, s + 1, 0)
            if ny > 1:
                start(s, 0, h, s, 1)
    for t in range(1, ny):
        for s in range(nz):
            for h in range(2):
                arrive(s, t, h)
                if t + 1 < ny:
                    start(s, t, h, s, t + 1)
    for k in range(1, n_dp):
        for a, target in enumerate((heads_all, pack_all)):
            place = target.at[lax.rem(group + n_dp - k, n_dp)]
            pltpu.make_async_remote_copy(
                src_ref=place, dst_ref=place, send_sem=dp_send.at[k - 1, a], recv_sem=dp_recv.at[k - 1, a],
                device_id={"dp": lax.rem(group + k, n_dp)}, device_id_type=MESH,
            ).wait_recv()
    for copy in keeps:
        copy.wait()
    for copy in sent:
        copy.wait_send()
    for k in range(1, n_dp):
        for a in range(2):
            across(k, a).wait_send()


def first_gather(rows, meta, heads, pack, n_dp, n_expert, cid):
    nz, ny = grid_of(n_expert)
    anywhere = pl.BlockSpec(memory_space=pl.ANY)
    dma = pltpu.SemaphoreType.DMA
    ring, peers = dma((nz, ny, 2)), dma((max(n_dp - 1, 1), 2))
    return pl.pallas_call(
        functools.partial(first_kernel, n_dp, nz, ny),
        out_shape=[
            jax.ShapeDtypeStruct((rows.shape[0] * n_expert, rows.shape[1]), rows.dtype),
            jax.ShapeDtypeStruct((n_expert,) + meta.shape, meta.dtype),
            jax.ShapeDtypeStruct((n_dp,) + heads.shape, heads.dtype),
            jax.ShapeDtypeStruct((n_dp,) + pack.shape, pack.dtype),
        ],
        in_specs=[anywhere] * 4,
        out_specs=[anywhere] * 4,
        scratch_shapes=[ring, ring, ring, ring, peers, peers, dma((4,))],
        compiler_params=pltpu.CompilerParams(collective_id=cid, has_side_effects=True),
        name="first_gather",
    )(rows, meta, heads, pack)


def attend_kernel(
    nz, ny, low, high, key_pos, query, key, value_t, cotangent,
    out, lse, own_in, everyone,
    score_buf, weight_buf, send_buf, own_send, own_recv, send_sem, recv_sem, keep_sem,
):
    z, y = places(nz, ny)
    me = lax.axis_index("expert")
    n_expert = nz * ny
    heads, width, tile = query.shape
    low_row, high_row = low[...], high[...]
    steps = key.shape[0] // K_TILE
    tok_rows = cotangent.shape[0]
    half_rows = tok_rows // 2
    per_tile = tile // tok_rows
    i = pl.program_id(0)
    count = key.shape[0] // tile

    def piece(s, t, h):
        sign = -1 if h == 0 else 1
        begin = device(z + sign * s, y + sign * t, nz, ny) * tok_rows + h * half_rows
        return pl.ds(pl.multiple_of(begin, half_rows), half_rows)

    def row_copy(s, t, h, s2, t2):
        mine = s == 0 and t == 0
        step = 1 if h == 0 else -1
        to = device(z + step, y, nz, ny) if t2 == 0 else device(z, y + step, nz, ny)
        return pltpu.make_async_remote_copy(
            src_ref=cotangent.at[pl.ds(h * half_rows, half_rows)] if mine else everyone.at[piece(s, t, h)],
            dst_ref=everyone.at[piece(s, t, h)],
            send_sem=send_sem.at[s2, t2, h], recv_sem=recv_sem.at[s2, t2, h],
            device_id={"expert": to}, device_id_type=MESH,
        )

    def arrive(s, t, h):
        place = everyone.at[piece(s, t, h)]
        pltpu.make_async_remote_copy(
            src_ref=place, dst_ref=place, send_sem=send_sem.at[s, t, h], recv_sem=recv_sem.at[s, t, h],
            device_id={"expert": device(z + 1, y, nz, ny)}, device_id_type=MESH,
        ).wait_recv()

    def forward(s):
        for h in range(2):
            arrive(s, 0, h)
            if s + 1 < nz:
                row_copy(s, 0, h, s + 1, 0).start()
            if ny > 1:
                row_copy(s, 0, h, s, 1).start()

    def own_copy(other, source):
        return pltpu.make_async_remote_copy(
            src_ref=send_buf.at[other], dst_ref=own_in.at[source],
            send_sem=own_send.at[other], recv_sem=own_recv.at[source],
            device_id={"expert": other}, device_id_type=MESH,
        )

    keep = pltpu.make_async_copy(
        cotangent, everyone.at[pl.ds(pl.multiple_of(me * tok_rows, tok_rows), tok_rows)], keep_sem.at[0]
    )

    @pl.when(i == 0)
    def _():
        barrier = pltpu.get_barrier_semaphore()
        for k in range(1, n_expert):
            pl.semaphore_signal(
                barrier, inc=1, device_id={"expert": lax.rem(me + k, n_expert)}, device_id_type=MESH
            )
        pl.semaphore_wait(barrier, n_expert - 1)
        for h in range(2):
            row_copy(0, 0, h, 1, 0).start()
        if ny > 1:
            for h in range(2):
                row_copy(0, 0, h, 0, 1).start()
        keep.start()

    early = [s for s in range(1, nz) if 3 * s < count]
    for s in early:
        pl.when(i == 3 * s)(functools.partial(forward, s))

    def score_step(step, maxima):
        rows = pl.ds(pl.multiple_of(step * K_TILE, K_TILE), K_TILE)
        at = key_pos[rows, :]
        allowed = (at >= low_row) & (at <= high_row)
        found = []
        for head in range(heads):
            scores = jnp.dot(key[rows, :], query[head], preferred_element_type=F32)
            scores = jnp.where(allowed, scores, MASKED)
            score_buf[head, rows, :] = scores
            found.append(jnp.maximum(maxima[head], jnp.max(scores, axis=0, keepdims=True)))
        return tuple(found)

    begin = tuple(jnp.full(low_row.shape, MASKED, F32) for _ in range(heads))
    maxima = lax.fori_loop(0, steps, score_step, begin)

    def weight_step(step, totals):
        rows = pl.ds(pl.multiple_of(step * K_TILE, K_TILE), K_TILE)
        found = []
        for head in range(heads):
            weights = jnp.exp(score_buf[head, rows, :] - maxima[head])
            weight_buf[head, rows, :] = weights.astype(BF16)
            found.append(totals[head] + jnp.sum(weights, axis=0, keepdims=True))
        return tuple(found)

    begin = tuple(jnp.zeros(low_row.shape, F32) for _ in range(heads))
    totals = lax.fori_loop(0, steps, weight_step, begin)
    for head in range(heads):
        summed = jnp.dot(value_t[...], weight_buf[head], preferred_element_type=F32)
        attended = (summed / totals[head]).astype(BF16)
        out[head] = attended
        lse[head] = maxima[head] + jnp.log(totals[head])
        for j in range(per_tile):
            send_buf[i * per_tile + j, head * width : (head + 1) * width, :] = attended[
                :, j * tok_rows : (j + 1) * tok_rows
            ]
    for j in range(per_tile):
        other = i * per_tile + j

        @pl.when(other != me)
        def _():
            own_copy(other, me).start()

    @pl.when(i == count - 1)
    def _():
        mine = pltpu.make_async_copy(send_buf.at[me], own_in.at[me], keep_sem.at[1])
        mine.start()
        for s in range(1, nz):
            if s not in early:
                forward(s)
        for t in range(1, ny):
            for s in range(nz):
                for h in range(2):
                    arrive(s, t, h)
                    if t + 1 < ny:
                        row_copy(s, t, h, s, t + 1).start()
        for k in range(1, n_expert):
            other = lax.rem(me + k, n_expert)
            own_copy(other, other).wait_recv()
            own_copy(other, other).wait_send()
        for s in range(nz):
            for t in range(ny):
                for h in range(2):
                    if t > 0:
                        row_copy(s, t - 1, h, s, t).wait_send()
                    elif s > 0:
                        row_copy(s - 1, 0, h, s, 0).wait_send()
        keep.wait()
        mine.wait()


def attend(low, high, key_pos, query, key, value_t, cotangent, cid):
    heads, width, rows = query.shape
    tok_rows, model = cotangent.shape
    n_expert = rows // tok_rows
    nz, ny = grid_of(n_expert)
    tile = low_tile(rows)
    whole = lambda i: (0, 0)
    lane = lambda i: (0, i)
    anywhere = pl.BlockSpec(memory_space=pl.ANY)
    dma = pltpu.SemaphoreType.DMA
    return pl.pallas_call(
        functools.partial(attend_kernel, nz, ny),
        grid=(rows // tile,),
        in_specs=[
            pl.BlockSpec((1, tile), lane),
            pl.BlockSpec((1, tile), lane),
            pl.BlockSpec((rows, tile), whole),
            pl.BlockSpec((heads, width, tile), lambda i: (0, 0, i)),
            pl.BlockSpec((rows, width), whole),
            pl.BlockSpec((width, rows), whole),
            anywhere,
        ],
        out_specs=[
            pl.BlockSpec((heads, width, tile), lambda i: (0, 0, i)),
            pl.BlockSpec((heads, 1, tile), lambda i: (0, 0, i)),
            anywhere, anywhere,
        ],
        out_shape=[
            jax.ShapeDtypeStruct((heads, width, rows), BF16),
            jax.ShapeDtypeStruct((heads, 1, rows), F32),
            jax.ShapeDtypeStruct((n_expert, heads * width, tok_rows), BF16),
            jax.ShapeDtypeStruct((rows, model), BF16),
        ],
        scratch_shapes=[
            pltpu.VMEM((heads, rows, tile), F32),
            pltpu.VMEM((heads, rows, tile), BF16),
            pltpu.VMEM((n_expert, heads * width, tok_rows), BF16),
            dma((n_expert,)), dma((n_expert,)), dma((nz, ny, 2)), dma((nz, ny, 2)), dma((2,)),
        ],
        compiler_params=pltpu.CompilerParams(
            collective_id=cid, has_side_effects=True, vmem_limit_bytes=40 << 20
        ),
        cost_estimate=pl.CostEstimate(
            flops=4 * heads * rows * rows * 256,
            bytes_accessed=8 * rows * 256,
            transcendentals=heads * rows * rows,
        ),
        name="attend",
    )(low, high, key_pos, query, key, value_t, cotangent)


def low_tile(rows):
    return min(Q_TILE, rows)


def attend_back_kernel(
    nz, ny,
    low, high, key_pos, query, key, key_t, value, attended, lse,
    cos_tab, sin_tab, made, out_part, d_att,
    own_in, proj, summed, out_sum,
    d_key, d_value, query_n, grad_n, grad, delta, grad_in, out_in, out_own, score_buf, send_buf, part_buf, from_y, from_z, to_y, to_z,
    part_sem, own_send, own_recv, tail_send, tail_recv, keep_sem, mine_sem,
    send_y, recv_y, send_z, recv_z, dp_send, dp_recv, grad_send, grad_recv,
):
    z, y = places(nz, ny)
    me, group = lax.axis_index("expert"), lax.axis_index("dp")
    n_expert, n_dp = nz * ny, out_part.shape[0]
    heads, width, tile = query.shape
    low_row, high_row = low[...], high[...]
    steps = key.shape[0] // K_TILE
    tok_rows = summed.shape[0]
    half_rows = tok_rows // 2
    per_tile = tile // tok_rows
    i = pl.program_id(0)
    count = key.shape[0] // tile
    q_cols = heads * width

    def piece(r, t, h):
        sign = -1 if h == 0 else 1
        start = device(z + sign * (r + 1), y + sign * (t + 1), nz, ny) * tok_rows + h * half_rows
        return pl.ds(pl.multiple_of(start, half_rows), half_rows)

    def near(along_z, h):
        step = 1 if h == 0 else -1
        to = device(z + step, y, nz, ny) if along_z else device(z, y + step, nz, ny)
        return {"expert": to}

    def part_copy(r, t, h):
        return pltpu.make_async_copy(
            made.at[piece(r, t, h)], part_buf.at[r, t, h], part_sem.at[r, t, h]
        )

    def y_copy(r, t, h):
        source = made.at[piece(r, 0, h)] if t == 0 else to_y.at[r, t - 1, h]
        return pltpu.make_async_remote_copy(
            src_ref=source, dst_ref=from_y.at[r, t, h],
            send_sem=send_y.at[r, t, h], recv_sem=recv_y.at[r, t, h],
            device_id=near(False, h), device_id_type=MESH,
        )

    def z_copy(r, h):
        return pltpu.make_async_remote_copy(
            src_ref=to_z.at[r, h], dst_ref=from_z.at[r, h],
            send_sem=send_z.at[r, h], recv_sem=recv_z.at[r, h],
            device_id=near(True, h), device_id_type=MESH,
        )

    def finish(r):
        for t in range(1, ny - 1):
            for h in range(2):
                y_copy(r, t - 1, h).wait_recv()
                part_copy(r, t, h).wait()
                to_y[r, t - 1, h] = (
                    part_buf[r, t, h].astype(F32) + from_y[r, t - 1, h].astype(F32)
                ).astype(BF16)
                y_copy(r, t, h).start()
        for h in range(2):
            part_copy(r, ny - 1, h).wait()
            total = part_buf[r, ny - 1, h].astype(F32)
            if ny > 1:
                y_copy(r, ny - 2, h).wait_recv()
                total += from_y[r, ny - 2, h].astype(F32)
            if r > 0:
                z_copy(r - 1, h).wait_recv()
                total += from_z[r - 1, h].astype(F32)
            if r < nz - 1:
                to_z[r, h] = total.astype(BF16)
                z_copy(r, h).start()
            else:
                summed[h * half_rows : (h + 1) * half_rows, :] = total

    def across(k):
        other = lax.rem(group + k, n_dp)
        return pltpu.make_async_remote_copy(
            src_ref=out_part.at[other], dst_ref=out_in.at[k - 1],
            send_sem=dp_send.at[k - 1], recv_sem=dp_recv.at[k - 1],
            device_id={"dp": other}, device_id_type=MESH,
        )

    spans = (
        (0, q_cols, 0),
        (q_cols, width, n_expert * q_cols),
        (q_cols + width, width, n_expert * (q_cols + width)),
    )

    def own_rows(a, source):
        _, rows, base = spans[a]
        return own_in.at[pl.ds(pl.multiple_of(base + source * rows, rows), rows)]

    def own_copy(a, other, source):
        begin, rows, _ = spans[a]
        return pltpu.make_async_remote_copy(
            src_ref=send_buf.at[other, pl.ds(begin, rows)], dst_ref=own_rows(a, source),
            send_sem=(own_send if a == 0 else tail_send.at[a - 1]).at[other],
            recv_sem=(own_recv if a == 0 else tail_recv.at[a - 1]).at[source],
            device_id={"expert": other}, device_id_type=MESH,
        )

    def grad_copy(other, source):
        return pltpu.make_async_remote_copy(
            src_ref=d_att.at[other], dst_ref=grad_in.at[source],
            send_sem=grad_send.at[other], recv_sem=grad_recv.at[source],
            device_id={"expert": other}, device_id_type=MESH,
        )

    @pl.when(i == 0)
    def _():
        barrier = pltpu.get_barrier_semaphore()
        for k in range(1, n_expert):
            pl.semaphore_signal(
                barrier, inc=1, device_id={"expert": lax.rem(me + k, n_expert)}, device_id_type=MESH
            )
        for k in range(1, n_dp):
            pl.semaphore_signal(
                barrier, inc=1, device_id={"dp": lax.rem(group + k, n_dp)}, device_id_type=MESH
            )
        pl.semaphore_wait(barrier, n_expert + n_dp - 2)
        for k in range(1, n_expert):
            grad_copy(lax.rem(me + k, n_expert), me).start()
        for k in range(1, n_dp):
            across(k).start()
        pltpu.make_async_copy(out_part.at[group], out_own, keep_sem.at[2]).start()
        grad_in[me] = d_att[me]
        for r in range(nz):
            for h in range(2):
                if ny > 1:
                    y_copy(r, 0, h).start()
                for t in range(1, ny - 1):
                    part_copy(r, t, h).start()
                part_copy(r, ny - 1, h).start()
        d_key[...] = jnp.zeros_like(d_key)
        d_value[...] = jnp.zeros_like(d_value)

    for r in range(nz - 1):
        pl.when(i == (r + 1) * count // nz)(functools.partial(finish, r))

    for j in range(per_tile):
        source = i * per_tile + j

        @pl.when(source != me)
        def _():
            grad_copy(source, source).wait_recv()

        for head in range(heads):
            grad[head, :, j * tok_rows : (j + 1) * tok_rows] = grad_in[
                source, head * width : (head + 1) * width, :
            ]
    for head in range(heads):
        query_n[head] = query[head].T
        grad_n[head] = grad[head].T
        delta[head] = jnp.sum(
            grad[head].astype(F32) * attended[head].astype(F32), axis=0, keepdims=True
        )

    @pl.loop(0, steps)
    def _(step):
        rows = pl.ds(pl.multiple_of(step * K_TILE, K_TILE), K_TILE)
        at = key_pos[rows, :]
        allowed = (at >= low_row) & (at <= high_row)
        key_sum, value_sum = d_key[rows, :], d_value[rows, :]
        for head in range(heads):
            scores = jnp.dot(key[rows, :], query[head], preferred_element_type=F32)
            weights = jnp.exp(jnp.where(allowed, scores - lse[head], MASKED))
            d_soft = jnp.dot(value[rows, :], grad[head], preferred_element_type=F32)
            d_scores = (weights * (d_soft - delta[head])).astype(BF16)
            score_buf[head, rows, :] = d_scores
            key_sum += jnp.dot(d_scores, query_n[head], preferred_element_type=F32)
            value_sum += jnp.dot(weights.astype(BF16), grad_n[head], preferred_element_type=F32)
        d_key[rows, :] = key_sum
        d_value[rows, :] = value_sum

    lanes = pl.ds(pl.multiple_of(i * tile, tile), tile)
    for head in range(heads):
        d_query = jnp.dot(key_t[...], score_buf[head], preferred_element_type=F32) * SCORE_SCALE
        turned = rotate_back(d_query, cos_tab[:, lanes], sin_tab[:, lanes]).astype(BF16)
        for j in range(per_tile):
            send_buf[i * per_tile + j, head * width : (head + 1) * width, :] = turned[
                :, j * tok_rows : (j + 1) * tok_rows
            ]
    for j in range(per_tile):
        other = i * per_tile + j

        @pl.when(other != me)
        def _():
            own_copy(0, other, me).start()

    @pl.when(i == count - 1)
    def _():
        for other in range(n_expert):
            rows = pl.ds(other * tok_rows, tok_rows)
            turned = rotate_back(d_key[rows, :].T, cos_tab[:, rows], sin_tab[:, rows])
            send_buf[other, q_cols : q_cols + width, :] = turned.astype(BF16)
            send_buf[other, q_cols + width :, :] = d_value[rows, :].T.astype(BF16)

            @pl.when(other != me)
            def _():
                own_copy(1, other, me).start()
                own_copy(2, other, me).start()

        keep = pltpu.make_async_copy(send_buf, proj, keep_sem.at[0])
        keep.start()
        mine = [
            pltpu.make_async_copy(
                send_buf.at[me, pl.ds(begin, rows)], own_rows(a, me), mine_sem.at[a]
            )
            for a, (begin, rows, _) in enumerate(spans)
        ]
        for copy in mine:
            copy.start()
        finish(nz - 1)
        pltpu.make_async_copy(out_part.at[group], out_own, keep_sem.at[2]).wait()
        for k in range(1, n_dp):
            across(k).wait_recv()
        few = out_sum.shape[2]
        for m in range(n_expert):
            cols = slice(m * few, (m + 1) * few)
            out_total = out_own[:, cols].astype(F32)
            for k in range(1, n_dp):
                out_total += out_in[k - 1, :, cols].astype(F32)
            out_sum[m] = out_total.astype(BF16)
        for k in range(1, n_dp):
            across(k).wait_send()
        for k in range(1, n_expert):
            other = lax.rem(me + k, n_expert)
            for a in range(3):
                own_copy(a, other, other).wait_recv()
                own_copy(a, other, other).wait_send()
            grad_copy(other, other).wait_send()
        for r in range(nz):
            for h in range(2):
                for t in range(ny - 1):
                    y_copy(r, t, h).wait_send()
                if r < nz - 1:
                    z_copy(r, h).wait_send()
        keep.wait()
        for copy in mine:
            copy.wait()


def attend_back(
    low, high, key_pos, query, key, key_t, value, attended, lse,
    cosine, sine, made, out_part, d_att, tok_rows, cid,
):
    heads, width, rows = query.shape
    n_expert = rows // tok_rows
    nz, ny = grid_of(n_expert)
    cols = (heads + 2) * width
    half_rows, model = tok_rows // 2, made.shape[1]
    tile = low_tile(rows)
    whole = lambda i: (0, 0)
    lane = lambda i: (0, i)
    wide = pl.BlockSpec((heads, width, tile), lambda i: (0, 0, i))
    row = pl.BlockSpec((heads, 1, tile), lambda i: (0, 0, i))
    keys = pl.BlockSpec((rows, width), whole)
    anywhere = pl.BlockSpec(memory_space=pl.ANY)
    dma = pltpu.SemaphoreType.DMA
    y_steps, y_mid, z_steps = max(ny - 1, 1), max(ny - 2, 1), max(nz - 1, 1)
    peers = max(out_part.shape[0] - 1, 1)
    out_tiles = (n_expert, out_part.shape[1], out_part.shape[2] // n_expert)
    return pl.pallas_call(
        functools.partial(attend_back_kernel, nz, ny),
        grid=(rows // tile,),
        in_specs=[
            pl.BlockSpec((1, tile), lane),
            pl.BlockSpec((1, tile), lane),
            pl.BlockSpec((rows, tile), whole),
            wide, keys, pl.BlockSpec((width, rows), whole), keys, wide, row,
            pl.BlockSpec((width // 2, rows), whole), pl.BlockSpec((width // 2, rows), whole),
            anywhere, anywhere, pl.BlockSpec(d_att.shape, lambda i: (0, 0, 0)),
        ],
        out_specs=[
            anywhere, anywhere, pl.BlockSpec((tok_rows, model), whole),
            pl.BlockSpec(out_tiles, lambda i: (0, 0, 0)),
        ],
        out_shape=[
            jax.ShapeDtypeStruct((n_expert * cols, tok_rows), BF16),
            jax.ShapeDtypeStruct((n_expert, cols, tok_rows), BF16),
            jax.ShapeDtypeStruct((tok_rows, model), F32),
            jax.ShapeDtypeStruct(out_tiles, BF16),
        ],
        scratch_shapes=[
            pltpu.VMEM((rows, width), F32),
            pltpu.VMEM((rows, width), F32),
            pltpu.VMEM((heads, tile, width), BF16),
            pltpu.VMEM((heads, tile, width), BF16),
            pltpu.VMEM((heads, width, tile), BF16),
            pltpu.VMEM((heads, 1, tile), F32),
            pltpu.VMEM((n_expert, heads * width, tok_rows), BF16),
            pltpu.VMEM((peers,) + out_part.shape[1:], BF16),
            pltpu.VMEM(out_part.shape[1:], BF16),
            pltpu.VMEM((heads, rows, tile), BF16),
            pltpu.VMEM((n_expert, cols, tok_rows), BF16),
            pltpu.VMEM((nz, ny, 2, half_rows, model), BF16),
            pltpu.VMEM((nz, y_steps, 2, half_rows, model), BF16),
            pltpu.VMEM((z_steps, 2, half_rows, model), BF16),
            pltpu.VMEM((nz, y_mid, 2, half_rows if ny > 2 else 16, model), BF16),
            pltpu.VMEM((z_steps, 2, half_rows, model), BF16),
            dma((nz, ny, 2)), dma((n_expert,)), dma((n_expert,)), dma((2, n_expert)), dma((2, n_expert)), dma((3,)), dma((3,)),
            dma((nz, y_steps, 2)), dma((nz, y_steps, 2)), dma((z_steps, 2)), dma((z_steps, 2)),
            dma((peers,)), dma((peers,)), dma((n_expert,)), dma((n_expert,)),
        ],
        compiler_params=pltpu.CompilerParams(
            collective_id=cid, has_side_effects=True, vmem_limit_bytes=56 << 20
        ),
        cost_estimate=pl.CostEstimate(
            flops=10 * heads * rows * rows * 256,
            bytes_accessed=8 * rows * 256,
            transcendentals=heads * rows * rows,
        ),
        name="attend_back",
    )(low, high, key_pos, query, key, key_t, value, attended, lse, cosine, sine, made, out_part, d_att)


def finish_kernel(
    n_dp, nz, ny, q_cols, qkv, proj, small, into, out_of,
    qkv_rows, proj_rows, small_sum, into_wide, out_of_wide,
    qkv_in, small_in, proj_in, own_qkv, own_proj, own_small, qkv_all, proj_all, small_all,
    dp_send, dp_recv, ring_send, ring_recv, part_send, part_recv, keep_sem,
):
    z, y = places(nz, ny)
    me, group = lax.axis_index("expert"), lax.axis_index("dp")
    n_expert = nz * ny
    barrier = pltpu.get_barrier_semaphore()
    near = [{"dp": lax.rem(group + k, n_dp)} for k in range(1, n_dp)]
    near += [{"expert": lax.rem(me + k, n_expert)} for k in range(1, n_expert)]
    for other in near:
        pl.semaphore_signal(barrier, inc=1, device_id=other, device_id_type=MESH)
    pl.semaphore_wait(barrier, len(near))

    arrays = {0: (qkv, qkv_in, own_qkv), 2: (small, small_in, own_small)}

    def across(k, a):
        source, target, _ = arrays[a]
        other = lax.rem(group + k, n_dp)
        return pltpu.make_async_remote_copy(
            src_ref=source.at[other], dst_ref=target.at[k - 1],
            send_sem=dp_send.at[k - 1, a], recv_sem=dp_recv.at[k - 1, a],
            device_id={"dp": other}, device_id_type=MESH,
        )

    rings = ((own_qkv, qkv_all), (own_proj, proj_all), (own_small, small_all))

    def origin(s, t, h):
        sign = -1 if h == 0 else 1
        return device(z + sign * s, y + sign * t, nz, ny)

    def ring_copy(s, t, h, s2, t2, a):
        own, everyone = rings[a]
        of = origin(s, t, h)
        rows = own.shape[0] // 2 if a < 2 else own.shape[0]
        part = pl.ds(h * rows, rows)
        source = own.at[part] if s == 0 and t == 0 else everyone.at[of, part]
        step = 1 if h == 0 else -1
        to = device(z + step, y, nz, ny) if t2 == 0 else device(z, y + step, nz, ny)
        return pltpu.make_async_remote_copy(
            src_ref=source, dst_ref=everyone.at[of, part],
            send_sem=ring_send.at[s2, t2, h, a], recv_sem=ring_recv.at[s2, t2, h, a],
            device_id={"expert": to}, device_id_type=MESH,
        )

    def arrive(s, t, h, a):
        own, everyone = rings[a]
        rows = own.shape[0] // 2 if a < 2 else own.shape[0]
        place = everyone.at[origin(s, t, h), pl.ds(h * rows, rows)]
        pltpu.make_async_remote_copy(
            src_ref=place, dst_ref=place,
            send_sem=ring_send.at[s, t, h, a], recv_sem=ring_recv.at[s, t, h, a],
            device_id={"expert": device(z + 1, y, nz, ny)}, device_id_type=MESH,
        ).wait_recv()

    sent, keeps = [], []

    def start(*key):
        copy = ring_copy(*key)
        copy.start()
        sent.append(copy)

    def begin(moves):
        for a in sorted({a for _, a in moves}):
            own, everyone = rings[a]
            keeps.append(pltpu.make_async_copy(own, everyone.at[me], keep_sem.at[a]))
            keeps[-1].start()
        for h, a in moves:
            if nz > 1:
                start(0, 0, h, 1, 0, a)
            if ny > 1:
                start(0, 0, h, 0, 1, a)

    def along_z(moves):
        for s in range(1, nz):
            for h, a in moves:
                arrive(s, 0, h, a)
                if s + 1 < nz:
                    start(s, 0, h, s + 1, 0, a)
                if ny > 1:
                    start(s, 0, h, s, 1, a)

    def along_y(moves):
        for t in range(1, ny):
            for s in range(nz):
                for h, a in moves:
                    arrive(s, t, h, a)
                    if t + 1 < ny:
                        start(s, t, h, s, t + 1, a)

    def part_copy(k):
        other = lax.rem(me + k, n_expert)
        return pltpu.make_async_remote_copy(
            src_ref=proj.at[other], dst_ref=proj_in.at[k - 1],
            send_sem=part_send.at[k - 1], recv_sem=part_recv.at[k - 1],
            device_id={"expert": other}, device_id_type=MESH,
        )

    first, second = [(0, 0), (1, 0), (0, 2)], [(0, 1), (1, 1)]
    for k in range(1, n_dp):
        for a in arrays:
            across(k, a).start()
    for k in range(1, n_expert):
        part_copy(k).start()
    for e in range(into.shape[0]):
        into_wide[e] = into[e].astype(F32)
        out_of_wide[e] = out_of[e].astype(F32)
    for a, (source, target, own) in arrays.items():
        total = source[group].astype(F32)
        for k in range(1, n_dp):
            across(k, a).wait_recv()
            total += target[k - 1].astype(F32)
        own[...] = total.astype(own.dtype)
    begin(first)
    total = proj[me].astype(F32)
    for k in range(1, n_expert):
        part_copy(k).wait_recv()
        total += proj_in[k - 1].astype(F32)
    own_proj[...] = total.astype(BF16)
    begin(second)
    along_z(first + second)
    along_y(first + second)
    for copy in keeps:
        copy.wait()
    total = small_all[0]
    for other in range(1, n_expert):
        total += small_all[other]
    small_sum[...] = total
    alike = max(n_expert // KV_HEADS, 1)
    pieces = [qkv_all[m, :, :q_cols].astype(F32) for m in range(n_expert)]
    for first in (q_cols, q_cols + HEAD_DIM):
        for head in range(KV_HEADS):
            total = qkv_all[head * alike, :, first : first + HEAD_DIM].astype(F32)
            for more in range(1, alike):
                total += qkv_all[head * alike + more, :, first : first + HEAD_DIM].astype(F32)
            pieces.append(total)
    outs = [proj_all[m].astype(F32) for m in range(n_expert)]
    for target, pieces in ((qkv_rows, pieces), (proj_rows, outs)):
        lay(target, pieces)
    for copy in sent:
        copy.wait_send()
    for k in range(1, n_expert):
        part_copy(k).wait_send()
    for k in range(1, n_dp):
        for a in arrays:
            across(k, a).wait_send()


def lay(target, pieces):
    at = 0
    while pieces:
        block = [pieces.pop(0)]
        if block[0].shape[1] % 128:
            block.append(pieces.pop(0))
        joined = jnp.concatenate(block, axis=1) if len(block) > 1 else block[0]
        target[:, at : at + joined.shape[1]] = joined
        at += joined.shape[1]


def finish_sums(qkv, proj, small, into, out_of, q_cols, n_expert, cid):
    nz, ny = grid_of(n_expert)
    n_dp = qkv.shape[0]
    whole = pl.BlockSpec(memory_space=pltpu.VMEM)
    dma = pltpu.SemaphoreType.DMA
    peers = max(n_dp - 1, 1)
    return pl.pallas_call(
        functools.partial(finish_kernel, n_dp, nz, ny, q_cols),
        out_shape=[
            jax.ShapeDtypeStruct((qkv.shape[1], (HEADS + 2 * KV_HEADS) * HEAD_DIM), F32),
            jax.ShapeDtypeStruct((proj.shape[1], n_expert * proj.shape[2]), F32),
            jax.ShapeDtypeStruct(small.shape[1:], F32),
            jax.ShapeDtypeStruct(into.shape, F32),
            jax.ShapeDtypeStruct(out_of.shape, F32),
        ],
        in_specs=[whole] * 5,
        out_specs=[whole] * 5,
        scratch_shapes=[
            pltpu.VMEM((peers,) + qkv.shape[1:], BF16),
            pltpu.VMEM((peers,) + small.shape[1:], F32),
            pltpu.VMEM((n_expert - 1,) + proj.shape[1:], BF16),
            pltpu.VMEM(qkv.shape[1:], BF16),
            pltpu.VMEM(proj.shape[1:], BF16),
            pltpu.VMEM(small.shape[1:], F32),
            pltpu.VMEM((n_expert,) + qkv.shape[1:], BF16),
            pltpu.VMEM(proj.shape, BF16),
            pltpu.VMEM((n_expert,) + small.shape[1:], F32),
            dma((peers, 3)), dma((peers, 3)), dma((nz, ny, 2, 3)), dma((nz, ny, 2, 3)),
            dma((n_expert - 1,)), dma((n_expert - 1,)), dma((3,)),
        ],
        compiler_params=pltpu.CompilerParams(
            collective_id=cid, has_side_effects=True, vmem_limit_bytes=40 << 20
        ),
        name="finish_sums",
    )(qkv, proj, small, into, out_of)


def experts_kernel(
    nz, ny, own, named, router, cotangent, weight_in, weight_out,
    back, d_gate, made, grads_in, grads_out,
    rows_buf, cot_buf, in_buf, out_buf, hid_buf, gu_buf, part_buf, made_buf, gin_buf, gout_buf,
    gate_out, gate_in, from_y, from_z, to_y, to_z,
    load_sem, cot_sem, made_sem, grad_sem, send_sem, recv_sem, gate_send, gate_recv,
    send_y, recv_y, send_z, recv_z,
):
    z, y = places(nz, ny)
    me = lax.axis_index("expert")
    n_expert = nz * ny
    tok_rows, width = own.shape
    half = tok_rows // 2
    step_rows = ny * tok_rows
    exp_dev, ff, _ = out_buf.shape
    experts = named.shape[1]

    barrier = pltpu.get_barrier_semaphore()
    for k in range(1, n_expert):
        pl.semaphore_signal(
            barrier, inc=1, device_id={"expert": lax.rem(me + k, n_expert)}, device_id_type=MESH
        )
    pl.semaphore_wait(barrier, n_expert - 1)

    def owner(s, t, h):
        sign = -1 if h == 0 else 1
        return device(z + sign * s, y + sign * t, nz, ny)

    def piece(s, t, h):
        return pl.ds(pl.multiple_of(owner(s, t, h) * tok_rows + h * half, half), half)

    def slot(s, t, h):
        return pl.ds(((s * ny + t) * 2 + h) * half, half)

    def near(along_z, h):
        step = 1 if h == 0 else -1
        to = device(z + step, y, nz, ny) if along_z else device(z, y + step, nz, ny)
        return {"expert": to}

    def row_copy(s, t, h, s2, t2):
        source = own.at[pl.ds(h * half, half)] if s == 0 and t == 0 else rows_buf.at[slot(s, t, h)]
        return pltpu.make_async_remote_copy(
            src_ref=source, dst_ref=rows_buf.at[slot(s2, t2, h)],
            send_sem=send_sem.at[s2, t2, h], recv_sem=recv_sem.at[s2, t2, h],
            device_id=near(t2 == 0, h), device_id_type=MESH,
        )

    def arrive(s, t, h):
        if t == 0:
            row_copy(s - 1, 0, h, s, 0).wait_recv()
        else:
            row_copy(s, t - 1, h, s, t).wait_recv()

    sent = []

    def start(*key):
        copy = row_copy(*key)
        copy.start()
        sent.append(copy)

    for h in range(2):
        start(0, 0, h, 1, 0)
    if ny > 1:
        for h in range(2):
            start(0, 0, h, 0, 1)
    loads = [
        pltpu.make_async_copy(weight_in, in_buf, load_sem.at[0]),
        pltpu.make_async_copy(weight_out, out_buf, load_sem.at[1]),
    ]
    for copy in loads:
        copy.start()
    cots = {
        (s, t, h): pltpu.make_async_copy(
            cotangent.at[piece(s, t, h)], cot_buf.at[slot(s, t, h)], cot_sem.at[s, t, h]
        )
        for s in range(nz) for t in range(ny) for h in range(2)
    }
    for copy in cots.values():
        copy.start()
    rows_buf[0:tok_rows, :] = own[...]
    for copy in loads:
        copy.wait()

    lane = lax.broadcasted_iota(jnp.int32, (step_rows, experts), 1)
    wide_lane = lax.broadcasted_iota(jnp.int32, (step_rows, 128), 1)
    tile = 256

    def compute(s):
        rows = pl.ds(s * step_rows, step_rows)
        picked = jnp.concatenate(
            [named[piece(s, t, h), :] for t in range(ny) for h in range(2)], axis=0
        ) > 0.5
        logits = jnp.where(picked, dot(rows_buf[rows, :], router[...], 1, 1), MASKED)
        powers = jnp.exp(logits - jnp.max(logits, axis=1, keepdims=True))
        powers = jnp.where(picked, powers, 0.0)
        gates = powers / jnp.sum(powers, axis=1, keepdims=True)
        found = jnp.zeros((step_rows, 128), F32)
        for e in range(exp_dev):
            weight = jnp.sum(
                jnp.where(lane == me * exp_dev + e, gates, 0.0), axis=1, keepdims=True
            )

            def hidden_step(j, total):
                at = pl.multiple_of(j * tile, tile)
                cols, late = pl.ds(at, tile), pl.ds(pl.multiple_of(ff + at, tile), tile)
                gate_pre = dot(rows_buf[rows, :], in_buf[e, :, cols])
                up_pre = dot(rows_buf[rows, :], in_buf[e, :, late])
                d_plain = dot(cot_buf[rows, :], out_buf[e, cols, :], 1, 1)
                sigmoid = jax.nn.sigmoid(gate_pre)
                active = gate_pre * sigmoid
                hidden = active * up_pre
                hid_buf[e, rows, cols] = (weight * hidden).astype(BF16)
                d_hidden = weight * d_plain
                gu_buf[e, rows, cols] = (
                    d_hidden * up_pre * sigmoid * (1.0 + gate_pre * (1.0 - sigmoid))
                ).astype(BF16)
                gu_buf[e, rows, late] = (d_hidden * active).astype(BF16)
                return total + jnp.sum(hidden * d_plain, axis=1, keepdims=True)

            total = lax.fori_loop(0, ff // tile, hidden_step, jnp.zeros((step_rows, 1), F32))
            found += jnp.where(wide_lane == me * exp_dev + e, total, 0.0)

        @pl.loop(0, width // tile)
        def _(n):
            cols = pl.ds(pl.multiple_of(n * tile, tile), tile)
            d_rows = dot(gu_buf[0, rows, :], in_buf[0, cols, :], 1, 1)
            for e in range(1, exp_dev):
                d_rows += dot(gu_buf[e, rows, :], in_buf[e, cols, :], 1, 1)
            part_buf[rows, cols] = d_rows.astype(BF16)
            made_sum = dot(hid_buf[0, rows, :], out_buf[0, :, cols])
            for e in range(1, exp_dev):
                made_sum += dot(hid_buf[e, rows, :], out_buf[e, :, cols])
            made_buf[rows, cols] = made_sum.astype(BF16)

        for t in range(ny):
            for h in range(2):
                low = (t * 2 + h) * half
                gate_out[s, t, h] = found[low : low + half, :].T[:experts, :]
                if s or t:
                    gate_copy(s, t, h).start()
                made_copy(s, t, h).start()

    def gate_copy(s, t, h):
        return pltpu.make_async_remote_copy(
            src_ref=gate_out.at[s, t, h], dst_ref=gate_in.at[s, t, h],
            send_sem=gate_send.at[s, t, h], recv_sem=gate_recv.at[s, t, h],
            device_id={"expert": owner(s, t, h)}, device_id_type=MESH,
        )

    def made_copy(s, t, h):
        return pltpu.make_async_copy(
            made_buf.at[slot(s, t, h)], made.at[piece(s, t, h)], made_sem.at[s, t, h]
        )

    def part(r, t, h):
        return slot((r + 1) % nz, (t + 1) % ny, h)

    def y_copy(r, t, h):
        source = part_buf.at[part(r, 0, h)] if t == 0 else to_y.at[r, t - 1, h]
        return pltpu.make_async_remote_copy(
            src_ref=source, dst_ref=from_y.at[r, t, h],
            send_sem=send_y.at[r, t, h], recv_sem=recv_y.at[r, t, h],
            device_id=near(False, h), device_id_type=MESH,
        )

    def z_copy(r, h):
        return pltpu.make_async_remote_copy(
            src_ref=to_z.at[r, h], dst_ref=from_z.at[r, h],
            send_sem=send_z.at[r, h], recv_sem=recv_z.at[r, h],
            device_id=near(True, h), device_id_type=MESH,
        )

    def first_y(r):
        if ny > 1:
            for h in range(2):
                y_copy(r, 0, h).start()

    def finish(r):
        for t in range(1, ny - 1):
            for h in range(2):
                y_copy(r, t - 1, h).wait_recv()
                to_y[r, t - 1, h] = (
                    part_buf[part(r, t, h), :].astype(F32) + from_y[r, t - 1, h].astype(F32)
                ).astype(BF16)
                y_copy(r, t, h).start()
        for h in range(2):
            total = part_buf[part(r, ny - 1, h), :].astype(F32)
            if ny > 1:
                y_copy(r, ny - 2, h).wait_recv()
                total += from_y[r, ny - 2, h].astype(F32)
            if r > 0:
                z_copy(r - 1, h).wait_recv()
                total += from_z[r - 1, h].astype(F32)
            if r < nz - 1:
                to_z[r, h] = total.astype(BF16)
                z_copy(r, h).start()
            else:
                back[h * half : (h + 1) * half, :] = total

    def forward(s):
        for h in range(2):
            arrive(s, 0, h)
            if s + 1 < nz:
                start(s, 0, h, s + 1, 0)
            if ny > 1:
                start(s, 0, h, s, 1)

    def whole_step(s):
        for t in range(1, ny):
            for h in range(2):
                arrive(s, t, h)
                if t + 1 < ny:
                    start(s, t, h, s, t + 1)
        for t in range(ny):
            for h in range(2):
                cots[s, t, h].wait()
        compute(s)

    for s in range(nz):
        if s + 1 < nz:
            forward(s + 1)
        whole_step(s)
        if s > 0:
            first_y(s - 1)
        if s > 1:
            finish(s - 2)
    first_y(nz - 1)

    chunk = gin_buf.shape[2]

    def grad_step(i):
        cols = pl.ds(pl.multiple_of(i * tile, tile), tile)
        for e in range(exp_dev):
            found = dot(rows_buf[:, cols], gu_buf[e], 0, 0).astype(BF16)
            for c in range(tile // chunk):
                gin_buf[i * (tile // chunk) + c, e] = found[c * chunk : (c + 1) * chunk, :]

    def grad_out_step(i):
        cols = pl.ds(pl.multiple_of(i * tile, tile), tile)
        for e in range(exp_dev):
            found = dot(hid_buf[e, :, cols], cot_buf[...], 0, 0).astype(BF16)
            for c in range(width // chunk):
                gout_buf[c, e, cols, :] = found[:, c * chunk : (c + 1) * chunk]

    pl.loop(0, ff // tile)(grad_out_step)
    gout_copy = pltpu.make_async_copy(gout_buf, grads_out, grad_sem.at[0])
    gout_copy.start()
    if nz > 1:
        finish(nz - 2)
    pl.loop(0, width // tile)(grad_step)
    gin_copy = pltpu.make_async_copy(gin_buf, grads_in, grad_sem.at[1])
    gin_copy.start()
    finish(nz - 1)
    for h in range(2):
        gate_sum = gate_out[0, 0, h]
        for s in range(nz):
            for t in range(ny):
                if s or t:
                    gate_copy(s, t, h).wait_recv()
                    gate_sum += gate_in[s, t, h]
        d_gate[h] = gate_sum
    for copy in sent:
        copy.wait_send()
    for s in range(nz):
        for h in range(2):
            for t in range(ny):
                made_copy(s, t, h).wait()
                if s or t:
                    gate_copy(s, t, h).wait_send()
            for t in range(ny - 1):
                y_copy(s, t, h).wait_send()
            if s < nz - 1:
                z_copy(s, h).wait_send()
    gout_copy.wait()
    gin_copy.wait()


def experts_pass(own, named, router, cotangent, weight_in, weight_out, n_dp, n_expert, cid):
    nz, ny = grid_of(n_expert)
    tok_rows, width = own.shape
    exp_dev, ff, _ = weight_out.shape
    half, group = tok_rows // 2, tok_rows * n_expert
    experts = named.shape[1]
    whole, anywhere = pl.BlockSpec(memory_space=pltpu.VMEM), pl.BlockSpec(memory_space=pl.ANY)
    dma = pltpu.SemaphoreType.DMA
    ring = dma((nz, ny, 2))
    y_steps, y_mid, z_steps = max(ny - 1, 1), max(ny - 2, 1), max(nz - 1, 1)
    return pl.pallas_call(
        functools.partial(experts_kernel, nz, ny),
        out_shape=[
            jax.ShapeDtypeStruct((tok_rows, width), F32),
            jax.ShapeDtypeStruct((2, experts, half), F32),
            jax.ShapeDtypeStruct((group, width), BF16),
            jax.ShapeDtypeStruct((n_dp, exp_dev, width // n_dp, 2 * ff), BF16),
            jax.ShapeDtypeStruct((n_dp, exp_dev, ff, width // n_dp), BF16),
        ],
        in_specs=[whole, whole, whole, anywhere, anywhere, anywhere],
        out_specs=[whole, whole, anywhere, anywhere, anywhere],
        scratch_shapes=[
            pltpu.VMEM((group, width), BF16),
            pltpu.VMEM((group, width), BF16),
            pltpu.VMEM((exp_dev, width, 2 * ff), BF16),
            pltpu.VMEM((exp_dev, ff, width), BF16),
            pltpu.VMEM((exp_dev, group, ff), BF16),
            pltpu.VMEM((exp_dev, group, 2 * ff), BF16),
            pltpu.VMEM((group, width), BF16),
            pltpu.VMEM((group, width), BF16),
            pltpu.VMEM((n_dp, exp_dev, width // n_dp, 2 * ff), BF16),
            pltpu.VMEM((n_dp, exp_dev, ff, width // n_dp), BF16),
            pltpu.VMEM((nz, ny, 2, experts, half), F32),
            pltpu.VMEM((nz, ny, 2, experts, half), F32),
            pltpu.VMEM((nz, y_steps, 2, half, width), BF16),
            pltpu.VMEM((z_steps, 2, half, width), BF16),
            pltpu.VMEM((nz, y_mid, 2, half if ny > 2 else 16, width), BF16),
            pltpu.VMEM((z_steps, 2, half, width), BF16),
            dma((2,)), ring, ring, dma((2,)), ring, ring, ring, ring,
            dma((nz, y_steps, 2)), dma((nz, y_steps, 2)), dma((z_steps, 2)), dma((z_steps, 2)),
        ],
        compiler_params=pltpu.CompilerParams(
            collective_id=cid, has_side_effects=True, vmem_limit_bytes=60 << 20
        ),
        cost_estimate=pl.CostEstimate(
            flops=18 * exp_dev * group * width * ff,
            bytes_accessed=16 * group * width,
            transcendentals=exp_dev * group * ff,
        ),
        name="experts_pass",
    )(own, named, router, cotangent, weight_in, weight_out)


def gather(values, name, axis=0):
    return lax.all_gather(values, name, axis=axis, tiled=True)


def local(
    hidden_in, d_out, gain_attn, w_qkv, w_o, gain_moe, w_router, w_in, w_out,
    seq_lengths, assign, routes,
):
    tok_rows, width = hidden_in.shape
    exp_dev, _, ff_two = w_in.shape
    ff = ff_two // 2
    n_expert = lax.axis_size("expert")
    me = lax.axis_index("expert")
    experts = exp_dev * n_expert
    group_rows = tok_rows * n_expert
    q_per = HEADS // n_expert
    share = GROUPS // q_per
    q_cols = q_per * HEAD_DIM
    k_base = HEADS * HEAD_DIM
    v_base = k_base + KV_HEADS * HEAD_DIM
    cols = q_cols + 2 * HEAD_DIM

    n_dp = lax.axis_size("dp")
    wide = width // n_dp
    kv_head = (me * q_per) // GROUPS
    heads_part = jnp.concatenate(
        [
            lax.dynamic_slice_in_dim(w_qkv, me * q_cols, q_cols, 1),
            lax.dynamic_slice_in_dim(w_qkv, k_base + kv_head * HEAD_DIM, HEAD_DIM, 1),
            lax.dynamic_slice_in_dim(w_qkv, v_base + kv_head * HEAD_DIM, HEAD_DIM, 1),
        ],
        axis=1,
    )
    few = 2 + experts
    pack = jnp.concatenate(
        [gain_attn[None], gain_moe[None], w_router.T, jnp.zeros((-few % 16, wide), BF16)], axis=0
    )
    top = routes.shape[1]
    meta = jnp.concatenate(
        [assign, routes.T, jnp.zeros((-(1 + top) % 8, tok_rows), jnp.int32)], axis=0
    )
    meta = meta.reshape(meta.shape[0], 2, tok_rows // 2).transpose(1, 0, 2)
    qkv_full = gather(w_qkv, "dp")
    hidden_all, meta, w_heads, pack = first_gather(
        hidden_in, meta, heads_part, pack, n_dp, n_expert, 0
    )
    w_heads = w_heads.reshape(width, cols)
    pack = pack.transpose(1, 0, 2).reshape(-1, width)
    gain_one, gain_two = pack[0].astype(F32), pack[1].astype(F32)
    router_t = pack[2:few]
    position = meta[:, :, 0].reshape(group_rows)
    routes_all = meta[:, :, 1 : 1 + top]
    named = jnp.any(
        routes_all[:, :, :, None, :] == jnp.arange(experts, dtype=jnp.int32)[:, None], axis=2
    ).transpose(0, 1, 3, 2).reshape(group_rows, experts)
    stream_in = hidden_in.astype(F32)
    normed_all = rms_norm(hidden_all.astype(F32), gain_one).astype(BF16)
    proj_full = gather(w_o, "dp")
    weight_in = gather(w_in, "dp", axis=1)
    weight_out = gather(w_out, "dp", axis=2)
    lengths = seq_lengths[0]
    order = jnp.arange(lengths.shape[0], dtype=jnp.int32)
    ends = jnp.sum(jnp.where(order[None, :] <= order[:, None], lengths[None, :], 0), axis=1)
    starts = ends - lengths
    seq_id = jnp.sum((position[None, :] >= ends[:, None]).astype(jnp.int32), axis=0)
    picks = seq_id[None, :] == jnp.arange(lengths.shape[0], dtype=jnp.int32)[:, None]
    start_of = jnp.sum(jnp.where(picks, starts[:, None], 0), axis=0)
    rot_pos = position - start_of
    half = HEAD_DIM // 2
    frequency = ROPE_BASE ** (-(jnp.arange(half).astype(F32) * (2.0 / HEAD_DIM)))
    angles = frequency[:, None] * rot_pos.astype(F32)[None, :]
    cosine, sine = jnp.cos(angles), jnp.sin(angles)
    low, high = start_of[None, :], position[None, :]
    key_pos = jnp.broadcast_to(position[:, None], (group_rows, low_tile(group_rows)))

    projected = dot(w_heads, normed_all, 0, 1)
    query = jnp.stack(
        [
            rotate(projected[h * HEAD_DIM : (h + 1) * HEAD_DIM], cosine, sine).astype(BF16)
            for h in range(q_per)
        ]
    ) * jnp.asarray(SCORE_SCALE, BF16)
    key_t = rotate(projected[q_cols : q_cols + HEAD_DIM], cosine, sine).astype(BF16)
    value_t = projected[q_cols + HEAD_DIM :].astype(BF16)
    key, value = key_t.T, value_t.T
    heads_out, lse, attended, d_out_all = attend(low, high, key_pos, query, key, value_t, d_out, 6)
    attended = attended.reshape(n_expert * q_cols, tok_rows)
    mid_stream = stream_in + dot(attended, proj_full, 0, 0)
    normed_two = rms_norm(mid_stream, gain_two).astype(BF16)

    d_back, d_gate, made, grads_in, grads_out = experts_pass(
        normed_two, named.astype(F32), router_t, d_out_all, weight_in, weight_out, n_dp, n_expert, 1
    )
    d_gate = d_gate.transpose(0, 2, 1).reshape(tok_rows, experts)
    own_named = jnp.any(
        routes[:, :, None] == jnp.arange(experts, dtype=jnp.int32)[None, None, :], axis=1
    )
    own_gates = jax.nn.softmax(
        jnp.where(own_named, dot(normed_two, router_t, 1, 1), -jnp.inf), axis=1
    )
    d_logits = (
        own_gates * (d_gate - jnp.sum(own_gates * d_gate, axis=1, keepdims=True))
    ).astype(BF16)
    grad_router = dot(d_logits, normed_two, 0, 0)
    d_normed_two = d_back + dot(d_logits, router_t)
    _, norm_two_back = jax.vjp(rms_norm, mid_stream, gain_two)
    d_mid_norm, grad_gain_two = norm_two_back(d_normed_two)
    d_mid = d_out.astype(F32) + d_mid_norm

    d_attn = d_mid.astype(BF16)
    d_attn, grads_in, grads_out, made = lax.optimization_barrier((d_attn, grads_in, grads_out, made))
    grad_w_in = lax.psum_scatter(grads_in, "dp", scatter_dimension=0, tiled=True)
    grad_w_out = lax.psum_scatter(grads_out, "dp", scatter_dimension=0, tiled=True)
    d_att = dot(proj_full, d_attn, 1, 1).astype(BF16).reshape(n_expert, q_cols, tok_rows)
    part_o = dot(attended, d_attn).astype(BF16).reshape(n_dp, wide, width)
    d_own, d_projected, returned, sum_o = attend_back(
        low, high, key_pos, query, key, key_t, value, heads_out, lse,
        cosine, sine, made, part_o, d_att, tok_rows, 4,
    )
    layer_out = (mid_stream + returned).astype(BF16)
    if share > 1:
        fan = lambda part: jnp.repeat(part.reshape(width, KV_HEADS, HEAD_DIM), share, axis=1).reshape(width, -1)
        qkv_full = jnp.concatenate(
            [qkv_full[:, :k_base], fan(qkv_full[:, k_base:v_base]), fan(qkv_full[:, v_base:])], axis=1
        )
    d_normed_one = dot(d_own, qkv_full, 0, 1)
    _, norm_one_back = jax.vjp(rms_norm, stream_in, gain_one)
    d_in_norm, grad_gain_one = norm_one_back(d_normed_one)
    grad_in = d_mid + d_in_norm

    part_qkv = dot(
        normed_all, d_projected.transpose(1, 0, 2).reshape(cols, group_rows), 0, 1
    ).astype(BF16).reshape(n_dp, wide, cols)
    small = jnp.concatenate(
        [grad_gain_one[None], grad_gain_two[None], grad_router, jnp.zeros((-few % 8, width), F32)], axis=0
    )
    small = small.reshape(-1, n_dp, wide).transpose(1, 0, 2)
    grad_w_qkv, grad_w_o, small, grad_w_in, grad_w_out = finish_sums(
        part_qkv, sum_o, small, grad_w_in[0], grad_w_out[0], q_cols, n_expert, 5
    )
    return (
        layer_out, grad_in, small[0], grad_w_qkv, grad_w_o, small[1], small[2:few].T,
        grad_w_in, grad_w_out,
    )


def solution(mesh):
    rows = P(("dp", "expert"), None)
    in_specs = (
        rows, rows, P("dp"), P("dp", None), P("dp", None), P("dp"), P("dp", None),
        P("expert", "dp", None), P("expert", None, "dp"), P("dp", None), P("dp", "expert"), rows,
    )
    out_specs = (
        rows, rows, P("dp"), P("dp", None), P("dp", None), P("dp"), P("dp", None),
        P("expert", "dp", None), P("expert", None, "dp"),
    )
    return jax.shard_map(local, mesh=mesh, in_specs=in_specs, out_specs=out_specs, check_vma=False)
```

```python
import functools

import jax
import jax.numpy as jnp
from jax import lax
from jax.experimental import pallas as pl
from jax.experimental.pallas import tpu as pltpu
from jax.sharding import PartitionSpec as P

HEADS = 16
KV_HEADS = 8
HEAD_DIM = 64
GROUPS = HEADS // KV_HEADS
EPSILON = 1e-06
ROPE_BASE = 10000.0
SCORE_SCALE = 0.015625
MASKED = -1e30
F32 = jnp.float32
BF16 = jnp.bfloat16
Q_TILE = 256
K_TILE = 256


MESH = pl.DeviceIdType.MESH
Z_SIZE = 4

def grid_of(n_expert):
    nz = Z_SIZE if n_expert % Z_SIZE == 0 else 1
    return nz, n_expert // nz

def places(nz, ny):
    me = lax.axis_index("expert")
    return me // ny, lax.rem(me, ny)

def device(z, y, nz, ny):
    return lax.rem(z + 2 * nz, nz) * ny + lax.rem(y + 2 * ny, ny)

def rms_norm(values, gain_vec):
    factor = lax.rsqrt(jnp.mean(values * values, axis=-1, keepdims=True) + EPSILON)
    return values * factor * gain_vec


def dot(left, right, left_dim=1, right_dim=0):
    return lax.dot_general(
        left, right, (((left_dim,), (right_dim,)), ((), ())), preferred_element_type=F32
    )


def rotate(values, cosine, sine):
    half = HEAD_DIM // 2
    one, two = values[:half], values[half:]
    return jnp.concatenate([one * cosine - two * sine, two * cosine + one * sine], axis=0)


def rotate_back(grads, cosine, sine):
    half = HEAD_DIM // 2
    one, two = grads[:half], grads[half:]
    return jnp.concatenate([one * cosine + two * sine, two * cosine - one * sine], axis=0)


def first_kernel(
    n_dp, nz, ny, rows, meta, heads, pack,
    rows_all, meta_all, heads_all, pack_all,
    send_sem, recv_sem, meta_send, meta_recv, dp_send, dp_recv, keep_sem,
):
    z, y = places(nz, ny)
    me, group = lax.axis_index("expert"), lax.axis_index("dp")
    count = rows.shape[0]
    half = count // 2
    barrier = pltpu.get_barrier_semaphore()
    near = [{"dp": lax.rem(group + k, n_dp)} for k in range(1, n_dp)]
    near += [{"expert": device(z + k, y, nz, ny)} for k in sorted({1, nz - 1} - {0})]
    near += [{"expert": device(z, y + k, nz, ny)} for k in sorted({1, ny - 1} - {0})]
    for other in near:
        pl.semaphore_signal(barrier, inc=1, device_id=other, device_id_type=MESH)
    pl.semaphore_wait(barrier, len(near))

    def origin(s, t, h):
        sign = -1 if h == 0 else 1
        return device(z + sign * s, y + sign * t, nz, ny)

    def copies(s, t, h, s2, t2):
        of = origin(s, t, h)
        mine = s == 0 and t == 0
        part = pl.ds(pl.multiple_of(of * count + h * half, half), half)
        step = 1 if h == 0 else -1
        to = device(z + step, y, nz, ny) if t2 == 0 else device(z, y + step, nz, ny)
        big = pltpu.make_async_remote_copy(
            src_ref=rows.at[pl.ds(h * half, half)] if mine else rows_all.at[part],
            dst_ref=rows_all.at[part],
            send_sem=send_sem.at[s2, t2, h], recv_sem=recv_sem.at[s2, t2, h],
            device_id={"expert": to}, device_id_type=MESH,
        )
        little = pltpu.make_async_remote_copy(
            src_ref=meta.at[h] if mine else meta_all.at[of, h], dst_ref=meta_all.at[of, h],
            send_sem=meta_send.at[s2, t2, h], recv_sem=meta_recv.at[s2, t2, h],
            device_id={"expert": to}, device_id_type=MESH,
        )
        return little, big

    def arrive(s, t, h):
        of = origin(s, t, h)
        part = pl.ds(pl.multiple_of(of * count + h * half, half), half)
        for place, sends, receives in (
            (meta_all.at[of, h], meta_send, meta_recv), (rows_all.at[part], send_sem, recv_sem)
        ):
            pltpu.make_async_remote_copy(
                src_ref=place, dst_ref=place, send_sem=sends.at[s, t, h], recv_sem=receives.at[s, t, h],
                device_id={"expert": device(z + 1, y, nz, ny)}, device_id_type=MESH,
            ).wait_recv()

    sent = []

    def start(*key):
        for copy in copies(*key):
            copy.start()
            sent.append(copy)

    for h in range(2):
        start(0, 0, h, 1, 0)
    if ny > 1:
        for h in range(2):
            start(0, 0, h, 0, 1)

    def across(k, a):
        source, target = ((heads, heads_all), (pack, pack_all))[a]
        return pltpu.make_async_remote_copy(
            src_ref=source, dst_ref=target.at[group],
            send_sem=dp_send.at[k - 1, a], recv_sem=dp_recv.at[k - 1, a],
            device_id={"dp": lax.rem(group + k, n_dp)}, device_id_type=MESH,
        )

    for k in range(1, n_dp):
        for a in range(2):
            across(k, a).start()
    keeps = [
        pltpu.make_async_copy(
            rows, rows_all.at[pl.ds(pl.multiple_of(me * count, count), count)], keep_sem.at[0]
        ),
        pltpu.make_async_copy(meta, meta_all.at[me], keep_sem.at[1]),
        pltpu.make_async_copy(heads, heads_all.at[group], keep_sem.at[2]),
        pltpu.make_async_copy(pack, pack_all.at[group], keep_sem.at[3]),
    ]
    for copy in keeps:
        copy.start()
    for s in range(1, nz):
        for h in range(2):
            arrive(s, 0, h)
            if s + 1 < nz:
                start(s, 0, h, s + 1, 0)
            if ny > 1:
                start(s, 0, h, s, 1)
    for t in range(1, ny):
        for s in range(nz):
            for h in range(2):
                arrive(s, t, h)
                if t + 1 < ny:
                    start(s, t, h, s, t + 1)
    for k in range(1, n_dp):
        for a, target in enumerate((heads_all, pack_all)):
            place = target.at[lax.rem(group + n_dp - k, n_dp)]
            pltpu.make_async_remote_copy(
                src_ref=place, dst_ref=place, send_sem=dp_send.at[k - 1, a], recv_sem=dp_recv.at[k - 1, a],
                device_id={"dp": lax.rem(group + k, n_dp)}, device_id_type=MESH,
            ).wait_recv()
    for copy in keeps:
        copy.wait()
    for copy in sent:
        copy.wait_send()
    for k in range(1, n_dp):
        for a in range(2):
            across(k, a).wait_send()


def first_gather(rows, meta, heads, pack, n_dp, n_expert, cid):
    nz, ny = grid_of(n_expert)
    anywhere = pl.BlockSpec(memory_space=pl.ANY)
    dma = pltpu.SemaphoreType.DMA
    ring, peers = dma((nz, ny, 2)), dma((max(n_dp - 1, 1), 2))
    return pl.pallas_call(
        functools.partial(first_kernel, n_dp, nz, ny),
        out_shape=[
            jax.ShapeDtypeStruct((rows.shape[0] * n_expert, rows.shape[1]), rows.dtype),
            jax.ShapeDtypeStruct((n_expert,) + meta.shape, meta.dtype),
            jax.ShapeDtypeStruct((n_dp,) + heads.shape, heads.dtype),
            jax.ShapeDtypeStruct((n_dp,) + pack.shape, pack.dtype),
        ],
        in_specs=[anywhere] * 4,
        out_specs=[anywhere] * 4,
        scratch_shapes=[ring, ring, ring, ring, peers, peers, dma((4,))],
        compiler_params=pltpu.CompilerParams(collective_id=cid, has_side_effects=True),
        name="first_gather",
    )(rows, meta, heads, pack)


def attend_kernel(
    nz, ny, low, high, key_pos, cos_tab, sin_tab, gain, head_weights, hidden, cotangent,
    out, lse, own_in, everyone, normed, query_all, key, key_t, value,
    score_buf, weight_buf, send_buf, rows_buf, value_t, query,
    own_send, own_recv, send_sem, recv_sem, keep_sem, load_sem,
):
    z, y = places(nz, ny)
    me = lax.axis_index("expert")
    n_expert = nz * ny
    heads, width, tile = query.shape
    q_cols = heads * width
    low_row, high_row = low[...], high[...]
    steps = key.shape[0] // K_TILE
    tok_rows = cotangent.shape[0]
    half_rows = tok_rows // 2
    per_tile = tile // tok_rows
    i = pl.program_id(0)
    count = key.shape[0] // tile

    def piece(s, t, h):
        sign = -1 if h == 0 else 1
        begin = device(z + sign * s, y + sign * t, nz, ny) * tok_rows + h * half_rows
        return pl.ds(pl.multiple_of(begin, half_rows), half_rows)

    def row_copy(s, t, h, s2, t2):
        mine = s == 0 and t == 0
        step = 1 if h == 0 else -1
        to = device(z + step, y, nz, ny) if t2 == 0 else device(z, y + step, nz, ny)
        return pltpu.make_async_remote_copy(
            src_ref=cotangent.at[pl.ds(h * half_rows, half_rows)] if mine else everyone.at[piece(s, t, h)],
            dst_ref=everyone.at[piece(s, t, h)],
            send_sem=send_sem.at[s2, t2, h], recv_sem=recv_sem.at[s2, t2, h],
            device_id={"expert": to}, device_id_type=MESH,
        )

    def arrive(s, t, h):
        place = everyone.at[piece(s, t, h)]
        pltpu.make_async_remote_copy(
            src_ref=place, dst_ref=place, send_sem=send_sem.at[s, t, h], recv_sem=recv_sem.at[s, t, h],
            device_id={"expert": device(z + 1, y, nz, ny)}, device_id_type=MESH,
        ).wait_recv()

    def forward(s):
        for h in range(2):
            arrive(s, 0, h)
            if s + 1 < nz:
                row_copy(s, 0, h, s + 1, 0).start()
            if ny > 1:
                row_copy(s, 0, h, s, 1).start()

    def own_copy(other, source):
        return pltpu.make_async_remote_copy(
            src_ref=send_buf.at[other], dst_ref=own_in.at[source],
            send_sem=own_send.at[other], recv_sem=own_recv.at[source],
            device_id={"expert": other}, device_id_type=MESH,
        )

    keep = pltpu.make_async_copy(
        cotangent, everyone.at[pl.ds(pl.multiple_of(me * tok_rows, tok_rows), tok_rows)], keep_sem.at[0]
    )

    whole_out = pltpu.make_async_copy(rows_buf, normed, keep_sem.at[2])

    def load(j):
        rows = pl.ds(pl.multiple_of(j * tile, tile), tile)
        return pltpu.make_async_copy(hidden.at[rows], rows_buf.at[rows], load_sem.at[j])

    @pl.when(i == 0)
    def _():
        barrier = pltpu.get_barrier_semaphore()
        for k in range(1, n_expert):
            pl.semaphore_signal(
                barrier, inc=1, device_id={"expert": lax.rem(me + k, n_expert)}, device_id_type=MESH
            )
        pl.semaphore_wait(barrier, n_expert - 1)
        for h in range(2):
            row_copy(0, 0, h, 1, 0).start()
        if ny > 1:
            for h in range(2):
                row_copy(0, 0, h, 0, 1).start()
        keep.start()
        for j in range(count):
            load(j).start()

        @pl.loop(0, count)
        def _(j):
            rows = pl.ds(pl.multiple_of(j * tile, tile), tile)
            load(j).wait()
            rows_buf[rows, :] = rms_norm(rows_buf[rows, :].astype(F32), gain[...]).astype(BF16)
            cosine, sine = cos_tab[:, rows], sin_tab[:, rows]
            projected = dot(head_weights[...], rows_buf[rows, :], 0, 1)
            for head in range(heads):
                part = projected[head * width : (head + 1) * width]
                query_all[head, :, rows] = rotate(part, cosine, sine).astype(BF16) * jnp.asarray(
                    SCORE_SCALE, BF16
                )
            turned = rotate(projected[q_cols : q_cols + width], cosine, sine).astype(BF16)
            key_t[:, rows] = turned
            key[rows, :] = turned.T
            plain = projected[q_cols + width :].astype(BF16)
            value_t[:, rows] = plain
            value[rows, :] = plain.T

        whole_out.start()
        if nz > 1:
            forward(1)

    early = [s for s in range(2, nz) if 3 * (s - 1) < count]
    for s in early:
        pl.when(i == 3 * (s - 1))(functools.partial(forward, s))
    query[...] = query_all[:, :, pl.ds(pl.multiple_of(i * tile, tile), tile)]

    def score_step(step, maxima):
        rows = pl.ds(pl.multiple_of(step * K_TILE, K_TILE), K_TILE)
        at = key_pos[rows, :]
        allowed = (at >= low_row) & (at <= high_row)
        found = []
        for head in range(heads):
            scores = jnp.dot(key[rows, :], query[head], preferred_element_type=F32)
            scores = jnp.where(allowed, scores, MASKED)
            score_buf[head, rows, :] = scores
            found.append(jnp.maximum(maxima[head], jnp.max(scores, axis=0, keepdims=True)))
        return tuple(found)

    begin = tuple(jnp.full(low_row.shape, MASKED, F32) for _ in range(heads))
    maxima = lax.fori_loop(0, steps, score_step, begin)

    def weight_step(step, totals):
        rows = pl.ds(pl.multiple_of(step * K_TILE, K_TILE), K_TILE)
        found = []
        for head in range(heads):
            weights = jnp.exp(score_buf[head, rows, :] - maxima[head])
            weight_buf[head, rows, :] = weights.astype(BF16)
            found.append(totals[head] + jnp.sum(weights, axis=0, keepdims=True))
        return tuple(found)

    begin = tuple(jnp.zeros(low_row.shape, F32) for _ in range(heads))
    totals = lax.fori_loop(0, steps, weight_step, begin)
    for head in range(heads):
        summed = jnp.dot(value_t[...], weight_buf[head], preferred_element_type=F32)
        attended = (summed / totals[head]).astype(BF16)
        out[head] = attended
        lse[head] = maxima[head] + jnp.log(totals[head])
        for j in range(per_tile):
            send_buf[i * per_tile + j, head * width : (head + 1) * width, :] = attended[
                :, j * tok_rows : (j + 1) * tok_rows
            ]
    for j in range(per_tile):
        other = i * per_tile + j

        @pl.when(other != me)
        def _():
            own_copy(other, me).start()

    @pl.when(i == count - 1)
    def _():
        mine = pltpu.make_async_copy(send_buf.at[me], own_in.at[me], keep_sem.at[1])
        mine.start()
        for s in range(2, nz):
            if s not in early:
                forward(s)
        for t in range(1, ny):
            for s in range(nz):
                for h in range(2):
                    arrive(s, t, h)
                    if t + 1 < ny:
                        row_copy(s, t, h, s, t + 1).start()
        for k in range(1, n_expert):
            other = lax.rem(me + k, n_expert)
            own_copy(other, other).wait_recv()
            own_copy(other, other).wait_send()
        for s in range(nz):
            for t in range(ny):
                for h in range(2):
                    if t > 0:
                        row_copy(s, t - 1, h, s, t).wait_send()
                    elif s > 0:
                        row_copy(s - 1, 0, h, s, 0).wait_send()
        keep.wait()
        mine.wait()
        whole_out.wait()


def attend(low, high, key_pos, cosine, sine, gain, head_weights, hidden, cotangent, heads, cid):
    tok_rows, model = cotangent.shape
    rows = hidden.shape[0]
    width = HEAD_DIM
    n_expert = rows // tok_rows
    nz, ny = grid_of(n_expert)
    tile = low_tile(rows)
    whole = lambda i: (0, 0)
    lane = lambda i: (0, i)
    anywhere = pl.BlockSpec(memory_space=pl.ANY)
    dma = pltpu.SemaphoreType.DMA
    tables = pl.BlockSpec((width // 2, rows), whole)
    return pl.pallas_call(
        functools.partial(attend_kernel, nz, ny),
        grid=(rows // tile,),
        in_specs=[
            pl.BlockSpec((1, tile), lane),
            pl.BlockSpec((1, tile), lane),
            pl.BlockSpec((rows, tile), whole),
            tables, tables,
            pl.BlockSpec((1, model), whole),
            pl.BlockSpec(head_weights.shape, whole),
            anywhere, anywhere,
        ],
        out_specs=[
            pl.BlockSpec((heads, width, tile), lambda i: (0, 0, i)),
            pl.BlockSpec((heads, 1, tile), lambda i: (0, 0, i)),
            anywhere, anywhere, anywhere,
            pl.BlockSpec((heads, width, rows), lambda i: (0, 0, 0)),
            pl.BlockSpec((rows, width), whole),
            pl.BlockSpec((width, rows), whole),
            pl.BlockSpec((rows, width), whole),
        ],
        out_shape=[
            jax.ShapeDtypeStruct((heads, width, rows), BF16),
            jax.ShapeDtypeStruct((heads, 1, rows), F32),
            jax.ShapeDtypeStruct((n_expert, heads * width, tok_rows), BF16),
            jax.ShapeDtypeStruct((rows, model), BF16),
            jax.ShapeDtypeStruct((rows, model), BF16),
            jax.ShapeDtypeStruct((heads, width, rows), BF16),
            jax.ShapeDtypeStruct((rows, width), BF16),
            jax.ShapeDtypeStruct((width, rows), BF16),
            jax.ShapeDtypeStruct((rows, width), BF16),
        ],
        scratch_shapes=[
            pltpu.VMEM((heads, rows, tile), F32),
            pltpu.VMEM((heads, rows, tile), BF16),
            pltpu.VMEM((n_expert, heads * width, tok_rows), BF16),
            pltpu.VMEM((rows, model), BF16),
            pltpu.VMEM((width, rows), BF16),
            pltpu.VMEM((heads, width, tile), BF16),
            dma((n_expert,)), dma((n_expert,)), dma((nz, ny, 2)), dma((nz, ny, 2)), dma((3,)),
            dma((rows // tile,)),
        ],
        compiler_params=pltpu.CompilerParams(
            collective_id=cid, has_side_effects=True, vmem_limit_bytes=56 << 20
        ),
        cost_estimate=pl.CostEstimate(
            flops=4 * heads * rows * rows * 256,
            bytes_accessed=8 * rows * 256,
            transcendentals=heads * rows * rows,
        ),
        name="attend",
    )(low, high, key_pos, cosine, sine, gain, head_weights, hidden, cotangent)


def low_tile(rows):
    return min(Q_TILE, rows)


def attend_back_kernel(
    nz, ny,
    low, high, key_pos, query, key, key_t, value, attended, lse,
    cos_tab, sin_tab, made, out_part, d_att,
    own_in, proj, summed, out_sum,
    d_key, d_value, query_n, grad_n, grad, delta, grad_in, out_in, out_own, score_buf, send_buf, part_buf, from_y, from_z, to_y, to_z,
    part_sem, own_send, own_recv, tail_send, tail_recv, keep_sem, mine_sem,
    send_y, recv_y, send_z, recv_z, dp_send, dp_recv, grad_send, grad_recv,
):
    z, y = places(nz, ny)
    me, group = lax.axis_index("expert"), lax.axis_index("dp")
    n_expert, n_dp = nz * ny, out_part.shape[0]
    heads, width, tile = query.shape
    low_row, high_row = low[...], high[...]
    steps = key.shape[0] // K_TILE
    tok_rows = summed.shape[0]
    half_rows = tok_rows // 2
    per_tile = tile // tok_rows
    i = pl.program_id(0)
    count = key.shape[0] // tile
    q_cols = heads * width

    def piece(r, t, h):
        sign = -1 if h == 0 else 1
        start = device(z + sign * (r + 1), y + sign * (t + 1), nz, ny) * tok_rows + h * half_rows
        return pl.ds(pl.multiple_of(start, half_rows), half_rows)

    def near(along_z, h):
        step = 1 if h == 0 else -1
        to = device(z + step, y, nz, ny) if along_z else device(z, y + step, nz, ny)
        return {"expert": to}

    def part_copy(r, t, h):
        return pltpu.make_async_copy(
            made.at[piece(r, t, h)], part_buf.at[r, t, h], part_sem.at[r, t, h]
        )

    def y_copy(r, t, h):
        source = made.at[piece(r, 0, h)] if t == 0 else to_y.at[r, t - 1, h]
        return pltpu.make_async_remote_copy(
            src_ref=source, dst_ref=from_y.at[r, t, h],
            send_sem=send_y.at[r, t, h], recv_sem=recv_y.at[r, t, h],
            device_id=near(False, h), device_id_type=MESH,
        )

    def z_copy(r, h):
        return pltpu.make_async_remote_copy(
            src_ref=to_z.at[r, h], dst_ref=from_z.at[r, h],
            send_sem=send_z.at[r, h], recv_sem=recv_z.at[r, h],
            device_id=near(True, h), device_id_type=MESH,
        )

    def finish(r):
        for t in range(1, ny - 1):
            for h in range(2):
                y_copy(r, t - 1, h).wait_recv()
                part_copy(r, t, h).wait()
                to_y[r, t - 1, h] = (
                    part_buf[r, t, h].astype(F32) + from_y[r, t - 1, h].astype(F32)
                ).astype(BF16)
                y_copy(r, t, h).start()
        for h in range(2):
            part_copy(r, ny - 1, h).wait()
            total = part_buf[r, ny - 1, h].astype(F32)
            if ny > 1:
                y_copy(r, ny - 2, h).wait_recv()
                total += from_y[r, ny - 2, h].astype(F32)
            if r > 0:
                z_copy(r - 1, h).wait_recv()
                total += from_z[r - 1, h].astype(F32)
            if r < nz - 1:
                to_z[r, h] = total.astype(BF16)
                z_copy(r, h).start()
            else:
                summed[h * half_rows : (h + 1) * half_rows, :] = total

    def across(k):
        other = lax.rem(group + k, n_dp)
        return pltpu.make_async_remote_copy(
            src_ref=out_part.at[other], dst_ref=out_in.at[k - 1],
            send_sem=dp_send.at[k - 1], recv_sem=dp_recv.at[k - 1],
            device_id={"dp": other}, device_id_type=MESH,
        )

    spans = (
        (0, q_cols, 0),
        (q_cols, width, n_expert * q_cols),
        (q_cols + width, width, n_expert * (q_cols + width)),
    )

    def own_rows(a, source):
        _, rows, base = spans[a]
        return own_in.at[pl.ds(pl.multiple_of(base + source * rows, rows), rows)]

    def own_copy(a, other, source):
        begin, rows, _ = spans[a]
        return pltpu.make_async_remote_copy(
            src_ref=send_buf.at[other, pl.ds(begin, rows)], dst_ref=own_rows(a, source),
            send_sem=(own_send if a == 0 else tail_send.at[a - 1]).at[other],
            recv_sem=(own_recv if a == 0 else tail_recv.at[a - 1]).at[source],
            device_id={"expert": other}, device_id_type=MESH,
        )

    def grad_copy(other, source):
        return pltpu.make_async_remote_copy(
            src_ref=d_att.at[other], dst_ref=grad_in.at[source],
            send_sem=grad_send.at[other], recv_sem=grad_recv.at[source],
            device_id={"expert": other}, device_id_type=MESH,
        )

    @pl.when(i == 0)
    def _():
        barrier = pltpu.get_barrier_semaphore()
        for k in range(1, n_expert):
            pl.semaphore_signal(
                barrier, inc=1, device_id={"expert": lax.rem(me + k, n_expert)}, device_id_type=MESH
            )
        for k in range(1, n_dp):
            pl.semaphore_signal(
                barrier, inc=1, device_id={"dp": lax.rem(group + k, n_dp)}, device_id_type=MESH
            )
        pl.semaphore_wait(barrier, n_expert + n_dp - 2)
        for k in range(1, n_expert):
            grad_copy(lax.rem(me + k, n_expert), me).start()
        for k in range(1, n_dp):
            across(k).start()
        pltpu.make_async_copy(out_part.at[group], out_own, keep_sem.at[2]).start()
        grad_in[me] = d_att[me]
        for r in range(nz):
            for h in range(2):
                if ny > 1:
                    y_copy(r, 0, h).start()
                for t in range(1, ny - 1):
                    part_copy(r, t, h).start()
                part_copy(r, ny - 1, h).start()
        d_key[...] = jnp.zeros_like(d_key)
        d_value[...] = jnp.zeros_like(d_value)

    for r in range(nz - 1):
        pl.when(i == (r + 1) * count // nz)(functools.partial(finish, r))

    for j in range(per_tile):
        source = i * per_tile + j

        @pl.when(source != me)
        def _():
            grad_copy(source, source).wait_recv()

        for head in range(heads):
            grad[head, :, j * tok_rows : (j + 1) * tok_rows] = grad_in[
                source, head * width : (head + 1) * width, :
            ]
    for head in range(heads):
        query_n[head] = query[head].T
        grad_n[head] = grad[head].T
        delta[head] = jnp.sum(
            grad[head].astype(F32) * attended[head].astype(F32), axis=0, keepdims=True
        )

    @pl.loop(0, steps)
    def _(step):
        rows = pl.ds(pl.multiple_of(step * K_TILE, K_TILE), K_TILE)
        at = key_pos[rows, :]
        allowed = (at >= low_row) & (at <= high_row)
        key_sum, value_sum = d_key[rows, :], d_value[rows, :]
        for head in range(heads):
            scores = jnp.dot(key[rows, :], query[head], preferred_element_type=F32)
            weights = jnp.exp(jnp.where(allowed, scores - lse[head], MASKED))
            d_soft = jnp.dot(value[rows, :], grad[head], preferred_element_type=F32)
            d_scores = (weights * (d_soft - delta[head])).astype(BF16)
            score_buf[head, rows, :] = d_scores
            key_sum += jnp.dot(d_scores, query_n[head], preferred_element_type=F32)
            value_sum += jnp.dot(weights.astype(BF16), grad_n[head], preferred_element_type=F32)
        d_key[rows, :] = key_sum
        d_value[rows, :] = value_sum

    lanes = pl.ds(pl.multiple_of(i * tile, tile), tile)
    for head in range(heads):
        d_query = jnp.dot(key_t[...], score_buf[head], preferred_element_type=F32) * SCORE_SCALE
        turned = rotate_back(d_query, cos_tab[:, lanes], sin_tab[:, lanes]).astype(BF16)
        for j in range(per_tile):
            send_buf[i * per_tile + j, head * width : (head + 1) * width, :] = turned[
                :, j * tok_rows : (j + 1) * tok_rows
            ]
    for j in range(per_tile):
        other = i * per_tile + j

        @pl.when(other != me)
        def _():
            own_copy(0, other, me).start()

    @pl.when(i == count - 1)
    def _():
        for other in range(n_expert):
            rows = pl.ds(other * tok_rows, tok_rows)
            turned = rotate_back(d_key[rows, :].T, cos_tab[:, rows], sin_tab[:, rows])
            send_buf[other, q_cols : q_cols + width, :] = turned.astype(BF16)
            send_buf[other, q_cols + width :, :] = d_value[rows, :].T.astype(BF16)

            @pl.when(other != me)
            def _():
                own_copy(1, other, me).start()
                own_copy(2, other, me).start()

        keep = pltpu.make_async_copy(send_buf, proj, keep_sem.at[0])
        keep.start()
        mine = [
            pltpu.make_async_copy(
                send_buf.at[me, pl.ds(begin, rows)], own_rows(a, me), mine_sem.at[a]
            )
            for a, (begin, rows, _) in enumerate(spans)
        ]
        for copy in mine:
            copy.start()
        finish(nz - 1)
        pltpu.make_async_copy(out_part.at[group], out_own, keep_sem.at[2]).wait()
        for k in range(1, n_dp):
            across(k).wait_recv()
        few = out_sum.shape[2]
        for m in range(n_expert):
            cols = slice(m * few, (m + 1) * few)
            out_total = out_own[:, cols].astype(F32)
            for k in range(1, n_dp):
                out_total += out_in[k - 1, :, cols].astype(F32)
            out_sum[m] = out_total.astype(BF16)
        for k in range(1, n_dp):
            across(k).wait_send()
        for k in range(1, n_expert):
            other = lax.rem(me + k, n_expert)
            for a in range(3):
                own_copy(a, other, other).wait_recv()
                own_copy(a, other, other).wait_send()
            grad_copy(other, other).wait_send()
        for r in range(nz):
            for h in range(2):
                for t in range(ny - 1):
                    y_copy(r, t, h).wait_send()
                if r < nz - 1:
                    z_copy(r, h).wait_send()
        keep.wait()
        for copy in mine:
            copy.wait()


def attend_back(
    low, high, key_pos, query, key, key_t, value, attended, lse,
    cosine, sine, made, out_part, d_att, tok_rows, cid,
):
    heads, width, rows = query.shape
    n_expert = rows // tok_rows
    nz, ny = grid_of(n_expert)
    cols = (heads + 2) * width
    half_rows, model = tok_rows // 2, made.shape[1]
    tile = low_tile(rows)
    whole = lambda i: (0, 0)
    lane = lambda i: (0, i)
    wide = pl.BlockSpec((heads, width, tile), lambda i: (0, 0, i))
    row = pl.BlockSpec((heads, 1, tile), lambda i: (0, 0, i))
    keys = pl.BlockSpec((rows, width), whole)
    anywhere = pl.BlockSpec(memory_space=pl.ANY)
    dma = pltpu.SemaphoreType.DMA
    y_steps, y_mid, z_steps = max(ny - 1, 1), max(ny - 2, 1), max(nz - 1, 1)
    peers = max(out_part.shape[0] - 1, 1)
    out_tiles = (n_expert, out_part.shape[1], out_part.shape[2] // n_expert)
    return pl.pallas_call(
        functools.partial(attend_back_kernel, nz, ny),
        grid=(rows // tile,),
        in_specs=[
            pl.BlockSpec((1, tile), lane),
            pl.BlockSpec((1, tile), lane),
            pl.BlockSpec((rows, tile), whole),
            wide, keys, pl.BlockSpec((width, rows), whole), keys, wide, row,
            pl.BlockSpec((width // 2, rows), whole), pl.BlockSpec((width // 2, rows), whole),
            anywhere, anywhere, pl.BlockSpec(d_att.shape, lambda i: (0, 0, 0)),
        ],
        out_specs=[
            anywhere, anywhere, pl.BlockSpec((tok_rows, model), whole),
            pl.BlockSpec(out_tiles, lambda i: (0, 0, 0)),
        ],
        out_shape=[
            jax.ShapeDtypeStruct((n_expert * cols, tok_rows), BF16),
            jax.ShapeDtypeStruct((n_expert, cols, tok_rows), BF16),
            jax.ShapeDtypeStruct((tok_rows, model), F32),
            jax.ShapeDtypeStruct(out_tiles, BF16),
        ],
        scratch_shapes=[
            pltpu.VMEM((rows, width), F32),
            pltpu.VMEM((rows, width), F32),
            pltpu.VMEM((heads, tile, width), BF16),
            pltpu.VMEM((heads, tile, width), BF16),
            pltpu.VMEM((heads, width, tile), BF16),
            pltpu.VMEM((heads, 1, tile), F32),
            pltpu.VMEM((n_expert, heads * width, tok_rows), BF16),
            pltpu.VMEM((peers,) + out_part.shape[1:], BF16),
            pltpu.VMEM(out_part.shape[1:], BF16),
            pltpu.VMEM((heads, rows, tile), BF16),
            pltpu.VMEM((n_expert, cols, tok_rows), BF16),
            pltpu.VMEM((nz, ny, 2, half_rows, model), BF16),
            pltpu.VMEM((nz, y_steps, 2, half_rows, model), BF16),
            pltpu.VMEM((z_steps, 2, half_rows, model), BF16),
            pltpu.VMEM((nz, y_mid, 2, half_rows if ny > 2 else 16, model), BF16),
            pltpu.VMEM((z_steps, 2, half_rows, model), BF16),
            dma((nz, ny, 2)), dma((n_expert,)), dma((n_expert,)), dma((2, n_expert)), dma((2, n_expert)), dma((3,)), dma((3,)),
            dma((nz, y_steps, 2)), dma((nz, y_steps, 2)), dma((z_steps, 2)), dma((z_steps, 2)),
            dma((peers,)), dma((peers,)), dma((n_expert,)), dma((n_expert,)),
        ],
        compiler_params=pltpu.CompilerParams(
            collective_id=cid, has_side_effects=True, vmem_limit_bytes=56 << 20
        ),
        cost_estimate=pl.CostEstimate(
            flops=10 * heads * rows * rows * 256,
            bytes_accessed=8 * rows * 256,
            transcendentals=heads * rows * rows,
        ),
        name="attend_back",
    )(low, high, key_pos, query, key, key_t, value, attended, lse, cosine, sine, made, out_part, d_att)


def finish_kernel(
    n_dp, nz, ny, q_cols, qkv, proj, small, into, out_of,
    qkv_rows, proj_rows, small_sum, into_wide, out_of_wide,
    qkv_in, small_in, proj_in, own_qkv, own_proj, own_small, qkv_all, proj_all, small_all,
    dp_send, dp_recv, ring_send, ring_recv, part_send, part_recv, keep_sem,
):
    z, y = places(nz, ny)
    me, group = lax.axis_index("expert"), lax.axis_index("dp")
    n_expert = nz * ny
    barrier = pltpu.get_barrier_semaphore()
    near = [{"dp": lax.rem(group + k, n_dp)} for k in range(1, n_dp)]
    near += [{"expert": lax.rem(me + k, n_expert)} for k in range(1, n_expert)]
    for other in near:
        pl.semaphore_signal(barrier, inc=1, device_id=other, device_id_type=MESH)
    pl.semaphore_wait(barrier, len(near))

    arrays = {0: (qkv, qkv_in, own_qkv), 2: (small, small_in, own_small)}

    def across(k, a):
        source, target, _ = arrays[a]
        other = lax.rem(group + k, n_dp)
        return pltpu.make_async_remote_copy(
            src_ref=source.at[other], dst_ref=target.at[k - 1],
            send_sem=dp_send.at[k - 1, a], recv_sem=dp_recv.at[k - 1, a],
            device_id={"dp": other}, device_id_type=MESH,
        )

    rings = ((own_qkv, qkv_all), (own_proj, proj_all), (own_small, small_all))

    def origin(s, t, h):
        sign = -1 if h == 0 else 1
        return device(z + sign * s, y + sign * t, nz, ny)

    def ring_copy(s, t, h, s2, t2, a):
        own, everyone = rings[a]
        of = origin(s, t, h)
        rows = own.shape[0] // 2 if a < 2 else own.shape[0]
        part = pl.ds(h * rows, rows)
        source = own.at[part] if s == 0 and t == 0 else everyone.at[of, part]
        step = 1 if h == 0 else -1
        to = device(z + step, y, nz, ny) if t2 == 0 else device(z, y + step, nz, ny)
        return pltpu.make_async_remote_copy(
            src_ref=source, dst_ref=everyone.at[of, part],
            send_sem=ring_send.at[s2, t2, h, a], recv_sem=ring_recv.at[s2, t2, h, a],
            device_id={"expert": to}, device_id_type=MESH,
        )

    def arrive(s, t, h, a):
        own, everyone = rings[a]
        rows = own.shape[0] // 2 if a < 2 else own.shape[0]
        place = everyone.at[origin(s, t, h), pl.ds(h * rows, rows)]
        pltpu.make_async_remote_copy(
            src_ref=place, dst_ref=place,
            send_sem=ring_send.at[s, t, h, a], recv_sem=ring_recv.at[s, t, h, a],
            device_id={"expert": device(z + 1, y, nz, ny)}, device_id_type=MESH,
        ).wait_recv()

    sent, keeps = [], []

    def start(*key):
        copy = ring_copy(*key)
        copy.start()
        sent.append(copy)

    def begin(moves):
        for a in sorted({a for _, a in moves}):
            own, everyone = rings[a]
            keeps.append(pltpu.make_async_copy(own, everyone.at[me], keep_sem.at[a]))
            keeps[-1].start()
        for h, a in moves:
            if nz > 1:
                start(0, 0, h, 1, 0, a)
            if ny > 1:
                start(0, 0, h, 0, 1, a)

    def along_z(moves):
        for s in range(1, nz):
            for h, a in moves:
                arrive(s, 0, h, a)
                if s + 1 < nz:
                    start(s, 0, h, s + 1, 0, a)
                if ny > 1:
                    start(s, 0, h, s, 1, a)

    def along_y(moves):
        for t in range(1, ny):
            for s in range(nz):
                for h, a in moves:
                    arrive(s, t, h, a)
                    if t + 1 < ny:
                        start(s, t, h, s, t + 1, a)

    def part_copy(k):
        other = lax.rem(me + k, n_expert)
        return pltpu.make_async_remote_copy(
            src_ref=proj.at[other], dst_ref=proj_in.at[k - 1],
            send_sem=part_send.at[k - 1], recv_sem=part_recv.at[k - 1],
            device_id={"expert": other}, device_id_type=MESH,
        )

    first, second = [(0, 0), (1, 0), (0, 2)], [(0, 1), (1, 1)]
    for k in range(1, n_dp):
        for a in arrays:
            across(k, a).start()
    for k in range(1, n_expert):
        part_copy(k).start()
    for e in range(into.shape[0]):
        into_wide[e] = into[e].astype(F32)
        out_of_wide[e] = out_of[e].astype(F32)
    for a, (source, target, own) in arrays.items():
        total = source[group].astype(F32)
        for k in range(1, n_dp):
            across(k, a).wait_recv()
            total += target[k - 1].astype(F32)
        own[...] = total.astype(own.dtype)
    begin(first)
    total = proj[me].astype(F32)
    for k in range(1, n_expert):
        part_copy(k).wait_recv()
        total += proj_in[k - 1].astype(F32)
    own_proj[...] = total.astype(BF16)
    begin(second)
    along_z(first + second)
    along_y(first + second)
    for copy in keeps:
        copy.wait()
    total = small_all[0]
    for other in range(1, n_expert):
        total += small_all[other]
    small_sum[...] = total
    alike = max(n_expert // KV_HEADS, 1)
    pieces = [qkv_all[m, :, :q_cols].astype(F32) for m in range(n_expert)]
    for first in (q_cols, q_cols + HEAD_DIM):
        for head in range(KV_HEADS):
            total = qkv_all[head * alike, :, first : first + HEAD_DIM].astype(F32)
            for more in range(1, alike):
                total += qkv_all[head * alike + more, :, first : first + HEAD_DIM].astype(F32)
            pieces.append(total)
    outs = [proj_all[m].astype(F32) for m in range(n_expert)]
    for target, pieces in ((qkv_rows, pieces), (proj_rows, outs)):
        lay(target, pieces)
    for copy in sent:
        copy.wait_send()
    for k in range(1, n_expert):
        part_copy(k).wait_send()
    for k in range(1, n_dp):
        for a in arrays:
            across(k, a).wait_send()


def lay(target, pieces):
    at = 0
    while pieces:
        block = [pieces.pop(0)]
        if block[0].shape[1] % 128:
            block.append(pieces.pop(0))
        joined = jnp.concatenate(block, axis=1) if len(block) > 1 else block[0]
        target[:, at : at + joined.shape[1]] = joined
        at += joined.shape[1]


def finish_sums(qkv, proj, small, into, out_of, q_cols, n_expert, cid):
    nz, ny = grid_of(n_expert)
    n_dp = qkv.shape[0]
    whole = pl.BlockSpec(memory_space=pltpu.VMEM)
    dma = pltpu.SemaphoreType.DMA
    peers = max(n_dp - 1, 1)
    return pl.pallas_call(
        functools.partial(finish_kernel, n_dp, nz, ny, q_cols),
        out_shape=[
            jax.ShapeDtypeStruct((qkv.shape[1], (HEADS + 2 * KV_HEADS) * HEAD_DIM), F32),
            jax.ShapeDtypeStruct((proj.shape[1], n_expert * proj.shape[2]), F32),
            jax.ShapeDtypeStruct(small.shape[1:], F32),
            jax.ShapeDtypeStruct(into.shape, F32),
            jax.ShapeDtypeStruct(out_of.shape, F32),
        ],
        in_specs=[whole] * 5,
        out_specs=[whole] * 5,
        scratch_shapes=[
            pltpu.VMEM((peers,) + qkv.shape[1:], BF16),
            pltpu.VMEM((peers,) + small.shape[1:], F32),
            pltpu.VMEM((n_expert - 1,) + proj.shape[1:], BF16),
            pltpu.VMEM(qkv.shape[1:], BF16),
            pltpu.VMEM(proj.shape[1:], BF16),
            pltpu.VMEM(small.shape[1:], F32),
            pltpu.VMEM((n_expert,) + qkv.shape[1:], BF16),
            pltpu.VMEM(proj.shape, BF16),
            pltpu.VMEM((n_expert,) + small.shape[1:], F32),
            dma((peers, 3)), dma((peers, 3)), dma((nz, ny, 2, 3)), dma((nz, ny, 2, 3)),
            dma((n_expert - 1,)), dma((n_expert - 1,)), dma((3,)),
        ],
        compiler_params=pltpu.CompilerParams(
            collective_id=cid, has_side_effects=True, vmem_limit_bytes=40 << 20
        ),
        name="finish_sums",
    )(qkv, proj, small, into, out_of)


def experts_kernel(
    nz, ny, own, named, router, cotangent, weight_in, weight_out,
    back, d_gate, made, grads_in, grads_out,
    rows_buf, cot_buf, in_buf, out_buf, hid_buf, gu_buf, part_buf, made_buf, gin_buf, gout_buf,
    gate_out, gate_in, from_y, from_z, to_y, to_z,
    load_sem, cot_sem, made_sem, grad_sem, send_sem, recv_sem, gate_send, gate_recv,
    send_y, recv_y, send_z, recv_z,
):
    z, y = places(nz, ny)
    me = lax.axis_index("expert")
    n_expert = nz * ny
    tok_rows, width = own.shape
    half = tok_rows // 2
    step_rows = ny * tok_rows
    exp_dev, ff, _ = out_buf.shape
    experts = named.shape[1]

    barrier = pltpu.get_barrier_semaphore()
    for k in range(1, n_expert):
        pl.semaphore_signal(
            barrier, inc=1, device_id={"expert": lax.rem(me + k, n_expert)}, device_id_type=MESH
        )
    pl.semaphore_wait(barrier, n_expert - 1)

    def owner(s, t, h):
        sign = -1 if h == 0 else 1
        return device(z + sign * s, y + sign * t, nz, ny)

    def piece(s, t, h):
        return pl.ds(pl.multiple_of(owner(s, t, h) * tok_rows + h * half, half), half)

    def slot(s, t, h):
        return pl.ds(((s * ny + t) * 2 + h) * half, half)

    def near(along_z, h):
        step = 1 if h == 0 else -1
        to = device(z + step, y, nz, ny) if along_z else device(z, y + step, nz, ny)
        return {"expert": to}

    def row_copy(s, t, h, s2, t2):
        source = own.at[pl.ds(h * half, half)] if s == 0 and t == 0 else rows_buf.at[slot(s, t, h)]
        return pltpu.make_async_remote_copy(
            src_ref=source, dst_ref=rows_buf.at[slot(s2, t2, h)],
            send_sem=send_sem.at[s2, t2, h], recv_sem=recv_sem.at[s2, t2, h],
            device_id=near(t2 == 0, h), device_id_type=MESH,
        )

    def arrive(s, t, h):
        if t == 0:
            row_copy(s - 1, 0, h, s, 0).wait_recv()
        else:
            row_copy(s, t - 1, h, s, t).wait_recv()

    sent = []

    def start(*key):
        copy = row_copy(*key)
        copy.start()
        sent.append(copy)

    for h in range(2):
        start(0, 0, h, 1, 0)
    if ny > 1:
        for h in range(2):
            start(0, 0, h, 0, 1)
    loads = [
        pltpu.make_async_copy(weight_in, in_buf, load_sem.at[0]),
        pltpu.make_async_copy(weight_out, out_buf, load_sem.at[1]),
    ]
    for copy in loads:
        copy.start()
    cots = {
        (s, t, h): pltpu.make_async_copy(
            cotangent.at[piece(s, t, h)], cot_buf.at[slot(s, t, h)], cot_sem.at[s, t, h]
        )
        for s in range(nz) for t in range(ny) for h in range(2)
    }
    for copy in cots.values():
        copy.start()
    rows_buf[0:tok_rows, :] = own[...]
    for copy in loads:
        copy.wait()

    lane = lax.broadcasted_iota(jnp.int32, (step_rows, experts), 1)
    wide_lane = lax.broadcasted_iota(jnp.int32, (step_rows, 128), 1)
    tile = 256

    def compute(s):
        rows = pl.ds(s * step_rows, step_rows)
        picked = jnp.concatenate(
            [named[piece(s, t, h), :] for t in range(ny) for h in range(2)], axis=0
        ) > 0.5
        logits = jnp.where(picked, dot(rows_buf[rows, :], router[...], 1, 1), MASKED)
        powers = jnp.exp(logits - jnp.max(logits, axis=1, keepdims=True))
        powers = jnp.where(picked, powers, 0.0)
        gates = powers / jnp.sum(powers, axis=1, keepdims=True)
        found = jnp.zeros((step_rows, 128), F32)
        for e in range(exp_dev):
            weight = jnp.sum(
                jnp.where(lane == me * exp_dev + e, gates, 0.0), axis=1, keepdims=True
            )

            def hidden_step(j, total):
                at = pl.multiple_of(j * tile, tile)
                cols, late = pl.ds(at, tile), pl.ds(pl.multiple_of(ff + at, tile), tile)
                gate_pre = dot(rows_buf[rows, :], in_buf[e, :, cols])
                up_pre = dot(rows_buf[rows, :], in_buf[e, :, late])
                d_plain = dot(cot_buf[rows, :], out_buf[e, cols, :], 1, 1)
                sigmoid = jax.nn.sigmoid(gate_pre)
                active = gate_pre * sigmoid
                hidden = active * up_pre
                hid_buf[e, rows, cols] = (weight * hidden).astype(BF16)
                d_hidden = weight * d_plain
                gu_buf[e, rows, cols] = (
                    d_hidden * up_pre * sigmoid * (1.0 + gate_pre * (1.0 - sigmoid))
                ).astype(BF16)
                gu_buf[e, rows, late] = (d_hidden * active).astype(BF16)
                return total + jnp.sum(hidden * d_plain, axis=1, keepdims=True)

            total = lax.fori_loop(0, ff // tile, hidden_step, jnp.zeros((step_rows, 1), F32))
            found += jnp.where(wide_lane == me * exp_dev + e, total, 0.0)

        @pl.loop(0, width // tile)
        def _(n):
            cols = pl.ds(pl.multiple_of(n * tile, tile), tile)
            d_rows = dot(gu_buf[0, rows, :], in_buf[0, cols, :], 1, 1)
            for e in range(1, exp_dev):
                d_rows += dot(gu_buf[e, rows, :], in_buf[e, cols, :], 1, 1)
            part_buf[rows, cols] = d_rows.astype(BF16)
            made_sum = dot(hid_buf[0, rows, :], out_buf[0, :, cols])
            for e in range(1, exp_dev):
                made_sum += dot(hid_buf[e, rows, :], out_buf[e, :, cols])
            made_buf[rows, cols] = made_sum.astype(BF16)

        for t in range(ny):
            for h in range(2):
                low = (t * 2 + h) * half
                gate_out[s, t, h] = found[low : low + half, :].T[:experts, :]
                if s or t:
                    gate_copy(s, t, h).start()
                made_copy(s, t, h).start()

    def gate_copy(s, t, h):
        return pltpu.make_async_remote_copy(
            src_ref=gate_out.at[s, t, h], dst_ref=gate_in.at[s, t, h],
            send_sem=gate_send.at[s, t, h], recv_sem=gate_recv.at[s, t, h],
            device_id={"expert": owner(s, t, h)}, device_id_type=MESH,
        )

    def made_copy(s, t, h):
        return pltpu.make_async_copy(
            made_buf.at[slot(s, t, h)], made.at[piece(s, t, h)], made_sem.at[s, t, h]
        )

    def part(r, t, h):
        return slot((r + 1) % nz, (t + 1) % ny, h)

    def y_copy(r, t, h):
        source = part_buf.at[part(r, 0, h)] if t == 0 else to_y.at[r, t - 1, h]
        return pltpu.make_async_remote_copy(
            src_ref=source, dst_ref=from_y.at[r, t, h],
            send_sem=send_y.at[r, t, h], recv_sem=recv_y.at[r, t, h],
            device_id=near(False, h), device_id_type=MESH,
        )

    def z_copy(r, h):
        return pltpu.make_async_remote_copy(
            src_ref=to_z.at[r, h], dst_ref=from_z.at[r, h],
            send_sem=send_z.at[r, h], recv_sem=recv_z.at[r, h],
            device_id=near(True, h), device_id_type=MESH,
        )

    def first_y(r):
        if ny > 1:
            for h in range(2):
                y_copy(r, 0, h).start()

    def finish(r):
        for t in range(1, ny - 1):
            for h in range(2):
                y_copy(r, t - 1, h).wait_recv()
                to_y[r, t - 1, h] = (
                    part_buf[part(r, t, h), :].astype(F32) + from_y[r, t - 1, h].astype(F32)
                ).astype(BF16)
                y_copy(r, t, h).start()
        for h in range(2):
            total = part_buf[part(r, ny - 1, h), :].astype(F32)
            if ny > 1:
                y_copy(r, ny - 2, h).wait_recv()
                total += from_y[r, ny - 2, h].astype(F32)
            if r > 0:
                z_copy(r - 1, h).wait_recv()
                total += from_z[r - 1, h].astype(F32)
            if r < nz - 1:
                to_z[r, h] = total.astype(BF16)
                z_copy(r, h).start()
            else:
                back[h * half : (h + 1) * half, :] = total

    def forward(s):
        for h in range(2):
            arrive(s, 0, h)
            if s + 1 < nz:
                start(s, 0, h, s + 1, 0)
            if ny > 1:
                start(s, 0, h, s, 1)

    def whole_step(s):
        for t in range(1, ny):
            for h in range(2):
                arrive(s, t, h)
                if t + 1 < ny:
                    start(s, t, h, s, t + 1)
        for t in range(ny):
            for h in range(2):
                cots[s, t, h].wait()
        compute(s)

    for s in range(nz):
        if s + 1 < nz:
            forward(s + 1)
        whole_step(s)
        if s > 0:
            first_y(s - 1)
        if s > 1:
            finish(s - 2)
    first_y(nz - 1)

    chunk = gin_buf.shape[2]

    def grad_step(i):
        cols = pl.ds(pl.multiple_of(i * tile, tile), tile)
        for e in range(exp_dev):
            found = dot(rows_buf[:, cols], gu_buf[e], 0, 0).astype(BF16)
            for c in range(tile // chunk):
                gin_buf[i * (tile // chunk) + c, e] = found[c * chunk : (c + 1) * chunk, :]

    def grad_out_step(i):
        cols = pl.ds(pl.multiple_of(i * tile, tile), tile)
        for e in range(exp_dev):
            found = dot(hid_buf[e, :, cols], cot_buf[...], 0, 0).astype(BF16)
            for c in range(width // chunk):
                gout_buf[c, e, cols, :] = found[:, c * chunk : (c + 1) * chunk]

    pl.loop(0, ff // tile)(grad_out_step)
    gout_copy = pltpu.make_async_copy(gout_buf, grads_out, grad_sem.at[0])
    gout_copy.start()
    if nz > 1:
        finish(nz - 2)
    pl.loop(0, width // tile)(grad_step)
    gin_copy = pltpu.make_async_copy(gin_buf, grads_in, grad_sem.at[1])
    gin_copy.start()
    finish(nz - 1)
    for h in range(2):
        gate_sum = gate_out[0, 0, h]
        for s in range(nz):
            for t in range(ny):
                if s or t:
                    gate_copy(s, t, h).wait_recv()
                    gate_sum += gate_in[s, t, h]
        d_gate[h] = gate_sum
    for copy in sent:
        copy.wait_send()
    for s in range(nz):
        for h in range(2):
            for t in range(ny):
                made_copy(s, t, h).wait()
                if s or t:
                    gate_copy(s, t, h).wait_send()
            for t in range(ny - 1):
                y_copy(s, t, h).wait_send()
            if s < nz - 1:
                z_copy(s, h).wait_send()
    gout_copy.wait()
    gin_copy.wait()


def experts_pass(own, named, router, cotangent, weight_in, weight_out, n_dp, n_expert, cid):
    nz, ny = grid_of(n_expert)
    tok_rows, width = own.shape
    exp_dev, ff, _ = weight_out.shape
    half, group = tok_rows // 2, tok_rows * n_expert
    experts = named.shape[1]
    whole, anywhere = pl.BlockSpec(memory_space=pltpu.VMEM), pl.BlockSpec(memory_space=pl.ANY)
    dma = pltpu.SemaphoreType.DMA
    ring = dma((nz, ny, 2))
    y_steps, y_mid, z_steps = max(ny - 1, 1), max(ny - 2, 1), max(nz - 1, 1)
    return pl.pallas_call(
        functools.partial(experts_kernel, nz, ny),
        out_shape=[
            jax.ShapeDtypeStruct((tok_rows, width), F32),
            jax.ShapeDtypeStruct((2, experts, half), F32),
            jax.ShapeDtypeStruct((group, width), BF16),
            jax.ShapeDtypeStruct((n_dp, exp_dev, width // n_dp, 2 * ff), BF16),
            jax.ShapeDtypeStruct((n_dp, exp_dev, ff, width // n_dp), BF16),
        ],
        in_specs=[whole, whole, whole, anywhere, anywhere, anywhere],
        out_specs=[whole, whole, anywhere, anywhere, anywhere],
        scratch_shapes=[
            pltpu.VMEM((group, width), BF16),
            pltpu.VMEM((group, width), BF16),
            pltpu.VMEM((exp_dev, width, 2 * ff), BF16),
            pltpu.VMEM((exp_dev, ff, width), BF16),
            pltpu.VMEM((exp_dev, group, ff), BF16),
            pltpu.VMEM((exp_dev, group, 2 * ff), BF16),
            pltpu.VMEM((group, width), BF16),
            pltpu.VMEM((group, width), BF16),
            pltpu.VMEM((n_dp, exp_dev, width // n_dp, 2 * ff), BF16),
            pltpu.VMEM((n_dp, exp_dev, ff, width // n_dp), BF16),
            pltpu.VMEM((nz, ny, 2, experts, half), F32),
            pltpu.VMEM((nz, ny, 2, experts, half), F32),
            pltpu.VMEM((nz, y_steps, 2, half, width), BF16),
            pltpu.VMEM((z_steps, 2, half, width), BF16),
            pltpu.VMEM((nz, y_mid, 2, half if ny > 2 else 16, width), BF16),
            pltpu.VMEM((z_steps, 2, half, width), BF16),
            dma((2,)), ring, ring, dma((2,)), ring, ring, ring, ring,
            dma((nz, y_steps, 2)), dma((nz, y_steps, 2)), dma((z_steps, 2)), dma((z_steps, 2)),
        ],
        compiler_params=pltpu.CompilerParams(
            collective_id=cid, has_side_effects=True, vmem_limit_bytes=60 << 20
        ),
        cost_estimate=pl.CostEstimate(
            flops=18 * exp_dev * group * width * ff,
            bytes_accessed=16 * group * width,
            transcendentals=exp_dev * group * ff,
        ),
        name="experts_pass",
    )(own, named, router, cotangent, weight_in, weight_out)


def gather(values, name, axis=0):
    return lax.all_gather(values, name, axis=axis, tiled=True)


def local(
    hidden_in, d_out, gain_attn, w_qkv, w_o, gain_moe, w_router, w_in, w_out,
    seq_lengths, assign, routes,
):
    tok_rows, width = hidden_in.shape
    exp_dev, _, ff_two = w_in.shape
    ff = ff_two // 2
    n_expert = lax.axis_size("expert")
    me = lax.axis_index("expert")
    experts = exp_dev * n_expert
    group_rows = tok_rows * n_expert
    q_per = HEADS // n_expert
    share = GROUPS // q_per
    q_cols = q_per * HEAD_DIM
    k_base = HEADS * HEAD_DIM
    v_base = k_base + KV_HEADS * HEAD_DIM
    cols = q_cols + 2 * HEAD_DIM

    n_dp = lax.axis_size("dp")
    wide = width // n_dp
    kv_head = (me * q_per) // GROUPS
    heads_part = jnp.concatenate(
        [
            lax.dynamic_slice_in_dim(w_qkv, me * q_cols, q_cols, 1),
            lax.dynamic_slice_in_dim(w_qkv, k_base + kv_head * HEAD_DIM, HEAD_DIM, 1),
            lax.dynamic_slice_in_dim(w_qkv, v_base + kv_head * HEAD_DIM, HEAD_DIM, 1),
        ],
        axis=1,
    )
    few = 2 + experts
    pack = jnp.concatenate(
        [gain_attn[None], gain_moe[None], w_router.T, jnp.zeros((-few % 16, wide), BF16)], axis=0
    )
    top = routes.shape[1]
    meta = jnp.concatenate(
        [assign, routes.T, jnp.zeros((-(1 + top) % 8, tok_rows), jnp.int32)], axis=0
    )
    meta = meta.reshape(meta.shape[0], 2, tok_rows // 2).transpose(1, 0, 2)
    qkv_full = gather(w_qkv, "dp")
    hidden_all, meta, w_heads, pack = first_gather(
        hidden_in, meta, heads_part, pack, n_dp, n_expert, 0
    )
    w_heads = w_heads.reshape(width, cols)
    pack = pack.transpose(1, 0, 2).reshape(-1, width)
    gain_one, gain_two = pack[0].astype(F32), pack[1].astype(F32)
    router_t = pack[2:few]
    position = meta[:, :, 0].reshape(group_rows)
    routes_all = meta[:, :, 1 : 1 + top]
    named = jnp.any(
        routes_all[:, :, :, None, :] == jnp.arange(experts, dtype=jnp.int32)[:, None], axis=2
    ).transpose(0, 1, 3, 2).reshape(group_rows, experts)
    stream_in = hidden_in.astype(F32)
    proj_full = gather(w_o, "dp")
    weight_in = gather(w_in, "dp", axis=1)
    weight_out = gather(w_out, "dp", axis=2)
    lengths = seq_lengths[0]
    order = jnp.arange(lengths.shape[0], dtype=jnp.int32)
    ends = jnp.sum(jnp.where(order[None, :] <= order[:, None], lengths[None, :], 0), axis=1)
    starts = ends - lengths
    seq_id = jnp.sum((position[None, :] >= ends[:, None]).astype(jnp.int32), axis=0)
    picks = seq_id[None, :] == jnp.arange(lengths.shape[0], dtype=jnp.int32)[:, None]
    start_of = jnp.sum(jnp.where(picks, starts[:, None], 0), axis=0)
    rot_pos = position - start_of
    half = HEAD_DIM // 2
    frequency = ROPE_BASE ** (-(jnp.arange(half).astype(F32) * (2.0 / HEAD_DIM)))
    angles = frequency[:, None] * rot_pos.astype(F32)[None, :]
    cosine, sine = jnp.cos(angles), jnp.sin(angles)
    low, high = start_of[None, :], position[None, :]
    key_pos = jnp.broadcast_to(position[:, None], (group_rows, low_tile(group_rows)))

    heads_out, lse, attended, d_out_all, normed_all, query, key, key_t, value = attend(
        low, high, key_pos, cosine, sine, gain_one[None], w_heads, hidden_all, d_out, q_per, 6
    )
    attended = attended.reshape(n_expert * q_cols, tok_rows)
    mid_stream = stream_in + dot(attended, proj_full, 0, 0)
    normed_two = rms_norm(mid_stream, gain_two).astype(BF16)

    d_back, d_gate, made, grads_in, grads_out = experts_pass(
        normed_two, named.astype(F32), router_t, d_out_all, weight_in, weight_out, n_dp, n_expert, 1
    )
    d_gate = d_gate.transpose(0, 2, 1).reshape(tok_rows, experts)
    own_named = jnp.any(
        routes[:, :, None] == jnp.arange(experts, dtype=jnp.int32)[None, None, :], axis=1
    )
    own_gates = jax.nn.softmax(
        jnp.where(own_named, dot(normed_two, router_t, 1, 1), -jnp.inf), axis=1
    )
    d_logits = (
        own_gates * (d_gate - jnp.sum(own_gates * d_gate, axis=1, keepdims=True))
    ).astype(BF16)
    grad_router = dot(d_logits, normed_two, 0, 0)
    d_normed_two = d_back + dot(d_logits, router_t)
    _, norm_two_back = jax.vjp(rms_norm, mid_stream, gain_two)
    d_mid_norm, grad_gain_two = norm_two_back(d_normed_two)
    d_mid = d_out.astype(F32) + d_mid_norm

    d_attn = d_mid.astype(BF16)
    d_attn, grads_in, grads_out, made = lax.optimization_barrier((d_attn, grads_in, grads_out, made))
    grad_w_in = lax.psum_scatter(grads_in, "dp", scatter_dimension=0, tiled=True)
    grad_w_out = lax.psum_scatter(grads_out, "dp", scatter_dimension=0, tiled=True)
    d_att = dot(proj_full, d_attn, 1, 1).astype(BF16).reshape(n_expert, q_cols, tok_rows)
    part_o = dot(attended, d_attn).astype(BF16).reshape(n_dp, wide, width)
    d_own, d_projected, returned, sum_o = attend_back(
        low, high, key_pos, query, key, key_t, value, heads_out, lse,
        cosine, sine, made, part_o, d_att, tok_rows, 4,
    )
    layer_out = (mid_stream + returned).astype(BF16)
    if share > 1:
        fan = lambda part: jnp.repeat(part.reshape(width, KV_HEADS, HEAD_DIM), share, axis=1).reshape(width, -1)
        qkv_full = jnp.concatenate(
            [qkv_full[:, :k_base], fan(qkv_full[:, k_base:v_base]), fan(qkv_full[:, v_base:])], axis=1
        )
    d_normed_one = dot(d_own, qkv_full, 0, 1)
    _, norm_one_back = jax.vjp(rms_norm, stream_in, gain_one)
    d_in_norm, grad_gain_one = norm_one_back(d_normed_one)
    grad_in = d_mid + d_in_norm

    part_qkv = dot(
        normed_all, d_projected.transpose(1, 0, 2).reshape(cols, group_rows), 0, 1
    ).astype(BF16).reshape(n_dp, wide, cols)
    small = jnp.concatenate(
        [grad_gain_one[None], grad_gain_two[None], grad_router, jnp.zeros((-few % 8, width), F32)], axis=0
    )
    small = small.reshape(-1, n_dp, wide).transpose(1, 0, 2)
    grad_w_qkv, grad_w_o, small, grad_w_in, grad_w_out = finish_sums(
        part_qkv, sum_o, small, grad_w_in[0], grad_w_out[0], q_cols, n_expert, 5
    )
    return (
        layer_out, grad_in, small[0], grad_w_qkv, grad_w_o, small[1], small[2:few].T,
        grad_w_in, grad_w_out,
    )


def solution(mesh):
    rows = P(("dp", "expert"), None)
    in_specs = (
        rows, rows, P("dp"), P("dp", None), P("dp", None), P("dp"), P("dp", None),
        P("expert", "dp", None), P("expert", None, "dp"), P("dp", None), P("dp", "expert"), rows,
    )
    out_specs = (
        rows, rows, P("dp"), P("dp", None), P("dp", None), P("dp"), P("dp", None),
        P("expert", "dp", None), P("expert", None, "dp"),
    )
    return jax.shard_map(local, mesh=mesh, in_specs=in_specs, out_specs=out_specs, check_vma=False)
```

```python
import functools

import jax
import jax.numpy as jnp
from jax import lax
from jax.experimental import pallas as pl
from jax.experimental.pallas import tpu as pltpu
from jax.sharding import PartitionSpec as P

HEADS = 16
KV_HEADS = 8
HEAD_DIM = 64
GROUPS = HEADS // KV_HEADS
EPSILON = 1e-06
ROPE_BASE = 10000.0
SCORE_SCALE = 0.015625
MASKED = -1e30
F32 = jnp.float32
BF16 = jnp.bfloat16
Q_TILE = 256
K_TILE = 256


MESH = pl.DeviceIdType.MESH
Z_SIZE = 4

def grid_of(n_expert):
    nz = Z_SIZE if n_expert % Z_SIZE == 0 else 1
    return nz, n_expert // nz

def places(nz, ny):
    me = lax.axis_index("expert")
    return me // ny, lax.rem(me, ny)

def device(z, y, nz, ny):
    return lax.rem(z + 2 * nz, nz) * ny + lax.rem(y + 2 * ny, ny)

def rms_norm(values, gain_vec):
    factor = lax.rsqrt(jnp.mean(values * values, axis=-1, keepdims=True) + EPSILON)
    return values * factor * gain_vec


def dot(left, right, left_dim=1, right_dim=0):
    return lax.dot_general(
        left, right, (((left_dim,), (right_dim,)), ((), ())), preferred_element_type=F32
    )


def rotate(values, cosine, sine):
    half = HEAD_DIM // 2
    one, two = values[:half], values[half:]
    return jnp.concatenate([one * cosine - two * sine, two * cosine + one * sine], axis=0)


def rotate_back(grads, cosine, sine):
    half = HEAD_DIM // 2
    one, two = grads[:half], grads[half:]
    return jnp.concatenate([one * cosine + two * sine, two * cosine - one * sine], axis=0)


def first_kernel(
    n_dp, nz, ny, rows, meta, heads, pack,
    rows_all, meta_all, heads_all, pack_all,
    send_sem, recv_sem, meta_send, meta_recv, dp_send, dp_recv, keep_sem,
):
    z, y = places(nz, ny)
    me, group = lax.axis_index("expert"), lax.axis_index("dp")
    count = rows.shape[0]
    half = count // 2
    barrier = pltpu.get_barrier_semaphore()
    near = [{"dp": lax.rem(group + k, n_dp)} for k in range(1, n_dp)]
    near += [{"expert": device(z + k, y, nz, ny)} for k in sorted({1, nz - 1} - {0})]
    near += [{"expert": device(z, y + k, nz, ny)} for k in sorted({1, ny - 1} - {0})]
    for other in near:
        pl.semaphore_signal(barrier, inc=1, device_id=other, device_id_type=MESH)
    pl.semaphore_wait(barrier, len(near))

    def origin(s, t, h):
        sign = -1 if h == 0 else 1
        return device(z + sign * s, y + sign * t, nz, ny)

    def copies(s, t, h, s2, t2):
        of = origin(s, t, h)
        mine = s == 0 and t == 0
        part = pl.ds(pl.multiple_of(of * count + h * half, half), half)
        step = 1 if h == 0 else -1
        to = device(z + step, y, nz, ny) if t2 == 0 else device(z, y + step, nz, ny)
        big = pltpu.make_async_remote_copy(
            src_ref=rows.at[pl.ds(h * half, half)] if mine else rows_all.at[part],
            dst_ref=rows_all.at[part],
            send_sem=send_sem.at[s2, t2, h], recv_sem=recv_sem.at[s2, t2, h],
            device_id={"expert": to}, device_id_type=MESH,
        )
        little = pltpu.make_async_remote_copy(
            src_ref=meta.at[h] if mine else meta_all.at[of, h], dst_ref=meta_all.at[of, h],
            send_sem=meta_send.at[s2, t2, h], recv_sem=meta_recv.at[s2, t2, h],
            device_id={"expert": to}, device_id_type=MESH,
        )
        return little, big

    def arrive(s, t, h):
        of = origin(s, t, h)
        part = pl.ds(pl.multiple_of(of * count + h * half, half), half)
        for place, sends, receives in (
            (meta_all.at[of, h], meta_send, meta_recv), (rows_all.at[part], send_sem, recv_sem)
        ):
            pltpu.make_async_remote_copy(
                src_ref=place, dst_ref=place, send_sem=sends.at[s, t, h], recv_sem=receives.at[s, t, h],
                device_id={"expert": device(z + 1, y, nz, ny)}, device_id_type=MESH,
            ).wait_recv()

    sent = []

    def start(*key):
        for copy in copies(*key):
            copy.start()
            sent.append(copy)

    for h in range(2):
        start(0, 0, h, 1, 0)
    if ny > 1:
        for h in range(2):
            start(0, 0, h, 0, 1)

    def across(k, a):
        source, target = ((heads, heads_all), (pack, pack_all))[a]
        return pltpu.make_async_remote_copy(
            src_ref=source, dst_ref=target.at[group],
            send_sem=dp_send.at[k - 1, a], recv_sem=dp_recv.at[k - 1, a],
            device_id={"dp": lax.rem(group + k, n_dp)}, device_id_type=MESH,
        )

    for k in range(1, n_dp):
        for a in range(2):
            across(k, a).start()
    keeps = [
        pltpu.make_async_copy(
            rows, rows_all.at[pl.ds(pl.multiple_of(me * count, count), count)], keep_sem.at[0]
        ),
        pltpu.make_async_copy(meta, meta_all.at[me], keep_sem.at[1]),
        pltpu.make_async_copy(heads, heads_all.at[group], keep_sem.at[2]),
        pltpu.make_async_copy(pack, pack_all.at[group], keep_sem.at[3]),
    ]
    for copy in keeps:
        copy.start()
    for s in range(1, nz):
        for h in range(2):
            arrive(s, 0, h)
            if s + 1 < nz:
                start(s, 0, h, s + 1, 0)
            if ny > 1:
                start(s, 0, h, s, 1)
    for t in range(1, ny):
        for s in range(nz):
            for h in range(2):
                arrive(s, t, h)
                if t + 1 < ny:
                    start(s, t, h, s, t + 1)
    for k in range(1, n_dp):
        for a, target in enumerate((heads_all, pack_all)):
            place = target.at[lax.rem(group + n_dp - k, n_dp)]
            pltpu.make_async_remote_copy(
                src_ref=place, dst_ref=place, send_sem=dp_send.at[k - 1, a], recv_sem=dp_recv.at[k - 1, a],
                device_id={"dp": lax.rem(group + k, n_dp)}, device_id_type=MESH,
            ).wait_recv()
    for copy in keeps:
        copy.wait()
    for copy in sent:
        copy.wait_send()
    for k in range(1, n_dp):
        for a in range(2):
            across(k, a).wait_send()


def first_gather(rows, meta, heads, pack, n_dp, n_expert, cid):
    nz, ny = grid_of(n_expert)
    anywhere = pl.BlockSpec(memory_space=pl.ANY)
    dma = pltpu.SemaphoreType.DMA
    ring, peers = dma((nz, ny, 2)), dma((max(n_dp - 1, 1), 2))
    return pl.pallas_call(
        functools.partial(first_kernel, n_dp, nz, ny),
        out_shape=[
            jax.ShapeDtypeStruct((rows.shape[0] * n_expert, rows.shape[1]), rows.dtype),
            jax.ShapeDtypeStruct((n_expert,) + meta.shape, meta.dtype),
            jax.ShapeDtypeStruct((n_dp,) + heads.shape, heads.dtype),
            jax.ShapeDtypeStruct((n_dp,) + pack.shape, pack.dtype),
        ],
        in_specs=[anywhere] * 4,
        out_specs=[anywhere] * 4,
        scratch_shapes=[ring, ring, ring, ring, peers, peers, dma((4,))],
        compiler_params=pltpu.CompilerParams(collective_id=cid, has_side_effects=True),
        name="first_gather",
    )(rows, meta, heads, pack)


def attend_kernel(
    nz, ny, low, high, key_pos, cos_tab, sin_tab, gain, head_weights, hidden, cotangent,
    out, lse, own_in, everyone, normed, query_all, key, key_t, value,
    score_buf, weight_buf, send_buf, rows_buf, value_t, query,
    own_send, own_recv, send_sem, recv_sem, keep_sem, load_sem,
):
    z, y = places(nz, ny)
    me = lax.axis_index("expert")
    n_expert = nz * ny
    heads, width, tile = query.shape
    q_cols = heads * width
    low_row, high_row = low[...], high[...]
    steps = key.shape[0] // K_TILE
    tok_rows = cotangent.shape[0]
    half_rows = tok_rows // 2
    per_tile = tile // tok_rows
    i = pl.program_id(0)
    count = key.shape[0] // tile

    def piece(s, t, h):
        sign = -1 if h == 0 else 1
        begin = device(z + sign * s, y + sign * t, nz, ny) * tok_rows + h * half_rows
        return pl.ds(pl.multiple_of(begin, half_rows), half_rows)

    def row_copy(s, t, h, s2, t2):
        mine = s == 0 and t == 0
        step = 1 if h == 0 else -1
        to = device(z + step, y, nz, ny) if t2 == 0 else device(z, y + step, nz, ny)
        return pltpu.make_async_remote_copy(
            src_ref=cotangent.at[pl.ds(h * half_rows, half_rows)] if mine else everyone.at[piece(s, t, h)],
            dst_ref=everyone.at[piece(s, t, h)],
            send_sem=send_sem.at[s2, t2, h], recv_sem=recv_sem.at[s2, t2, h],
            device_id={"expert": to}, device_id_type=MESH,
        )

    def arrive(s, t, h):
        place = everyone.at[piece(s, t, h)]
        pltpu.make_async_remote_copy(
            src_ref=place, dst_ref=place, send_sem=send_sem.at[s, t, h], recv_sem=recv_sem.at[s, t, h],
            device_id={"expert": device(z + 1, y, nz, ny)}, device_id_type=MESH,
        ).wait_recv()

    def forward(s):
        for h in range(2):
            arrive(s, 0, h)
            if s + 1 < nz:
                row_copy(s, 0, h, s + 1, 0).start()
            if ny > 1:
                row_copy(s, 0, h, s, 1).start()

    def own_copy(other, source):
        return pltpu.make_async_remote_copy(
            src_ref=send_buf.at[other], dst_ref=own_in.at[source],
            send_sem=own_send.at[other], recv_sem=own_recv.at[source],
            device_id={"expert": other}, device_id_type=MESH,
        )

    keep = pltpu.make_async_copy(
        cotangent, everyone.at[pl.ds(pl.multiple_of(me * tok_rows, tok_rows), tok_rows)], keep_sem.at[0]
    )

    whole_out = pltpu.make_async_copy(rows_buf, normed, keep_sem.at[2])

    def load(j):
        rows = pl.ds(pl.multiple_of(j * tile, tile), tile)
        return pltpu.make_async_copy(hidden.at[rows], rows_buf.at[rows], load_sem.at[j])

    @pl.when(i == 0)
    def _():
        barrier = pltpu.get_barrier_semaphore()
        for k in range(1, n_expert):
            pl.semaphore_signal(
                barrier, inc=1, device_id={"expert": lax.rem(me + k, n_expert)}, device_id_type=MESH
            )
        pl.semaphore_wait(barrier, n_expert - 1)
        for h in range(2):
            row_copy(0, 0, h, 1, 0).start()
        if ny > 1:
            for h in range(2):
                row_copy(0, 0, h, 0, 1).start()
        keep.start()
        for j in range(count):
            load(j).start()

        @pl.loop(0, count)
        def _(j):
            rows = pl.ds(pl.multiple_of(j * tile, tile), tile)
            load(j).wait()
            rows_buf[rows, :] = rms_norm(rows_buf[rows, :].astype(F32), gain[...]).astype(BF16)
            cosine, sine = cos_tab[:, rows], sin_tab[:, rows]
            projected = dot(head_weights[...], rows_buf[rows, :], 0, 1)
            for head in range(heads):
                part = projected[head * width : (head + 1) * width]
                query_all[head, :, rows] = rotate(part, cosine, sine).astype(BF16) * jnp.asarray(
                    SCORE_SCALE, BF16
                )
            turned = rotate(projected[q_cols : q_cols + width], cosine, sine).astype(BF16)
            key_t[:, rows] = turned
            key[rows, :] = turned.T
            plain = projected[q_cols + width :].astype(BF16)
            value_t[:, rows] = plain
            value[rows, :] = plain.T

        whole_out.start()
        if nz > 1:
            forward(1)

    early = [s for s in range(2, nz) if 3 * (s - 1) < count]
    for s in early:
        pl.when(i == 3 * (s - 1))(functools.partial(forward, s))
    query[...] = query_all[:, :, pl.ds(pl.multiple_of(i * tile, tile), tile)]

    def score_step(step, maxima):
        rows = pl.ds(pl.multiple_of(step * K_TILE, K_TILE), K_TILE)
        at = key_pos[rows, :]
        allowed = (at >= low_row) & (at <= high_row)
        found = []
        for head in range(heads):
            scores = jnp.dot(key[rows, :], query[head], preferred_element_type=F32)
            scores = jnp.where(allowed, scores, MASKED)
            score_buf[head, rows, :] = scores
            found.append(jnp.maximum(maxima[head], jnp.max(scores, axis=0, keepdims=True)))
        return tuple(found)

    begin = tuple(jnp.full(low_row.shape, MASKED, F32) for _ in range(heads))
    maxima = lax.fori_loop(0, steps, score_step, begin)

    def weight_step(step, totals):
        rows = pl.ds(pl.multiple_of(step * K_TILE, K_TILE), K_TILE)
        found = []
        for head in range(heads):
            weights = jnp.exp(score_buf[head, rows, :] - maxima[head])
            weight_buf[head, rows, :] = weights.astype(BF16)
            found.append(totals[head] + jnp.sum(weights, axis=0, keepdims=True))
        return tuple(found)

    begin = tuple(jnp.zeros(low_row.shape, F32) for _ in range(heads))
    totals = lax.fori_loop(0, steps, weight_step, begin)
    for head in range(heads):
        summed = jnp.dot(value_t[...], weight_buf[head], preferred_element_type=F32)
        attended = (summed / totals[head]).astype(BF16)
        out[head] = attended
        lse[head] = maxima[head] + jnp.log(totals[head])
        for j in range(per_tile):
            send_buf[i * per_tile + j, head * width : (head + 1) * width, :] = attended[
                :, j * tok_rows : (j + 1) * tok_rows
            ]
    for j in range(per_tile):
        other = i * per_tile + j

        @pl.when(other != me)
        def _():
            own_copy(other, me).start()

    @pl.when(i == count - 1)
    def _():
        mine = pltpu.make_async_copy(send_buf.at[me], own_in.at[me], keep_sem.at[1])
        mine.start()
        for s in range(2, nz):
            if s not in early:
                forward(s)
        for t in range(1, ny):
            for s in range(nz):
                for h in range(2):
                    arrive(s, t, h)
                    if t + 1 < ny:
                        row_copy(s, t, h, s, t + 1).start()
        for k in range(1, n_expert):
            other = lax.rem(me + k, n_expert)
            own_copy(other, other).wait_recv()
            own_copy(other, other).wait_send()
        for s in range(nz):
            for t in range(ny):
                for h in range(2):
                    if t > 0:
                        row_copy(s, t - 1, h, s, t).wait_send()
                    elif s > 0:
                        row_copy(s - 1, 0, h, s, 0).wait_send()
        keep.wait()
        mine.wait()
        whole_out.wait()


def attend(low, high, key_pos, cosine, sine, gain, head_weights, hidden, cotangent, heads, cid):
    tok_rows, model = cotangent.shape
    rows = hidden.shape[0]
    width = HEAD_DIM
    n_expert = rows // tok_rows
    nz, ny = grid_of(n_expert)
    tile = low_tile(rows)
    whole = lambda i: (0, 0)
    lane = lambda i: (0, i)
    anywhere = pl.BlockSpec(memory_space=pl.ANY)
    dma = pltpu.SemaphoreType.DMA
    tables = pl.BlockSpec((width // 2, rows), whole)
    return pl.pallas_call(
        functools.partial(attend_kernel, nz, ny),
        grid=(rows // tile,),
        in_specs=[
            pl.BlockSpec((1, tile), lane),
            pl.BlockSpec((1, tile), lane),
            pl.BlockSpec((rows, tile), whole),
            tables, tables,
            pl.BlockSpec((1, model), whole),
            pl.BlockSpec(head_weights.shape, whole),
            anywhere, anywhere,
        ],
        out_specs=[
            pl.BlockSpec((heads, width, tile), lambda i: (0, 0, i)),
            pl.BlockSpec((heads, 1, tile), lambda i: (0, 0, i)),
            anywhere, anywhere, anywhere,
            pl.BlockSpec((heads, width, rows), lambda i: (0, 0, 0)),
            pl.BlockSpec((rows, width), whole),
            pl.BlockSpec((width, rows), whole),
            pl.BlockSpec((rows, width), whole),
        ],
        out_shape=[
            jax.ShapeDtypeStruct((heads, width, rows), BF16),
            jax.ShapeDtypeStruct((heads, 1, rows), F32),
            jax.ShapeDtypeStruct((n_expert, heads * width, tok_rows), BF16),
            jax.ShapeDtypeStruct((rows, model), BF16),
            jax.ShapeDtypeStruct((rows, model), BF16),
            jax.ShapeDtypeStruct((heads, width, rows), BF16),
            jax.ShapeDtypeStruct((rows, width), BF16),
            jax.ShapeDtypeStruct((width, rows), BF16),
            jax.ShapeDtypeStruct((rows, width), BF16),
        ],
        scratch_shapes=[
            pltpu.VMEM((heads, rows, tile), F32),
            pltpu.VMEM((heads, rows, tile), BF16),
            pltpu.VMEM((n_expert, heads * width, tok_rows), BF16),
            pltpu.VMEM((rows, model), BF16),
            pltpu.VMEM((width, rows), BF16),
            pltpu.VMEM((heads, width, tile), BF16),
            dma((n_expert,)), dma((n_expert,)), dma((nz, ny, 2)), dma((nz, ny, 2)), dma((3,)),
            dma((rows // tile,)),
        ],
        compiler_params=pltpu.CompilerParams(
            collective_id=cid, has_side_effects=True, vmem_limit_bytes=56 << 20
        ),
        cost_estimate=pl.CostEstimate(
            flops=4 * heads * rows * rows * 256,
            bytes_accessed=8 * rows * 256,
            transcendentals=heads * rows * rows,
        ),
        name="attend",
    )(low, high, key_pos, cosine, sine, gain, head_weights, hidden, cotangent)


def low_tile(rows):
    return min(Q_TILE, rows)


def attend_back_kernel(
    nz, ny,
    low, high, key_pos, query, key, key_t, value, attended, lse,
    cos_tab, sin_tab, made, out_part, d_att, normed,
    own_in, qkv_part, summed, out_sum,
    norm_buf, qkv_acc,
    d_key, d_value, query_n, grad_n, grad, delta, grad_in, out_in, out_own, score_buf, send_buf, part_buf, from_y, from_z, to_y, to_z,
    part_sem, own_send, own_recv, tail_send, tail_recv, keep_sem, mine_sem,
    send_y, recv_y, send_z, recv_z, dp_send, dp_recv, grad_send, grad_recv,
):
    z, y = places(nz, ny)
    me, group = lax.axis_index("expert"), lax.axis_index("dp")
    n_expert, n_dp = nz * ny, out_part.shape[0]
    heads, width, tile = query.shape
    low_row, high_row = low[...], high[...]
    steps = key.shape[0] // K_TILE
    tok_rows = summed.shape[0]
    half_rows = tok_rows // 2
    per_tile = tile // tok_rows
    i = pl.program_id(0)
    count = key.shape[0] // tile
    q_cols = heads * width

    def piece(r, t, h):
        sign = -1 if h == 0 else 1
        start = device(z + sign * (r + 1), y + sign * (t + 1), nz, ny) * tok_rows + h * half_rows
        return pl.ds(pl.multiple_of(start, half_rows), half_rows)

    def near(along_z, h):
        step = 1 if h == 0 else -1
        to = device(z + step, y, nz, ny) if along_z else device(z, y + step, nz, ny)
        return {"expert": to}

    def part_copy(r, t, h):
        return pltpu.make_async_copy(
            made.at[piece(r, t, h)], part_buf.at[r, t, h], part_sem.at[r, t, h]
        )

    def y_copy(r, t, h):
        source = made.at[piece(r, 0, h)] if t == 0 else to_y.at[r, t - 1, h]
        return pltpu.make_async_remote_copy(
            src_ref=source, dst_ref=from_y.at[r, t, h],
            send_sem=send_y.at[r, t, h], recv_sem=recv_y.at[r, t, h],
            device_id=near(False, h), device_id_type=MESH,
        )

    def z_copy(r, h):
        return pltpu.make_async_remote_copy(
            src_ref=to_z.at[r, h], dst_ref=from_z.at[r, h],
            send_sem=send_z.at[r, h], recv_sem=recv_z.at[r, h],
            device_id=near(True, h), device_id_type=MESH,
        )

    def finish(r):
        for t in range(1, ny - 1):
            for h in range(2):
                y_copy(r, t - 1, h).wait_recv()
                part_copy(r, t, h).wait()
                to_y[r, t - 1, h] = (
                    part_buf[r, t, h].astype(F32) + from_y[r, t - 1, h].astype(F32)
                ).astype(BF16)
                y_copy(r, t, h).start()
        for h in range(2):
            part_copy(r, ny - 1, h).wait()
            total = part_buf[r, ny - 1, h].astype(F32)
            if ny > 1:
                y_copy(r, ny - 2, h).wait_recv()
                total += from_y[r, ny - 2, h].astype(F32)
            if r > 0:
                z_copy(r - 1, h).wait_recv()
                total += from_z[r - 1, h].astype(F32)
            if r < nz - 1:
                to_z[r, h] = total.astype(BF16)
                z_copy(r, h).start()
            else:
                summed[h * half_rows : (h + 1) * half_rows, :] = total

    def across(k):
        other = lax.rem(group + k, n_dp)
        return pltpu.make_async_remote_copy(
            src_ref=out_part.at[other], dst_ref=out_in.at[k - 1],
            send_sem=dp_send.at[k - 1], recv_sem=dp_recv.at[k - 1],
            device_id={"dp": other}, device_id_type=MESH,
        )

    spans = (
        (0, q_cols, 0),
        (q_cols, width, n_expert * q_cols),
        (q_cols + width, width, n_expert * (q_cols + width)),
    )

    def own_rows(a, source):
        _, rows, base = spans[a]
        return own_in.at[pl.ds(pl.multiple_of(base + source * rows, rows), rows)]

    def own_copy(a, other, source):
        begin, rows, _ = spans[a]
        return pltpu.make_async_remote_copy(
            src_ref=send_buf.at[other, pl.ds(begin, rows)], dst_ref=own_rows(a, source),
            send_sem=(own_send if a == 0 else tail_send.at[a - 1]).at[other],
            recv_sem=(own_recv if a == 0 else tail_recv.at[a - 1]).at[source],
            device_id={"expert": other}, device_id_type=MESH,
        )

    def grad_copy(other, source):
        return pltpu.make_async_remote_copy(
            src_ref=d_att.at[other], dst_ref=grad_in.at[source],
            send_sem=grad_send.at[other], recv_sem=grad_recv.at[source],
            device_id={"expert": other}, device_id_type=MESH,
        )

    @pl.when(i == 0)
    def _():
        barrier = pltpu.get_barrier_semaphore()
        for k in range(1, n_expert):
            pl.semaphore_signal(
                barrier, inc=1, device_id={"expert": lax.rem(me + k, n_expert)}, device_id_type=MESH
            )
        for k in range(1, n_dp):
            pl.semaphore_signal(
                barrier, inc=1, device_id={"dp": lax.rem(group + k, n_dp)}, device_id_type=MESH
            )
        pl.semaphore_wait(barrier, n_expert + n_dp - 2)
        for k in range(1, n_expert):
            grad_copy(lax.rem(me + k, n_expert), me).start()
        for k in range(1, n_dp):
            across(k).start()
        pltpu.make_async_copy(out_part.at[group], out_own, keep_sem.at[2]).start()
        grad_in[me] = d_att[me]
        pltpu.make_async_copy(normed, norm_buf, keep_sem.at[0]).start()
        qkv_acc[...] = jnp.zeros_like(qkv_acc)
        for r in range(nz):
            for h in range(2):
                if ny > 1:
                    y_copy(r, 0, h).start()
                for t in range(1, ny - 1):
                    part_copy(r, t, h).start()
                part_copy(r, ny - 1, h).start()
        d_key[...] = jnp.zeros_like(d_key)
        d_value[...] = jnp.zeros_like(d_value)

    for r in range(nz - 1):
        pl.when(i == (r + 1) * count // nz)(functools.partial(finish, r))

    for j in range(per_tile):
        source = i * per_tile + j

        @pl.when(source != me)
        def _():
            grad_copy(source, source).wait_recv()

        for head in range(heads):
            grad[head, :, j * tok_rows : (j + 1) * tok_rows] = grad_in[
                source, head * width : (head + 1) * width, :
            ]
    for head in range(heads):
        query_n[head] = query[head].T
        grad_n[head] = grad[head].T
        delta[head] = jnp.sum(
            grad[head].astype(F32) * attended[head].astype(F32), axis=0, keepdims=True
        )

    @pl.loop(0, steps)
    def _(step):
        rows = pl.ds(pl.multiple_of(step * K_TILE, K_TILE), K_TILE)
        at = key_pos[rows, :]
        allowed = (at >= low_row) & (at <= high_row)
        key_sum, value_sum = d_key[rows, :], d_value[rows, :]
        for head in range(heads):
            scores = jnp.dot(key[rows, :], query[head], preferred_element_type=F32)
            weights = jnp.exp(jnp.where(allowed, scores - lse[head], MASKED))
            d_soft = jnp.dot(value[rows, :], grad[head], preferred_element_type=F32)
            d_scores = (weights * (d_soft - delta[head])).astype(BF16)
            score_buf[head, rows, :] = d_scores
            key_sum += jnp.dot(d_scores, query_n[head], preferred_element_type=F32)
            value_sum += jnp.dot(weights.astype(BF16), grad_n[head], preferred_element_type=F32)
        d_key[rows, :] = key_sum
        d_value[rows, :] = value_sum

    lanes = pl.ds(pl.multiple_of(i * tile, tile), tile)
    for head in range(heads):
        d_query = jnp.dot(key_t[...], score_buf[head], preferred_element_type=F32) * SCORE_SCALE
        turned = rotate_back(d_query, cos_tab[:, lanes], sin_tab[:, lanes]).astype(BF16)
        for j in range(per_tile):
            send_buf[i * per_tile + j, head * width : (head + 1) * width, :] = turned[
                :, j * tok_rows : (j + 1) * tok_rows
            ]
    for j in range(per_tile):
        other = i * per_tile + j

        @pl.when(other != me)
        def _():
            own_copy(0, other, me).start()

    @pl.when(i == 0)
    def _():
        pltpu.make_async_copy(normed, norm_buf, keep_sem.at[0]).wait()

    for j in range(per_tile):
        other = i * per_tile + j
        rows = pl.ds(pl.multiple_of(other * tok_rows, tok_rows), tok_rows)
        qkv_acc[:q_cols, :] += dot(send_buf[other, :q_cols, :], norm_buf[rows, :])

    @pl.when(i == count - 1)
    def _():
        for other in range(n_expert):
            rows = pl.ds(other * tok_rows, tok_rows)
            turned = rotate_back(d_key[rows, :].T, cos_tab[:, rows], sin_tab[:, rows])
            send_buf[other, q_cols : q_cols + width, :] = turned.astype(BF16)
            send_buf[other, q_cols + width :, :] = d_value[rows, :].T.astype(BF16)

            @pl.when(other != me)
            def _():
                own_copy(1, other, me).start()
                own_copy(2, other, me).start()

        for other in range(n_expert):
            rows = pl.ds(other * tok_rows, tok_rows)
            qkv_acc[q_cols:, :] += dot(send_buf[other, q_cols:, :], norm_buf[rows, :])
        span = qkv_part.shape[2]
        for c in range(n_dp):
            qkv_part[c] = qkv_acc[:, c * span : (c + 1) * span].astype(BF16)
        mine = [
            pltpu.make_async_copy(
                send_buf.at[me, pl.ds(begin, rows)], own_rows(a, me), mine_sem.at[a]
            )
            for a, (begin, rows, _) in enumerate(spans)
        ]
        for copy in mine:
            copy.start()
        finish(nz - 1)
        pltpu.make_async_copy(out_part.at[group], out_own, keep_sem.at[2]).wait()
        for k in range(1, n_dp):
            across(k).wait_recv()
        few = out_sum.shape[2]
        for m in range(n_expert):
            cols = slice(m * few, (m + 1) * few)
            out_total = out_own[:, cols].astype(F32)
            for k in range(1, n_dp):
                out_total += out_in[k - 1, :, cols].astype(F32)
            out_sum[m] = out_total.astype(BF16)
        for k in range(1, n_dp):
            across(k).wait_send()
        for k in range(1, n_expert):
            other = lax.rem(me + k, n_expert)
            for a in range(3):
                own_copy(a, other, other).wait_recv()
                own_copy(a, other, other).wait_send()
            grad_copy(other, other).wait_send()
        for r in range(nz):
            for h in range(2):
                for t in range(ny - 1):
                    y_copy(r, t, h).wait_send()
                if r < nz - 1:
                    z_copy(r, h).wait_send()
        for copy in mine:
            copy.wait()


def attend_back(
    low, high, key_pos, query, key, key_t, value, attended, lse,
    cosine, sine, made, out_part, d_att, normed, tok_rows, cid,
):
    heads, width, rows = query.shape
    n_expert = rows // tok_rows
    nz, ny = grid_of(n_expert)
    cols = (heads + 2) * width
    half_rows, model = tok_rows // 2, made.shape[1]
    tile = low_tile(rows)
    whole = lambda i: (0, 0)
    lane = lambda i: (0, i)
    wide = pl.BlockSpec((heads, width, tile), lambda i: (0, 0, i))
    row = pl.BlockSpec((heads, 1, tile), lambda i: (0, 0, i))
    keys = pl.BlockSpec((rows, width), whole)
    anywhere = pl.BlockSpec(memory_space=pl.ANY)
    dma = pltpu.SemaphoreType.DMA
    y_steps, y_mid, z_steps = max(ny - 1, 1), max(ny - 2, 1), max(nz - 1, 1)
    peers = max(out_part.shape[0] - 1, 1)
    qkv_tiles = (out_part.shape[0], cols, out_part.shape[1])
    out_tiles = (n_expert, out_part.shape[1], out_part.shape[2] // n_expert)
    return pl.pallas_call(
        functools.partial(attend_back_kernel, nz, ny),
        grid=(rows // tile,),
        in_specs=[
            pl.BlockSpec((1, tile), lane),
            pl.BlockSpec((1, tile), lane),
            pl.BlockSpec((rows, tile), whole),
            wide, keys, pl.BlockSpec((width, rows), whole), keys, wide, row,
            pl.BlockSpec((width // 2, rows), whole), pl.BlockSpec((width // 2, rows), whole),
            anywhere, anywhere, pl.BlockSpec(d_att.shape, lambda i: (0, 0, 0)), anywhere,
        ],
        out_specs=[
            anywhere, pl.BlockSpec(qkv_tiles, lambda i: (0, 0, 0)),
            pl.BlockSpec((tok_rows, model), whole),
            pl.BlockSpec(out_tiles, lambda i: (0, 0, 0)),
        ],
        out_shape=[
            jax.ShapeDtypeStruct((n_expert * cols, tok_rows), BF16),
            jax.ShapeDtypeStruct(qkv_tiles, BF16),
            jax.ShapeDtypeStruct((tok_rows, model), F32),
            jax.ShapeDtypeStruct(out_tiles, BF16),
        ],
        scratch_shapes=[
            pltpu.VMEM((rows, model), BF16),
            pltpu.VMEM((cols, model), F32),
            pltpu.VMEM((rows, width), F32),
            pltpu.VMEM((rows, width), F32),
            pltpu.VMEM((heads, tile, width), BF16),
            pltpu.VMEM((heads, tile, width), BF16),
            pltpu.VMEM((heads, width, tile), BF16),
            pltpu.VMEM((heads, 1, tile), F32),
            pltpu.VMEM((n_expert, heads * width, tok_rows), BF16),
            pltpu.VMEM((peers,) + out_part.shape[1:], BF16),
            pltpu.VMEM(out_part.shape[1:], BF16),
            pltpu.VMEM((heads, rows, tile), BF16),
            pltpu.VMEM((n_expert, cols, tok_rows), BF16),
            pltpu.VMEM((nz, ny, 2, half_rows, model), BF16),
            pltpu.VMEM((nz, y_steps, 2, half_rows, model), BF16),
            pltpu.VMEM((z_steps, 2, half_rows, model), BF16),
            pltpu.VMEM((nz, y_mid, 2, half_rows if ny > 2 else 16, model), BF16),
            pltpu.VMEM((z_steps, 2, half_rows, model), BF16),
            dma((nz, ny, 2)), dma((n_expert,)), dma((n_expert,)), dma((2, n_expert)), dma((2, n_expert)), dma((3,)), dma((3,)),
            dma((nz, y_steps, 2)), dma((nz, y_steps, 2)), dma((z_steps, 2)), dma((z_steps, 2)),
            dma((peers,)), dma((peers,)), dma((n_expert,)), dma((n_expert,)),
        ],
        compiler_params=pltpu.CompilerParams(
            collective_id=cid, has_side_effects=True, vmem_limit_bytes=56 << 20
        ),
        cost_estimate=pl.CostEstimate(
            flops=10 * heads * rows * rows * 256,
            bytes_accessed=8 * rows * 256,
            transcendentals=heads * rows * rows,
        ),
        name="attend_back",
    )(low, high, key_pos, query, key, key_t, value, attended, lse, cosine, sine, made, out_part, d_att, normed)


def finish_kernel(
    n_dp, nz, ny, q_cols, qkv, proj, small_rest, into, out_of, d_own, weights, stream, d_mid, gain,
    qkv_rows, proj_rows, small_sum, into_wide, out_of_wide, grad_in,
    small, own_t, d_normed,
    qkv_in, small_in, proj_in, own_qkv, own_proj, own_small, qkv_all, proj_all, small_all,
    dp_send, dp_recv, ring_send, ring_recv, part_send, part_recv, keep_sem,
):
    z, y = places(nz, ny)
    me, group = lax.axis_index("expert"), lax.axis_index("dp")
    n_expert = nz * ny
    barrier = pltpu.get_barrier_semaphore()
    near = [{"dp": lax.rem(group + k, n_dp)} for k in range(1, n_dp)]
    near += [{"expert": lax.rem(me + k, n_expert)} for k in range(1, n_expert)]
    for other in near:
        pl.semaphore_signal(barrier, inc=1, device_id=other, device_id_type=MESH)
    pl.semaphore_wait(barrier, len(near))

    arrays = {0: (qkv, qkv_in, own_qkv), 2: (small, small_in, own_small)}

    def across(k, a):
        source, target, _ = arrays[a]
        other = lax.rem(group + k, n_dp)
        return pltpu.make_async_remote_copy(
            src_ref=source.at[other], dst_ref=target.at[k - 1],
            send_sem=dp_send.at[k - 1, a], recv_sem=dp_recv.at[k - 1, a],
            device_id={"dp": other}, device_id_type=MESH,
        )

    rings = ((own_qkv, qkv_all), (own_proj, proj_all), (own_small, small_all))

    def origin(s, t, h):
        sign = -1 if h == 0 else 1
        return device(z + sign * s, y + sign * t, nz, ny)

    def ring_copy(s, t, h, s2, t2, a):
        own, everyone = rings[a]
        of = origin(s, t, h)
        rows = own.shape[0] // 2 if a < 2 else own.shape[0]
        part = pl.ds(h * rows, rows)
        source = own.at[part] if s == 0 and t == 0 else everyone.at[of, part]
        step = 1 if h == 0 else -1
        to = device(z + step, y, nz, ny) if t2 == 0 else device(z, y + step, nz, ny)
        return pltpu.make_async_remote_copy(
            src_ref=source, dst_ref=everyone.at[of, part],
            send_sem=ring_send.at[s2, t2, h, a], recv_sem=ring_recv.at[s2, t2, h, a],
            device_id={"expert": to}, device_id_type=MESH,
        )

    def arrive(s, t, h, a):
        own, everyone = rings[a]
        rows = own.shape[0] // 2 if a < 2 else own.shape[0]
        place = everyone.at[origin(s, t, h), pl.ds(h * rows, rows)]
        pltpu.make_async_remote_copy(
            src_ref=place, dst_ref=place,
            send_sem=ring_send.at[s, t, h, a], recv_sem=ring_recv.at[s, t, h, a],
            device_id={"expert": device(z + 1, y, nz, ny)}, device_id_type=MESH,
        ).wait_recv()

    sent, keeps = [], []

    def start(*key):
        copy = ring_copy(*key)
        copy.start()
        sent.append(copy)

    def begin(moves):
        for a in sorted({a for _, a in moves}):
            own, everyone = rings[a]
            keeps.append(pltpu.make_async_copy(own, everyone.at[me], keep_sem.at[a]))
            keeps[-1].start()
        for h, a in moves:
            if nz > 1:
                start(0, 0, h, 1, 0, a)
            if ny > 1:
                start(0, 0, h, 0, 1, a)

    def along_z(moves):
        for s in range(1, nz):
            for h, a in moves:
                arrive(s, 0, h, a)
                if s + 1 < nz:
                    start(s, 0, h, s + 1, 0, a)
                if ny > 1:
                    start(s, 0, h, s, 1, a)

    def along_y(moves):
        for t in range(1, ny):
            for s in range(nz):
                for h, a in moves:
                    arrive(s, t, h, a)
                    if t + 1 < ny:
                        start(s, t, h, s, t + 1, a)

    def part_copy(k):
        other = lax.rem(me + k, n_expert)
        return pltpu.make_async_remote_copy(
            src_ref=proj.at[other], dst_ref=proj_in.at[k - 1],
            send_sem=part_send.at[k - 1], recv_sem=part_recv.at[k - 1],
            device_id={"expert": other}, device_id_type=MESH,
        )

    first, second, third = [(0, 0), (1, 0)], [(0, 1), (1, 1)], [(0, 2)]
    for k in range(1, n_dp):
        across(k, 0).start()
    for k in range(1, n_expert):
        part_copy(k).start()
    own_t[...] = d_own[...].T
    tile = 256

    @pl.loop(0, d_normed.shape[1] // tile)
    def _(n):
        cols = pl.ds(pl.multiple_of(n * tile, tile), tile)
        d_normed[:, cols] = dot(own_t[...], weights[cols, :], 1, 1)

    def sum_across(a):
        source, target, own = arrays[a]
        total = source[group].astype(F32)
        for k in range(1, n_dp):
            across(k, a).wait_recv()
            total += target[k - 1].astype(F32)
        own[...] = total.astype(own.dtype)

    sum_across(0)
    begin(first)
    values = stream[...].astype(F32)
    factor = lax.rsqrt(jnp.mean(values * values, axis=1, keepdims=True) + EPSILON)
    small[...] = small_rest[...]
    gain_row = jnp.sum(d_normed[...] * values * factor, axis=0, keepdims=True)
    span = small.shape[2]
    for c in range(n_dp):
        small[c, 0:1, :] = gain_row[:, c * span : (c + 1) * span]
    for k in range(1, n_dp):
        across(k, 2).start()
    total = proj[me].astype(F32)
    for k in range(1, n_expert):
        part_copy(k).wait_recv()
        total += proj_in[k - 1].astype(F32)
    own_proj[...] = total.astype(BF16)
    begin(second)
    sum_across(2)
    begin(third)
    scaled = gain[...] * d_normed[...]
    inner = jnp.mean(scaled * values, axis=1, keepdims=True)
    grad_in[...] = d_mid[...] + factor * scaled - values * (factor * factor * factor * inner)
    for e in range(into.shape[0]):
        into_wide[e] = into[e].astype(F32)
        out_of_wide[e] = out_of[e].astype(F32)
    along_z(first + second + third)
    along_y(first + second + third)
    for copy in keeps:
        copy.wait()
    total = small_all[0]
    for other in range(1, n_expert):
        total += small_all[other]
    small_sum[...] = total
    alike = max(n_expert // KV_HEADS, 1)
    pieces = [qkv_all[m, :q_cols, :].T.astype(F32) for m in range(n_expert)]
    for first in (q_cols, q_cols + HEAD_DIM):
        for head in range(KV_HEADS):
            total = qkv_all[head * alike, first : first + HEAD_DIM, :].T.astype(F32)
            for more in range(1, alike):
                total += qkv_all[head * alike + more, first : first + HEAD_DIM, :].T.astype(F32)
            pieces.append(total)
    outs = [proj_all[m].astype(F32) for m in range(n_expert)]
    for target, pieces in ((qkv_rows, pieces), (proj_rows, outs)):
        lay(target, pieces)
    for copy in sent:
        copy.wait_send()
    for k in range(1, n_expert):
        part_copy(k).wait_send()
    for k in range(1, n_dp):
        for a in arrays:
            across(k, a).wait_send()


def lay(target, pieces):
    at = 0
    while pieces:
        block = [pieces.pop(0)]
        if block[0].shape[1] % 128:
            block.append(pieces.pop(0))
        joined = jnp.concatenate(block, axis=1) if len(block) > 1 else block[0]
        target[:, at : at + joined.shape[1]] = joined
        at += joined.shape[1]


def finish_sums(
    qkv, proj, small, into, out_of, d_own, weights, stream, d_mid, gain, q_cols, n_expert, cid
):
    nz, ny = grid_of(n_expert)
    n_dp = qkv.shape[0]
    whole = pl.BlockSpec(memory_space=pltpu.VMEM)
    dma = pltpu.SemaphoreType.DMA
    peers = max(n_dp - 1, 1)
    return pl.pallas_call(
        functools.partial(finish_kernel, n_dp, nz, ny, q_cols),
        out_shape=[
            jax.ShapeDtypeStruct((qkv.shape[2], (HEADS + 2 * KV_HEADS) * HEAD_DIM), F32),
            jax.ShapeDtypeStruct((proj.shape[1], n_expert * proj.shape[2]), F32),
            jax.ShapeDtypeStruct(small.shape[1:], F32),
            jax.ShapeDtypeStruct(into.shape, F32),
            jax.ShapeDtypeStruct(out_of.shape, F32),
            jax.ShapeDtypeStruct(d_mid.shape, F32),
        ],
        in_specs=[whole] * 10,
        out_specs=[whole] * 6,
        scratch_shapes=[
            pltpu.VMEM(small.shape, F32),
            pltpu.VMEM(d_own.shape[::-1], BF16),
            pltpu.VMEM(d_mid.shape, F32),
            pltpu.VMEM((peers,) + qkv.shape[1:], BF16),
            pltpu.VMEM((peers,) + small.shape[1:], F32),
            pltpu.VMEM((n_expert - 1,) + proj.shape[1:], BF16),
            pltpu.VMEM(qkv.shape[1:], BF16),
            pltpu.VMEM(proj.shape[1:], BF16),
            pltpu.VMEM(small.shape[1:], F32),
            pltpu.VMEM((n_expert,) + qkv.shape[1:], BF16),
            pltpu.VMEM(proj.shape, BF16),
            pltpu.VMEM((n_expert,) + small.shape[1:], F32),
            dma((peers, 3)), dma((peers, 3)), dma((nz, ny, 2, 3)), dma((nz, ny, 2, 3)),
            dma((n_expert - 1,)), dma((n_expert - 1,)), dma((3,)),
        ],
        compiler_params=pltpu.CompilerParams(
            collective_id=cid, has_side_effects=True, vmem_limit_bytes=56 << 20
        ),
        name="finish_sums",
    )(qkv, proj, small, into, out_of, d_own, weights, stream, d_mid, gain)


def experts_kernel(
    nz, ny, own, named, router, cotangent, weight_in, weight_out,
    back, d_gate, made, grads_in, grads_out,
    rows_buf, cot_buf, in_buf, out_buf, hid_buf, gu_buf, part_buf, made_buf, gin_buf, gout_buf,
    gate_out, gate_in, from_y, from_z, to_y, to_z,
    load_sem, cot_sem, made_sem, grad_sem, send_sem, recv_sem, gate_send, gate_recv,
    send_y, recv_y, send_z, recv_z,
):
    z, y = places(nz, ny)
    me = lax.axis_index("expert")
    n_expert = nz * ny
    tok_rows, width = own.shape
    half = tok_rows // 2
    step_rows = ny * tok_rows
    exp_dev, ff, _ = out_buf.shape
    experts = named.shape[1]

    barrier = pltpu.get_barrier_semaphore()
    for k in range(1, n_expert):
        pl.semaphore_signal(
            barrier, inc=1, device_id={"expert": lax.rem(me + k, n_expert)}, device_id_type=MESH
        )
    pl.semaphore_wait(barrier, n_expert - 1)

    def owner(s, t, h):
        sign = -1 if h == 0 else 1
        return device(z + sign * s, y + sign * t, nz, ny)

    def piece(s, t, h):
        return pl.ds(pl.multiple_of(owner(s, t, h) * tok_rows + h * half, half), half)

    def slot(s, t, h):
        return pl.ds(((s * ny + t) * 2 + h) * half, half)

    def near(along_z, h):
        step = 1 if h == 0 else -1
        to = device(z + step, y, nz, ny) if along_z else device(z, y + step, nz, ny)
        return {"expert": to}

    def row_copy(s, t, h, s2, t2):
        source = own.at[pl.ds(h * half, half)] if s == 0 and t == 0 else rows_buf.at[slot(s, t, h)]
        return pltpu.make_async_remote_copy(
            src_ref=source, dst_ref=rows_buf.at[slot(s2, t2, h)],
            send_sem=send_sem.at[s2, t2, h], recv_sem=recv_sem.at[s2, t2, h],
            device_id=near(t2 == 0, h), device_id_type=MESH,
        )

    def arrive(s, t, h):
        if t == 0:
            row_copy(s - 1, 0, h, s, 0).wait_recv()
        else:
            row_copy(s, t - 1, h, s, t).wait_recv()

    sent = []

    def start(*key):
        copy = row_copy(*key)
        copy.start()
        sent.append(copy)

    for h in range(2):
        start(0, 0, h, 1, 0)
    if ny > 1:
        for h in range(2):
            start(0, 0, h, 0, 1)
    loads = [
        pltpu.make_async_copy(weight_in, in_buf, load_sem.at[0]),
        pltpu.make_async_copy(weight_out, out_buf, load_sem.at[1]),
    ]
    for copy in loads:
        copy.start()
    cots = {
        (s, t, h): pltpu.make_async_copy(
            cotangent.at[piece(s, t, h)], cot_buf.at[slot(s, t, h)], cot_sem.at[s, t, h]
        )
        for s in range(nz) for t in range(ny) for h in range(2)
    }
    for copy in cots.values():
        copy.start()
    rows_buf[0:tok_rows, :] = own[...]
    for copy in loads:
        copy.wait()

    lane = lax.broadcasted_iota(jnp.int32, (step_rows, experts), 1)
    wide_lane = lax.broadcasted_iota(jnp.int32, (step_rows, 128), 1)
    tile = 256

    def compute(s):
        rows = pl.ds(s * step_rows, step_rows)
        picked = jnp.concatenate(
            [named[piece(s, t, h), :] for t in range(ny) for h in range(2)], axis=0
        ) > 0.5
        logits = jnp.where(picked, dot(rows_buf[rows, :], router[...], 1, 1), MASKED)
        powers = jnp.exp(logits - jnp.max(logits, axis=1, keepdims=True))
        powers = jnp.where(picked, powers, 0.0)
        gates = powers / jnp.sum(powers, axis=1, keepdims=True)
        found = jnp.zeros((step_rows, 128), F32)
        for e in range(exp_dev):
            weight = jnp.sum(
                jnp.where(lane == me * exp_dev + e, gates, 0.0), axis=1, keepdims=True
            )

            def hidden_step(j, total):
                at = pl.multiple_of(j * tile, tile)
                cols, late = pl.ds(at, tile), pl.ds(pl.multiple_of(ff + at, tile), tile)
                gate_pre = dot(rows_buf[rows, :], in_buf[e, :, cols])
                up_pre = dot(rows_buf[rows, :], in_buf[e, :, late])
                d_plain = dot(cot_buf[rows, :], out_buf[e, cols, :], 1, 1)
                sigmoid = jax.nn.sigmoid(gate_pre)
                active = gate_pre * sigmoid
                hidden = active * up_pre
                hid_buf[e, rows, cols] = (weight * hidden).astype(BF16)
                d_hidden = weight * d_plain
                gu_buf[e, rows, cols] = (
                    d_hidden * up_pre * sigmoid * (1.0 + gate_pre * (1.0 - sigmoid))
                ).astype(BF16)
                gu_buf[e, rows, late] = (d_hidden * active).astype(BF16)
                return total + jnp.sum(hidden * d_plain, axis=1, keepdims=True)

            total = lax.fori_loop(0, ff // tile, hidden_step, jnp.zeros((step_rows, 1), F32))
            found += jnp.where(wide_lane == me * exp_dev + e, total, 0.0)

        @pl.loop(0, width // tile)
        def _(n):
            cols = pl.ds(pl.multiple_of(n * tile, tile), tile)
            d_rows = dot(gu_buf[0, rows, :], in_buf[0, cols, :], 1, 1)
            for e in range(1, exp_dev):
                d_rows += dot(gu_buf[e, rows, :], in_buf[e, cols, :], 1, 1)
            part_buf[rows, cols] = d_rows.astype(BF16)
            made_sum = dot(hid_buf[0, rows, :], out_buf[0, :, cols])
            for e in range(1, exp_dev):
                made_sum += dot(hid_buf[e, rows, :], out_buf[e, :, cols])
            made_buf[rows, cols] = made_sum.astype(BF16)

        for t in range(ny):
            for h in range(2):
                low = (t * 2 + h) * half
                gate_out[s, t, h] = found[low : low + half, :].T[:experts, :]
                if s or t:
                    gate_copy(s, t, h).start()
                made_copy(s, t, h).start()

    def gate_copy(s, t, h):
        return pltpu.make_async_remote_copy(
            src_ref=gate_out.at[s, t, h], dst_ref=gate_in.at[s, t, h],
            send_sem=gate_send.at[s, t, h], recv_sem=gate_recv.at[s, t, h],
            device_id={"expert": owner(s, t, h)}, device_id_type=MESH,
        )

    def made_copy(s, t, h):
        return pltpu.make_async_copy(
            made_buf.at[slot(s, t, h)], made.at[piece(s, t, h)], made_sem.at[s, t, h]
        )

    def part(r, t, h):
        return slot((r + 1) % nz, (t + 1) % ny, h)

    def y_copy(r, t, h):
        source = part_buf.at[part(r, 0, h)] if t == 0 else to_y.at[r, t - 1, h]
        return pltpu.make_async_remote_copy(
            src_ref=source, dst_ref=from_y.at[r, t, h],
            send_sem=send_y.at[r, t, h], recv_sem=recv_y.at[r, t, h],
            device_id=near(False, h), device_id_type=MESH,
        )

    def z_copy(r, h):
        return pltpu.make_async_remote_copy(
            src_ref=to_z.at[r, h], dst_ref=from_z.at[r, h],
            send_sem=send_z.at[r, h], recv_sem=recv_z.at[r, h],
            device_id=near(True, h), device_id_type=MESH,
        )

    def first_y(r):
        if ny > 1:
            for h in range(2):
                y_copy(r, 0, h).start()

    def finish(r):
        for t in range(1, ny - 1):
            for h in range(2):
                y_copy(r, t - 1, h).wait_recv()
                to_y[r, t - 1, h] = (
                    part_buf[part(r, t, h), :].astype(F32) + from_y[r, t - 1, h].astype(F32)
                ).astype(BF16)
                y_copy(r, t, h).start()
        for h in range(2):
            total = part_buf[part(r, ny - 1, h), :].astype(F32)
            if ny > 1:
                y_copy(r, ny - 2, h).wait_recv()
                total += from_y[r, ny - 2, h].astype(F32)
            if r > 0:
                z_copy(r - 1, h).wait_recv()
                total += from_z[r - 1, h].astype(F32)
            if r < nz - 1:
                to_z[r, h] = total.astype(BF16)
                z_copy(r, h).start()
            else:
                back[h * half : (h + 1) * half, :] = total

    def forward(s):
        for h in range(2):
            arrive(s, 0, h)
            if s + 1 < nz:
                start(s, 0, h, s + 1, 0)
            if ny > 1:
                start(s, 0, h, s, 1)

    def whole_step(s):
        for t in range(1, ny):
            for h in range(2):
                arrive(s, t, h)
                if t + 1 < ny:
                    start(s, t, h, s, t + 1)
        for t in range(ny):
            for h in range(2):
                cots[s, t, h].wait()
        compute(s)

    for s in range(nz):
        if s + 1 < nz:
            forward(s + 1)
        whole_step(s)
        if s > 0:
            first_y(s - 1)
        if s == nz - 2:
            first_y(nz - 1)
        if s > 1:
            finish(s - 2)
    if nz < 2:
        first_y(nz - 1)

    chunk = gin_buf.shape[2]

    def grad_step(i):
        cols = pl.ds(pl.multiple_of(i * tile, tile), tile)
        for e in range(exp_dev):
            found = dot(rows_buf[:, cols], gu_buf[e], 0, 0).astype(BF16)
            for c in range(tile // chunk):
                gin_buf[i * (tile // chunk) + c, e] = found[c * chunk : (c + 1) * chunk, :]

    def grad_out_step(i):
        cols = pl.ds(pl.multiple_of(i * tile, tile), tile)
        for e in range(exp_dev):
            found = dot(hid_buf[e, :, cols], cot_buf[...], 0, 0).astype(BF16)
            for c in range(width // chunk):
                gout_buf[c, e, cols, :] = found[:, c * chunk : (c + 1) * chunk]

    pl.loop(0, ff // tile)(grad_out_step)
    gout_copy = pltpu.make_async_copy(gout_buf, grads_out, grad_sem.at[0])
    gout_copy.start()
    if nz > 1:
        finish(nz - 2)
    pl.loop(0, width // tile)(grad_step)
    gin_copy = pltpu.make_async_copy(gin_buf, grads_in, grad_sem.at[1])
    gin_copy.start()
    finish(nz - 1)
    for h in range(2):
        gate_sum = gate_out[0, 0, h]
        for s in range(nz):
            for t in range(ny):
                if s or t:
                    gate_copy(s, t, h).wait_recv()
                    gate_sum += gate_in[s, t, h]
        d_gate[h] = gate_sum
    for copy in sent:
        copy.wait_send()
    for s in range(nz):
        for h in range(2):
            for t in range(ny):
                made_copy(s, t, h).wait()
                if s or t:
                    gate_copy(s, t, h).wait_send()
            for t in range(ny - 1):
                y_copy(s, t, h).wait_send()
            if s < nz - 1:
                z_copy(s, h).wait_send()
    gout_copy.wait()
    gin_copy.wait()


def experts_pass(own, named, router, cotangent, weight_in, weight_out, n_dp, n_expert, cid):
    nz, ny = grid_of(n_expert)
    tok_rows, width = own.shape
    exp_dev, ff, _ = weight_out.shape
    half, group = tok_rows // 2, tok_rows * n_expert
    experts = named.shape[1]
    whole, anywhere = pl.BlockSpec(memory_space=pltpu.VMEM), pl.BlockSpec(memory_space=pl.ANY)
    dma = pltpu.SemaphoreType.DMA
    ring = dma((nz, ny, 2))
    y_steps, y_mid, z_steps = max(ny - 1, 1), max(ny - 2, 1), max(nz - 1, 1)
    return pl.pallas_call(
        functools.partial(experts_kernel, nz, ny),
        out_shape=[
            jax.ShapeDtypeStruct((tok_rows, width), F32),
            jax.ShapeDtypeStruct((2, experts, half), F32),
            jax.ShapeDtypeStruct((group, width), BF16),
            jax.ShapeDtypeStruct((n_dp, exp_dev, width // n_dp, 2 * ff), BF16),
            jax.ShapeDtypeStruct((n_dp, exp_dev, ff, width // n_dp), BF16),
        ],
        in_specs=[whole, whole, whole, anywhere, anywhere, anywhere],
        out_specs=[whole, whole, anywhere, anywhere, anywhere],
        scratch_shapes=[
            pltpu.VMEM((group, width), BF16),
            pltpu.VMEM((group, width), BF16),
            pltpu.VMEM((exp_dev, width, 2 * ff), BF16),
            pltpu.VMEM((exp_dev, ff, width), BF16),
            pltpu.VMEM((exp_dev, group, ff), BF16),
            pltpu.VMEM((exp_dev, group, 2 * ff), BF16),
            pltpu.VMEM((group, width), BF16),
            pltpu.VMEM((group, width), BF16),
            pltpu.VMEM((n_dp, exp_dev, width // n_dp, 2 * ff), BF16),
            pltpu.VMEM((n_dp, exp_dev, ff, width // n_dp), BF16),
            pltpu.VMEM((nz, ny, 2, experts, half), F32),
            pltpu.VMEM((nz, ny, 2, experts, half), F32),
            pltpu.VMEM((nz, y_steps, 2, half, width), BF16),
            pltpu.VMEM((z_steps, 2, half, width), BF16),
            pltpu.VMEM((nz, y_mid, 2, half if ny > 2 else 16, width), BF16),
            pltpu.VMEM((z_steps, 2, half, width), BF16),
            dma((2,)), ring, ring, dma((2,)), ring, ring, ring, ring,
            dma((nz, y_steps, 2)), dma((nz, y_steps, 2)), dma((z_steps, 2)), dma((z_steps, 2)),
        ],
        compiler_params=pltpu.CompilerParams(
            collective_id=cid, has_side_effects=True, vmem_limit_bytes=60 << 20
        ),
        cost_estimate=pl.CostEstimate(
            flops=18 * exp_dev * group * width * ff,
            bytes_accessed=16 * group * width,
            transcendentals=exp_dev * group * ff,
        ),
        name="experts_pass",
    )(own, named, router, cotangent, weight_in, weight_out)


def gather(values, name, axis=0):
    return lax.all_gather(values, name, axis=axis, tiled=True)


def local(
    hidden_in, d_out, gain_attn, w_qkv, w_o, gain_moe, w_router, w_in, w_out,
    seq_lengths, assign, routes,
):
    tok_rows, width = hidden_in.shape
    exp_dev, _, ff_two = w_in.shape
    ff = ff_two // 2
    n_expert = lax.axis_size("expert")
    me = lax.axis_index("expert")
    experts = exp_dev * n_expert
    group_rows = tok_rows * n_expert
    q_per = HEADS // n_expert
    share = GROUPS // q_per
    q_cols = q_per * HEAD_DIM
    k_base = HEADS * HEAD_DIM
    v_base = k_base + KV_HEADS * HEAD_DIM
    cols = q_cols + 2 * HEAD_DIM

    n_dp = lax.axis_size("dp")
    wide = width // n_dp
    kv_head = (me * q_per) // GROUPS
    heads_part = jnp.concatenate(
        [
            lax.dynamic_slice_in_dim(w_qkv, me * q_cols, q_cols, 1),
            lax.dynamic_slice_in_dim(w_qkv, k_base + kv_head * HEAD_DIM, HEAD_DIM, 1),
            lax.dynamic_slice_in_dim(w_qkv, v_base + kv_head * HEAD_DIM, HEAD_DIM, 1),
        ],
        axis=1,
    )
    few = 2 + experts
    pack = jnp.concatenate(
        [gain_attn[None], gain_moe[None], w_router.T, jnp.zeros((-few % 16, wide), BF16)], axis=0
    )
    top = routes.shape[1]
    meta = jnp.concatenate(
        [assign, routes.T, jnp.zeros((-(1 + top) % 8, tok_rows), jnp.int32)], axis=0
    )
    meta = meta.reshape(meta.shape[0], 2, tok_rows // 2).transpose(1, 0, 2)
    qkv_full = gather(w_qkv, "dp")
    hidden_all, meta, w_heads, pack = first_gather(
        hidden_in, meta, heads_part, pack, n_dp, n_expert, 0
    )
    w_heads = w_heads.reshape(width, cols)
    pack = pack.transpose(1, 0, 2).reshape(-1, width)
    gain_one, gain_two = pack[0].astype(F32), pack[1].astype(F32)
    router_t = pack[2:few]
    position = meta[:, :, 0].reshape(group_rows)
    routes_all = meta[:, :, 1 : 1 + top]
    named = jnp.any(
        routes_all[:, :, :, None, :] == jnp.arange(experts, dtype=jnp.int32)[:, None], axis=2
    ).transpose(0, 1, 3, 2).reshape(group_rows, experts)
    stream_in = hidden_in.astype(F32)
    proj_full = gather(w_o, "dp")
    weight_in = gather(w_in, "dp", axis=1)
    weight_out = gather(w_out, "dp", axis=2)
    lengths = seq_lengths[0]
    order = jnp.arange(lengths.shape[0], dtype=jnp.int32)
    ends = jnp.sum(jnp.where(order[None, :] <= order[:, None], lengths[None, :], 0), axis=1)
    starts = ends - lengths
    seq_id = jnp.sum((position[None, :] >= ends[:, None]).astype(jnp.int32), axis=0)
    picks = seq_id[None, :] == jnp.arange(lengths.shape[0], dtype=jnp.int32)[:, None]
    start_of = jnp.sum(jnp.where(picks, starts[:, None], 0), axis=0)
    rot_pos = position - start_of
    half = HEAD_DIM // 2
    frequency = ROPE_BASE ** (-(jnp.arange(half).astype(F32) * (2.0 / HEAD_DIM)))
    angles = frequency[:, None] * rot_pos.astype(F32)[None, :]
    cosine, sine = jnp.cos(angles), jnp.sin(angles)
    low, high = start_of[None, :], position[None, :]
    key_pos = jnp.broadcast_to(position[:, None], (group_rows, low_tile(group_rows)))

    heads_out, lse, attended, d_out_all, normed_all, query, key, key_t, value = attend(
        low, high, key_pos, cosine, sine, gain_one[None], w_heads, hidden_all, d_out, q_per, 6
    )
    attended = attended.reshape(n_expert * q_cols, tok_rows)
    mid_stream = stream_in + dot(attended, proj_full, 0, 0)
    normed_two = rms_norm(mid_stream, gain_two).astype(BF16)

    d_back, d_gate, made, grads_in, grads_out = experts_pass(
        normed_two, named.astype(F32), router_t, d_out_all, weight_in, weight_out, n_dp, n_expert, 1
    )
    d_gate = d_gate.transpose(0, 2, 1).reshape(tok_rows, experts)
    own_named = jnp.any(
        routes[:, :, None] == jnp.arange(experts, dtype=jnp.int32)[None, None, :], axis=1
    )
    own_gates = jax.nn.softmax(
        jnp.where(own_named, dot(normed_two, router_t, 1, 1), -jnp.inf), axis=1
    )
    d_logits = (
        own_gates * (d_gate - jnp.sum(own_gates * d_gate, axis=1, keepdims=True))
    ).astype(BF16)
    grad_router = dot(d_logits, normed_two, 0, 0)
    d_normed_two = d_back + dot(d_logits, router_t)
    _, norm_two_back = jax.vjp(rms_norm, mid_stream, gain_two)
    d_mid_norm, grad_gain_two = norm_two_back(d_normed_two)
    d_mid = d_out.astype(F32) + d_mid_norm

    d_attn = d_mid.astype(BF16)
    d_attn, grads_in, grads_out, made = lax.optimization_barrier((d_attn, grads_in, grads_out, made))
    grad_w_in = lax.psum_scatter(grads_in, "dp", scatter_dimension=0, tiled=True)
    grad_w_out = lax.psum_scatter(grads_out, "dp", scatter_dimension=0, tiled=True)
    d_att = dot(proj_full, d_attn, 1, 1).astype(BF16).reshape(n_expert, q_cols, tok_rows)
    part_o = dot(attended, d_attn).astype(BF16).reshape(n_dp, wide, width)
    d_own, part_qkv, returned, sum_o = attend_back(
        low, high, key_pos, query, key, key_t, value, heads_out, lse,
        cosine, sine, made, part_o, d_att, normed_all, tok_rows, 4,
    )
    layer_out = (mid_stream + returned).astype(BF16)
    if share > 1:
        fan = lambda part: jnp.repeat(part.reshape(width, KV_HEADS, HEAD_DIM), share, axis=1).reshape(width, -1)
        qkv_full = jnp.concatenate(
            [qkv_full[:, :k_base], fan(qkv_full[:, k_base:v_base]), fan(qkv_full[:, v_base:])], axis=1
        )
    small = jnp.concatenate(
        [jnp.zeros((1, width), F32), grad_gain_two[None], grad_router, jnp.zeros((-few % 8, width), F32)], axis=0
    )
    small = small.reshape(-1, n_dp, wide).transpose(1, 0, 2)
    grad_w_qkv, grad_w_o, small, grad_w_in, grad_w_out, grad_in = finish_sums(
        part_qkv, sum_o, small, grad_w_in[0], grad_w_out[0],
        d_own, qkv_full, hidden_in, d_mid, gain_one[None], q_cols, n_expert, 5,
    )
    return (
        layer_out, grad_in, small[0], grad_w_qkv, grad_w_o, small[1], small[2:few].T,
        grad_w_in, grad_w_out,
    )


def solution(mesh):
    rows = P(("dp", "expert"), None)
    in_specs = (
        rows, rows, P("dp"), P("dp", None), P("dp", None), P("dp"), P("dp", None),
        P("expert", "dp", None), P("expert", None, "dp"), P("dp", None), P("dp", "expert"), rows,
    )
    out_specs = (
        rows, rows, P("dp"), P("dp", None), P("dp", None), P("dp"), P("dp", None),
        P("expert", "dp", None), P("expert", None, "dp"),
    )
    return jax.shard_map(local, mesh=mesh, in_specs=in_specs, out_specs=out_specs, check_vma=False)
```

```python
import functools

import jax
import jax.numpy as jnp
from jax import lax
from jax.experimental import pallas as pl
from jax.experimental.pallas import tpu as pltpu
from jax.sharding import PartitionSpec as P

HEADS = 16
KV_HEADS = 8
HEAD_DIM = 64
GROUPS = HEADS // KV_HEADS
EPSILON = 1e-06
ROPE_BASE = 10000.0
SCORE_SCALE = 0.015625
MASKED = -1e30
F32 = jnp.float32
BF16 = jnp.bfloat16
Q_TILE = 256
K_TILE = 256


MESH = pl.DeviceIdType.MESH
Z_SIZE = 4

def grid_of(n_expert):
    nz = Z_SIZE if n_expert % Z_SIZE == 0 else 1
    return nz, n_expert // nz

def places(nz, ny):
    me = lax.axis_index("expert")
    return me // ny, lax.rem(me, ny)

def device(z, y, nz, ny):
    return lax.rem(z + 2 * nz, nz) * ny + lax.rem(y + 2 * ny, ny)

def rms_norm(values, gain_vec):
    factor = lax.rsqrt(jnp.mean(values * values, axis=-1, keepdims=True) + EPSILON)
    return values * factor * gain_vec


def dot(left, right, left_dim=1, right_dim=0):
    return lax.dot_general(
        left, right, (((left_dim,), (right_dim,)), ((), ())), preferred_element_type=F32
    )


def rotate(values, cosine, sine):
    half = HEAD_DIM // 2
    one, two = values[:half], values[half:]
    return jnp.concatenate([one * cosine - two * sine, two * cosine + one * sine], axis=0)


def rotate_back(grads, cosine, sine):
    half = HEAD_DIM // 2
    one, two = grads[:half], grads[half:]
    return jnp.concatenate([one * cosine + two * sine, two * cosine - one * sine], axis=0)


def first_kernel(
    n_dp, nz, ny, rows, meta, heads, pack,
    rows_all, meta_all, heads_all, pack_all,
    send_sem, recv_sem, meta_send, meta_recv, dp_send, dp_recv, keep_sem,
):
    z, y = places(nz, ny)
    me, group = lax.axis_index("expert"), lax.axis_index("dp")
    count = rows.shape[0]
    half = count // 2
    barrier = pltpu.get_barrier_semaphore()
    near = [{"dp": lax.rem(group + k, n_dp)} for k in range(1, n_dp)]
    near += [{"expert": device(z + k, y, nz, ny)} for k in sorted({1, nz - 1} - {0})]
    near += [{"expert": device(z, y + k, nz, ny)} for k in sorted({1, ny - 1} - {0})]
    for other in near:
        pl.semaphore_signal(barrier, inc=1, device_id=other, device_id_type=MESH)
    pl.semaphore_wait(barrier, len(near))

    def origin(s, t, h):
        sign = -1 if h == 0 else 1
        return device(z + sign * s, y + sign * t, nz, ny)

    def copies(s, t, h, s2, t2):
        of = origin(s, t, h)
        mine = s == 0 and t == 0
        part = pl.ds(pl.multiple_of(of * count + h * half, half), half)
        step = 1 if h == 0 else -1
        to = device(z + step, y, nz, ny) if t2 == 0 else device(z, y + step, nz, ny)
        big = pltpu.make_async_remote_copy(
            src_ref=rows.at[pl.ds(h * half, half)] if mine else rows_all.at[part],
            dst_ref=rows_all.at[part],
            send_sem=send_sem.at[s2, t2, h], recv_sem=recv_sem.at[s2, t2, h],
            device_id={"expert": to}, device_id_type=MESH,
        )
        little = pltpu.make_async_remote_copy(
            src_ref=meta.at[h] if mine else meta_all.at[of, h], dst_ref=meta_all.at[of, h],
            send_sem=meta_send.at[s2, t2, h], recv_sem=meta_recv.at[s2, t2, h],
            device_id={"expert": to}, device_id_type=MESH,
        )
        return little, big

    def arrive(s, t, h):
        of = origin(s, t, h)
        part = pl.ds(pl.multiple_of(of * count + h * half, half), half)
        for place, sends, receives in (
            (meta_all.at[of, h], meta_send, meta_recv), (rows_all.at[part], send_sem, recv_sem)
        ):
            pltpu.make_async_remote_copy(
                src_ref=place, dst_ref=place, send_sem=sends.at[s, t, h], recv_sem=receives.at[s, t, h],
                device_id={"expert": device(z + 1, y, nz, ny)}, device_id_type=MESH,
            ).wait_recv()

    sent = []

    def start(*key):
        for copy in copies(*key):
            copy.start()
            sent.append(copy)

    for h in range(2):
        start(0, 0, h, 1, 0)
    if ny > 1:
        for h in range(2):
            start(0, 0, h, 0, 1)

    def across(k, a):
        source, target = ((heads, heads_all), (pack, pack_all))[a]
        return pltpu.make_async_remote_copy(
            src_ref=source, dst_ref=target.at[group],
            send_sem=dp_send.at[k - 1, a], recv_sem=dp_recv.at[k - 1, a],
            device_id={"dp": lax.rem(group + k, n_dp)}, device_id_type=MESH,
        )

    for k in range(1, n_dp):
        for a in range(2):
            across(k, a).start()
    keeps = [
        pltpu.make_async_copy(
            rows, rows_all.at[pl.ds(pl.multiple_of(me * count, count), count)], keep_sem.at[0]
        ),
        pltpu.make_async_copy(meta, meta_all.at[me], keep_sem.at[1]),
        pltpu.make_async_copy(heads, heads_all.at[group], keep_sem.at[2]),
        pltpu.make_async_copy(pack, pack_all.at[group], keep_sem.at[3]),
    ]
    for copy in keeps:
        copy.start()
    for s in range(1, nz):
        for h in range(2):
            arrive(s, 0, h)
            if s + 1 < nz:
                start(s, 0, h, s + 1, 0)
            if ny > 1:
                start(s, 0, h, s, 1)
    for t in range(1, ny):
        for s in range(nz):
            for h in range(2):
                arrive(s, t, h)
                if t + 1 < ny:
                    start(s, t, h, s, t + 1)
    for k in range(1, n_dp):
        for a, target in enumerate((heads_all, pack_all)):
            place = target.at[lax.rem(group + n_dp - k, n_dp)]
            pltpu.make_async_remote_copy(
                src_ref=place, dst_ref=place, send_sem=dp_send.at[k - 1, a], recv_sem=dp_recv.at[k - 1, a],
                device_id={"dp": lax.rem(group + k, n_dp)}, device_id_type=MESH,
            ).wait_recv()
    for copy in keeps:
        copy.wait()
    for copy in sent:
        copy.wait_send()
    for k in range(1, n_dp):
        for a in range(2):
            across(k, a).wait_send()


def first_gather(rows, meta, heads, pack, n_dp, n_expert, cid):
    nz, ny = grid_of(n_expert)
    anywhere = pl.BlockSpec(memory_space=pl.ANY)
    dma = pltpu.SemaphoreType.DMA
    ring, peers = dma((nz, ny, 2)), dma((max(n_dp - 1, 1), 2))
    return pl.pallas_call(
        functools.partial(first_kernel, n_dp, nz, ny),
        out_shape=[
            jax.ShapeDtypeStruct((rows.shape[0] * n_expert, rows.shape[1]), rows.dtype),
            jax.ShapeDtypeStruct((n_expert,) + meta.shape, meta.dtype),
            jax.ShapeDtypeStruct((n_dp,) + heads.shape, heads.dtype),
            jax.ShapeDtypeStruct((n_dp,) + pack.shape, pack.dtype),
        ],
        in_specs=[anywhere] * 4,
        out_specs=[anywhere] * 4,
        scratch_shapes=[ring, ring, ring, ring, peers, peers, dma((4,))],
        compiler_params=pltpu.CompilerParams(collective_id=cid, has_side_effects=True),
        name="first_gather",
    )(rows, meta, heads, pack)


def attend_kernel(
    nz, ny, low, high, key_pos, cos_tab, sin_tab, gain, head_weights, hidden, cotangent,
    out, lse, own_in, everyone, normed, query_all, key, key_t, value,
    score_buf, weight_buf, send_buf, rows_buf, value_t, query,
    own_send, own_recv, send_sem, recv_sem, keep_sem, load_sem,
):
    z, y = places(nz, ny)
    me = lax.axis_index("expert")
    n_expert = nz * ny
    heads, width, tile = query.shape
    q_cols = heads * width
    low_row, high_row = low[...], high[...]
    steps = key.shape[0] // K_TILE
    tok_rows = cotangent.shape[0]
    half_rows = tok_rows // 2
    per_tile = tile // tok_rows
    i = pl.program_id(0)
    count = key.shape[0] // tile

    def piece(s, t, h):
        sign = -1 if h == 0 else 1
        begin = device(z + sign * s, y + sign * t, nz, ny) * tok_rows + h * half_rows
        return pl.ds(pl.multiple_of(begin, half_rows), half_rows)

    def row_copy(s, t, h, s2, t2):
        mine = s == 0 and t == 0
        step = 1 if h == 0 else -1
        to = device(z + step, y, nz, ny) if t2 == 0 else device(z, y + step, nz, ny)
        return pltpu.make_async_remote_copy(
            src_ref=cotangent.at[pl.ds(h * half_rows, half_rows)] if mine else everyone.at[piece(s, t, h)],
            dst_ref=everyone.at[piece(s, t, h)],
            send_sem=send_sem.at[s2, t2, h], recv_sem=recv_sem.at[s2, t2, h],
            device_id={"expert": to}, device_id_type=MESH,
        )

    def arrive(s, t, h):
        place = everyone.at[piece(s, t, h)]
        pltpu.make_async_remote_copy(
            src_ref=place, dst_ref=place, send_sem=send_sem.at[s, t, h], recv_sem=recv_sem.at[s, t, h],
            device_id={"expert": device(z + 1, y, nz, ny)}, device_id_type=MESH,
        ).wait_recv()

    def forward(s):
        for h in range(2):
            arrive(s, 0, h)
            if s + 1 < nz:
                row_copy(s, 0, h, s + 1, 0).start()
            if ny > 1:
                row_copy(s, 0, h, s, 1).start()

    def own_copy(other, source):
        return pltpu.make_async_remote_copy(
            src_ref=send_buf.at[other], dst_ref=own_in.at[source],
            send_sem=own_send.at[other], recv_sem=own_recv.at[source],
            device_id={"expert": other}, device_id_type=MESH,
        )

    keep = pltpu.make_async_copy(
        cotangent, everyone.at[pl.ds(pl.multiple_of(me * tok_rows, tok_rows), tok_rows)], keep_sem.at[0]
    )

    whole_out = pltpu.make_async_copy(rows_buf, normed, keep_sem.at[2])

    def load(j):
        rows = pl.ds(pl.multiple_of(j * tile, tile), tile)
        return pltpu.make_async_copy(hidden.at[rows], rows_buf.at[rows], load_sem.at[j])

    @pl.when(i == 0)
    def _():
        barrier = pltpu.get_barrier_semaphore()
        for k in range(1, n_expert):
            pl.semaphore_signal(
                barrier, inc=1, device_id={"expert": lax.rem(me + k, n_expert)}, device_id_type=MESH
            )
        pl.semaphore_wait(barrier, n_expert - 1)
        for h in range(2):
            row_copy(0, 0, h, 1, 0).start()
        if ny > 1:
            for h in range(2):
                row_copy(0, 0, h, 0, 1).start()
        keep.start()
        for j in range(count):
            load(j).start()

        @pl.loop(0, count)
        def _(j):
            rows = pl.ds(pl.multiple_of(j * tile, tile), tile)
            load(j).wait()
            rows_buf[rows, :] = rms_norm(rows_buf[rows, :].astype(F32), gain[...]).astype(BF16)
            cosine, sine = cos_tab[:, rows], sin_tab[:, rows]
            projected = dot(head_weights[...], rows_buf[rows, :], 0, 1)
            for head in range(heads):
                part = projected[head * width : (head + 1) * width]
                query_all[head, :, rows] = rotate(part, cosine, sine).astype(BF16) * jnp.asarray(
                    SCORE_SCALE, BF16
                )
            turned = rotate(projected[q_cols : q_cols + width], cosine, sine).astype(BF16)
            key_t[:, rows] = turned
            key[rows, :] = turned.T
            plain = projected[q_cols + width :].astype(BF16)
            value_t[:, rows] = plain
            value[rows, :] = plain.T

        whole_out.start()
        if nz > 1:
            forward(1)

    early = [s for s in range(2, nz) if 3 * (s - 1) < count]
    for s in early:
        pl.when(i == 3 * (s - 1))(functools.partial(forward, s))
    query[...] = query_all[:, :, pl.ds(pl.multiple_of(i * tile, tile), tile)]

    def score_step(step, maxima):
        rows = pl.ds(pl.multiple_of(step * K_TILE, K_TILE), K_TILE)
        at = key_pos[rows, :]
        allowed = (at >= low_row) & (at <= high_row)
        found = []
        for head in range(heads):
            scores = jnp.dot(key[rows, :], query[head], preferred_element_type=F32)
            scores = jnp.where(allowed, scores, MASKED)
            score_buf[head, rows, :] = scores
            found.append(jnp.maximum(maxima[head], jnp.max(scores, axis=0, keepdims=True)))
        return tuple(found)

    begin = tuple(jnp.full(low_row.shape, MASKED, F32) for _ in range(heads))
    maxima = lax.fori_loop(0, steps, score_step, begin)

    def weight_step(step, totals):
        rows = pl.ds(pl.multiple_of(step * K_TILE, K_TILE), K_TILE)
        found = []
        for head in range(heads):
            weights = jnp.exp(score_buf[head, rows, :] - maxima[head])
            weight_buf[head, rows, :] = weights.astype(BF16)
            found.append(totals[head] + jnp.sum(weights, axis=0, keepdims=True))
        return tuple(found)

    begin = tuple(jnp.zeros(low_row.shape, F32) for _ in range(heads))
    totals = lax.fori_loop(0, steps, weight_step, begin)
    for head in range(heads):
        summed = jnp.dot(value_t[...], weight_buf[head], preferred_element_type=F32)
        attended = (summed / totals[head]).astype(BF16)
        out[head] = attended
        lse[head] = maxima[head] + jnp.log(totals[head])
        for j in range(per_tile):
            send_buf[i * per_tile + j, head * width : (head + 1) * width, :] = attended[
                :, j * tok_rows : (j + 1) * tok_rows
            ]
    for j in range(per_tile):
        other = i * per_tile + j

        @pl.when(other != me)
        def _():
            own_copy(other, me).start()

    @pl.when(i == count - 1)
    def _():
        mine = pltpu.make_async_copy(send_buf.at[me], own_in.at[me], keep_sem.at[1])
        mine.start()
        for s in range(2, nz):
            if s not in early:
                forward(s)
        for t in range(1, ny):
            for s in range(nz):
                for h in range(2):
                    arrive(s, t, h)
                    if t + 1 < ny:
                        row_copy(s, t, h, s, t + 1).start()
        for k in range(1, n_expert):
            other = lax.rem(me + k, n_expert)
            own_copy(other, other).wait_recv()
            own_copy(other, other).wait_send()
        for s in range(nz):
            for t in range(ny):
                for h in range(2):
                    if t > 0:
                        row_copy(s, t - 1, h, s, t).wait_send()
                    elif s > 0:
                        row_copy(s - 1, 0, h, s, 0).wait_send()
        keep.wait()
        mine.wait()
        whole_out.wait()


def attend(low, high, key_pos, cosine, sine, gain, head_weights, hidden, cotangent, heads, cid):
    tok_rows, model = cotangent.shape
    rows = hidden.shape[0]
    width = HEAD_DIM
    n_expert = rows // tok_rows
    nz, ny = grid_of(n_expert)
    tile = low_tile(rows)
    whole = lambda i: (0, 0)
    lane = lambda i: (0, i)
    anywhere = pl.BlockSpec(memory_space=pl.ANY)
    dma = pltpu.SemaphoreType.DMA
    tables = pl.BlockSpec((width // 2, rows), whole)
    return pl.pallas_call(
        functools.partial(attend_kernel, nz, ny),
        grid=(rows // tile,),
        in_specs=[
            pl.BlockSpec((1, tile), lane),
            pl.BlockSpec((1, tile), lane),
            pl.BlockSpec((rows, tile), whole),
            tables, tables,
            pl.BlockSpec((1, model), whole),
            pl.BlockSpec(head_weights.shape, whole),
            anywhere, anywhere,
        ],
        out_specs=[
            pl.BlockSpec((heads, width, tile), lambda i: (0, 0, i)),
            pl.BlockSpec((heads, 1, tile), lambda i: (0, 0, i)),
            anywhere, anywhere, anywhere,
            pl.BlockSpec((heads, width, rows), lambda i: (0, 0, 0)),
            pl.BlockSpec((rows, width), whole),
            pl.BlockSpec((width, rows), whole),
            pl.BlockSpec((rows, width), whole),
        ],
        out_shape=[
            jax.ShapeDtypeStruct((heads, width, rows), BF16),
            jax.ShapeDtypeStruct((heads, 1, rows), F32),
            jax.ShapeDtypeStruct((n_expert, heads * width, tok_rows), BF16),
            jax.ShapeDtypeStruct((rows, model), BF16),
            jax.ShapeDtypeStruct((rows, model), BF16),
            jax.ShapeDtypeStruct((heads, width, rows), BF16),
            jax.ShapeDtypeStruct((rows, width), BF16),
            jax.ShapeDtypeStruct((width, rows), BF16),
            jax.ShapeDtypeStruct((rows, width), BF16),
        ],
        scratch_shapes=[
            pltpu.VMEM((heads, rows, tile), F32),
            pltpu.VMEM((heads, rows, tile), BF16),
            pltpu.VMEM((n_expert, heads * width, tok_rows), BF16),
            pltpu.VMEM((rows, model), BF16),
            pltpu.VMEM((width, rows), BF16),
            pltpu.VMEM((heads, width, tile), BF16),
            dma((n_expert,)), dma((n_expert,)), dma((nz, ny, 2)), dma((nz, ny, 2)), dma((3,)),
            dma((rows // tile,)),
        ],
        compiler_params=pltpu.CompilerParams(
            collective_id=cid, has_side_effects=True, vmem_limit_bytes=56 << 20
        ),
        cost_estimate=pl.CostEstimate(
            flops=4 * heads * rows * rows * 256,
            bytes_accessed=8 * rows * 256,
            transcendentals=heads * rows * rows,
        ),
        name="attend",
    )(low, high, key_pos, cosine, sine, gain, head_weights, hidden, cotangent)


def low_tile(rows):
    return min(Q_TILE, rows)


def attend_back_kernel(
    nz, ny,
    low, high, key_pos, query, key, key_t, value, attended, lse,
    cos_tab, sin_tab, made, out_part, d_att,
    own_in, proj, summed, out_sum,
    d_key, d_value, query_n, grad_n, grad, delta, grad_in, out_in, out_own, pair_in, pair_sum, score_buf, send_buf, part_buf, from_y, from_z, to_y, to_z,
    part_sem, own_send, own_recv, tail_send, tail_recv, keep_sem, mine_sem,
    send_y, recv_y, send_z, recv_z, dp_send, dp_recv, pair_send, pair_recv, pair_load, grad_send, grad_recv,
):
    z, y = places(nz, ny)
    me, group = lax.axis_index("expert"), lax.axis_index("dp")
    n_expert, n_dp = nz * ny, out_part.shape[0]
    heads, width, tile = query.shape
    low_row, high_row = low[...], high[...]
    steps = key.shape[0] // K_TILE
    tok_rows = summed.shape[0]
    half_rows = tok_rows // 2
    per_tile = tile // tok_rows
    i = pl.program_id(0)
    count = key.shape[0] // tile
    q_cols = heads * width

    def piece(r, t, h):
        sign = -1 if h == 0 else 1
        start = device(z + sign * (r + 1), y + sign * (t + 1), nz, ny) * tok_rows + h * half_rows
        return pl.ds(pl.multiple_of(start, half_rows), half_rows)

    def near(along_z, h):
        step = 1 if h == 0 else -1
        to = device(z + step, y, nz, ny) if along_z else device(z, y + step, nz, ny)
        return {"expert": to}

    def part_copy(r, t, h):
        return pltpu.make_async_copy(
            made.at[piece(r, t, h)], part_buf.at[r, t, h], part_sem.at[r, t, h]
        )

    def y_copy(r, t, h):
        source = made.at[piece(r, 0, h)] if t == 0 else to_y.at[r, t - 1, h]
        return pltpu.make_async_remote_copy(
            src_ref=source, dst_ref=from_y.at[r, t, h],
            send_sem=send_y.at[r, t, h], recv_sem=recv_y.at[r, t, h],
            device_id=near(False, h), device_id_type=MESH,
        )

    def z_copy(r, h):
        return pltpu.make_async_remote_copy(
            src_ref=to_z.at[r, h], dst_ref=from_z.at[r, h],
            send_sem=send_z.at[r, h], recv_sem=recv_z.at[r, h],
            device_id=near(True, h), device_id_type=MESH,
        )

    def finish(r):
        for t in range(1, ny - 1):
            for h in range(2):
                y_copy(r, t - 1, h).wait_recv()
                part_copy(r, t, h).wait()
                to_y[r, t - 1, h] = (
                    part_buf[r, t, h].astype(F32) + from_y[r, t - 1, h].astype(F32)
                ).astype(BF16)
                y_copy(r, t, h).start()
        for h in range(2):
            part_copy(r, ny - 1, h).wait()
            total = part_buf[r, ny - 1, h].astype(F32)
            if ny > 1:
                y_copy(r, ny - 2, h).wait_recv()
                total += from_y[r, ny - 2, h].astype(F32)
            if r > 0:
                z_copy(r - 1, h).wait_recv()
                total += from_z[r - 1, h].astype(F32)
            if r < nz - 1:
                to_z[r, h] = total.astype(BF16)
                z_copy(r, h).start()
            else:
                summed[h * half_rows : (h + 1) * half_rows, :] = total

    pairs = n_dp // 2
    chip, core = group // 2, lax.rem(group, 2)

    def pair_copy(j):
        return pltpu.make_async_remote_copy(
            src_ref=out_part.at[2 * j + 1 - core], dst_ref=pair_in.at[j],
            send_sem=pair_send.at[j], recv_sem=pair_recv.at[j],
            device_id={"dp": group + 1 - 2 * core}, device_id_type=MESH,
        )

    def own_load(j):
        return pltpu.make_async_copy(out_part.at[2 * j + core], out_own.at[j], pair_load.at[j])

    def across(k):
        other = lax.rem(chip + k, pairs)
        return pltpu.make_async_remote_copy(
            src_ref=pair_sum.at[other], dst_ref=out_in.at[k - 1],
            send_sem=dp_send.at[k - 1], recv_sem=dp_recv.at[k - 1],
            device_id={"dp": 2 * other + core}, device_id_type=MESH,
        )

    def over_chips():
        for j in range(pairs):
            pair_copy(j).wait_recv()
            own_load(j).wait()
            pair_sum[j] = (out_own[j].astype(F32) + pair_in[j].astype(F32)).astype(BF16)
        for k in range(1, pairs):
            across(k).start()

    spans = (
        (0, q_cols, 0),
        (q_cols, width, n_expert * q_cols),
        (q_cols + width, width, n_expert * (q_cols + width)),
    )

    def own_rows(a, source):
        _, rows, base = spans[a]
        return own_in.at[pl.ds(pl.multiple_of(base + source * rows, rows), rows)]

    def own_copy(a, other, source):
        begin, rows, _ = spans[a]
        return pltpu.make_async_remote_copy(
            src_ref=send_buf.at[other, pl.ds(begin, rows)], dst_ref=own_rows(a, source),
            send_sem=(own_send if a == 0 else tail_send.at[a - 1]).at[other],
            recv_sem=(own_recv if a == 0 else tail_recv.at[a - 1]).at[source],
            device_id={"expert": other}, device_id_type=MESH,
        )

    def grad_copy(other, source):
        return pltpu.make_async_remote_copy(
            src_ref=d_att.at[other], dst_ref=grad_in.at[source],
            send_sem=grad_send.at[other], recv_sem=grad_recv.at[source],
            device_id={"expert": other}, device_id_type=MESH,
        )

    @pl.when(i == 0)
    def _():
        barrier = pltpu.get_barrier_semaphore()
        for k in range(1, n_expert):
            pl.semaphore_signal(
                barrier, inc=1, device_id={"expert": lax.rem(me + k, n_expert)}, device_id_type=MESH
            )
        for k in range(1, n_dp):
            pl.semaphore_signal(
                barrier, inc=1, device_id={"dp": lax.rem(group + k, n_dp)}, device_id_type=MESH
            )
        pl.semaphore_wait(barrier, n_expert + n_dp - 2)
        for k in range(1, n_expert):
            grad_copy(lax.rem(me + k, n_expert), me).start()
        for j in range(pairs):
            pair_copy(j).start()
            own_load(j).start()
        grad_in[me] = d_att[me]
        for r in range(nz):
            for h in range(2):
                if ny > 1:
                    y_copy(r, 0, h).start()
                for t in range(1, ny - 1):
                    part_copy(r, t, h).start()
                part_copy(r, ny - 1, h).start()
        d_key[...] = jnp.zeros_like(d_key)
        d_value[...] = jnp.zeros_like(d_value)

    pl.when(i == 1)(over_chips)
    for r in range(nz - 1):
        pl.when(i == (r + 1) * count // nz)(functools.partial(finish, r))

    for j in range(per_tile):
        source = i * per_tile + j

        @pl.when(source != me)
        def _():
            grad_copy(source, source).wait_recv()

        for head in range(heads):
            grad[head, :, j * tok_rows : (j + 1) * tok_rows] = grad_in[
                source, head * width : (head + 1) * width, :
            ]
    for head in range(heads):
        query_n[head] = query[head].T
        grad_n[head] = grad[head].T
        delta[head] = jnp.sum(
            grad[head].astype(F32) * attended[head].astype(F32), axis=0, keepdims=True
        )

    @pl.loop(0, steps)
    def _(step):
        rows = pl.ds(pl.multiple_of(step * K_TILE, K_TILE), K_TILE)
        at = key_pos[rows, :]
        allowed = (at >= low_row) & (at <= high_row)
        key_sum, value_sum = d_key[rows, :], d_value[rows, :]
        for head in range(heads):
            scores = jnp.dot(key[rows, :], query[head], preferred_element_type=F32)
            weights = jnp.exp(jnp.where(allowed, scores - lse[head], MASKED))
            d_soft = jnp.dot(value[rows, :], grad[head], preferred_element_type=F32)
            d_scores = (weights * (d_soft - delta[head])).astype(BF16)
            score_buf[head, rows, :] = d_scores
            key_sum += jnp.dot(d_scores, query_n[head], preferred_element_type=F32)
            value_sum += jnp.dot(weights.astype(BF16), grad_n[head], preferred_element_type=F32)
        d_key[rows, :] = key_sum
        d_value[rows, :] = value_sum

    lanes = pl.ds(pl.multiple_of(i * tile, tile), tile)
    for head in range(heads):
        d_query = jnp.dot(key_t[...], score_buf[head], preferred_element_type=F32) * SCORE_SCALE
        turned = rotate_back(d_query, cos_tab[:, lanes], sin_tab[:, lanes]).astype(BF16)
        for j in range(per_tile):
            send_buf[i * per_tile + j, head * width : (head + 1) * width, :] = turned[
                :, j * tok_rows : (j + 1) * tok_rows
            ]
    for j in range(per_tile):
        other = i * per_tile + j

        @pl.when(other != me)
        def _():
            own_copy(0, other, me).start()

    @pl.when(i == count - 1)
    def _():
        for other in range(n_expert):
            rows = pl.ds(other * tok_rows, tok_rows)
            turned = rotate_back(d_key[rows, :].T, cos_tab[:, rows], sin_tab[:, rows])
            send_buf[other, q_cols : q_cols + width, :] = turned.astype(BF16)
            send_buf[other, q_cols + width :, :] = d_value[rows, :].T.astype(BF16)

            @pl.when(other != me)
            def _():
                own_copy(1, other, me).start()
                own_copy(2, other, me).start()

        keep = pltpu.make_async_copy(send_buf, proj, keep_sem.at[0])
        keep.start()
        mine = [
            pltpu.make_async_copy(
                send_buf.at[me, pl.ds(begin, rows)], own_rows(a, me), mine_sem.at[a]
            )
            for a, (begin, rows, _) in enumerate(spans)
        ]
        for copy in mine:
            copy.start()
        finish(nz - 1)
        for k in range(1, pairs):
            across(k).wait_recv()
        few = out_sum.shape[2]
        for m in range(n_expert):
            cols = slice(m * few, (m + 1) * few)
            out_total = pair_sum[chip, :, cols].astype(F32)
            for k in range(1, pairs):
                out_total += out_in[k - 1, :, cols].astype(F32)
            out_sum[m] = out_total.astype(BF16)
        for k in range(1, pairs):
            across(k).wait_send()
        for j in range(pairs):
            pair_copy(j).wait_send()
        for k in range(1, n_expert):
            other = lax.rem(me + k, n_expert)
            for a in range(3):
                own_copy(a, other, other).wait_recv()
                own_copy(a, other, other).wait_send()
            grad_copy(other, other).wait_send()
        for r in range(nz):
            for h in range(2):
                for t in range(ny - 1):
                    y_copy(r, t, h).wait_send()
                if r < nz - 1:
                    z_copy(r, h).wait_send()
        keep.wait()
        for copy in mine:
            copy.wait()


def attend_back(
    low, high, key_pos, query, key, key_t, value, attended, lse,
    cosine, sine, made, out_part, d_att, tok_rows, cid,
):
    heads, width, rows = query.shape
    n_expert = rows // tok_rows
    nz, ny = grid_of(n_expert)
    cols = (heads + 2) * width
    half_rows, model = tok_rows // 2, made.shape[1]
    tile = low_tile(rows)
    whole = lambda i: (0, 0)
    lane = lambda i: (0, i)
    wide = pl.BlockSpec((heads, width, tile), lambda i: (0, 0, i))
    row = pl.BlockSpec((heads, 1, tile), lambda i: (0, 0, i))
    keys = pl.BlockSpec((rows, width), whole)
    anywhere = pl.BlockSpec(memory_space=pl.ANY)
    dma = pltpu.SemaphoreType.DMA
    y_steps, y_mid, z_steps = max(ny - 1, 1), max(ny - 2, 1), max(nz - 1, 1)
    pairs = out_part.shape[0] // 2
    peers = max(pairs - 1, 1)
    out_tiles = (n_expert, out_part.shape[1], out_part.shape[2] // n_expert)
    return pl.pallas_call(
        functools.partial(attend_back_kernel, nz, ny),
        grid=(rows // tile,),
        in_specs=[
            pl.BlockSpec((1, tile), lane),
            pl.BlockSpec((1, tile), lane),
            pl.BlockSpec((rows, tile), whole),
            wide, keys, pl.BlockSpec((width, rows), whole), keys, wide, row,
            pl.BlockSpec((width // 2, rows), whole), pl.BlockSpec((width // 2, rows), whole),
            anywhere, anywhere, pl.BlockSpec(d_att.shape, lambda i: (0, 0, 0)),
        ],
        out_specs=[
            anywhere, anywhere, pl.BlockSpec((tok_rows, model), whole),
            pl.BlockSpec(out_tiles, lambda i: (0, 0, 0)),
        ],
        out_shape=[
            jax.ShapeDtypeStruct((n_expert * cols, tok_rows), BF16),
            jax.ShapeDtypeStruct((n_expert, cols, tok_rows), BF16),
            jax.ShapeDtypeStruct((tok_rows, model), F32),
            jax.ShapeDtypeStruct(out_tiles, BF16),
        ],
        scratch_shapes=[
            pltpu.VMEM((rows, width), F32),
            pltpu.VMEM((rows, width), F32),
            pltpu.VMEM((heads, tile, width), BF16),
            pltpu.VMEM((heads, tile, width), BF16),
            pltpu.VMEM((heads, width, tile), BF16),
            pltpu.VMEM((heads, 1, tile), F32),
            pltpu.VMEM((n_expert, heads * width, tok_rows), BF16),
            pltpu.VMEM((peers,) + out_part.shape[1:], BF16),
            pltpu.VMEM((pairs,) + out_part.shape[1:], BF16),
            pltpu.VMEM((pairs,) + out_part.shape[1:], BF16),
            pltpu.VMEM((pairs,) + out_part.shape[1:], BF16),
            pltpu.VMEM((heads, rows, tile), BF16),
            pltpu.VMEM((n_expert, cols, tok_rows), BF16),
            pltpu.VMEM((nz, ny, 2, half_rows, model), BF16),
            pltpu.VMEM((nz, y_steps, 2, half_rows, model), BF16),
            pltpu.VMEM((z_steps, 2, half_rows, model), BF16),
            pltpu.VMEM((nz, y_mid, 2, half_rows if ny > 2 else 16, model), BF16),
            pltpu.VMEM((z_steps, 2, half_rows, model), BF16),
            dma((nz, ny, 2)), dma((n_expert,)), dma((n_expert,)), dma((2, n_expert)), dma((2, n_expert)), dma((3,)), dma((3,)),
            dma((nz, y_steps, 2)), dma((nz, y_steps, 2)), dma((z_steps, 2)), dma((z_steps, 2)),
            dma((peers,)), dma((peers,)), dma((pairs,)), dma((pairs,)), dma((pairs,)), dma((n_expert,)), dma((n_expert,)),
        ],
        compiler_params=pltpu.CompilerParams(
            collective_id=cid, has_side_effects=True, vmem_limit_bytes=56 << 20
        ),
        cost_estimate=pl.CostEstimate(
            flops=10 * heads * rows * rows * 256,
            bytes_accessed=8 * rows * 256,
            transcendentals=heads * rows * rows,
        ),
        name="attend_back",
    )(low, high, key_pos, query, key, key_t, value, attended, lse, cosine, sine, made, out_part, d_att)


def finish_kernel(
    n_dp, nz, ny, q_cols, qkv, proj, small, into, out_of,
    qkv_rows, proj_rows, small_sum, into_wide, out_of_wide,
    qkv_in, small_in, proj_in, own_qkv, own_proj, own_small, qkv_all, proj_all, small_all,
    dp_send, dp_recv, ring_send, ring_recv, part_send, part_recv, keep_sem,
):
    z, y = places(nz, ny)
    me, group = lax.axis_index("expert"), lax.axis_index("dp")
    n_expert = nz * ny
    barrier = pltpu.get_barrier_semaphore()
    near = [{"dp": lax.rem(group + k, n_dp)} for k in range(1, n_dp)]
    near += [{"expert": lax.rem(me + k, n_expert)} for k in range(1, n_expert)]
    for other in near:
        pl.semaphore_signal(barrier, inc=1, device_id=other, device_id_type=MESH)
    pl.semaphore_wait(barrier, len(near))

    arrays = {0: (qkv, qkv_in, own_qkv), 2: (small, small_in, own_small)}

    def across(k, a):
        source, target, _ = arrays[a]
        other = lax.rem(group + k, n_dp)
        return pltpu.make_async_remote_copy(
            src_ref=source.at[other], dst_ref=target.at[k - 1],
            send_sem=dp_send.at[k - 1, a], recv_sem=dp_recv.at[k - 1, a],
            device_id={"dp": other}, device_id_type=MESH,
        )

    rings = ((own_qkv, qkv_all), (own_proj, proj_all), (own_small, small_all))

    def origin(s, t, h):
        sign = -1 if h == 0 else 1
        return device(z + sign * s, y + sign * t, nz, ny)

    def ring_copy(s, t, h, s2, t2, a):
        own, everyone = rings[a]
        of = origin(s, t, h)
        rows = own.shape[0] // 2 if a < 2 else own.shape[0]
        part = pl.ds(h * rows, rows)
        source = own.at[part] if s == 0 and t == 0 else everyone.at[of, part]
        step = 1 if h == 0 else -1
        to = device(z + step, y, nz, ny) if t2 == 0 else device(z, y + step, nz, ny)
        return pltpu.make_async_remote_copy(
            src_ref=source, dst_ref=everyone.at[of, part],
            send_sem=ring_send.at[s2, t2, h, a], recv_sem=ring_recv.at[s2, t2, h, a],
            device_id={"expert": to}, device_id_type=MESH,
        )

    def arrive(s, t, h, a):
        own, everyone = rings[a]
        rows = own.shape[0] // 2 if a < 2 else own.shape[0]
        place = everyone.at[origin(s, t, h), pl.ds(h * rows, rows)]
        pltpu.make_async_remote_copy(
            src_ref=place, dst_ref=place,
            send_sem=ring_send.at[s, t, h, a], recv_sem=ring_recv.at[s, t, h, a],
            device_id={"expert": device(z + 1, y, nz, ny)}, device_id_type=MESH,
        ).wait_recv()

    sent, keeps = [], []

    def start(*key):
        copy = ring_copy(*key)
        copy.start()
        sent.append(copy)

    def begin(moves):
        for a in sorted({a for _, a in moves}):
            own, everyone = rings[a]
            keeps.append(pltpu.make_async_copy(own, everyone.at[me], keep_sem.at[a]))
            keeps[-1].start()
        for h, a in moves:
            if nz > 1:
                start(0, 0, h, 1, 0, a)
            if ny > 1:
                start(0, 0, h, 0, 1, a)

    def along_z(moves):
        for s in range(1, nz):
            for h, a in moves:
                arrive(s, 0, h, a)
                if s + 1 < nz:
                    start(s, 0, h, s + 1, 0, a)
                if ny > 1:
                    start(s, 0, h, s, 1, a)

    def along_y(moves):
        for t in range(1, ny):
            for s in range(nz):
                for h, a in moves:
                    arrive(s, t, h, a)
                    if t + 1 < ny:
                        start(s, t, h, s, t + 1, a)

    def part_copy(k):
        other = lax.rem(me + k, n_expert)
        return pltpu.make_async_remote_copy(
            src_ref=proj.at[other], dst_ref=proj_in.at[k - 1],
            send_sem=part_send.at[k - 1], recv_sem=part_recv.at[k - 1],
            device_id={"expert": other}, device_id_type=MESH,
        )

    first, second = [(0, 0), (1, 0), (0, 2)], [(0, 1), (1, 1)]
    for k in range(1, n_dp):
        for a in arrays:
            across(k, a).start()
    for k in range(1, n_expert):
        part_copy(k).start()
    for e in range(into.shape[0]):
        into_wide[e] = into[e].astype(F32)
        out_of_wide[e] = out_of[e].astype(F32)
    for a, (source, target, own) in arrays.items():
        total = source[group].astype(F32)
        for k in range(1, n_dp):
            across(k, a).wait_recv()
            total += target[k - 1].astype(F32)
        own[...] = total.astype(own.dtype)
    begin(first)
    total = proj[me].astype(F32)
    for k in range(1, n_expert):
        part_copy(k).wait_recv()
        total += proj_in[k - 1].astype(F32)
    own_proj[...] = total.astype(BF16)
    begin(second)
    along_z(first + second)
    along_y(first + second)
    for copy in keeps:
        copy.wait()
    total = small_all[0]
    for other in range(1, n_expert):
        total += small_all[other]
    small_sum[...] = total
    alike = max(n_expert // KV_HEADS, 1)
    pieces = [qkv_all[m, :, :q_cols].astype(F32) for m in range(n_expert)]
    for first in (q_cols, q_cols + HEAD_DIM):
        for head in range(KV_HEADS):
            total = qkv_all[head * alike, :, first : first + HEAD_DIM].astype(F32)
            for more in range(1, alike):
                total += qkv_all[head * alike + more, :, first : first + HEAD_DIM].astype(F32)
            pieces.append(total)
    outs = [proj_all[m].astype(F32) for m in range(n_expert)]
    for target, pieces in ((qkv_rows, pieces), (proj_rows, outs)):
        lay(target, pieces)
    for copy in sent:
        copy.wait_send()
    for k in range(1, n_expert):
        part_copy(k).wait_send()
    for k in range(1, n_dp):
        for a in arrays:
            across(k, a).wait_send()


def lay(target, pieces):
    at = 0
    while pieces:
        block = [pieces.pop(0)]
        if block[0].shape[1] % 128:
            block.append(pieces.pop(0))
        joined = jnp.concatenate(block, axis=1) if len(block) > 1 else block[0]
        target[:, at : at + joined.shape[1]] = joined
        at += joined.shape[1]


def finish_sums(qkv, proj, small, into, out_of, q_cols, n_expert, cid):
    nz, ny = grid_of(n_expert)
    n_dp = qkv.shape[0]
    whole = pl.BlockSpec(memory_space=pltpu.VMEM)
    dma = pltpu.SemaphoreType.DMA
    peers = max(n_dp - 1, 1)
    return pl.pallas_call(
        functools.partial(finish_kernel, n_dp, nz, ny, q_cols),
        out_shape=[
            jax.ShapeDtypeStruct((qkv.shape[1], (HEADS + 2 * KV_HEADS) * HEAD_DIM), F32),
            jax.ShapeDtypeStruct((proj.shape[1], n_expert * proj.shape[2]), F32),
            jax.ShapeDtypeStruct(small.shape[1:], F32),
            jax.ShapeDtypeStruct(into.shape, F32),
            jax.ShapeDtypeStruct(out_of.shape, F32),
        ],
        in_specs=[whole] * 5,
        out_specs=[whole] * 5,
        scratch_shapes=[
            pltpu.VMEM((peers,) + qkv.shape[1:], BF16),
            pltpu.VMEM((peers,) + small.shape[1:], F32),
            pltpu.VMEM((n_expert - 1,) + proj.shape[1:], BF16),
            pltpu.VMEM(qkv.shape[1:], BF16),
            pltpu.VMEM(proj.shape[1:], BF16),
            pltpu.VMEM(small.shape[1:], F32),
            pltpu.VMEM((n_expert,) + qkv.shape[1:], BF16),
            pltpu.VMEM(proj.shape, BF16),
            pltpu.VMEM((n_expert,) + small.shape[1:], F32),
            dma((peers, 3)), dma((peers, 3)), dma((nz, ny, 2, 3)), dma((nz, ny, 2, 3)),
            dma((n_expert - 1,)), dma((n_expert - 1,)), dma((3,)),
        ],
        compiler_params=pltpu.CompilerParams(
            collective_id=cid, has_side_effects=True, vmem_limit_bytes=40 << 20
        ),
        name="finish_sums",
    )(qkv, proj, small, into, out_of)


def experts_kernel(
    nz, ny, own, named, router, cotangent, weight_in, weight_out,
    back, d_gate, made, grads_in, grads_out,
    rows_buf, cot_buf, in_buf, out_buf, hid_buf, gu_buf, part_buf, made_buf, gin_buf, gout_buf,
    gate_out, gate_in, from_y, from_z, to_y, to_z,
    load_sem, cot_sem, made_sem, grad_sem, send_sem, recv_sem, gate_send, gate_recv,
    send_y, recv_y, send_z, recv_z,
):
    z, y = places(nz, ny)
    me = lax.axis_index("expert")
    n_expert = nz * ny
    tok_rows, width = own.shape
    half = tok_rows // 2
    step_rows = ny * tok_rows
    exp_dev, ff, _ = out_buf.shape
    experts = named.shape[1]

    barrier = pltpu.get_barrier_semaphore()
    for k in range(1, n_expert):
        pl.semaphore_signal(
            barrier, inc=1, device_id={"expert": lax.rem(me + k, n_expert)}, device_id_type=MESH
        )
    pl.semaphore_wait(barrier, n_expert - 1)

    def owner(s, t, h):
        sign = -1 if h == 0 else 1
        return device(z + sign * s, y + sign * t, nz, ny)

    def piece(s, t, h):
        return pl.ds(pl.multiple_of(owner(s, t, h) * tok_rows + h * half, half), half)

    def slot(s, t, h):
        return pl.ds(((s * ny + t) * 2 + h) * half, half)

    def near(along_z, h):
        step = 1 if h == 0 else -1
        to = device(z + step, y, nz, ny) if along_z else device(z, y + step, nz, ny)
        return {"expert": to}

    def row_copy(s, t, h, s2, t2):
        source = own.at[pl.ds(h * half, half)] if s == 0 and t == 0 else rows_buf.at[slot(s, t, h)]
        return pltpu.make_async_remote_copy(
            src_ref=source, dst_ref=rows_buf.at[slot(s2, t2, h)],
            send_sem=send_sem.at[s2, t2, h], recv_sem=recv_sem.at[s2, t2, h],
            device_id=near(t2 == 0, h), device_id_type=MESH,
        )

    def arrive(s, t, h):
        if t == 0:
            row_copy(s - 1, 0, h, s, 0).wait_recv()
        else:
            row_copy(s, t - 1, h, s, t).wait_recv()

    sent = []

    def start(*key):
        copy = row_copy(*key)
        copy.start()
        sent.append(copy)

    for h in range(2):
        start(0, 0, h, 1, 0)
    if ny > 1:
        for h in range(2):
            start(0, 0, h, 0, 1)
    loads = [
        pltpu.make_async_copy(weight_in, in_buf, load_sem.at[0]),
        pltpu.make_async_copy(weight_out, out_buf, load_sem.at[1]),
    ]
    for copy in loads:
        copy.start()
    cots = {
        (s, t, h): pltpu.make_async_copy(
            cotangent.at[piece(s, t, h)], cot_buf.at[slot(s, t, h)], cot_sem.at[s, t, h]
        )
        for s in range(nz) for t in range(ny) for h in range(2)
    }
    for copy in cots.values():
        copy.start()
    rows_buf[0:tok_rows, :] = own[...]
    for copy in loads:
        copy.wait()

    lane = lax.broadcasted_iota(jnp.int32, (step_rows, experts), 1)
    wide_lane = lax.broadcasted_iota(jnp.int32, (step_rows, 128), 1)
    tile = 256

    def compute(s):
        rows = pl.ds(s * step_rows, step_rows)
        picked = jnp.concatenate(
            [named[piece(s, t, h), :] for t in range(ny) for h in range(2)], axis=0
        ) > 0.5
        logits = jnp.where(picked, dot(rows_buf[rows, :], router[...], 1, 1), MASKED)
        powers = jnp.exp(logits - jnp.max(logits, axis=1, keepdims=True))
        powers = jnp.where(picked, powers, 0.0)
        gates = powers / jnp.sum(powers, axis=1, keepdims=True)
        found = jnp.zeros((step_rows, 128), F32)
        for e in range(exp_dev):
            weight = jnp.sum(
                jnp.where(lane == me * exp_dev + e, gates, 0.0), axis=1, keepdims=True
            )

            def hidden_step(j, total):
                at = pl.multiple_of(j * tile, tile)
                cols, late = pl.ds(at, tile), pl.ds(pl.multiple_of(ff + at, tile), tile)
                gate_pre = dot(rows_buf[rows, :], in_buf[e, :, cols])
                up_pre = dot(rows_buf[rows, :], in_buf[e, :, late])
                d_plain = dot(cot_buf[rows, :], out_buf[e, cols, :], 1, 1)
                sigmoid = jax.nn.sigmoid(gate_pre)
                active = gate_pre * sigmoid
                hidden = active * up_pre
                hid_buf[e, rows, cols] = (weight * hidden).astype(BF16)
                d_hidden = weight * d_plain
                gu_buf[e, rows, cols] = (
                    d_hidden * up_pre * sigmoid * (1.0 + gate_pre * (1.0 - sigmoid))
                ).astype(BF16)
                gu_buf[e, rows, late] = (d_hidden * active).astype(BF16)
                return total + jnp.sum(hidden * d_plain, axis=1, keepdims=True)

            total = lax.fori_loop(0, ff // tile, hidden_step, jnp.zeros((step_rows, 1), F32))
            found += jnp.where(wide_lane == me * exp_dev + e, total, 0.0)

        def back_rows(rows, n):
            cols = pl.ds(pl.multiple_of(n * tile, tile), tile)
            d_rows = dot(gu_buf[0, rows, :], in_buf[0, cols, :], 1, 1)
            for e in range(1, exp_dev):
                d_rows += dot(gu_buf[e, rows, :], in_buf[e, cols, :], 1, 1)
            part_buf[rows, cols] = d_rows.astype(BF16)

        if ny > 1:
            away = pl.ds(s * step_rows + tok_rows, step_rows - tok_rows)
            pl.loop(0, width // tile)(functools.partial(back_rows, away))
            if s > 0:
                first_y(s - 1)
        here = pl.ds(s * step_rows, tok_rows)
        pl.loop(0, width // tile)(functools.partial(back_rows, here))

        @pl.loop(0, width // tile)
        def _(n):
            cols = pl.ds(pl.multiple_of(n * tile, tile), tile)
            made_sum = dot(hid_buf[0, rows, :], out_buf[0, :, cols])
            for e in range(1, exp_dev):
                made_sum += dot(hid_buf[e, rows, :], out_buf[e, :, cols])
            made_buf[rows, cols] = made_sum.astype(BF16)

        for t in range(ny):
            for h in range(2):
                low = (t * 2 + h) * half
                gate_out[s, t, h] = found[low : low + half, :].T[:experts, :]
                if s or t:
                    gate_copy(s, t, h).start()
                made_copy(s, t, h).start()

    def gate_copy(s, t, h):
        return pltpu.make_async_remote_copy(
            src_ref=gate_out.at[s, t, h], dst_ref=gate_in.at[s, t, h],
            send_sem=gate_send.at[s, t, h], recv_sem=gate_recv.at[s, t, h],
            device_id={"expert": owner(s, t, h)}, device_id_type=MESH,
        )

    def made_copy(s, t, h):
        return pltpu.make_async_copy(
            made_buf.at[slot(s, t, h)], made.at[piece(s, t, h)], made_sem.at[s, t, h]
        )

    def part(r, t, h):
        return slot((r + 1) % nz, (t + 1) % ny, h)

    def y_copy(r, t, h):
        source = part_buf.at[part(r, 0, h)] if t == 0 else to_y.at[r, t - 1, h]
        return pltpu.make_async_remote_copy(
            src_ref=source, dst_ref=from_y.at[r, t, h],
            send_sem=send_y.at[r, t, h], recv_sem=recv_y.at[r, t, h],
            device_id=near(False, h), device_id_type=MESH,
        )

    def z_copy(r, h):
        return pltpu.make_async_remote_copy(
            src_ref=to_z.at[r, h], dst_ref=from_z.at[r, h],
            send_sem=send_z.at[r, h], recv_sem=recv_z.at[r, h],
            device_id=near(True, h), device_id_type=MESH,
        )

    def first_y(r):
        if ny > 1:
            for h in range(2):
                y_copy(r, 0, h).start()

    def finish(r):
        for t in range(1, ny - 1):
            for h in range(2):
                y_copy(r, t - 1, h).wait_recv()
                to_y[r, t - 1, h] = (
                    part_buf[part(r, t, h), :].astype(F32) + from_y[r, t - 1, h].astype(F32)
                ).astype(BF16)
                y_copy(r, t, h).start()
        for h in range(2):
            total = part_buf[part(r, ny - 1, h), :].astype(F32)
            if ny > 1:
                y_copy(r, ny - 2, h).wait_recv()
                total += from_y[r, ny - 2, h].astype(F32)
            if r > 0:
                z_copy(r - 1, h).wait_recv()
                total += from_z[r - 1, h].astype(F32)
            if r < nz - 1:
                to_z[r, h] = total.astype(BF16)
                z_copy(r, h).start()
            else:
                back[h * half : (h + 1) * half, :] = total

    def forward(s):
        for h in range(2):
            arrive(s, 0, h)
            if s + 1 < nz:
                start(s, 0, h, s + 1, 0)
            if ny > 1:
                start(s, 0, h, s, 1)

    def whole_step(s):
        for t in range(1, ny):
            for h in range(2):
                arrive(s, t, h)
                if t + 1 < ny:
                    start(s, t, h, s, t + 1)
        for t in range(ny):
            for h in range(2):
                cots[s, t, h].wait()
        compute(s)

    for s in range(nz):
        if s + 1 < nz:
            forward(s + 1)
        whole_step(s)
        if s > 1:
            finish(s - 2)
    first_y(nz - 1)

    chunk = gin_buf.shape[2]

    def grad_step(i):
        cols = pl.ds(pl.multiple_of(i * tile, tile), tile)
        for e in range(exp_dev):
            found = dot(rows_buf[:, cols], gu_buf[e], 0, 0).astype(BF16)
            for c in range(tile // chunk):
                gin_buf[i * (tile // chunk) + c, e] = found[c * chunk : (c + 1) * chunk, :]

    def grad_out_step(i):
        cols = pl.ds(pl.multiple_of(i * tile, tile), tile)
        for e in range(exp_dev):
            found = dot(hid_buf[e, :, cols], cot_buf[...], 0, 0).astype(BF16)
            for c in range(width // chunk):
                gout_buf[c, e, cols, :] = found[:, c * chunk : (c + 1) * chunk]

    pl.loop(0, ff // tile)(grad_out_step)
    gout_copy = pltpu.make_async_copy(gout_buf, grads_out, grad_sem.at[0])
    gout_copy.start()
    if nz > 1:
        finish(nz - 2)
    pl.loop(0, width // tile)(grad_step)
    gin_copy = pltpu.make_async_copy(gin_buf, grads_in, grad_sem.at[1])
    gin_copy.start()
    finish(nz - 1)
    for h in range(2):
        gate_sum = gate_out[0, 0, h]
        for s in range(nz):
            for t in range(ny):
                if s or t:
                    gate_copy(s, t, h).wait_recv()
                    gate_sum += gate_in[s, t, h]
        d_gate[h] = gate_sum
    for copy in sent:
        copy.wait_send()
    for s in range(nz):
        for h in range(2):
            for t in range(ny):
                made_copy(s, t, h).wait()
                if s or t:
                    gate_copy(s, t, h).wait_send()
            for t in range(ny - 1):
                y_copy(s, t, h).wait_send()
            if s < nz - 1:
                z_copy(s, h).wait_send()
    gout_copy.wait()
    gin_copy.wait()


def experts_pass(own, named, router, cotangent, weight_in, weight_out, n_dp, n_expert, cid):
    nz, ny = grid_of(n_expert)
    tok_rows, width = own.shape
    exp_dev, ff, _ = weight_out.shape
    half, group = tok_rows // 2, tok_rows * n_expert
    experts = named.shape[1]
    whole, anywhere = pl.BlockSpec(memory_space=pltpu.VMEM), pl.BlockSpec(memory_space=pl.ANY)
    dma = pltpu.SemaphoreType.DMA
    ring = dma((nz, ny, 2))
    y_steps, y_mid, z_steps = max(ny - 1, 1), max(ny - 2, 1), max(nz - 1, 1)
    return pl.pallas_call(
        functools.partial(experts_kernel, nz, ny),
        out_shape=[
            jax.ShapeDtypeStruct((tok_rows, width), F32),
            jax.ShapeDtypeStruct((2, experts, half), F32),
            jax.ShapeDtypeStruct((group, width), BF16),
            jax.ShapeDtypeStruct((n_dp, exp_dev, width // n_dp, 2 * ff), BF16),
            jax.ShapeDtypeStruct((n_dp, exp_dev, ff, width // n_dp), BF16),
        ],
        in_specs=[whole, whole, whole, anywhere, anywhere, anywhere],
        out_specs=[whole, whole, anywhere, anywhere, anywhere],
        scratch_shapes=[
            pltpu.VMEM((group, width), BF16),
            pltpu.VMEM((group, width), BF16),
            pltpu.VMEM((exp_dev, width, 2 * ff), BF16),
            pltpu.VMEM((exp_dev, ff, width), BF16),
            pltpu.VMEM((exp_dev, group, ff), BF16),
            pltpu.VMEM((exp_dev, group, 2 * ff), BF16),
            pltpu.VMEM((group, width), BF16),
            pltpu.VMEM((group, width), BF16),
            pltpu.VMEM((n_dp, exp_dev, width // n_dp, 2 * ff), BF16),
            pltpu.VMEM((n_dp, exp_dev, ff, width // n_dp), BF16),
            pltpu.VMEM((nz, ny, 2, experts, half), F32),
            pltpu.VMEM((nz, ny, 2, experts, half), F32),
            pltpu.VMEM((nz, y_steps, 2, half, width), BF16),
            pltpu.VMEM((z_steps, 2, half, width), BF16),
            pltpu.VMEM((nz, y_mid, 2, half if ny > 2 else 16, width), BF16),
            pltpu.VMEM((z_steps, 2, half, width), BF16),
            dma((2,)), ring, ring, dma((2,)), ring, ring, ring, ring,
            dma((nz, y_steps, 2)), dma((nz, y_steps, 2)), dma((z_steps, 2)), dma((z_steps, 2)),
        ],
        compiler_params=pltpu.CompilerParams(
            collective_id=cid, has_side_effects=True, vmem_limit_bytes=60 << 20
        ),
        cost_estimate=pl.CostEstimate(
            flops=18 * exp_dev * group * width * ff,
            bytes_accessed=16 * group * width,
            transcendentals=exp_dev * group * ff,
        ),
        name="experts_pass",
    )(own, named, router, cotangent, weight_in, weight_out)


def gather(values, name, axis=0):
    return lax.all_gather(values, name, axis=axis, tiled=True)


def local(
    hidden_in, d_out, gain_attn, w_qkv, w_o, gain_moe, w_router, w_in, w_out,
    seq_lengths, assign, routes,
):
    tok_rows, width = hidden_in.shape
    exp_dev, _, ff_two = w_in.shape
    ff = ff_two // 2
    n_expert = lax.axis_size("expert")
    me = lax.axis_index("expert")
    experts = exp_dev * n_expert
    group_rows = tok_rows * n_expert
    q_per = HEADS // n_expert
    share = GROUPS // q_per
    q_cols = q_per * HEAD_DIM
    k_base = HEADS * HEAD_DIM
    v_base = k_base + KV_HEADS * HEAD_DIM
    cols = q_cols + 2 * HEAD_DIM

    n_dp = lax.axis_size("dp")
    wide = width // n_dp
    kv_head = (me * q_per) // GROUPS
    heads_part = jnp.concatenate(
        [
            lax.dynamic_slice_in_dim(w_qkv, me * q_cols, q_cols, 1),
            lax.dynamic_slice_in_dim(w_qkv, k_base + kv_head * HEAD_DIM, HEAD_DIM, 1),
            lax.dynamic_slice_in_dim(w_qkv, v_base + kv_head * HEAD_DIM, HEAD_DIM, 1),
        ],
        axis=1,
    )
    few = 2 + experts
    pack = jnp.concatenate(
        [gain_attn[None], gain_moe[None], w_router.T, jnp.zeros((-few % 16, wide), BF16)], axis=0
    )
    top = routes.shape[1]
    meta = jnp.concatenate(
        [assign, routes.T, jnp.zeros((-(1 + top) % 8, tok_rows), jnp.int32)], axis=0
    )
    meta = meta.reshape(meta.shape[0], 2, tok_rows // 2).transpose(1, 0, 2)
    qkv_full = gather(w_qkv, "dp")
    hidden_all, meta, w_heads, pack = first_gather(
        hidden_in, meta, heads_part, pack, n_dp, n_expert, 0
    )
    w_heads = w_heads.reshape(width, cols)
    pack = pack.transpose(1, 0, 2).reshape(-1, width)
    gain_one, gain_two = pack[0].astype(F32), pack[1].astype(F32)
    router_t = pack[2:few]
    position = meta[:, :, 0].reshape(group_rows)
    routes_all = meta[:, :, 1 : 1 + top]
    named = jnp.any(
        routes_all[:, :, :, None, :] == jnp.arange(experts, dtype=jnp.int32)[:, None], axis=2
    ).transpose(0, 1, 3, 2).reshape(group_rows, experts)
    stream_in = hidden_in.astype(F32)
    proj_full = gather(w_o, "dp")
    weight_in = gather(w_in, "dp", axis=1)
    weight_out = gather(w_out, "dp", axis=2)
    lengths = seq_lengths[0]
    order = jnp.arange(lengths.shape[0], dtype=jnp.int32)
    ends = jnp.sum(jnp.where(order[None, :] <= order[:, None], lengths[None, :], 0), axis=1)
    starts = ends - lengths
    seq_id = jnp.sum((position[None, :] >= ends[:, None]).astype(jnp.int32), axis=0)
    picks = seq_id[None, :] == jnp.arange(lengths.shape[0], dtype=jnp.int32)[:, None]
    start_of = jnp.sum(jnp.where(picks, starts[:, None], 0), axis=0)
    rot_pos = position - start_of
    half = HEAD_DIM // 2
    frequency = ROPE_BASE ** (-(jnp.arange(half).astype(F32) * (2.0 / HEAD_DIM)))
    angles = frequency[:, None] * rot_pos.astype(F32)[None, :]
    cosine, sine = jnp.cos(angles), jnp.sin(angles)
    low, high = start_of[None, :], position[None, :]
    key_pos = jnp.broadcast_to(position[:, None], (group_rows, low_tile(group_rows)))

    heads_out, lse, attended, d_out_all, normed_all, query, key, key_t, value = attend(
        low, high, key_pos, cosine, sine, gain_one[None], w_heads, hidden_all, d_out, q_per, 6
    )
    attended = attended.reshape(n_expert * q_cols, tok_rows)
    mid_stream = stream_in + dot(attended, proj_full, 0, 0)
    normed_two = rms_norm(mid_stream, gain_two).astype(BF16)

    d_back, d_gate, made, grads_in, grads_out = experts_pass(
        normed_two, named.astype(F32), router_t, d_out_all, weight_in, weight_out, n_dp, n_expert, 1
    )
    d_gate = d_gate.transpose(0, 2, 1).reshape(tok_rows, experts)
    own_named = jnp.any(
        routes[:, :, None] == jnp.arange(experts, dtype=jnp.int32)[None, None, :], axis=1
    )
    own_gates = jax.nn.softmax(
        jnp.where(own_named, dot(normed_two, router_t, 1, 1), -jnp.inf), axis=1
    )
    d_logits = (
        own_gates * (d_gate - jnp.sum(own_gates * d_gate, axis=1, keepdims=True))
    ).astype(BF16)
    grad_router = dot(d_logits, normed_two, 0, 0)
    d_normed_two = d_back + dot(d_logits, router_t)
    _, norm_two_back = jax.vjp(rms_norm, mid_stream, gain_two)
    d_mid_norm, grad_gain_two = norm_two_back(d_normed_two)
    d_mid = d_out.astype(F32) + d_mid_norm

    d_attn = d_mid.astype(BF16)
    d_attn, grads_in, grads_out, made = lax.optimization_barrier((d_attn, grads_in, grads_out, made))
    grad_w_in = lax.psum_scatter(grads_in, "dp", scatter_dimension=0, tiled=True)
    grad_w_out = lax.psum_scatter(grads_out, "dp", scatter_dimension=0, tiled=True)
    d_att = dot(proj_full, d_attn, 1, 1).astype(BF16).reshape(n_expert, q_cols, tok_rows)
    part_o = dot(attended, d_attn).astype(BF16).reshape(n_dp, wide, width)
    d_own, d_projected, returned, sum_o = attend_back(
        low, high, key_pos, query, key, key_t, value, heads_out, lse,
        cosine, sine, made, part_o, d_att, tok_rows, 4,
    )
    layer_out = (mid_stream + returned).astype(BF16)
    if share > 1:
        fan = lambda part: jnp.repeat(part.reshape(width, KV_HEADS, HEAD_DIM), share, axis=1).reshape(width, -1)
        qkv_full = jnp.concatenate(
            [qkv_full[:, :k_base], fan(qkv_full[:, k_base:v_base]), fan(qkv_full[:, v_base:])], axis=1
        )
    d_normed_one = dot(d_own, qkv_full, 0, 1)
    _, norm_one_back = jax.vjp(rms_norm, stream_in, gain_one)
    d_in_norm, grad_gain_one = norm_one_back(d_normed_one)
    grad_in = d_mid + d_in_norm

    part_qkv = dot(
        normed_all, d_projected.transpose(1, 0, 2).reshape(cols, group_rows), 0, 1
    ).astype(BF16).reshape(n_dp, wide, cols)
    small = jnp.concatenate(
        [grad_gain_one[None], grad_gain_two[None], grad_router, jnp.zeros((-few % 8, width), F32)], axis=0
    )
    small = small.reshape(-1, n_dp, wide).transpose(1, 0, 2)
    grad_w_qkv, grad_w_o, small, grad_w_in, grad_w_out = finish_sums(
        part_qkv, sum_o, small, grad_w_in[0], grad_w_out[0], q_cols, n_expert, 5
    )
    return (
        layer_out, grad_in, small[0], grad_w_qkv, grad_w_o, small[1], small[2:few].T,
        grad_w_in, grad_w_out,
    )


def solution(mesh):
    rows = P(("dp", "expert"), None)
    in_specs = (
        rows, rows, P("dp"), P("dp", None), P("dp", None), P("dp"), P("dp", None),
        P("expert", "dp", None), P("expert", None, "dp"), P("dp", None), P("dp", "expert"), rows,
    )
    out_specs = (
        rows, rows, P("dp"), P("dp", None), P("dp", None), P("dp"), P("dp", None),
        P("expert", "dp", None), P("expert", None, "dp"),
    )
    return jax.shard_map(local, mesh=mesh, in_specs=in_specs, out_specs=out_specs, check_vma=False)
```

```python
import functools

import jax
import jax.numpy as jnp
from jax import lax
from jax.experimental import pallas as pl
from jax.experimental.pallas import tpu as pltpu
from jax.sharding import PartitionSpec as P

HEADS = 16
KV_HEADS = 8
HEAD_DIM = 64
GROUPS = HEADS // KV_HEADS
EPSILON = 1e-06
ROPE_BASE = 10000.0
SCORE_SCALE = 0.015625
MASKED = -1e30
F32 = jnp.float32
BF16 = jnp.bfloat16
Q_TILE = 256
K_TILE = 256


MESH = pl.DeviceIdType.MESH
Z_SIZE = 4

def grid_of(n_expert):
    nz = Z_SIZE if n_expert % Z_SIZE == 0 else 1
    return nz, n_expert // nz

def places(nz, ny):
    me = lax.axis_index("expert")
    return me // ny, lax.rem(me, ny)

def device(z, y, nz, ny):
    return lax.rem(z + 2 * nz, nz) * ny + lax.rem(y + 2 * ny, ny)

def rms_norm(values, gain_vec):
    factor = lax.rsqrt(jnp.mean(values * values, axis=-1, keepdims=True) + EPSILON)
    return values * factor * gain_vec


def dot(left, right, left_dim=1, right_dim=0):
    return lax.dot_general(
        left, right, (((left_dim,), (right_dim,)), ((), ())), preferred_element_type=F32
    )


def rotate(values, cosine, sine):
    half = HEAD_DIM // 2
    one, two = values[:half], values[half:]
    return jnp.concatenate([one * cosine - two * sine, two * cosine + one * sine], axis=0)


def rotate_back(grads, cosine, sine):
    half = HEAD_DIM // 2
    one, two = grads[:half], grads[half:]
    return jnp.concatenate([one * cosine + two * sine, two * cosine - one * sine], axis=0)


def first_kernel(
    n_dp, nz, ny, rows, meta, heads, pack,
    rows_all, meta_all, heads_all, pack_all,
    send_sem, recv_sem, meta_send, meta_recv, dp_send, dp_recv, keep_sem,
):
    z, y = places(nz, ny)
    me, group = lax.axis_index("expert"), lax.axis_index("dp")
    count = rows.shape[0]
    half = count // 2
    barrier = pltpu.get_barrier_semaphore()
    near = [{"dp": lax.rem(group + k, n_dp)} for k in range(1, n_dp)]
    near += [{"expert": device(z + k, y, nz, ny)} for k in sorted({1, nz - 1} - {0})]
    near += [{"expert": device(z, y + k, nz, ny)} for k in sorted({1, ny - 1} - {0})]
    for other in near:
        pl.semaphore_signal(barrier, inc=1, device_id=other, device_id_type=MESH)
    pl.semaphore_wait(barrier, len(near))

    def origin(s, t, h):
        sign = -1 if h == 0 else 1
        return device(z + sign * s, y + sign * t, nz, ny)

    def copies(s, t, h, s2, t2):
        of = origin(s, t, h)
        mine = s == 0 and t == 0
        part = pl.ds(pl.multiple_of(of * count + h * half, half), half)
        step = 1 if h == 0 else -1
        to = device(z + step, y, nz, ny) if t2 == 0 else device(z, y + step, nz, ny)
        big = pltpu.make_async_remote_copy(
            src_ref=rows.at[pl.ds(h * half, half)] if mine else rows_all.at[part],
            dst_ref=rows_all.at[part],
            send_sem=send_sem.at[s2, t2, h], recv_sem=recv_sem.at[s2, t2, h],
            device_id={"expert": to}, device_id_type=MESH,
        )
        little = pltpu.make_async_remote_copy(
            src_ref=meta.at[h] if mine else meta_all.at[of, h], dst_ref=meta_all.at[of, h],
            send_sem=meta_send.at[s2, t2, h], recv_sem=meta_recv.at[s2, t2, h],
            device_id={"expert": to}, device_id_type=MESH,
        )
        return little, big

    def arrive(s, t, h):
        of = origin(s, t, h)
        part = pl.ds(pl.multiple_of(of * count + h * half, half), half)
        for place, sends, receives in (
            (meta_all.at[of, h], meta_send, meta_recv), (rows_all.at[part], send_sem, recv_sem)
        ):
            pltpu.make_async_remote_copy(
                src_ref=place, dst_ref=place, send_sem=sends.at[s, t, h], recv_sem=receives.at[s, t, h],
                device_id={"expert": device(z + 1, y, nz, ny)}, device_id_type=MESH,
            ).wait_recv()

    sent = []

    def start(*key):
        for copy in copies(*key):
            copy.start()
            sent.append(copy)

    for h in range(2):
        start(0, 0, h, 1, 0)
    if ny > 1:
        for h in range(2):
            start(0, 0, h, 0, 1)

    def across(k, a):
        source, target = ((heads, heads_all), (pack, pack_all))[a]
        return pltpu.make_async_remote_copy(
            src_ref=source, dst_ref=target.at[group],
            send_sem=dp_send.at[k - 1, a], recv_sem=dp_recv.at[k - 1, a],
            device_id={"dp": lax.rem(group + k, n_dp)}, device_id_type=MESH,
        )

    for k in range(1, n_dp):
        for a in range(2):
            across(k, a).start()
    keeps = [
        pltpu.make_async_copy(
            rows, rows_all.at[pl.ds(pl.multiple_of(me * count, count), count)], keep_sem.at[0]
        ),
        pltpu.make_async_copy(meta, meta_all.at[me], keep_sem.at[1]),
        pltpu.make_async_copy(heads, heads_all.at[group], keep_sem.at[2]),
        pltpu.make_async_copy(pack, pack_all.at[group], keep_sem.at[3]),
    ]
    for copy in keeps:
        copy.start()
    for s in range(1, nz):
        for h in range(2):
            arrive(s, 0, h)
            if s + 1 < nz:
                start(s, 0, h, s + 1, 0)
            if ny > 1:
                start(s, 0, h, s, 1)
    for t in range(1, ny):
        for s in range(nz):
            for h in range(2):
                arrive(s, t, h)
                if t + 1 < ny:
                    start(s, t, h, s, t + 1)
    for k in range(1, n_dp):
        for a, target in enumerate((heads_all, pack_all)):
            place = target.at[lax.rem(group + n_dp - k, n_dp)]
            pltpu.make_async_remote_copy(
                src_ref=place, dst_ref=place, send_sem=dp_send.at[k - 1, a], recv_sem=dp_recv.at[k - 1, a],
                device_id={"dp": lax.rem(group + k, n_dp)}, device_id_type=MESH,
            ).wait_recv()
    for copy in keeps:
        copy.wait()
    for copy in sent:
        copy.wait_send()
    for k in range(1, n_dp):
        for a in range(2):
            across(k, a).wait_send()


def first_gather(rows, meta, heads, pack, n_dp, n_expert, cid):
    nz, ny = grid_of(n_expert)
    anywhere = pl.BlockSpec(memory_space=pl.ANY)
    dma = pltpu.SemaphoreType.DMA
    ring, peers = dma((nz, ny, 2)), dma((max(n_dp - 1, 1), 2))
    return pl.pallas_call(
        functools.partial(first_kernel, n_dp, nz, ny),
        out_shape=[
            jax.ShapeDtypeStruct((rows.shape[0] * n_expert, rows.shape[1]), rows.dtype),
            jax.ShapeDtypeStruct((n_expert,) + meta.shape, meta.dtype),
            jax.ShapeDtypeStruct((n_dp,) + heads.shape, heads.dtype),
            jax.ShapeDtypeStruct((n_dp,) + pack.shape, pack.dtype),
        ],
        in_specs=[anywhere] * 4,
        out_specs=[anywhere] * 4,
        scratch_shapes=[ring, ring, ring, ring, peers, peers, dma((4,))],
        compiler_params=pltpu.CompilerParams(collective_id=cid, has_side_effects=True),
        name="first_gather",
    )(rows, meta, heads, pack)


def attend_kernel(
    nz, ny, low, high, key_pos, cos_tab, sin_tab, gain, head_weights, hidden, cotangent,
    out, lse, own_in, everyone, normed, query_all, key, key_t, value,
    score_buf, weight_buf, send_buf, rows_buf, value_t, query,
    own_send, own_recv, send_sem, recv_sem, keep_sem, load_sem,
):
    z, y = places(nz, ny)
    me = lax.axis_index("expert")
    n_expert = nz * ny
    heads, width, tile = query.shape
    q_cols = heads * width
    low_row, high_row = low[...], high[...]
    steps = key.shape[0] // K_TILE
    tok_rows = cotangent.shape[0]
    half_rows = tok_rows // 2
    per_tile = tile // tok_rows
    i = pl.program_id(0)
    count = key.shape[0] // tile

    def piece(s, t, h):
        sign = -1 if h == 0 else 1
        begin = device(z + sign * s, y + sign * t, nz, ny) * tok_rows + h * half_rows
        return pl.ds(pl.multiple_of(begin, half_rows), half_rows)

    def row_copy(s, t, h, s2, t2):
        mine = s == 0 and t == 0
        step = 1 if h == 0 else -1
        to = device(z + step, y, nz, ny) if t2 == 0 else device(z, y + step, nz, ny)
        return pltpu.make_async_remote_copy(
            src_ref=cotangent.at[pl.ds(h * half_rows, half_rows)] if mine else everyone.at[piece(s, t, h)],
            dst_ref=everyone.at[piece(s, t, h)],
            send_sem=send_sem.at[s2, t2, h], recv_sem=recv_sem.at[s2, t2, h],
            device_id={"expert": to}, device_id_type=MESH,
        )

    def arrive(s, t, h):
        place = everyone.at[piece(s, t, h)]
        pltpu.make_async_remote_copy(
            src_ref=place, dst_ref=place, send_sem=send_sem.at[s, t, h], recv_sem=recv_sem.at[s, t, h],
            device_id={"expert": device(z + 1, y, nz, ny)}, device_id_type=MESH,
        ).wait_recv()

    def forward(s):
        for h in range(2):
            arrive(s, 0, h)
            if s + 1 < nz:
                row_copy(s, 0, h, s + 1, 0).start()
            if ny > 1:
                row_copy(s, 0, h, s, 1).start()

    def own_copy(other, source):
        return pltpu.make_async_remote_copy(
            src_ref=send_buf.at[other], dst_ref=own_in.at[source],
            send_sem=own_send.at[other], recv_sem=own_recv.at[source],
            device_id={"expert": other}, device_id_type=MESH,
        )

    keep = pltpu.make_async_copy(
        cotangent, everyone.at[pl.ds(pl.multiple_of(me * tok_rows, tok_rows), tok_rows)], keep_sem.at[0]
    )

    whole_out = pltpu.make_async_copy(rows_buf, normed, keep_sem.at[2])

    def load(j):
        rows = pl.ds(pl.multiple_of(j * tile, tile), tile)
        return pltpu.make_async_copy(hidden.at[rows], rows_buf.at[rows], load_sem.at[j])

    @pl.when(i == 0)
    def _():
        barrier = pltpu.get_barrier_semaphore()
        for k in range(1, n_expert):
            pl.semaphore_signal(
                barrier, inc=1, device_id={"expert": lax.rem(me + k, n_expert)}, device_id_type=MESH
            )
        pl.semaphore_wait(barrier, n_expert - 1)
        for h in range(2):
            row_copy(0, 0, h, 1, 0).start()
        if ny > 1:
            for h in range(2):
                row_copy(0, 0, h, 0, 1).start()
        keep.start()
        for j in range(count):
            load(j).start()

        @pl.loop(0, count)
        def _(j):
            rows = pl.ds(pl.multiple_of(j * tile, tile), tile)
            load(j).wait()
            rows_buf[rows, :] = rms_norm(rows_buf[rows, :].astype(F32), gain[...]).astype(BF16)
            cosine, sine = cos_tab[:, rows], sin_tab[:, rows]
            projected = dot(head_weights[...], rows_buf[rows, :], 0, 1)
            for head in range(heads):
                part = projected[head * width : (head + 1) * width]
                query_all[head, :, rows] = rotate(part, cosine, sine).astype(BF16) * jnp.asarray(
                    SCORE_SCALE, BF16
                )
            turned = rotate(projected[q_cols : q_cols + width], cosine, sine).astype(BF16)
            key_t[:, rows] = turned
            key[rows, :] = turned.T
            plain = projected[q_cols + width :].astype(BF16)
            value_t[:, rows] = plain
            value[rows, :] = plain.T

        whole_out.start()
        if nz > 1:
            forward(1)

    early = [s for s in range(2, nz) if 3 * (s - 1) < count]
    for s in early:
        pl.when(i == 3 * (s - 1))(functools.partial(forward, s))
    query[...] = query_all[:, :, pl.ds(pl.multiple_of(i * tile, tile), tile)]

    def score_step(step, maxima):
        rows = pl.ds(pl.multiple_of(step * K_TILE, K_TILE), K_TILE)
        at = key_pos[rows, :]
        allowed = (at >= low_row) & (at <= high_row)
        found = []
        for head in range(heads):
            scores = jnp.dot(key[rows, :], query[head], preferred_element_type=F32)
            scores = jnp.where(allowed, scores, MASKED)
            score_buf[head, rows, :] = scores
            found.append(jnp.maximum(maxima[head], jnp.max(scores, axis=0, keepdims=True)))
        return tuple(found)

    begin = tuple(jnp.full(low_row.shape, MASKED, F32) for _ in range(heads))
    maxima = lax.fori_loop(0, steps, score_step, begin)

    def weight_step(step, totals):
        rows = pl.ds(pl.multiple_of(step * K_TILE, K_TILE), K_TILE)
        found = []
        for head in range(heads):
            weights = jnp.exp(score_buf[head, rows, :] - maxima[head])
            weight_buf[head, rows, :] = weights.astype(BF16)
            found.append(totals[head] + jnp.sum(weights, axis=0, keepdims=True))
        return tuple(found)

    begin = tuple(jnp.zeros(low_row.shape, F32) for _ in range(heads))
    totals = lax.fori_loop(0, steps, weight_step, begin)
    for head in range(heads):
        summed = jnp.dot(value_t[...], weight_buf[head], preferred_element_type=F32)
        attended = (summed / totals[head]).astype(BF16)
        out[head] = attended
        lse[head] = maxima[head] + jnp.log(totals[head])
        for j in range(per_tile):
            send_buf[i * per_tile + j, head * width : (head + 1) * width, :] = attended[
                :, j * tok_rows : (j + 1) * tok_rows
            ]
    for j in range(per_tile):
        other = i * per_tile + j

        @pl.when(other != me)
        def _():
            own_copy(other, me).start()

    @pl.when(i == count - 1)
    def _():
        mine = pltpu.make_async_copy(send_buf.at[me], own_in.at[me], keep_sem.at[1])
        mine.start()
        for s in range(2, nz):
            if s not in early:
                forward(s)
        for t in range(1, ny):
            for s in range(nz):
                for h in range(2):
                    arrive(s, t, h)
                    if t + 1 < ny:
                        row_copy(s, t, h, s, t + 1).start()
        for k in range(1, n_expert):
            other = lax.rem(me + k, n_expert)
            own_copy(other, other).wait_recv()
            own_copy(other, other).wait_send()
        for s in range(nz):
            for t in range(ny):
                for h in range(2):
                    if t > 0:
                        row_copy(s, t - 1, h, s, t).wait_send()
                    elif s > 0:
                        row_copy(s - 1, 0, h, s, 0).wait_send()
        keep.wait()
        mine.wait()
        whole_out.wait()


def attend(low, high, key_pos, cosine, sine, gain, head_weights, hidden, cotangent, heads, cid):
    tok_rows, model = cotangent.shape
    rows = hidden.shape[0]
    width = HEAD_DIM
    n_expert = rows // tok_rows
    nz, ny = grid_of(n_expert)
    tile = low_tile(rows)
    whole = lambda i: (0, 0)
    lane = lambda i: (0, i)
    anywhere = pl.BlockSpec(memory_space=pl.ANY)
    dma = pltpu.SemaphoreType.DMA
    tables = pl.BlockSpec((width // 2, rows), whole)
    return pl.pallas_call(
        functools.partial(attend_kernel, nz, ny),
        grid=(rows // tile,),
        in_specs=[
            pl.BlockSpec((1, tile), lane),
            pl.BlockSpec((1, tile), lane),
            pl.BlockSpec((rows, tile), whole),
            tables, tables,
            pl.BlockSpec((1, model), whole),
            pl.BlockSpec(head_weights.shape, whole),
            anywhere, anywhere,
        ],
        out_specs=[
            pl.BlockSpec((heads, width, tile), lambda i: (0, 0, i)),
            pl.BlockSpec((heads, 1, tile), lambda i: (0, 0, i)),
            anywhere, anywhere, anywhere,
            pl.BlockSpec((heads, width, rows), lambda i: (0, 0, 0)),
            pl.BlockSpec((rows, width), whole),
            pl.BlockSpec((width, rows), whole),
            pl.BlockSpec((rows, width), whole),
        ],
        out_shape=[
            jax.ShapeDtypeStruct((heads, width, rows), BF16),
            jax.ShapeDtypeStruct((heads, 1, rows), F32),
            jax.ShapeDtypeStruct((n_expert, heads * width, tok_rows), BF16),
            jax.ShapeDtypeStruct((rows, model), BF16),
            jax.ShapeDtypeStruct((rows, model), BF16),
            jax.ShapeDtypeStruct((heads, width, rows), BF16),
            jax.ShapeDtypeStruct((rows, width), BF16),
            jax.ShapeDtypeStruct((width, rows), BF16),
            jax.ShapeDtypeStruct((rows, width), BF16),
        ],
        scratch_shapes=[
            pltpu.VMEM((heads, rows, tile), F32),
            pltpu.VMEM((heads, rows, tile), BF16),
            pltpu.VMEM((n_expert, heads * width, tok_rows), BF16),
            pltpu.VMEM((rows, model), BF16),
            pltpu.VMEM((width, rows), BF16),
            pltpu.VMEM((heads, width, tile), BF16),
            dma((n_expert,)), dma((n_expert,)), dma((nz, ny, 2)), dma((nz, ny, 2)), dma((3,)),
            dma((rows // tile,)),
        ],
        compiler_params=pltpu.CompilerParams(
            collective_id=cid, has_side_effects=True, vmem_limit_bytes=56 << 20
        ),
        cost_estimate=pl.CostEstimate(
            flops=4 * heads * rows * rows * 256,
            bytes_accessed=8 * rows * 256,
            transcendentals=heads * rows * rows,
        ),
        name="attend",
    )(low, high, key_pos, cosine, sine, gain, head_weights, hidden, cotangent)


def low_tile(rows):
    return min(Q_TILE, rows)


def attend_back_kernel(
    nz, ny,
    low, high, key_pos, query, key, key_t, value, attended, lse,
    cos_tab, sin_tab, made, out_part, d_att,
    own_in, proj, summed, out_sum,
    d_key, d_value, query_n, grad_n, grad, delta, grad_in, out_in, out_own, score_buf, send_buf, part_buf, from_y, from_z, to_y, to_z,
    part_sem, own_send, own_recv, tail_send, tail_recv, keep_sem, mine_sem,
    send_y, recv_y, send_z, recv_z, dp_send, dp_recv, grad_send, grad_recv,
):
    z, y = places(nz, ny)
    me, group = lax.axis_index("expert"), lax.axis_index("dp")
    n_expert, n_dp = nz * ny, out_part.shape[0]
    heads, width, tile = query.shape
    low_row, high_row = low[...], high[...]
    steps = key.shape[0] // K_TILE
    tok_rows = summed.shape[0]
    half_rows = tok_rows // 2
    per_tile = tile // tok_rows
    i = pl.program_id(0)
    count = key.shape[0] // tile
    q_cols = heads * width

    def piece(r, t, h):
        sign = -1 if h == 0 else 1
        start = device(z + sign * (r + 1), y + sign * (t + 1), nz, ny) * tok_rows + h * half_rows
        return pl.ds(pl.multiple_of(start, half_rows), half_rows)

    def near(along_z, h):
        step = 1 if h == 0 else -1
        to = device(z + step, y, nz, ny) if along_z else device(z, y + step, nz, ny)
        return {"expert": to}

    def part_copy(r, t, h):
        return pltpu.make_async_copy(
            made.at[piece(r, t, h)], part_buf.at[r, t, h], part_sem.at[r, t, h]
        )

    def y_copy(r, t, h):
        source = made.at[piece(r, 0, h)] if t == 0 else to_y.at[r, t - 1, h]
        return pltpu.make_async_remote_copy(
            src_ref=source, dst_ref=from_y.at[r, t, h],
            send_sem=send_y.at[r, t, h], recv_sem=recv_y.at[r, t, h],
            device_id=near(False, h), device_id_type=MESH,
        )

    def z_copy(r, h):
        return pltpu.make_async_remote_copy(
            src_ref=to_z.at[r, h], dst_ref=from_z.at[r, h],
            send_sem=send_z.at[r, h], recv_sem=recv_z.at[r, h],
            device_id=near(True, h), device_id_type=MESH,
        )

    def finish(r):
        for t in range(1, ny - 1):
            for h in range(2):
                y_copy(r, t - 1, h).wait_recv()
                part_copy(r, t, h).wait()
                to_y[r, t - 1, h] = (
                    part_buf[r, t, h].astype(F32) + from_y[r, t - 1, h].astype(F32)
                ).astype(BF16)
                y_copy(r, t, h).start()
        for h in range(2):
            part_copy(r, ny - 1, h).wait()
            total = part_buf[r, ny - 1, h].astype(F32)
            if ny > 1:
                y_copy(r, ny - 2, h).wait_recv()
                total += from_y[r, ny - 2, h].astype(F32)
            if r > 0:
                z_copy(r - 1, h).wait_recv()
                total += from_z[r - 1, h].astype(F32)
            if r < nz - 1:
                to_z[r, h] = total.astype(BF16)
                z_copy(r, h).start()
            else:
                summed[h * half_rows : (h + 1) * half_rows, :] = total

    def across(k):
        other = lax.rem(group + k, n_dp)
        return pltpu.make_async_remote_copy(
            src_ref=out_part.at[other], dst_ref=out_in.at[k - 1],
            send_sem=dp_send.at[k - 1], recv_sem=dp_recv.at[k - 1],
            device_id={"dp": other}, device_id_type=MESH,
        )

    spans = (
        (0, q_cols, 0),
        (q_cols, width, n_expert * q_cols),
        (q_cols + width, width, n_expert * (q_cols + width)),
    )

    def own_rows(a, source):
        _, rows, base = spans[a]
        return own_in.at[pl.ds(pl.multiple_of(base + source * rows, rows), rows)]

    def own_copy(a, other, source):
        begin, rows, _ = spans[a]
        return pltpu.make_async_remote_copy(
            src_ref=send_buf.at[other, pl.ds(begin, rows)], dst_ref=own_rows(a, source),
            send_sem=(own_send if a == 0 else tail_send.at[a - 1]).at[other],
            recv_sem=(own_recv if a == 0 else tail_recv.at[a - 1]).at[source],
            device_id={"expert": other}, device_id_type=MESH,
        )

    def grad_copy(other, source):
        return pltpu.make_async_remote_copy(
            src_ref=d_att.at[other], dst_ref=grad_in.at[source],
            send_sem=grad_send.at[other], recv_sem=grad_recv.at[source],
            device_id={"expert": other}, device_id_type=MESH,
        )

    @pl.when(i == 0)
    def _():
        barrier = pltpu.get_barrier_semaphore()
        for k in range(1, n_expert):
            pl.semaphore_signal(
                barrier, inc=1, device_id={"expert": lax.rem(me + k, n_expert)}, device_id_type=MESH
            )
        for k in range(1, n_dp):
            pl.semaphore_signal(
                barrier, inc=1, device_id={"dp": lax.rem(group + k, n_dp)}, device_id_type=MESH
            )
        pl.semaphore_wait(barrier, n_expert + n_dp - 2)
        for k in range(1, n_expert):
            grad_copy(lax.rem(me + k, n_expert), me).start()
        for k in range(1, n_dp):
            across(k).start()
        pltpu.make_async_copy(out_part.at[group], out_own, keep_sem.at[2]).start()
        grad_in[me] = d_att[me]
        for r in range(nz):
            for h in range(2):
                if ny > 1:
                    y_copy(r, 0, h).start()
                for t in range(1, ny - 1):
                    part_copy(r, t, h).start()
                part_copy(r, ny - 1, h).start()
        d_key[...] = jnp.zeros_like(d_key)
        d_value[...] = jnp.zeros_like(d_value)

    for r in range(nz - 1):
        pl.when(i == min((r + 1) * count // nz + 1, count - 1))(functools.partial(finish, r))

    for j in range(per_tile):
        source = i * per_tile + j

        @pl.when(source != me)
        def _():
            grad_copy(source, source).wait_recv()

        for head in range(heads):
            grad[head, :, j * tok_rows : (j + 1) * tok_rows] = grad_in[
                source, head * width : (head + 1) * width, :
            ]
    for head in range(heads):
        query_n[head] = query[head].T
        grad_n[head] = grad[head].T
        delta[head] = jnp.sum(
            grad[head].astype(F32) * attended[head].astype(F32), axis=0, keepdims=True
        )

    @pl.loop(0, steps)
    def _(step):
        rows = pl.ds(pl.multiple_of(step * K_TILE, K_TILE), K_TILE)
        at = key_pos[rows, :]
        allowed = (at >= low_row) & (at <= high_row)
        key_sum, value_sum = d_key[rows, :], d_value[rows, :]
        for head in range(heads):
            scores = jnp.dot(key[rows, :], query[head], preferred_element_type=F32)
            weights = jnp.exp(jnp.where(allowed, scores - lse[head], MASKED))
            d_soft = jnp.dot(value[rows, :], grad[head], preferred_element_type=F32)
            d_scores = (weights * (d_soft - delta[head])).astype(BF16)
            score_buf[head, rows, :] = d_scores
            key_sum += jnp.dot(d_scores, query_n[head], preferred_element_type=F32)
            value_sum += jnp.dot(weights.astype(BF16), grad_n[head], preferred_element_type=F32)
        d_key[rows, :] = key_sum
        d_value[rows, :] = value_sum

    lanes = pl.ds(pl.multiple_of(i * tile, tile), tile)
    for head in range(heads):
        d_query = jnp.dot(key_t[...], score_buf[head], preferred_element_type=F32) * SCORE_SCALE
        turned = rotate_back(d_query, cos_tab[:, lanes], sin_tab[:, lanes]).astype(BF16)
        for j in range(per_tile):
            send_buf[i * per_tile + j, head * width : (head + 1) * width, :] = turned[
                :, j * tok_rows : (j + 1) * tok_rows
            ]
    for j in range(per_tile):
        other = i * per_tile + j

        @pl.when(other != me)
        def _():
            own_copy(0, other, me).start()

    @pl.when(i == count - 1)
    def _():
        for other in range(n_expert):
            rows = pl.ds(other * tok_rows, tok_rows)
            turned = rotate_back(d_key[rows, :].T, cos_tab[:, rows], sin_tab[:, rows])
            send_buf[other, q_cols : q_cols + width, :] = turned.astype(BF16)
            send_buf[other, q_cols + width :, :] = d_value[rows, :].T.astype(BF16)

            @pl.when(other != me)
            def _():
                own_copy(1, other, me).start()
                own_copy(2, other, me).start()

        keep = pltpu.make_async_copy(send_buf, proj, keep_sem.at[0])
        keep.start()
        mine = [
            pltpu.make_async_copy(
                send_buf.at[me, pl.ds(begin, rows)], own_rows(a, me), mine_sem.at[a]
            )
            for a, (begin, rows, _) in enumerate(spans)
        ]
        for copy in mine:
            copy.start()
        finish(nz - 1)
        pltpu.make_async_copy(out_part.at[group], out_own, keep_sem.at[2]).wait()
        for k in range(1, n_dp):
            across(k).wait_recv()
        few = out_sum.shape[2]
        for m in range(n_expert):
            cols = slice(m * few, (m + 1) * few)
            out_total = out_own[:, cols].astype(F32)
            for k in range(1, n_dp):
                out_total += out_in[k - 1, :, cols].astype(F32)
            out_sum[m] = out_total.astype(BF16)
        for k in range(1, n_dp):
            across(k).wait_send()
        for k in range(1, n_expert):
            other = lax.rem(me + k, n_expert)
            for a in range(3):
                own_copy(a, other, other).wait_recv()
                own_copy(a, other, other).wait_send()
            grad_copy(other, other).wait_send()
        for r in range(nz):
            for h in range(2):
                for t in range(ny - 1):
                    y_copy(r, t, h).wait_send()
                if r < nz - 1:
                    z_copy(r, h).wait_send()
        keep.wait()
        for copy in mine:
            copy.wait()


def attend_back(
    low, high, key_pos, query, key, key_t, value, attended, lse,
    cosine, sine, made, out_part, d_att, tok_rows, cid,
):
    heads, width, rows = query.shape
    n_expert = rows // tok_rows
    nz, ny = grid_of(n_expert)
    cols = (heads + 2) * width
    half_rows, model = tok_rows // 2, made.shape[1]
    tile = low_tile(rows)
    whole = lambda i: (0, 0)
    lane = lambda i: (0, i)
    wide = pl.BlockSpec((heads, width, tile), lambda i: (0, 0, i))
    row = pl.BlockSpec((heads, 1, tile), lambda i: (0, 0, i))
    keys = pl.BlockSpec((rows, width), whole)
    anywhere = pl.BlockSpec(memory_space=pl.ANY)
    dma = pltpu.SemaphoreType.DMA
    y_steps, y_mid, z_steps = max(ny - 1, 1), max(ny - 2, 1), max(nz - 1, 1)
    peers = max(out_part.shape[0] - 1, 1)
    out_tiles = (n_expert, out_part.shape[1], out_part.shape[2] // n_expert)
    return pl.pallas_call(
        functools.partial(attend_back_kernel, nz, ny),
        grid=(rows // tile,),
        in_specs=[
            pl.BlockSpec((1, tile), lane),
            pl.BlockSpec((1, tile), lane),
            pl.BlockSpec((rows, tile), whole),
            wide, keys, pl.BlockSpec((width, rows), whole), keys, wide, row,
            pl.BlockSpec((width // 2, rows), whole), pl.BlockSpec((width // 2, rows), whole),
            anywhere, anywhere, pl.BlockSpec(d_att.shape, lambda i: (0, 0, 0)),
        ],
        out_specs=[
            anywhere, anywhere, pl.BlockSpec((tok_rows, model), whole),
            pl.BlockSpec(out_tiles, lambda i: (0, 0, 0)),
        ],
        out_shape=[
            jax.ShapeDtypeStruct((n_expert * cols, tok_rows), BF16),
            jax.ShapeDtypeStruct((n_expert, cols, tok_rows), BF16),
            jax.ShapeDtypeStruct((tok_rows, model), F32),
            jax.ShapeDtypeStruct(out_tiles, BF16),
        ],
        scratch_shapes=[
            pltpu.VMEM((rows, width), F32),
            pltpu.VMEM((rows, width), F32),
            pltpu.VMEM((heads, tile, width), BF16),
            pltpu.VMEM((heads, tile, width), BF16),
            pltpu.VMEM((heads, width, tile), BF16),
            pltpu.VMEM((heads, 1, tile), F32),
            pltpu.VMEM((n_expert, heads * width, tok_rows), BF16),
            pltpu.VMEM((peers,) + out_part.shape[1:], BF16),
            pltpu.VMEM(out_part.shape[1:], BF16),
            pltpu.VMEM((heads, rows, tile), BF16),
            pltpu.VMEM((n_expert, cols, tok_rows), BF16),
            pltpu.VMEM((nz, ny, 2, half_rows, model), BF16),
            pltpu.VMEM((nz, y_steps, 2, half_rows, model), BF16),
            pltpu.VMEM((z_steps, 2, half_rows, model), BF16),
            pltpu.VMEM((nz, y_mid, 2, half_rows if ny > 2 else 16, model), BF16),
            pltpu.VMEM((z_steps, 2, half_rows, model), BF16),
            dma((nz, ny, 2)), dma((n_expert,)), dma((n_expert,)), dma((2, n_expert)), dma((2, n_expert)), dma((3,)), dma((3,)),
            dma((nz, y_steps, 2)), dma((nz, y_steps, 2)), dma((z_steps, 2)), dma((z_steps, 2)),
            dma((peers,)), dma((peers,)), dma((n_expert,)), dma((n_expert,)),
        ],
        compiler_params=pltpu.CompilerParams(
            collective_id=cid, has_side_effects=True, vmem_limit_bytes=56 << 20
        ),
        cost_estimate=pl.CostEstimate(
            flops=10 * heads * rows * rows * 256,
            bytes_accessed=8 * rows * 256,
            transcendentals=heads * rows * rows,
        ),
        name="attend_back",
    )(low, high, key_pos, query, key, key_t, value, attended, lse, cosine, sine, made, out_part, d_att)


def finish_kernel(
    n_dp, nz, ny, q_cols, qkv, proj, small, into, out_of,
    qkv_rows, proj_rows, small_sum, into_wide, out_of_wide,
    qkv_in, small_in, proj_in, own_qkv, own_proj, own_small, qkv_all, proj_all, small_all,
    dp_send, dp_recv, ring_send, ring_recv, part_send, part_recv, keep_sem,
):
    z, y = places(nz, ny)
    me, group = lax.axis_index("expert"), lax.axis_index("dp")
    n_expert = nz * ny
    barrier = pltpu.get_barrier_semaphore()
    near = [{"dp": lax.rem(group + k, n_dp)} for k in range(1, n_dp)]
    near += [{"expert": lax.rem(me + k, n_expert)} for k in range(1, n_expert)]
    for other in near:
        pl.semaphore_signal(barrier, inc=1, device_id=other, device_id_type=MESH)
    pl.semaphore_wait(barrier, len(near))

    arrays = {0: (qkv, qkv_in, own_qkv), 2: (small, small_in, own_small)}

    def across(k, a):
        source, target, _ = arrays[a]
        other = lax.rem(group + k, n_dp)
        return pltpu.make_async_remote_copy(
            src_ref=source.at[other], dst_ref=target.at[k - 1],
            send_sem=dp_send.at[k - 1, a], recv_sem=dp_recv.at[k - 1, a],
            device_id={"dp": other}, device_id_type=MESH,
        )

    rings = ((own_qkv, qkv_all), (own_proj, proj_all), (own_small, small_all))

    def origin(s, t, h):
        sign = -1 if h == 0 else 1
        return device(z + sign * s, y + sign * t, nz, ny)

    def ring_copy(s, t, h, s2, t2, a):
        own, everyone = rings[a]
        of = origin(s, t, h)
        rows = own.shape[0] // 2 if a < 2 else own.shape[0]
        part = pl.ds(h * rows, rows)
        source = own.at[part] if s == 0 and t == 0 else everyone.at[of, part]
        step = 1 if h == 0 else -1
        to = device(z + step, y, nz, ny) if t2 == 0 else device(z, y + step, nz, ny)
        return pltpu.make_async_remote_copy(
            src_ref=source, dst_ref=everyone.at[of, part],
            send_sem=ring_send.at[s2, t2, h, a], recv_sem=ring_recv.at[s2, t2, h, a],
            device_id={"expert": to}, device_id_type=MESH,
        )

    def arrive(s, t, h, a):
        own, everyone = rings[a]
        rows = own.shape[0] // 2 if a < 2 else own.shape[0]
        place = everyone.at[origin(s, t, h), pl.ds(h * rows, rows)]
        pltpu.make_async_remote_copy(
            src_ref=place, dst_ref=place,
            send_sem=ring_send.at[s, t, h, a], recv_sem=ring_recv.at[s, t, h, a],
            device_id={"expert": device(z + 1, y, nz, ny)}, device_id_type=MESH,
        ).wait_recv()

    sent, keeps = [], []

    def start(*key):
        copy = ring_copy(*key)
        copy.start()
        sent.append(copy)

    def begin(moves):
        for a in sorted({a for _, a in moves}):
            own, everyone = rings[a]
            keeps.append(pltpu.make_async_copy(own, everyone.at[me], keep_sem.at[a]))
            keeps[-1].start()
        for h, a in moves:
            if nz > 1:
                start(0, 0, h, 1, 0, a)
            if ny > 1:
                start(0, 0, h, 0, 1, a)

    def along_z(moves):
        for s in range(1, nz):
            for h, a in moves:
                arrive(s, 0, h, a)
                if s + 1 < nz:
                    start(s, 0, h, s + 1, 0, a)
                if ny > 1:
                    start(s, 0, h, s, 1, a)

    def along_y(moves):
        for t in range(1, ny):
            for s in range(nz):
                for h, a in moves:
                    arrive(s, t, h, a)
                    if t + 1 < ny:
                        start(s, t, h, s, t + 1, a)

    def part_copy(k):
        other = lax.rem(me + k, n_expert)
        return pltpu.make_async_remote_copy(
            src_ref=proj.at[other], dst_ref=proj_in.at[k - 1],
            send_sem=part_send.at[k - 1], recv_sem=part_recv.at[k - 1],
            device_id={"expert": other}, device_id_type=MESH,
        )

    first, second = [(0, 0), (1, 0), (0, 2)], [(0, 1), (1, 1)]
    for k in range(1, n_dp):
        for a in arrays:
            across(k, a).start()
    for k in range(1, n_expert):
        part_copy(k).start()
    for e in range(into.shape[0]):
        into_wide[e] = into[e].astype(F32)
        out_of_wide[e] = out_of[e].astype(F32)
    for a, (source, target, own) in arrays.items():
        total = source[group].astype(F32)
        for k in range(1, n_dp):
            across(k, a).wait_recv()
            total += target[k - 1].astype(F32)
        own[...] = total.astype(own.dtype)
    begin(first)
    total = proj[me].astype(F32)
    for k in range(1, n_expert):
        part_copy(k).wait_recv()
        total += proj_in[k - 1].astype(F32)
    own_proj[...] = total.astype(BF16)
    begin(second)
    along_z(first + second)
    along_y(first + second)
    for copy in keeps:
        copy.wait()
    total = small_all[0]
    for other in range(1, n_expert):
        total += small_all[other]
    small_sum[...] = total
    alike = max(n_expert // KV_HEADS, 1)
    pieces = [qkv_all[m, :, :q_cols].astype(F32) for m in range(n_expert)]
    for first in (q_cols, q_cols + HEAD_DIM):
        for head in range(KV_HEADS):
            total = qkv_all[head * alike, :, first : first + HEAD_DIM].astype(F32)
            for more in range(1, alike):
                total += qkv_all[head * alike + more, :, first : first + HEAD_DIM].astype(F32)
            pieces.append(total)
    outs = [proj_all[m].astype(F32) for m in range(n_expert)]
    for target, pieces in ((qkv_rows, pieces), (proj_rows, outs)):
        lay(target, pieces)
    for copy in sent:
        copy.wait_send()
    for k in range(1, n_expert):
        part_copy(k).wait_send()
    for k in range(1, n_dp):
        for a in arrays:
            across(k, a).wait_send()


def lay(target, pieces):
    at = 0
    while pieces:
        block = [pieces.pop(0)]
        if block[0].shape[1] % 128:
            block.append(pieces.pop(0))
        joined = jnp.concatenate(block, axis=1) if len(block) > 1 else block[0]
        target[:, at : at + joined.shape[1]] = joined
        at += joined.shape[1]


def finish_sums(qkv, proj, small, into, out_of, q_cols, n_expert, cid):
    nz, ny = grid_of(n_expert)
    n_dp = qkv.shape[0]
    whole = pl.BlockSpec(memory_space=pltpu.VMEM)
    dma = pltpu.SemaphoreType.DMA
    peers = max(n_dp - 1, 1)
    return pl.pallas_call(
        functools.partial(finish_kernel, n_dp, nz, ny, q_cols),
        out_shape=[
            jax.ShapeDtypeStruct((qkv.shape[1], (HEADS + 2 * KV_HEADS) * HEAD_DIM), F32),
            jax.ShapeDtypeStruct((proj.shape[1], n_expert * proj.shape[2]), F32),
            jax.ShapeDtypeStruct(small.shape[1:], F32),
            jax.ShapeDtypeStruct(into.shape, F32),
            jax.ShapeDtypeStruct(out_of.shape, F32),
        ],
        in_specs=[whole] * 5,
        out_specs=[whole] * 5,
        scratch_shapes=[
            pltpu.VMEM((peers,) + qkv.shape[1:], BF16),
            pltpu.VMEM((peers,) + small.shape[1:], F32),
            pltpu.VMEM((n_expert - 1,) + proj.shape[1:], BF16),
            pltpu.VMEM(qkv.shape[1:], BF16),
            pltpu.VMEM(proj.shape[1:], BF16),
            pltpu.VMEM(small.shape[1:], F32),
            pltpu.VMEM((n_expert,) + qkv.shape[1:], BF16),
            pltpu.VMEM(proj.shape, BF16),
            pltpu.VMEM((n_expert,) + small.shape[1:], F32),
            dma((peers, 3)), dma((peers, 3)), dma((nz, ny, 2, 3)), dma((nz, ny, 2, 3)),
            dma((n_expert - 1,)), dma((n_expert - 1,)), dma((3,)),
        ],
        compiler_params=pltpu.CompilerParams(
            collective_id=cid, has_side_effects=True, vmem_limit_bytes=40 << 20
        ),
        name="finish_sums",
    )(qkv, proj, small, into, out_of)


def experts_kernel(
    nz, ny, own, named, router, cotangent, weight_in, weight_out,
    back, d_gate, made, grads_in, grads_out,
    rows_buf, cot_buf, in_buf, out_buf, hid_buf, gu_buf, part_buf, made_buf, gin_buf, gout_buf,
    gate_out, gate_in, from_y, from_z, to_y, to_z,
    load_sem, cot_sem, made_sem, grad_sem, send_sem, recv_sem, gate_send, gate_recv,
    send_y, recv_y, send_z, recv_z,
):
    z, y = places(nz, ny)
    me = lax.axis_index("expert")
    n_expert = nz * ny
    tok_rows, width = own.shape
    half = tok_rows // 2
    step_rows = ny * tok_rows
    exp_dev, ff, _ = out_buf.shape
    experts = named.shape[1]

    barrier = pltpu.get_barrier_semaphore()
    for k in range(1, n_expert):
        pl.semaphore_signal(
            barrier, inc=1, device_id={"expert": lax.rem(me + k, n_expert)}, device_id_type=MESH
        )
    pl.semaphore_wait(barrier, n_expert - 1)

    def owner(s, t, h):
        sign = -1 if h == 0 else 1
        return device(z + sign * s, y + sign * t, nz, ny)

    def piece(s, t, h):
        return pl.ds(pl.multiple_of(owner(s, t, h) * tok_rows + h * half, half), half)

    def slot(s, t, h):
        return pl.ds(((s * ny + t) * 2 + h) * half, half)

    def near(along_z, h):
        step = 1 if h == 0 else -1
        to = device(z + step, y, nz, ny) if along_z else device(z, y + step, nz, ny)
        return {"expert": to}

    def row_copy(s, t, h, s2, t2):
        source = own.at[pl.ds(h * half, half)] if s == 0 and t == 0 else rows_buf.at[slot(s, t, h)]
        return pltpu.make_async_remote_copy(
            src_ref=source, dst_ref=rows_buf.at[slot(s2, t2, h)],
            send_sem=send_sem.at[s2, t2, h], recv_sem=recv_sem.at[s2, t2, h],
            device_id=near(t2 == 0, h), device_id_type=MESH,
        )

    def arrive(s, t, h):
        if t == 0:
            row_copy(s - 1, 0, h, s, 0).wait_recv()
        else:
            row_copy(s, t - 1, h, s, t).wait_recv()

    sent = []

    def start(*key):
        copy = row_copy(*key)
        copy.start()
        sent.append(copy)

    for h in range(2):
        start(0, 0, h, 1, 0)
    if ny > 1:
        for h in range(2):
            start(0, 0, h, 0, 1)
    loads = [
        pltpu.make_async_copy(weight_in, in_buf, load_sem.at[0]),
        pltpu.make_async_copy(weight_out, out_buf, load_sem.at[1]),
    ]
    for copy in loads:
        copy.start()
    cots = {
        (s, t, h): pltpu.make_async_copy(
            cotangent.at[piece(s, t, h)], cot_buf.at[slot(s, t, h)], cot_sem.at[s, t, h]
        )
        for s in range(nz) for t in range(ny) for h in range(2)
    }
    for copy in cots.values():
        copy.start()
    rows_buf[0:tok_rows, :] = own[...]
    for copy in loads:
        copy.wait()

    lane = lax.broadcasted_iota(jnp.int32, (step_rows, experts), 1)
    wide_lane = lax.broadcasted_iota(jnp.int32, (step_rows, 128), 1)
    tile = 256

    def compute(s):
        rows = pl.ds(s * step_rows, step_rows)
        picked = jnp.concatenate(
            [named[piece(s, t, h), :] for t in range(ny) for h in range(2)], axis=0
        ) > 0.5
        logits = jnp.where(picked, dot(rows_buf[rows, :], router[...], 1, 1), MASKED)
        powers = jnp.exp(logits - jnp.max(logits, axis=1, keepdims=True))
        powers = jnp.where(picked, powers, 0.0)
        gates = powers / jnp.sum(powers, axis=1, keepdims=True)
        found = jnp.zeros((step_rows, 128), F32)
        for e in range(exp_dev):
            weight = jnp.sum(
                jnp.where(lane == me * exp_dev + e, gates, 0.0), axis=1, keepdims=True
            )

            def hidden_step(j, total):
                at = pl.multiple_of(j * tile, tile)
                cols, late = pl.ds(at, tile), pl.ds(pl.multiple_of(ff + at, tile), tile)
                gate_pre = dot(rows_buf[rows, :], in_buf[e, :, cols])
                up_pre = dot(rows_buf[rows, :], in_buf[e, :, late])
                d_plain = dot(cot_buf[rows, :], out_buf[e, cols, :], 1, 1)
                sigmoid = jax.nn.sigmoid(gate_pre)
                active = gate_pre * sigmoid
                hidden = active * up_pre
                hid_buf[e, rows, cols] = (weight * hidden).astype(BF16)
                d_hidden = weight * d_plain
                gu_buf[e, rows, cols] = (
                    d_hidden * up_pre * sigmoid * (1.0 + gate_pre * (1.0 - sigmoid))
                ).astype(BF16)
                gu_buf[e, rows, late] = (d_hidden * active).astype(BF16)
                return total + jnp.sum(hidden * d_plain, axis=1, keepdims=True)

            total = lax.fori_loop(0, ff // tile, hidden_step, jnp.zeros((step_rows, 1), F32))
            found += jnp.where(wide_lane == me * exp_dev + e, total, 0.0)

        @pl.loop(0, width // tile)
        def _(n):
            cols = pl.ds(pl.multiple_of(n * tile, tile), tile)
            d_rows = dot(gu_buf[0, rows, :], in_buf[0, cols, :], 1, 1)
            for e in range(1, exp_dev):
                d_rows += dot(gu_buf[e, rows, :], in_buf[e, cols, :], 1, 1)
            part_buf[rows, cols] = d_rows.astype(BF16)
            made_sum = dot(hid_buf[0, rows, :], out_buf[0, :, cols])
            for e in range(1, exp_dev):
                made_sum += dot(hid_buf[e, rows, :], out_buf[e, :, cols])
            made_buf[rows, cols] = made_sum.astype(BF16)

        for t in range(ny):
            for h in range(2):
                low = (t * 2 + h) * half
                gate_out[s, t, h] = found[low : low + half, :].T[:experts, :]
                if s or t:
                    gate_copy(s, t, h).start()
                made_copy(s, t, h).start()

    def gate_copy(s, t, h):
        return pltpu.make_async_remote_copy(
            src_ref=gate_out.at[s, t, h], dst_ref=gate_in.at[s, t, h],
            send_sem=gate_send.at[s, t, h], recv_sem=gate_recv.at[s, t, h],
            device_id={"expert": owner(s, t, h)}, device_id_type=MESH,
        )

    def made_copy(s, t, h):
        return pltpu.make_async_copy(
            made_buf.at[slot(s, t, h)], made.at[piece(s, t, h)], made_sem.at[s, t, h]
        )

    def part(r, t, h):
        return slot((r + 1) % nz, (t + 1) % ny, h)

    def y_copy(r, t, h):
        source = part_buf.at[part(r, 0, h)] if t == 0 else to_y.at[r, t - 1, h]
        return pltpu.make_async_remote_copy(
            src_ref=source, dst_ref=from_y.at[r, t, h],
            send_sem=send_y.at[r, t, h], recv_sem=recv_y.at[r, t, h],
            device_id=near(False, h), device_id_type=MESH,
        )

    def z_copy(r, h):
        return pltpu.make_async_remote_copy(
            src_ref=to_z.at[r, h], dst_ref=from_z.at[r, h],
            send_sem=send_z.at[r, h], recv_sem=recv_z.at[r, h],
            device_id=near(True, h), device_id_type=MESH,
        )

    def first_y(r):
        if ny > 1:
            for h in range(2):
                y_copy(r, 0, h).start()

    def finish(r):
        for t in range(1, ny - 1):
            for h in range(2):
                y_copy(r, t - 1, h).wait_recv()
                to_y[r, t - 1, h] = (
                    part_buf[part(r, t, h), :].astype(F32) + from_y[r, t - 1, h].astype(F32)
                ).astype(BF16)
                y_copy(r, t, h).start()
        for h in range(2):
            total = part_buf[part(r, ny - 1, h), :].astype(F32)
            if ny > 1:
                y_copy(r, ny - 2, h).wait_recv()
                total += from_y[r, ny - 2, h].astype(F32)
            if r > 0:
                z_copy(r - 1, h).wait_recv()
                total += from_z[r - 1, h].astype(F32)
            if r < nz - 1:
                to_z[r, h] = total.astype(BF16)
                z_copy(r, h).start()
            else:
                back[h * half : (h + 1) * half, :] = total

    def forward(s):
        for h in range(2):
            arrive(s, 0, h)
            if s + 1 < nz:
                start(s, 0, h, s + 1, 0)
            if ny > 1:
                start(s, 0, h, s, 1)

    def whole_step(s):
        for t in range(1, ny):
            for h in range(2):
                arrive(s, t, h)
                if t + 1 < ny:
                    start(s, t, h, s, t + 1)
        for t in range(ny):
            for h in range(2):
                cots[s, t, h].wait()
        compute(s)

    for s in range(nz):
        if s + 1 < nz:
            forward(s + 1)
        whole_step(s)
        if s > 0:
            first_y(s - 1)
        if s > 1:
            finish(s - 2)
    first_y(nz - 1)

    chunk = gin_buf.shape[2]

    def grad_step(i):
        cols = pl.ds(pl.multiple_of(i * tile, tile), tile)
        for e in range(exp_dev):
            found = dot(rows_buf[:, cols], gu_buf[e], 0, 0).astype(BF16)
            for c in range(tile // chunk):
                gin_buf[i * (tile // chunk) + c, e] = found[c * chunk : (c + 1) * chunk, :]

    def grad_out_step(i):
        cols = pl.ds(pl.multiple_of(i * tile, tile), tile)
        for e in range(exp_dev):
            found = dot(hid_buf[e, :, cols], cot_buf[...], 0, 0).astype(BF16)
            for c in range(width // chunk):
                gout_buf[c, e, cols, :] = found[:, c * chunk : (c + 1) * chunk]

    pl.loop(0, ff // tile)(grad_out_step)
    gout_copy = pltpu.make_async_copy(gout_buf, grads_out, grad_sem.at[0])
    gout_copy.start()
    if nz > 1:
        finish(nz - 2)
    pl.loop(0, width // tile)(grad_step)
    gin_copy = pltpu.make_async_copy(gin_buf, grads_in, grad_sem.at[1])
    gin_copy.start()
    finish(nz - 1)
    for h in range(2):
        gate_sum = gate_out[0, 0, h]
        for s in range(nz):
            for t in range(ny):
                if s or t:
                    gate_copy(s, t, h).wait_recv()
                    gate_sum += gate_in[s, t, h]
        d_gate[h] = gate_sum
    for copy in sent:
        copy.wait_send()
    for s in range(nz):
        for h in range(2):
            for t in range(ny):
                made_copy(s, t, h).wait()
                if s or t:
                    gate_copy(s, t, h).wait_send()
            for t in range(ny - 1):
                y_copy(s, t, h).wait_send()
            if s < nz - 1:
                z_copy(s, h).wait_send()
    gout_copy.wait()
    gin_copy.wait()


def experts_pass(own, named, router, cotangent, weight_in, weight_out, n_dp, n_expert, cid):
    nz, ny = grid_of(n_expert)
    tok_rows, width = own.shape
    exp_dev, ff, _ = weight_out.shape
    half, group = tok_rows // 2, tok_rows * n_expert
    experts = named.shape[1]
    whole, anywhere = pl.BlockSpec(memory_space=pltpu.VMEM), pl.BlockSpec(memory_space=pl.ANY)
    dma = pltpu.SemaphoreType.DMA
    ring = dma((nz, ny, 2))
    y_steps, y_mid, z_steps = max(ny - 1, 1), max(ny - 2, 1), max(nz - 1, 1)
    return pl.pallas_call(
        functools.partial(experts_kernel, nz, ny),
        out_shape=[
            jax.ShapeDtypeStruct((tok_rows, width), F32),
            jax.ShapeDtypeStruct((2, experts, half), F32),
            jax.ShapeDtypeStruct((group, width), BF16),
            jax.ShapeDtypeStruct((n_dp, exp_dev, width // n_dp, 2 * ff), BF16),
            jax.ShapeDtypeStruct((n_dp, exp_dev, ff, width // n_dp), BF16),
        ],
        in_specs=[whole, whole, whole, anywhere, anywhere, anywhere],
        out_specs=[whole, whole, anywhere, anywhere, anywhere],
        scratch_shapes=[
            pltpu.VMEM((group, width), BF16),
            pltpu.VMEM((group, width), BF16),
            pltpu.VMEM((exp_dev, width, 2 * ff), BF16),
            pltpu.VMEM((exp_dev, ff, width), BF16),
            pltpu.VMEM((exp_dev, group, ff), BF16),
            pltpu.VMEM((exp_dev, group, 2 * ff), BF16),
            pltpu.VMEM((group, width), BF16),
            pltpu.VMEM((group, width), BF16),
            pltpu.VMEM((n_dp, exp_dev, width // n_dp, 2 * ff), BF16),
            pltpu.VMEM((n_dp, exp_dev, ff, width // n_dp), BF16),
            pltpu.VMEM((nz, ny, 2, experts, half), F32),
            pltpu.VMEM((nz, ny, 2, experts, half), F32),
            pltpu.VMEM((nz, y_steps, 2, half, width), BF16),
            pltpu.VMEM((z_steps, 2, half, width), BF16),
            pltpu.VMEM((nz, y_mid, 2, half if ny > 2 else 16, width), BF16),
            pltpu.VMEM((z_steps, 2, half, width), BF16),
            dma((2,)), ring, ring, dma((2,)), ring, ring, ring, ring,
            dma((nz, y_steps, 2)), dma((nz, y_steps, 2)), dma((z_steps, 2)), dma((z_steps, 2)),
        ],
        compiler_params=pltpu.CompilerParams(
            collective_id=cid, has_side_effects=True, vmem_limit_bytes=60 << 20
        ),
        cost_estimate=pl.CostEstimate(
            flops=18 * exp_dev * group * width * ff,
            bytes_accessed=16 * group * width,
            transcendentals=exp_dev * group * ff,
        ),
        name="experts_pass",
    )(own, named, router, cotangent, weight_in, weight_out)


def gather(values, name, axis=0):
    return lax.all_gather(values, name, axis=axis, tiled=True)


def local(
    hidden_in, d_out, gain_attn, w_qkv, w_o, gain_moe, w_router, w_in, w_out,
    seq_lengths, assign, routes,
):
    tok_rows, width = hidden_in.shape
    exp_dev, _, ff_two = w_in.shape
    ff = ff_two // 2
    n_expert = lax.axis_size("expert")
    me = lax.axis_index("expert")
    experts = exp_dev * n_expert
    group_rows = tok_rows * n_expert
    q_per = HEADS // n_expert
    share = GROUPS // q_per
    q_cols = q_per * HEAD_DIM
    k_base = HEADS * HEAD_DIM
    v_base = k_base + KV_HEADS * HEAD_DIM
    cols = q_cols + 2 * HEAD_DIM

    n_dp = lax.axis_size("dp")
    wide = width // n_dp
    kv_head = (me * q_per) // GROUPS
    heads_part = jnp.concatenate(
        [
            lax.dynamic_slice_in_dim(w_qkv, me * q_cols, q_cols, 1),
            lax.dynamic_slice_in_dim(w_qkv, k_base + kv_head * HEAD_DIM, HEAD_DIM, 1),
            lax.dynamic_slice_in_dim(w_qkv, v_base + kv_head * HEAD_DIM, HEAD_DIM, 1),
        ],
        axis=1,
    )
    few = 2 + experts
    pack = jnp.concatenate(
        [gain_attn[None], gain_moe[None], w_router.T, jnp.zeros((-few % 16, wide), BF16)], axis=0
    )
    top = routes.shape[1]
    meta = jnp.concatenate(
        [assign, routes.T, jnp.zeros((-(1 + top) % 8, tok_rows), jnp.int32)], axis=0
    )
    meta = meta.reshape(meta.shape[0], 2, tok_rows // 2).transpose(1, 0, 2)
    qkv_full = gather(w_qkv, "dp")
    hidden_all, meta, w_heads, pack = first_gather(
        hidden_in, meta, heads_part, pack, n_dp, n_expert, 0
    )
    w_heads = w_heads.reshape(width, cols)
    pack = pack.transpose(1, 0, 2).reshape(-1, width)
    gain_one, gain_two = pack[0].astype(F32), pack[1].astype(F32)
    router_t = pack[2:few]
    position = meta[:, :, 0].reshape(group_rows)
    routes_all = meta[:, :, 1 : 1 + top]
    named = jnp.any(
        routes_all[:, :, :, None, :] == jnp.arange(experts, dtype=jnp.int32)[:, None], axis=2
    ).transpose(0, 1, 3, 2).reshape(group_rows, experts)
    stream_in = hidden_in.astype(F32)
    proj_full = gather(w_o, "dp")
    weight_in = gather(w_in, "dp", axis=1)
    weight_out = gather(w_out, "dp", axis=2)
    lengths = seq_lengths[0]
    order = jnp.arange(lengths.shape[0], dtype=jnp.int32)
    ends = jnp.sum(jnp.where(order[None, :] <= order[:, None], lengths[None, :], 0), axis=1)
    starts = ends - lengths
    seq_id = jnp.sum((position[None, :] >= ends[:, None]).astype(jnp.int32), axis=0)
    picks = seq_id[None, :] == jnp.arange(lengths.shape[0], dtype=jnp.int32)[:, None]
    start_of = jnp.sum(jnp.where(picks, starts[:, None], 0), axis=0)
    rot_pos = position - start_of
    half = HEAD_DIM // 2
    frequency = ROPE_BASE ** (-(jnp.arange(half).astype(F32) * (2.0 / HEAD_DIM)))
    angles = frequency[:, None] * rot_pos.astype(F32)[None, :]
    cosine, sine = jnp.cos(angles), jnp.sin(angles)
    low, high = start_of[None, :], position[None, :]
    key_pos = jnp.broadcast_to(position[:, None], (group_rows, low_tile(group_rows)))

    heads_out, lse, attended, d_out_all, normed_all, query, key, key_t, value = attend(
        low, high, key_pos, cosine, sine, gain_one[None], w_heads, hidden_all, d_out, q_per, 6
    )
    attended = attended.reshape(n_expert * q_cols, tok_rows)
    mid_stream = stream_in + dot(attended, proj_full, 0, 0)
    normed_two = rms_norm(mid_stream, gain_two).astype(BF16)

    d_back, d_gate, made, grads_in, grads_out = experts_pass(
        normed_two, named.astype(F32), router_t, d_out_all, weight_in, weight_out, n_dp, n_expert, 1
    )
    d_gate = d_gate.transpose(0, 2, 1).reshape(tok_rows, experts)
    own_named = jnp.any(
        routes[:, :, None] == jnp.arange(experts, dtype=jnp.int32)[None, None, :], axis=1
    )
    own_gates = jax.nn.softmax(
        jnp.where(own_named, dot(normed_two, router_t, 1, 1), -jnp.inf), axis=1
    )
    d_logits = (
        own_gates * (d_gate - jnp.sum(own_gates * d_gate, axis=1, keepdims=True))
    ).astype(BF16)
    grad_router = dot(d_logits, normed_two, 0, 0)
    d_normed_two = d_back + dot(d_logits, router_t)
    _, norm_two_back = jax.vjp(rms_norm, mid_stream, gain_two)
    d_mid_norm, grad_gain_two = norm_two_back(d_normed_two)
    d_mid = d_out.astype(F32) + d_mid_norm

    d_attn = d_mid.astype(BF16)
    d_attn, grads_in, grads_out, made = lax.optimization_barrier((d_attn, grads_in, grads_out, made))
    grad_w_in = lax.psum_scatter(grads_in, "dp", scatter_dimension=0, tiled=True)
    grad_w_out = lax.psum_scatter(grads_out, "dp", scatter_dimension=0, tiled=True)
    d_att = dot(proj_full, d_attn, 1, 1).astype(BF16).reshape(n_expert, q_cols, tok_rows)
    part_o = dot(attended, d_attn).astype(BF16).reshape(n_dp, wide, width)
    d_own, d_projected, returned, sum_o = attend_back(
        low, high, key_pos, query, key, key_t, value, heads_out, lse,
        cosine, sine, made, part_o, d_att, tok_rows, 4,
    )
    layer_out = (mid_stream + returned).astype(BF16)
    if share > 1:
        fan = lambda part: jnp.repeat(part.reshape(width, KV_HEADS, HEAD_DIM), share, axis=1).reshape(width, -1)
        qkv_full = jnp.concatenate(
            [qkv_full[:, :k_base], fan(qkv_full[:, k_base:v_base]), fan(qkv_full[:, v_base:])], axis=1
        )
    d_normed_one = dot(d_own, qkv_full, 0, 1)
    _, norm_one_back = jax.vjp(rms_norm, stream_in, gain_one)
    d_in_norm, grad_gain_one = norm_one_back(d_normed_one)
    grad_in = d_mid + d_in_norm

    part_qkv = dot(
        normed_all, d_projected.transpose(1, 0, 2).reshape(cols, group_rows), 0, 1
    ).astype(BF16).reshape(n_dp, wide, cols)
    small = jnp.concatenate(
        [grad_gain_one[None], grad_gain_two[None], grad_router, jnp.zeros((-few % 8, width), F32)], axis=0
    )
    small = small.reshape(-1, n_dp, wide).transpose(1, 0, 2)
    grad_w_qkv, grad_w_o, small, grad_w_in, grad_w_out = finish_sums(
        part_qkv, sum_o, small, grad_w_in[0], grad_w_out[0], q_cols, n_expert, 5
    )
    return (
        layer_out, grad_in, small[0], grad_w_qkv, grad_w_o, small[1], small[2:few].T,
        grad_w_in, grad_w_out,
    )


def solution(mesh):
    rows = P(("dp", "expert"), None)
    in_specs = (
        rows, rows, P("dp"), P("dp", None), P("dp", None), P("dp"), P("dp", None),
        P("expert", "dp", None), P("expert", None, "dp"), P("dp", None), P("dp", "expert"), rows,
    )
    out_specs = (
        rows, rows, P("dp"), P("dp", None), P("dp", None), P("dp"), P("dp", None),
        P("expert", "dp", None), P("expert", None, "dp"),
    )
    return jax.shard_map(local, mesh=mesh, in_specs=in_specs, out_specs=out_specs, check_vma=False)
```
